32 devices in a mesh: dp: 16 (over z, y, x), section: 2 (over core).
Axes of the slice: x: 2, y: 2, z: 4, core: 2. Of those that a mesh axis runs over, the one named last changes fastest.
Arguments:
- tokens: bfloat16 [32, 384, 768], P('dp'), may hold values from -6 to 6
- cotangent: float32 [32, 384, 768], P('dp'), may hold values from -6 to 6
- bucket: int32 [32], P('dp'), may hold values from 0 to 2, as said below
- batch_size: int32 [32], P('dp'), may hold values from 1 to 6, as said below
- lengths: int32 [32, 6], P('dp'), may hold values from 0 to 192, as said below
- query_weight: bfloat16 [2, 768, 768], P('section'), may hold values from -0.21875 to 0.21875
- query_offset: float32 [2, 768], P('section'), may hold values from -3 to 3
- keys_weight: bfloat16 [2, 768, 768], P('section'), may hold values from -0.21875 to 0.21875
- value_weight: bfloat16 [2, 768, 768], P('section'), may hold values from -0.21875 to 0.21875
- value_offset: float32 [2, 768], P('section'), may hold values from -3 to 3
- mixer_weight: bfloat16 [2, 768, 768], P('section'), may hold values from -1.75 to 1.75
- mixer_offset: float32 [2, 768], P('section'), may hold values from -3 to 3
- first_gain: float32 [2, 768], P('section'), may hold values from 0.25 to 1.75
- first_shift: float32 [2, 768], P('section'), may hold values from -3 to 3
- inner_weight: bfloat16 [2, 768, 3072], P('section'), may hold values from -0.21875 to 0.21875
- inner_offset: float32 [2, 3072], P('section'), may hold values from -3 to 3
- outer_weight: bfloat16 [2, 3072, 768], P('section'), may hold values from -0.15625 to 0.15625
- outer_offset: float32 [2, 768], P('section'), may hold values from -3 to 3
- second_gain: float32 [2, 768], P('section'), may hold values from 0.25 to 1.75
- second_shift: float32 [2, 768], P('section'), may hold values from -3 to 3
Outputs:
- layer_out: bfloat16 [2, 32, 384, 768], P('section', 'dp')
- input_grad: float32 [2, 32, 384, 768], P('section', 'dp')
- query_weight_gradient: float32 [2, 768, 768], P('section', 'dp')
- query_offset_gradient: float32 [2, 768], P('section', 'dp')
- keys_weight_gradient: float32 [2, 768, 768], P('section', 'dp')
- value_weight_gradient: float32 [2, 768, 768], P('section', 'dp')
- value_offset_gradient: float32 [2, 768], P('section', 'dp')
- mixer_weight_gradient: float32 [2, 768, 768], P('section', 'dp')
- mixer_offset_gradient: float32 [2, 768], P('section', 'dp')
- first_gain_gradient: float32 [2, 768], P('section', 'dp')
- first_shift_gradient: float32 [2, 768], P('section', 'dp')
- inner_weight_gradient: float32 [2, 768, 3072], P('section', 'dp')
- inner_offset_gradient: float32 [2, 3072], P('section', 'dp')
- outer_weight_gradient: float32 [2, 3072, 768], P('section', 'dp')
- outer_offset_gradient: float32 [2, 768], P('section', 'dp')
- second_gain_gradient: float32 [2, 768], P('section', 'dp')
- second_shift_gradient: float32 [2, 768], P('section', 'dp')
The draws below stay inside these ranges and needn't reach their ends.
Inputs may be any that keep to these rules, and one draw needn't show every extreme that they name: Bucket b holds sequences of more than b * 64 and at most (b + 1) * 64 tokens in 6 // (b + 1) slots of (b + 1) * 64 rows; every bucket occurs. `batch_size`: at most the bucket's slots; the first slots are the used ones; each bucket is full in some micro-batch. `lengths`: 0 for unused slots; a used slot's length lies in its bucket's range, and slot 0 holds exactly (b + 1) * 64 tokens.
All inputs are finite; a program needn't handle non-finite values.
Results may differ from the reference program's by a relative error of at most 0.03.
Values may be sent and summed in bfloat16 or wider, within the bound.
No kernel may reach another device: no remote copies, remote signals or barrier semaphores. Data moves between devices by JAX's collectives and lax.ppermute only.
A program may use at most 256 MiB of HBM per device.

```python
import jax
import jax.numpy as jnp
from jax import lax

D = 768
HEADS = 12
HEAD_DIM = 64
FF = 3072
BUCKET = 64
SLOTS = 6
ROWS = 384
MICRO = 32


def micro_plan(key):
    base = jax.random.fold_in(key, 7)
    key_order, key_bucket, key_spare, key_short = jax.random.split(base, 4)
    index = jnp.arange(MICRO, dtype=jnp.int32)
    order = jax.random.permutation(key_order, 3).astype(jnp.int32)
    random_bucket = jax.random.randint(key_bucket, (MICRO,), 0, 3, dtype=jnp.int32)
    bucket_ids = jnp.where(index < 3, order[jnp.minimum(index, 2)], random_bucket)
    slot_total = SLOTS // (bucket_ids + 1)
    spare = jax.random.randint(key_spare, (MICRO,), 0, 1000, dtype=jnp.int32) % ((slot_total + 1) // 2)
    seq_count = jnp.where(index < 3, slot_total, slot_total - spare)
    seq_span = BUCKET * (bucket_ids + 1)
    shorter = jax.random.randint(key_short, (MICRO, SLOTS), 0, BUCKET, dtype=jnp.int32)
    place = jnp.arange(SLOTS, dtype=jnp.int32)
    seq_lengths = seq_span[:, None] - shorter
    seq_lengths = jnp.where(place[None, :] == 0, seq_span[:, None], seq_lengths)
    seq_lengths = jnp.where(place[None, :] < seq_count[:, None], seq_lengths, 0)
    return (bucket_ids, seq_count, seq_lengths.astype(jnp.int32))


def draw_bucket(key, part):
    return micro_plan(key)[0]


def draw_batch_size(key, part):
    return micro_plan(key)[1]


def draw_lengths(key, part):
    return micro_plan(key)[2]


def steps_of(key, dims, pieces, smallest, largest):
    def one(axis_at, parts):
        heights = jax.random.uniform(jax.random.fold_in(jax.random.fold_in(key, 6), axis_at), (parts,), jnp.float32, smallest / len(pieces), largest / len(pieces))
        return jnp.repeat(jnp.exp(heights), dims[axis_at] // parts).reshape((-1,) + (1,) * (len(dims) - axis_at - 1))

    factor_of = one(*pieces[0])
    for cut in pieces[1:]:
        factor_of = factor_of * one(*cut)
    return factor_of


def noise(stream_key, extent, scale, most, cuts=(), held_as=jnp.bfloat16):
    array = scale * jax.random.normal(stream_key, extent, jnp.float32)
    if cuts:
        array = array * steps_of(stream_key, extent, cuts, -0.22, 0.18)
    return jnp.clip(array, -most, most).astype(held_as)


def setup_inputs(seed: int = 0) -> dict:
    streams_of = jax.random.split(jax.random.key(seed), 21)
    return {
        "tokens": noise(streams_of[0], (MICRO, ROWS, D), 1.0, 6.0, ((0, 16),)),
        "cotangent": noise(streams_of[1], (MICRO, ROWS, D), 1.0, 6.0, ((0, 16),), jnp.float32),
        "bucket": draw_bucket(jax.random.fold_in(streams_of[20], 71), 0),
        "batch_size": draw_batch_size(jax.random.fold_in(streams_of[20], 71), 0),
        "lengths": draw_lengths(jax.random.fold_in(streams_of[20], 71), 0),
        "query_weight": noise(streams_of[5], (2, D, D), D ** -0.5, 0.21875, ((0, 2),)),
        "query_offset": noise(streams_of[6], (2, D), 0.5, 3.0, ((0, 2),), jnp.float32),
        "keys_weight": noise(streams_of[7], (2, D, D), D ** -0.5, 0.21875, ((0, 2),)),
        "value_weight": noise(streams_of[8], (2, D, D), D ** -0.5, 0.21875, ((0, 2),)),
        "value_offset": noise(streams_of[9], (2, D), 0.5, 3.0, ((0, 2),), jnp.float32),
        "mixer_weight": noise(streams_of[10], (2, D, D), (D // 64) ** -0.5, 1.75, ((0, 2),)),
        "mixer_offset": noise(streams_of[11], (2, D), 0.5, 3.0, ((0, 2),), jnp.float32),
        "first_gain": jnp.clip(1.0 + 0.15 * jax.random.normal(streams_of[12], (2, D), jnp.float32), 0.25, 1.75),
        "first_shift": noise(streams_of[13], (2, D), 0.5, 3.0, ((0, 2),), jnp.float32),
        "inner_weight": noise(streams_of[14], (2, D, FF), D ** -0.5, 0.21875, ((0, 2),)),
        "inner_offset": noise(streams_of[15], (2, FF), 0.5, 3.0, ((0, 2),), jnp.float32),
        "outer_weight": noise(streams_of[16], (2, FF, D), (FF // 2) ** -0.5, 0.15625, ((0, 2),)),
        "outer_offset": noise(streams_of[17], (2, D), 0.5, 3.0, ((0, 2),), jnp.float32),
        "second_gain": jnp.clip(1.0 + 0.15 * jax.random.normal(streams_of[18], (2, D), jnp.float32), 0.25, 1.75),
        "second_shift": noise(streams_of[19], (2, D), 0.5, 3.0, ((0, 2),), jnp.float32),
    }


@jax.custom_vjp
def low(v):
    return lax.optimization_barrier(v.astype(jnp.bfloat16)).astype(jnp.float32)

@jax.custom_vjp
def low_back(v):
    return v

def low_keep(v):
    return (low(v), None)

def low_pass(kept, grad):
    return (grad,)

def back_keep(v):
    return (v, None)

def back_low(kept, grad):
    return (low(grad),)
low.defvjp(low_keep, low_pass)
low_back.defvjp(back_keep, back_low)
masked_score = -1000000000.0
norm_epsilon = 1e-06

def both_ways(value):
    return low(low_back(value))

def matmul(left, right):
    return jnp.dot(left, right, precision=lax.Precision.HIGHEST, preferred_element_type=jnp.float32)

def normalize(values, gain, shift):
    center = lax.optimization_barrier(jnp.mean(values, axis=-1, keepdims=True))
    centred = values - center
    spread = lax.optimization_barrier(jnp.mean(centred * centred, axis=-1, keepdims=True))
    return centred * lax.rsqrt(spread + norm_epsilon) * gain + shift

def build_masks(bucket_id, seq_count, seq_lengths, row_count):
    seq_span = BUCKET * (bucket_id + 1)
    position = jnp.arange(row_count, dtype=jnp.int32)
    slot_of = (position // seq_span).astype(jnp.int32)
    inner_place = (position - slot_of * seq_span).astype(jnp.int32)
    slot_ids = jnp.arange(seq_lengths.shape[0], dtype=jnp.int32)
    zero_int = jnp.zeros((), jnp.int32)
    seq_len = lax.optimization_barrier(jnp.sum(jnp.where(slot_of[:, None] == slot_ids[None, :], seq_lengths[None, :].astype(jnp.int32), zero_int), axis=1)).astype(jnp.int32)
    row_valid = (slot_of < seq_count) & (inner_place < seq_len)
    allowed = (slot_of[:, None] == slot_of[None, :]) & row_valid[None, :] | (position[:, None] == position[None, :])
    return (allowed, row_valid.astype(jnp.float32))

def layer(hidden, params, allowed, row_valid):
    w_query, b_query, w_keys, w_value, b_value, w_mixer, b_mixer, gain_one, shift_one, w_inner, b_inner, w_outer, b_outer, gain_two, shift_two = params
    row_count = hidden.shape[0]
    score_scale = HEAD_DIM ** (-0.5)
    hidden_low = low(hidden)
    query = both_ways(matmul(hidden_low, w_query) + b_query).reshape(row_count, HEADS, HEAD_DIM)
    keys_rows = both_ways(matmul(hidden_low, w_keys)).reshape(row_count, HEADS, HEAD_DIM)
    value = both_ways(matmul(hidden_low, w_value) + b_value).reshape(row_count, HEADS, HEAD_DIM)
    scores = jnp.einsum('qhe,khe->hqk', query, keys_rows, precision=lax.Precision.HIGHEST) * score_scale
    scores = low_back(jnp.where(allowed[None], scores, masked_score))
    attention = low(jax.nn.softmax(scores, axis=-1))
    context = jnp.einsum('hqk,khe->qhe', attention, value, precision=lax.Precision.HIGHEST)
    context = both_ways(context.reshape(row_count, HEADS * HEAD_DIM))
    branch = low_back(matmul(context, w_mixer) + b_mixer)
    middle = normalize(hidden + branch, gain_one, shift_one)
    inner = low_back(matmul(low(middle), w_inner) + b_inner)
    active = low(jax.nn.gelu(inner, approximate=False))
    outer = low_back(matmul(active, w_outer) + b_outer)
    return normalize(middle + outer, gain_two, shift_two) * row_valid[:, None]

def reference(tokens, cotangent, bucket, batch_size, lengths, query_weight, query_offset, keys_weight, value_weight, value_offset, mixer_weight, mixer_offset, first_gain, first_shift, inner_weight, inner_offset, outer_weight, outer_offset, second_gain, second_shift):
    stacked = (query_weight, query_offset, keys_weight, value_weight, value_offset, mixer_weight, mixer_offset, first_gain, first_shift, inner_weight, inner_offset, outer_weight, outer_offset, second_gain, second_shift)
    first_params = tuple((piece[0].astype(jnp.float32) for piece in stacked))
    second_params = tuple((piece[1].astype(jnp.float32) for piece in stacked))
    tokens_wide = tokens.astype(jnp.float32)
    nudges = jnp.zeros_like(tokens_wide)

    def forward(inputs, nudge_all, params_one, params_two):

        def step_block(unused, sliced):
            entry, nudge, bucket_id, seq_count, seq_lengths = sliced
            allowed, row_valid = build_masks(bucket_id, seq_count, seq_lengths, entry.shape[0])
            middle_out = low(layer(entry, params_one, allowed, row_valid))
            final_out = layer(low_back(middle_out) + nudge, params_two, allowed, row_valid)
            return (unused, (middle_out, final_out))
        _, results = lax.scan(jax.checkpoint(step_block), jnp.zeros((), jnp.float32), (inputs, nudge_all, bucket, batch_size, lengths))
        return results
    (middle_all, final_all), pullback = jax.vjp(forward, tokens_wide, nudges, first_params, second_params)
    grad_tokens, grad_nudges, grad_first, grad_second = pullback((jnp.zeros_like(middle_all), cotangent.astype(jnp.float32)))
    layer_out = jnp.stack([middle_all, final_all]).astype(jnp.bfloat16)
    input_grad = jnp.stack([grad_tokens, grad_nudges])
    g_qw, g_qo, g_kw, g_vw, g_vo, g_mw, g_mo, g_fg, g_fs, g_iw, g_io, g_ow, g_oo, g_sg, g_ss = tuple((jnp.stack([left, right]) for left, right in zip(grad_first, grad_second)))
    return (layer_out, input_grad, g_qw, g_qo, g_kw, g_vw, g_vo, g_mw, g_mo, g_fg, g_fs, g_iw, g_io, g_ow, g_oo, g_sg, g_ss)
```

```python
import functools
import jax
import jax.numpy as jnp
from jax import lax
from jax.experimental import pallas as pl
from jax.experimental.pallas import tpu as pltpu

HEADS = 12
HEAD_DIM = 64
BUCKET = 64
PAIR = 2 * HEAD_DIM
masked_score = -1000000000.0
norm_epsilon = 1e-06
F32 = jnp.float32
BF16 = jnp.bfloat16
CHUNK = 16
FFN_TILE = 512
ATT_UNROLL = 3


def rows_times(left, right):
    return lax.dot_general(left, right, (((1,), (0,)), ((), ())), preferred_element_type=F32)


def rows_times_transposed(left, right):
    return lax.dot_general(left, right, (((1,), (1,)), ((), ())), preferred_element_type=F32)


def transposed_times(left, right):
    return lax.dot_general(left, right, (((0,), (0,)), ((), ())), preferred_element_type=F32)


def slot_facts(block, span_rows, place, info, base):
    bucket = info[base]
    count = info[base + 1]

    def length_of(slot):
        return jnp.where(slot < count, info[base + 2 + slot], 0)

    if span_rows == 2 * BUCKET:
        return (jnp.full_like(place, block), place, jnp.full_like(place, length_of(block)))
    short = bucket == 0
    first = 3 * block
    slot_short = first + place // BUCKET
    length_short = jnp.where(
        place < BUCKET,
        length_of(first),
        jnp.where(place < 2 * BUCKET, length_of(first + 1), length_of(first + 2)),
    )
    slot = jnp.where(short, slot_short, block)
    inner = jnp.where(short, place % BUCKET, place)
    length = jnp.where(short, length_short, length_of(block))
    return (slot, inner, length)


def fill_masks(span_rows, row_count, info, base, bias_ref, valid_ref, row_base):
    for block in range(row_count // span_rows):
        row_place = lax.broadcasted_iota(jnp.int32, (span_rows, 1), 0)
        key_place = lax.broadcasted_iota(jnp.int32, (1, span_rows), 1)
        row_slot, row_inner, row_length = slot_facts(block, span_rows, row_place, info, base)
        key_slot, key_inner, key_length = slot_facts(block, span_rows, key_place, info, base)
        key_tag = jnp.where(key_inner < key_length, key_slot, -1)
        allowed = (row_slot == key_tag) | (row_place == key_place)
        rows = slice(row_base + block * span_rows, row_base + (block + 1) * span_rows)
        bias_ref[rows, 0:span_rows] = jnp.where(allowed, 0.0, masked_score)
        if valid_ref is not None:
            valid_ref[rows, :] = jnp.where(row_inner < row_length, 1.0, 0.0)


def softmax_rows(scores):
    top = jnp.max(scores, axis=-1, keepdims=True)
    weight = jnp.exp(scores - top)
    return weight * (1.0 / jnp.sum(weight, axis=-1, keepdims=True))


def attend_forward(span_rows, row_count, q_ref, k_ref, v_ref, bias_ref, c_ref):
    blocks = row_count // span_rows

    def one_pair(pair, carry):
        columns = pl.ds(pl.multiple_of(pair * PAIR, PAIR), PAIR)
        lane = lax.broadcasted_iota(jnp.int32, (span_rows, PAIR), 1)
        first_half = lane < HEAD_DIM
        weights = []
        for block in range(blocks):
            rows = slice(block * span_rows, (block + 1) * span_rows)
            query = q_ref[rows, columns] * jnp.asarray(HEAD_DIM ** (-0.5), BF16)
            keys = k_ref[rows, columns]
            zero = jnp.zeros_like(keys)
            bias = bias_ref[rows, 0:span_rows]
            for mine in (first_half, jnp.logical_not(first_half)):
                scores = rows_times_transposed(query, jnp.where(mine, keys, zero)) + bias
                top = jnp.max(scores, axis=-1, keepdims=True)
                weights.append(jnp.exp(scores - top).astype(BF16))
        for block in range(blocks):
            rows = slice(block * span_rows, (block + 1) * span_rows)
            value = v_ref[rows, columns]
            one = jnp.ones_like(value)
            left = rows_times(weights[2 * block], jnp.where(first_half, value, one))
            right = rows_times(weights[2 * block + 1], jnp.where(first_half, one, value))
            above = jnp.where(first_half, left, right)
            below = pltpu.roll(jnp.where(first_half, right, left), HEAD_DIM, 1)
            c_ref[rows, columns] = (above / below).astype(BF16)
        return carry

    lax.fori_loop(0, HEADS // 2, one_pair, 0, unroll=ATT_UNROLL)


def row_moments(values):
    center = jnp.mean(values, axis=-1, keepdims=True)
    centred = values - center
    spread = jnp.mean(centred * centred, axis=-1, keepdims=True)
    return centred, lax.rsqrt(spread + norm_epsilon)


def over_chunks(row_count, body, rows=CHUNK, group=6):
    def step(index, carry):
        for inner in range(group):
            start = pl.multiple_of(index * (rows * group) + inner * rows, rows)
            body(pl.ds(start, rows))
        return carry

    lax.fori_loop(0, row_count // (rows * group), step, 0)


def gelu_with_slope(values):
    cumulative = 0.5 + 0.5 * lax.erf(values * (0.5 ** 0.5))
    density = jnp.exp(values * values * -0.5) * 0.3989422804014327
    return values * cumulative, cumulative + values * density


def at_index(ref, index):
    return ref if index is None else ref.at[index]


def forward_kernel(
    tok_index, info, tok, rx, wq, wk, wv, wm, wi, wo, bq, bv, bm, g1, s1, bi, bo, g2, s2,
    y_o, q_o, k_o, v_o, c_o, a1_o, ml_o, u_o, gp_o, a2_o,
    h_s, wq_s, wk_s, wv_s, wm_s, wi_s, wo_s,
    q_s, k_s, v_s, c_s, a1_s, m_s, ml_s, u_s, gp_s, a2_s, y_s, f0_s, e0_s, e1_s, bias_s, valid_s,
    in_sem, out_sem,
):
    rows, width = h_s.shape
    hidden = wi_s.shape[1]

    @pl.when(info[0] == 1)
    def _():
        loads = []
        for index, (source, target) in enumerate(
            ((wq, wq_s), (wk, wk_s), (wv, wv_s), (wm, wm_s), (wi, wi_s), (wo, wo_s))
        ):
            loads.append(pltpu.make_async_copy(source.at[0], target, in_sem.at[index]))
        own = pltpu.make_async_copy(at_index(tok, tok_index), h_s, in_sem.at[6])
        other = pltpu.make_async_copy(rx, h_s, in_sem.at[6])

        @pl.when(info[1] == 0)
        def _():
            own.start()

        @pl.when(info[1] == 1)
        def _():
            other.start()

        for load in loads[:3]:
            load.start()
        stores = []

        def store(source, target):
            copy = pltpu.make_async_copy(source, target, out_sem.at[len(stores)])
            copy.start()
            stores.append(copy)

        even = info[2] == 1

        @pl.when(even)
        def _():
            fill_masks(2 * BUCKET, rows, info, 2, bias_s, valid_s, 0)

        @pl.when(jnp.logical_not(even))
        def _():
            fill_masks(3 * BUCKET, rows, info, 2, bias_s, valid_s, 0)

        own.wait()
        loads[0].wait()
        loads[3].start()
        q_s[...] = (rows_times(h_s[...], wq_s[...]) + bq[...]).astype(BF16)
        store(q_s, q_o)
        loads[1].wait()
        loads[4].start()
        k_s[...] = rows_times(h_s[...], wk_s[...]).astype(BF16)
        store(k_s, k_o)
        loads[2].wait()
        loads[5].start()
        v_s[...] = (rows_times(h_s[...], wv_s[...]) + bv[...]).astype(BF16)
        store(v_s, v_o)

        @pl.when(even)
        def _():
            attend_forward(2 * BUCKET, rows, q_s, k_s, v_s, bias_s, c_s)

        @pl.when(jnp.logical_not(even))
        def _():
            attend_forward(3 * BUCKET, rows, q_s, k_s, v_s, bias_s, c_s)

        store(c_s, c_o)
        loads[3].wait()
        f0_s[...] = rows_times(c_s[...], wm_s[...])

        def first_norm(part):
            total = h_s[part, :].astype(F32) + (f0_s[part, :] + bm[...])
            a1_s[part, :] = total
            centred, scale = row_moments(total)
            middle = centred * scale * g1[...] + s1[...]
            m_s[part, :] = middle
            ml_s[part, :] = middle.astype(BF16)

        over_chunks(rows, first_norm)
        store(a1_s, a1_o)
        store(ml_s, ml_o)
        loads[4].wait()
        tile = FFN_TILE
        tiles = hidden // tile

        def project(buffer, which):
            columns = pl.ds(pl.multiple_of(which * tile, tile), tile)
            buffer[...] = rows_times(ml_s[...], wi_s[:, columns])

        def activate(buffer, which):
            columns = pl.ds(pl.multiple_of(which * tile, tile), tile)
            offset = bi[:, columns]
            for start in range(0, rows, 32):
                part = slice(start, start + 32)
                value, slope = gelu_with_slope(buffer[part, :] + offset)
                u_s[part, columns] = value.astype(BF16)
                gp_s[part, columns] = slope.astype(BF16)

        project(e0_s, 0)

        def two_tiles(index, carry):
            project(e1_s, 2 * index + 1)
            activate(e0_s, 2 * index)
            project(e0_s, jnp.minimum(2 * index + 2, tiles - 1))
            activate(e1_s, 2 * index + 1)
            return carry

        lax.fori_loop(0, tiles // 2, two_tiles, 0)
        store(u_s, u_o)
        store(gp_s, gp_o)
        loads[5].wait()
        f0_s[...] = rows_times(u_s[...], wo_s[...])

        def second_norm(part):
            total = m_s[part, :] + (f0_s[part, :] + bo[...])
            a2_s[part, :] = total
            centred, scale = row_moments(total)
            y_s[part, :] = ((centred * scale * g2[...] + s2[...]) * valid_s[part, :]).astype(BF16)

        over_chunks(rows, second_norm)
        store(y_s, y_o)
        store(a2_s, a2_o)
        for copy in stores:
            copy.wait()


ANY = pl.BlockSpec(memory_space=pl.ANY)
VM = pl.BlockSpec(memory_space=pltpu.VMEM)
SM = pl.BlockSpec(memory_space=pltpu.SMEM)
VMEM_LIMIT = 63_000 * 1024


def forward_layer(info, tok, tok_index, rx, params):
    wq, bq, wk, wv, bv, wm, bm, g1, s1, wi, bi, wo, bo, g2, s2 = params
    rows, width = rx.shape
    hidden = wi.shape[-1]
    S = jax.ShapeDtypeStruct
    flat = (rows, width)
    wide = (rows, hidden)
    outs = (
        S(flat, BF16), S(flat, BF16), S(flat, BF16), S(flat, BF16), S(flat, BF16),
        S(flat, F32), S(flat, BF16), S(wide, BF16), S(wide, BF16), S(flat, F32),
    )
    V = pltpu.VMEM
    square = (width, width)
    scratch = [
        V(flat, BF16), V(square, BF16), V(square, BF16), V(square, BF16), V(square, BF16),
        V((width, hidden), BF16), V((hidden, width), BF16),
        V(flat, BF16), V(flat, BF16), V(flat, BF16), V(flat, BF16),
        V(flat, F32), V(flat, F32), V(flat, BF16), V(wide, BF16), V(wide, BF16), V(flat, F32), V(flat, BF16),
        V(flat, F32), V((rows, FFN_TILE), F32), V((rows, FFN_TILE), F32), V((rows, 3 * BUCKET), F32), V((rows, 1), F32),
        pltpu.SemaphoreType.DMA((7,)), pltpu.SemaphoreType.DMA((10,)),
    ]
    return pl.pallas_call(
        functools.partial(forward_kernel, tok_index),
        out_shape=outs,
        in_specs=[SM, ANY, ANY] + [ANY] * 6 + [VM] * 9,
        out_specs=[ANY] * 10,
        scratch_shapes=scratch,
        compiler_params=pltpu.CompilerParams(vmem_limit_bytes=VMEM_LIMIT),
        cost_estimate=pl.CostEstimate(flops=2 * rows * width * (4 * width + 2 * hidden), bytes_accessed=30_000_000, transcendentals=rows * hidden * 2),
        name="layer_forward",
    )(info, tok, rx, wq, wk, wv, wm, wi, wo, bq, bv, bm, g1, s1, bi, bo, g2, s2)


def norm_backward(grad, total, gain):
    centred, scale = row_moments(total)
    unit = centred * scale
    spread = grad * gain
    first = jnp.mean(spread, axis=-1, keepdims=True)
    second = jnp.mean(spread * unit, axis=-1, keepdims=True)
    return (spread - first - unit * second) * scale, grad * unit


def fold_rows(values):
    return jnp.sum(values.reshape(values.shape[0] // 8, 8, values.shape[1]), axis=0)


def add_rows(total_ref, values):
    total_ref[...] += fold_rows(values)


def put_blocks(target, product, tile, place, orders, spread_units):
    count = target.shape[1]
    height = product.shape[0] // count
    for block in range(count):
        if spread_units and count > 1:
            unit = block % 4
            dest = tile * (count // 4) + block // 4
        else:
            unit = tile
            dest = block
        if count > 1:
            spot = place[orders[unit % 2] * count + dest]
        else:
            spot = 0
        target[unit, spot] = product[block * height : (block + 1) * height, :].astype(BF16)


def outer_kernel(
    orders, info, place, g, a2a, a2b, ua, ub, g2,
    da2_o, dz_o, away_o, home_o, small_o,
    g_s, a2_s, u_s, da2_s, dz_s, w_s, valid_s, sums_s, in_sem, out_sem,
):
    rows = a2a.shape[0]
    width = a2_s.shape[1]
    hidden = u_s.shape[1]

    @pl.when(info[0] == 1)
    def _():
        loads = []
        for index, (source, target) in enumerate(((g.at[0], g_s), (a2a, a2_s), (ua, u_s))):
            loads.append(pltpu.make_async_copy(source, target.at[0:rows], in_sem.at[index]))
        for index, (source, target) in enumerate(((g.at[1], g_s), (a2b, a2_s), (ub, u_s))):
            loads.append(pltpu.make_async_copy(source, target.at[rows : 2 * rows], in_sem.at[3 + index]))
        for load in (loads[0], loads[1], loads[3], loads[4]):
            load.start()
        for micro in range(2):
            base = 2 + 8 * micro
            for span in (2, 3):
                @pl.when((info[base] == 1) == (span == 2))
                def _(span=span, micro=micro, base=base):
                    fill_valid(span * BUCKET, rows, info, base, valid_s, micro * rows)
        sums_s[...] = jnp.zeros_like(sums_s)
        for load in (loads[0], loads[1], loads[3], loads[4]):
            load.wait()
        loads[2].start()
        loads[5].start()

        def second_norm(part):
            grad = g_s[part, :].astype(F32) * valid_s[part, :]
            moved, gained = norm_backward(grad, a2_s[part, :], g2[...])
            da2_s[part, :] = moved
            low = moved.astype(BF16)
            dz_s[part, :] = low
            add_rows(sums_s.at[0], gained)
            add_rows(sums_s.at[1], grad)
            add_rows(sums_s.at[2], low.astype(F32))

        over_chunks(2 * rows, second_norm)
        stores = [
            pltpu.make_async_copy(da2_s, da2_o, out_sem.at[0]),
            pltpu.make_async_copy(dz_s, dz_o, out_sem.at[1]),
        ]
        for copy in stores:
            copy.start()
        for index in range(3):
            small_o[index : index + 1, :] = jnp.sum(sums_s[index], axis=0, keepdims=True)
        loads[2].wait()
        loads[5].wait()
        for tile in range(hidden // width):
            columns = slice(tile * width, (tile + 1) * width)
            put_blocks(w_s, transposed_times(u_s[:, columns], dz_s[...]), tile, place, orders, True)
        stores.append(pltpu.make_async_copy(w_s.at[0:2], away_o, out_sem.at[2]))
        stores.append(pltpu.make_async_copy(w_s.at[2:4], home_o, out_sem.at[3]))
        for copy in stores[2:]:
            copy.start()
        for copy in stores:
            copy.wait()


def fill_valid(span_rows, row_count, info, base, valid_ref, row_base):
    for block in range(row_count // span_rows):
        row_place = lax.broadcasted_iota(jnp.int32, (span_rows, 1), 0)
        row_slot, row_inner, row_length = slot_facts(block, span_rows, row_place, info, base)
        rows = slice(row_base + block * span_rows, row_base + (block + 1) * span_rows)
        valid_ref[rows, :] = jnp.where(row_inner < row_length, 1.0, 0.0)


def inner_kernel(
    orders, info, place, dz, gpa, gpb, mla, mlb, wo,
    df_o, away_o, home_o, small_o,
    dz_s, gp_s, ml_s, wo_s, df_s, w_s, e0_s, e1_s, sums_s, in_sem, out_sem,
):
    rows = mla.shape[0]
    width = dz_s.shape[1]
    hidden = df_s.shape[1]

    @pl.when(info[0] == 1)
    def _():
        loads = [
            pltpu.make_async_copy(dz, dz_s, in_sem.at[0]),
            pltpu.make_async_copy(wo.at[0], wo_s, in_sem.at[1]),
            pltpu.make_async_copy(gpa, gp_s.at[0:rows], in_sem.at[2]),
            pltpu.make_async_copy(gpb, gp_s.at[rows : 2 * rows], in_sem.at[3]),
            pltpu.make_async_copy(mla, ml_s.at[0:rows], in_sem.at[4]),
            pltpu.make_async_copy(mlb, ml_s.at[rows : 2 * rows], in_sem.at[5]),
        ]
        loads[0].start()
        loads[1].start()
        loads[0].wait()
        loads[1].wait()
        for load in loads[2:]:
            load.start()
        tile = FFN_TILE
        tiles = hidden // tile
        sums_s[...] = jnp.zeros_like(sums_s)

        def project(buffer, which):
            columns = pl.ds(pl.multiple_of(which * tile, tile), tile)
            buffer[...] = rows_times_transposed(dz_s[...], wo_s[columns, :])

        def slope(buffer, which):
            columns = pl.ds(pl.multiple_of(which * tile, tile), tile)
            for start in range(0, 2 * rows, 32):
                part = slice(start, start + 32)
                low = (buffer[part, :] * gp_s[part, columns].astype(F32)).astype(BF16)
                df_s[part, columns] = low
                sums_s[:, columns] += fold_rows(low.astype(F32))

        project(e0_s, 0)
        for load in loads[2:]:
            load.wait()

        def two_tiles(index, carry):
            project(e1_s, 2 * index + 1)
            slope(e0_s, 2 * index)
            project(e0_s, jnp.minimum(2 * index + 2, tiles - 1))
            slope(e1_s, 2 * index + 1)
            return carry

        lax.fori_loop(0, tiles // 2, two_tiles, 0)
        stores = [pltpu.make_async_copy(df_s, df_o, out_sem.at[0])]
        stores[0].start()
        small_o[...] = jnp.sum(sums_s[...], axis=0, keepdims=True)
        for which in range(hidden // width):
            columns = slice(which * width, (which + 1) * width)
            put_blocks(w_s, transposed_times(ml_s[...], df_s[:, columns]), which, place, orders, False)
        stores.append(pltpu.make_async_copy(w_s.at[0:2], away_o, out_sem.at[1]))
        stores.append(pltpu.make_async_copy(w_s.at[2:4], home_o, out_sem.at[2]))
        for copy in stores[1:]:
            copy.start()
        for copy in stores:
            copy.wait()


def mixer_kernel(
    orders, info, place, df, wi, da2, a1a, a1b, ca, cb, wm, g1,
    da1_o, dc_o, mix_o, small_o,
    df_s, wi_s, da2_s, a1_s, c_s, wm_s, dm_s, da1_s, da_s, dc_s, w_s, sums_s, in_sem, out_sem,
):
    rows = a1a.shape[0]

    @pl.when(info[0] == 1)
    def _():
        loads = [
            pltpu.make_async_copy(df, df_s, in_sem.at[0]),
            pltpu.make_async_copy(wi.at[0], wi_s, in_sem.at[1]),
            pltpu.make_async_copy(da2, da2_s, in_sem.at[2]),
            pltpu.make_async_copy(a1a, a1_s.at[0:rows], in_sem.at[3]),
            pltpu.make_async_copy(a1b, a1_s.at[rows : 2 * rows], in_sem.at[4]),
            pltpu.make_async_copy(ca, c_s.at[0:rows], in_sem.at[5]),
            pltpu.make_async_copy(cb, c_s.at[rows : 2 * rows], in_sem.at[6]),
            pltpu.make_async_copy(wm.at[0], wm_s, in_sem.at[7]),
        ]
        for load in loads[:2]:
            load.start()
        for load in loads[:2]:
            load.wait()
        for load in loads[2:]:
            load.start()
        sums_s[...] = jnp.zeros_like(sums_s)
        dm_s[...] = rows_times_transposed(df_s[...], wi_s[...])
        for load in loads[2:5]:
            load.wait()

        def first_norm(part):
            grad = dm_s[part, :] + da2_s[part, :]
            moved, gained = norm_backward(grad, a1_s[part, :], g1[...])
            da1_s[part, :] = moved
            low = moved.astype(BF16)
            da_s[part, :] = low
            add_rows(sums_s.at[0], gained)
            add_rows(sums_s.at[1], grad)
            add_rows(sums_s.at[2], low.astype(F32))

        over_chunks(2 * rows, first_norm)
        stores = [pltpu.make_async_copy(da1_s, da1_o, out_sem.at[0])]
        stores[0].start()
        for index in range(3):
            small_o[index : index + 1, :] = jnp.sum(sums_s[index], axis=0, keepdims=True)
        for load in loads[5:]:
            load.wait()
        dc_s[...] = rows_times_transposed(da_s[...], wm_s[...]).astype(BF16)
        stores.append(pltpu.make_async_copy(dc_s, dc_o, out_sem.at[1]))
        stores[1].start()
        put_blocks(w_s, transposed_times(c_s[...], da_s[...]), 0, place, orders[1:], False)
        stores.append(pltpu.make_async_copy(w_s.at[0], mix_o, out_sem.at[2]))
        stores[2].start()
        for copy in stores:
            copy.wait()


def attend_backward(span_rows, row_count, row_base, q_ref, k_ref, v_ref, dc_ref, bias_ref, dq_ref, dk_ref, dv_ref):
    blocks = row_count // span_rows
    scale = HEAD_DIM ** (-0.5)

    def one_pair(pair, carry):
        columns = pl.ds(pl.multiple_of(pair * PAIR, PAIR), PAIR)
        lane = lax.broadcasted_iota(jnp.int32, (span_rows, PAIR), 1)
        halves = (lane < HEAD_DIM, lane >= HEAD_DIM)
        for block in range(blocks):
            rows = pl.ds(pl.multiple_of(row_base + block * span_rows, BUCKET), span_rows)
            query = q_ref[rows, columns] * jnp.asarray(scale, BF16)
            keys = k_ref[rows, columns]
            value = v_ref[rows, columns]
            grad = dc_ref[rows, columns]
            zero = jnp.zeros_like(keys)
            bias = bias_ref[rows, 0:span_rows]
            dq = dk = dv = None
            for mine in halves:
                keys_own = jnp.where(mine, keys, zero)
                scores = rows_times_transposed(query, keys_own) + bias
                grad_part = rows_times_transposed(grad, jnp.where(mine, value, zero))
                top = jnp.max(scores, axis=-1, keepdims=True)
                weight = jnp.exp(scores - top)
                part = weight * (1.0 / jnp.sum(weight, axis=-1, keepdims=True))
                mean = jnp.sum(grad_part * part, axis=-1, keepdims=True)
                grad_scores = (part * (grad_part - mean)).astype(BF16)
                terms = (
                    rows_times(grad_scores, keys_own),
                    transposed_times(grad_scores, jnp.where(mine, query, zero)),
                    transposed_times(part.astype(BF16), jnp.where(mine, grad, zero)),
                )
                if dq is None:
                    dq, dk, dv = terms
                else:
                    dq, dk, dv = (dq + terms[0], dk + terms[1], dv + terms[2])
            dq_ref[rows, columns] = (dq * scale).astype(BF16)
            dk_ref[rows, columns] = dk.astype(BF16)
            dv_ref[rows, columns] = dv.astype(BF16)
        return carry

    lax.fori_loop(0, HEADS // 2, one_pair, 0)


def attend_kernel(
    orders, stacked, info, place, qa, qb, ka, kb, va, vb, dc, ha, hb, da1, wq, wk, wv, dh_in,
    dh_o, low_o, away_o, home_o, small_o,
    q_s, k_s, v_s, dc_s, h_s, dh_s, low_s, wq_s, wk_s, wv_s, dq_s, dk_s, dv_s, w_s, bias_s, sums_s, in_sem, out_sem,
):
    rows = qa.shape[0]

    @pl.when(info[0] == 1)
    def _():
        first = [
            pltpu.make_async_copy(source, target.at[part], in_sem.at[index])
            for index, (source, target, part) in enumerate(
                (
                    (qa, q_s, slice(0, rows)),
                    (ka, k_s, slice(0, rows)),
                    (va, v_s, slice(0, rows)),
                    (qb, q_s, slice(rows, 2 * rows)),
                    (kb, k_s, slice(rows, 2 * rows)),
                    (vb, v_s, slice(rows, 2 * rows)),
                    (dc, dc_s, slice(0, 2 * rows)),
                )
            )
        ]
        later = [
            pltpu.make_async_copy(da1, dh_s, in_sem.at[9]),
            pltpu.make_async_copy(wq.at[0], wq_s, in_sem.at[10]),
            pltpu.make_async_copy(wk.at[0], wk_s, in_sem.at[11]),
            pltpu.make_async_copy(wv.at[0], wv_s, in_sem.at[12]),
        ]
        for copy in first:
            copy.start()
        for micro, source in enumerate((ha, hb)):
            part = slice(micro * rows, (micro + 1) * rows)
            later.append(pltpu.make_async_copy(at_index(source, micro if stacked else None), h_s.at[part], in_sem.at[7 + micro]))
        for micro in range(2):
            base = 2 + 8 * micro
            for span in (2, 3):
                @pl.when((info[base] == 1) == (span == 2))
                def _(span=span, micro=micro, base=base):
                    fill_masks(span * BUCKET, rows, info, base, bias_s, None, micro * rows)
        for copy in first:
            copy.wait()
        for copy in later:
            copy.start()

        def one_micro(micro, carry):
            base = 2 + 8 * micro
            for span in (2, 3):
                @pl.when((info[base] == 1) == (span == 2))
                def _(span=span):
                    attend_backward(span * BUCKET, rows, micro * rows, q_s, k_s, v_s, dc_s, bias_s, dq_s, dk_s, dv_s)
            return carry

        lax.fori_loop(0, 2, one_micro, 0)
        for copy in later:
            copy.wait()
        stores = []
        for unit, grad in enumerate((dq_s, dk_s, dv_s)):
            put_blocks(w_s, transposed_times(h_s[...], grad[...]), unit, place, orders, False)
        stores.append(pltpu.make_async_copy(w_s.at[0:2], away_o, out_sem.at[0]))
        stores.append(pltpu.make_async_copy(w_s.at[2], home_o, out_sem.at[1]))
        for copy in stores:
            copy.start()
        dh_s[...] += rows_times_transposed(dq_s[...], wq_s[...])
        dh_s[...] += rows_times_transposed(dk_s[...], wk_s[...])
        dh_s[...] += rows_times_transposed(dv_s[...], wv_s[...])
        sums_s[...] = jnp.zeros_like(sums_s)

        def finish(part):
            low_s[part, :] = dh_s[part, :].astype(BF16)
            add_rows(sums_s.at[0], dq_s[part, :].astype(F32))
            add_rows(sums_s.at[1], dv_s[part, :].astype(F32))

        over_chunks(2 * rows, finish)
        for index in range(2):
            small_o[index : index + 1, :] = jnp.sum(sums_s[index], axis=0, keepdims=True)
        for micro in range(2):
            part = slice(micro * rows, (micro + 1) * rows)
            stores.append(pltpu.make_async_copy(dh_s.at[part], dh_o.at[micro], out_sem.at[2 + micro]))
            stores.append(pltpu.make_async_copy(low_s.at[part], low_o.at[micro], out_sem.at[4 + micro]))
        for copy in stores[2:]:
            copy.start()
        for copy in stores:
            copy.wait()


def run_kernel(kernel, outs, out_specs, in_specs, scratch, loads, stores, flops, bytes_moved, name, aliases=None):
    return pl.pallas_call(
        kernel,
        out_shape=outs,
        in_specs=in_specs,
        out_specs=out_specs,
        scratch_shapes=list(scratch) + [pltpu.SemaphoreType.DMA((loads,)), pltpu.SemaphoreType.DMA((stores,))],
        compiler_params=pltpu.CompilerParams(vmem_limit_bytes=VMEM_LIMIT),
        cost_estimate=pl.CostEstimate(flops=flops, bytes_accessed=bytes_moved, transcendentals=0),
        input_output_aliases=aliases or {},
        name=name,
    )


S = jax.ShapeDtypeStruct
V = pltpu.VMEM


def outer_gradient(info, place, orders, count, g, a2a, a2b, ua, ub, g2):
    rows, width = a2a.shape
    hidden = ua.shape[1]
    both = (2 * rows, width)
    block = (count, width // count, width)
    return run_kernel(
        functools.partial(outer_kernel, orders),
        (S(both, F32), S(both, BF16), S((2,) + block, BF16), S((2,) + block, BF16), S((3, width), F32)),
        [ANY] * 4 + [VM],
        [SM, SM] + [ANY] * 5 + [VM],
        [V(both, g.dtype), V(both, F32), V((2 * rows, hidden), BF16), V(both, F32), V(both, BF16), V((4,) + block, BF16), V((2 * rows, 1), F32), V((3, 8, width), F32)],
        6, 4, 4 * rows * width * hidden, 20_000_000, "outer_gradient",
    )(info, place, g, a2a, a2b, ua, ub, g2)


def inner_gradient(info, place, orders, count, dz, gpa, gpb, mla, mlb, wo):
    rows, width = mla.shape
    hidden = gpa.shape[1]
    both = (2 * rows, width)
    wide = (2 * rows, hidden)
    block = (count, width // count, width)
    return run_kernel(
        functools.partial(inner_kernel, orders),
        (S(wide, BF16), S((2,) + block, BF16), S((2,) + block, BF16), S((1, hidden), F32)),
        [ANY] * 3 + [VM],
        [SM, SM] + [ANY] * 6,
        [V(both, BF16), V(wide, BF16), V(both, BF16), V((hidden, width), BF16), V(wide, BF16), V((4,) + block, BF16), V((2 * rows, FFN_TILE), F32), V((2 * rows, FFN_TILE), F32), V((8, hidden), F32)],
        6, 3, 8 * rows * width * hidden, 25_000_000, "inner_gradient",
    )(info, place, dz, gpa, gpb, mla, mlb, wo)


def mixer_gradient(info, place, orders, count, df, wi, da2, a1a, a1b, ca, cb, wm, g1):
    rows, width = a1a.shape
    hidden = df.shape[1]
    both = (2 * rows, width)
    wide = (2 * rows, hidden)
    block = (count, width // count, width)
    return run_kernel(
        functools.partial(mixer_kernel, orders),
        (S(both, F32), S(both, BF16), S(block, BF16), S((3, width), F32)),
        [ANY] * 3 + [VM],
        [SM, SM] + [ANY] * 8 + [VM],
        [V(wide, BF16), V((width, hidden), BF16), V(both, F32), V(both, F32), V(both, BF16), V((width, width), BF16), V(both, F32), V(both, F32), V(both, BF16), V(both, BF16), V((1,) + block, BF16), V((3, 8, width), F32)],
        8, 3, 4 * rows * width * (hidden + 2 * width), 22_000_000, "mixer_gradient",
    )(info, place, df, wi, da2, a1a, a1b, ca, cb, wm, g1)


def attend_gradient(info, place, orders, count, qa, qb, ka, kb, va, vb, dc, ha, hb, da1, wq, wk, wv, dh_in):
    rows, width = qa.shape
    both = (2 * rows, width)
    block = (count, width // count, width)
    square = (width, width)
    return run_kernel(
        functools.partial(attend_kernel, orders, len(ha.shape) == 3),
        (S((2, rows, width), F32), S((2, rows, width), BF16), S((2,) + block, BF16), S(block, BF16), S((2, width), F32)),
        [ANY] * 4 + [VM],
        [SM, SM] + [ANY] * 14,
        [V(both, BF16)] * 5 + [V(both, F32), V(both, BF16)] + [V(square, BF16)] * 3 + [V(both, BF16)] * 3 + [V((3,) + block, BF16), V((2 * rows, 3 * BUCKET), F32), V((2, 8, width), F32)],
        13, 6, 24 * rows * width * width, 20_000_000, "attend_gradient",
        {15: 0},
    )(info, place, qa, qb, ka, kb, va, vb, dc, ha, hb, da1, wq, wk, wv, dh_in)


EXCHANGES = ((1, 2, 4, 8), (2, 1, 4, 8), (4, 1, 2, 8), (4, 2, 1, 8))


def exchange(value, bit):
    count = lax.axis_size("dp")
    return lax.ppermute(value, "dp", [(index, index ^ bit) for index in range(count)])


def reduce_units(orders, owned, away, home, extra):
    received = lax.ppermute(away, "section", [(owned[1], 1 - owned[1])])
    count = away.shape[1]
    sends, keeps = ([], [])
    for color in range(2):
        mine = home[color]
        other = received[color]
        if extra is not None and color == 1:
            mine = jnp.concatenate([mine, extra], axis=1)
            other = jnp.concatenate([other, jnp.zeros_like(extra)], axis=1)
        half = count // 2
        sends.append(jnp.where(owned[0], mine[half:], other[half:]))
        keeps.append(jnp.where(owned[0], mine[:half], other[:half]))
    paths = [EXCHANGES[order] for order in orders]
    for step in range(4):
        bits = [path[step] for path in paths]
        if bits[0] == bits[1] and sends[0].shape == sends[1].shape:
            both = exchange(jnp.stack(sends), bits[0])
            arrived = [both[0], both[1]]
        elif bits[0] == bits[1]:
            joined = exchange(jnp.concatenate(sends, axis=1), bits[0])
            height = sends[0].shape[1]
            arrived = [joined[:, :height], joined[:, height:]]
        else:
            arrived = [exchange(value, bit) for value, bit in zip(sends, bits)]
        totals = [keep.astype(F32) + part.astype(F32) for keep, part in zip(keeps, arrived)]
        if step == 3:
            return [total[0] for total in totals]
        half = totals[0].shape[0] // 2
        sends = [total[half:].astype(BF16) for total in totals]
        keeps = [total[:half].astype(BF16) for total in totals]


def layer_backward(live, metas, place, orders, count, saved, inputs, grad, params, grad_buffer):
    wq, bq, wk, wv, bv, wm, bm, g1, s1, wi, bi, wo, bo, g2, s2 = params
    (ya, qa, ka, va, ca, a1a, mla, ua, gpa, a2a), (yb, qb, kb, vb, cb, a1b, mlb, ub, gpb, a2b) = saved
    info = jnp.concatenate([jnp.stack([live, live]), metas[0], metas[1]])
    da2, dz, outer_away, outer_home, small_two = outer_gradient(info, place, orders[0], count, grad, a2a, a2b, ua, ub, g2)
    df, inner_away, inner_home, small_inner = inner_gradient(info, place, orders[1], count, dz, gpa, gpb, mla, mlb, wo)
    da1, dc, mix_home, small_one = mixer_gradient(info, place, orders[2], count, df, wi, da2, a1a, a1b, ca, cb, wm, g1)
    dh, low, attend_away, value_home, small_attend = attend_gradient(
        info, place, orders[2], count, qa, qb, ka, kb, va, vb, dc, inputs[0], inputs[1], da1, wq, wk, wv, grad_buffer
    )
    smalls = (small_attend[0], small_attend[1], small_one[2], small_one[0], small_one[1], small_two[2], small_two[0], small_two[1])
    return (dh, low, (outer_away, outer_home), (inner_away, inner_home), (attend_away, (value_home, mix_home)), smalls, small_inner[0])


def per_device(
    tokens, cotangent, bucket, batch_size, lengths, query_weight, query_offset, keys_weight, value_weight, value_offset,
    mixer_weight, mixer_offset, first_gain, first_shift, inner_weight, inner_offset, outer_weight, outer_offset,
    second_gain, second_shift,
):
    params = (
        query_weight, query_offset, keys_weight, value_weight, value_offset, mixer_weight, mixer_offset, first_gain,
        first_shift, inner_weight, inner_offset, outer_weight, outer_offset, second_gain, second_shift,
    )
    section = lax.axis_index("section")
    group = lax.axis_index("dp")
    groups = lax.axis_size("dp")
    width = tokens.shape[2]
    hidden = inner_offset.shape[1]
    hypercube = groups == 16 and width % (16 * groups) == 0
    count = groups if hypercube else 1
    one = jnp.ones((), jnp.int32)
    at_first = (section == 0).astype(jnp.int32)
    at_second = (section == 1).astype(jnp.int32)
    metas = [jnp.concatenate([bucket[m : m + 1], batch_size[m : m + 1], lengths[m]]) for m in range(2)]

    def forward_info(live, source, meta):
        return jnp.concatenate([jnp.stack([live, source]), meta])

    down = [(0, 1)]
    slot_a = forward_layer(forward_info(at_first, 0 * one, metas[0]), tokens, 0, tokens[0], params)
    received_a = lax.ppermute(slot_a[0], "section", down)
    meta_b = jnp.where(section == 0, metas[1], metas[0])
    slot_b = forward_layer(forward_info(one, at_second, meta_b), tokens, 1, received_a, params)
    received_b = lax.ppermute(slot_b[0], "section", down)
    slot_c = forward_layer(forward_info(at_second, one, metas[1]), tokens, 0, received_b, params)
    layer_out = jnp.stack([jnp.where(section == 0, slot_a[0], slot_b[0]), jnp.where(section == 0, slot_b[0], slot_c[0])])

    dest = jnp.arange(groups, dtype=jnp.int32)
    relative = jnp.bitwise_xor(dest, group)
    if hypercube:
        spots = []
        for path in EXCHANGES:
            spot = jnp.zeros_like(dest)
            for index, bit in enumerate(path):
                spot = spot + jnp.bitwise_and(relative // bit, 1) * (8 >> index)
            spots.append(spot)
        place = jnp.concatenate(spots)
    else:
        place = dest
    orders = ((0, 1), (2, 3), (0, 1))
    buffer = jnp.zeros(tokens.shape, F32)
    second = layer_backward(
        at_second, metas, place, orders, count, (slot_b, slot_c), (received_a, received_b), cotangent, params, buffer
    )
    received_grad = lax.ppermute(second[1], "section", [(1, 0)])
    first = layer_backward(
        at_first, metas, place, orders, count, (slot_a, slot_b), (tokens, tokens), received_grad, params, second[0]
    )
    input_grad = first[0]
    at_owner = section == 1

    def small_blocks(smalls, small_inner):
        flat = jnp.stack(smalls).reshape(8, groups, width // groups).transpose(1, 0, 2).reshape(groups, -1)
        return jnp.concatenate([flat, small_inner.reshape(groups, -1)], axis=1)

    if hypercube:
        summed = []
        for layer, parts in ((1, second), (0, first)):
            owned = (section == layer, layer)
            dh, low, outer, inner, attend, smalls, small_inner = parts
            blocks = small_blocks(smalls, small_inner)
            blocks = jnp.pad(blocks, ((0, 0), (0, width - blocks.shape[1]))).astype(BF16)
            order = jnp.argsort(place[groups : 2 * groups])
            blocks = jnp.where(owned[0], blocks[order], jnp.zeros_like(blocks))
            extra = jnp.pad(blocks[:, None, :], ((0, 0), (0, 7), (0, 0)))
            results = [
                reduce_units(orders[0], owned, outer[0], outer[1], None),
                reduce_units(orders[1], owned, inner[0], inner[1], None),
                reduce_units(orders[2], owned, attend[0], attend[1], extra),
            ]
            summed.append(results)
        final = []
        for second_part, first_part in zip(summed[0], summed[1]):
            height = width // groups
            send = jnp.stack([jnp.where(section == 0, a[:height], b[:height]) for a, b in zip(second_part, first_part)])
            back = lax.ppermute(send, "section", [(0, 1), (1, 0)])
            mine = [jnp.where(at_owner, a, b) for a, b in zip(second_part, first_part)]
            final.append((back[0], back[1], mine[0], mine[1]))
        height = width // groups
        outer_grad = jnp.concatenate(final[0], axis=0)
        inner_grad = jnp.concatenate(final[1], axis=1)
        query_grad, keys_grad, value_grad, mixed = final[2]
        mixer_grad = mixed[:height]
        line = mixed[height]
        small = [line[index * height : (index + 1) * height] for index in range(8)]
        small_wide = line[8 * height : 8 * height + hidden // groups]
    else:
        def scatter(value):
            return lax.psum_scatter(value, "dp", scatter_dimension=0, tiled=True)

        final = []
        for dh, low, outer, inner, attend, smalls, small_inner in (second, first):
            outer_full = jnp.concatenate([outer[0], outer[1]]).reshape(hidden, width)
            inner_full = jnp.concatenate([inner[0][0, 0], inner[0][1, 0], inner[1][0, 0], inner[1][1, 0]], axis=1)
            squares = [attend[0][0, 0], attend[0][1, 0], attend[1][0][0], attend[1][1][0]]
            final.append([scatter(outer_full), scatter(inner_full)] + [scatter(square) for square in squares] + [scatter(value) for value in smalls] + [scatter(small_inner)])
        chosen = [jnp.where(at_owner, a, b).astype(F32) for a, b in zip(final[0], final[1])]
        outer_grad, inner_grad, query_grad, keys_grad, value_grad, mixer_grad = chosen[:6]
        small = chosen[6:14]
        small_wide = chosen[14]
    outputs = (
        layer_out, input_grad, query_grad, small[0], keys_grad, value_grad, small[1], mixer_grad, small[2], small[3],
        small[4], inner_grad, small_wide, outer_grad, small[5], small[6], small[7],
    )
    return tuple(piece[None] for piece in outputs)


def solution(mesh):
    from jax.sharding import PartitionSpec as P

    matrix = P("section", None, None)
    vector = P("section", None)
    in_specs = (
        P("dp", None, None), P("dp", None, None), P("dp"), P("dp"), P("dp", None), matrix, vector, matrix, matrix, vector,
        matrix, vector, vector, vector, matrix, vector, matrix, vector, vector, vector,
    )
    rows = P("section", "dp", None, None)
    grad = P("section", "dp", None)
    small = P("section", "dp")
    out_specs = (rows, rows, grad, small, grad, grad, small, grad, small, small, small, grad, small, grad, small, small, small)
    return jax.shard_map(per_device, mesh=mesh, in_specs=in_specs, out_specs=out_specs, check_vma=False)
```

```python
import functools
import jax
import jax.numpy as jnp
from jax import lax
from jax.experimental import pallas as pl
from jax.experimental.pallas import tpu as pltpu
from jax.sharding import PartitionSpec as P

HEADS = 12
HEAD_DIM = 64
BUCKET = 64
PAIR = 2 * HEAD_DIM
masked_score = -1000000000.0
norm_epsilon = 1e-06
F32 = jnp.float32
BF16 = jnp.bfloat16
CHUNK = 16
FFN_TILE = 512
ATT_UNROLL = 3


def rows_times(left, right):
    return lax.dot_general(left, right, (((1,), (0,)), ((), ())), preferred_element_type=F32)


def rows_times_transposed(left, right):
    return lax.dot_general(left, right, (((1,), (1,)), ((), ())), preferred_element_type=F32)


def transposed_times(left, right):
    return lax.dot_general(left, right, (((0,), (0,)), ((), ())), preferred_element_type=F32)


def slot_facts(block, span_rows, place, meta, micro):
    bucket_ref, count_ref, lengths_ref = meta
    bucket = bucket_ref[micro]
    count = count_ref[micro]

    def length_of(slot):
        return jnp.where(slot < count, lengths_ref[micro, slot], 0)

    if span_rows == 2 * BUCKET:
        return (jnp.full_like(place, block), place, jnp.full_like(place, length_of(block)))
    short = bucket == 0
    first = 3 * block
    slot_short = first + place // BUCKET
    length_short = jnp.where(
        place < BUCKET,
        length_of(first),
        jnp.where(place < 2 * BUCKET, length_of(first + 1), length_of(first + 2)),
    )
    slot = jnp.where(short, slot_short, block)
    inner = jnp.where(short, place % BUCKET, place)
    length = jnp.where(short, length_short, length_of(block))
    return (slot, inner, length)


def fill_masks(span_rows, row_count, meta, micro, bias_ref, valid_ref):
    for block in range(row_count // span_rows):
        row_place = lax.broadcasted_iota(jnp.int32, (span_rows, 1), 0)
        row_slot, row_inner, row_length = slot_facts(block, span_rows, row_place, meta, micro)
        rows = slice(block * span_rows, (block + 1) * span_rows)
        if bias_ref is not None:
            key_place = lax.broadcasted_iota(jnp.int32, (1, span_rows), 1)
            key_slot, key_inner, key_length = slot_facts(block, span_rows, key_place, meta, micro)
            key_tag = jnp.where(key_inner < key_length, key_slot, -1)
            allowed = (row_slot == key_tag) | (row_place == key_place)
            bias_ref[rows, 0:span_rows] = jnp.where(allowed, 0.0, masked_score)
        if valid_ref is not None:
            valid_ref[rows, :] = jnp.where(row_inner < row_length, 1.0, 0.0)


def by_span(meta, micro, body):
    even = meta[0][micro] == 1

    @pl.when(even)
    def _():
        body(2 * BUCKET)

    @pl.when(jnp.logical_not(even))
    def _():
        body(3 * BUCKET)


def attend_forward(span_rows, row_count, q_ref, k_ref, v_ref, bias_ref, c_ref):
    blocks = row_count // span_rows

    def one_pair(pair, carry):
        columns = pl.ds(pl.multiple_of(pair * PAIR, PAIR), PAIR)
        lane = lax.broadcasted_iota(jnp.int32, (span_rows, PAIR), 1)
        first_half = lane < HEAD_DIM
        weights = []
        for block in range(blocks):
            rows = slice(block * span_rows, (block + 1) * span_rows)
            query = q_ref[rows, columns] * jnp.asarray(HEAD_DIM ** (-0.5), BF16)
            keys = k_ref[rows, columns]
            zero = jnp.zeros_like(keys)
            bias = bias_ref[rows, 0:span_rows]
            for mine in (first_half, jnp.logical_not(first_half)):
                scores = rows_times_transposed(query, jnp.where(mine, keys, zero)) + bias
                top = jnp.max(scores, axis=-1, keepdims=True)
                weights.append(jnp.exp(scores - top).astype(BF16))
        for block in range(blocks):
            rows = slice(block * span_rows, (block + 1) * span_rows)
            value = v_ref[rows, columns]
            one = jnp.ones_like(value)
            left = rows_times(weights[2 * block], jnp.where(first_half, value, one))
            right = rows_times(weights[2 * block + 1], jnp.where(first_half, one, value))
            above = jnp.where(first_half, left, right)
            below = pltpu.roll(jnp.where(first_half, right, left), HEAD_DIM, 1)
            c_ref[rows, columns] = (above / below).astype(BF16)
        return carry

    lax.fori_loop(0, HEADS // 2, one_pair, 0, unroll=ATT_UNROLL)


def row_moments(values):
    center = jnp.mean(values, axis=-1, keepdims=True)
    centred = values - center
    spread = jnp.mean(centred * centred, axis=-1, keepdims=True)
    return centred, lax.rsqrt(spread + norm_epsilon)


def over_chunks(row_count, body, rows=CHUNK, group=6):
    def step(index, carry):
        for inner in range(group):
            start = pl.multiple_of(index * (rows * group) + inner * rows, rows)
            body(pl.ds(start, rows))
        return carry

    lax.fori_loop(0, row_count // (rows * group), step, 0)


def gelu_with_slope(values):
    cumulative = 0.5 + 0.5 * lax.erf(values * (0.5 ** 0.5))
    density = jnp.exp(values * values * -0.5) * 0.3989422804014327
    return values * cumulative, cumulative + values * density


ANY = pl.BlockSpec(memory_space=pl.ANY)
VM = pl.BlockSpec(memory_space=pltpu.VMEM)
SM = pl.BlockSpec(memory_space=pltpu.SMEM)
VMEM_LIMIT = 63_000 * 1024
S = jax.ShapeDtypeStruct
V = pltpu.VMEM
B_QUERY, B_VALUE, B_MIXER, GAIN_ONE, SHIFT_ONE, B_OUTER, GAIN_TWO, SHIFT_TWO = range(8)
QUERY, KEYS, VALUE, CONTEXT, MIDDLE, RESULT = range(6)
EXCHANGES = ((1, 2, 4, 8), (2, 1, 4, 8), (4, 1, 2, 8), (4, 2, 1, 8))


class Loads:
    def __init__(self, semaphores):
        self.semaphores = semaphores
        self.copies = {}

    def start(self, name, source, target, other=None, take_other=None):
        semaphore = self.semaphores.at[len(self.copies)]
        copy = pltpu.make_async_copy(source, target, semaphore)
        self.copies[name] = copy
        if other is None:
            copy.start()
            return
        second = pltpu.make_async_copy(other, target, semaphore)

        @pl.when(take_other)
        def _():
            second.start()

        @pl.when(jnp.logical_not(take_other))
        def _():
            copy.start()

    def wait(self, *names):
        for name in names:
            self.copies[name].wait()


class Stores:
    def __init__(self, semaphores):
        self.semaphores = semaphores
        self.copies = []

    def start(self, source, target):
        copy = pltpu.make_async_copy(source, target, self.semaphores.at[len(self.copies)])
        copy.start()
        self.copies.append(copy)

    def wait(self):
        for copy in self.copies:
            copy.wait()


def spot_of(order, dest, me):
    relative = jnp.bitwise_xor(dest, me)
    spot = 0
    for index, bit in enumerate(EXCHANGES[order]):
        one = jnp.bitwise_and(lax.shift_right_logical(relative, bit.bit_length() - 1), 1)
        spot = spot + one * (8 >> index)
    return spot


def put_blocks(target, product, unit_at, tile, orders, me, spread_units):
    count = target.shape[1]
    height = product.shape[0] // count
    for block in range(count):
        if spread_units and count > 1:
            unit = block % 4
            dest = tile * (count // 4) + block // 4
        else:
            unit = tile
            dest = block
        spot = 0 if count == 1 else spot_of(orders[unit % 2], dest, me)
        target[unit_at + unit, spot] = product[block * height : (block + 1) * height, :].astype(BF16)


def forward_body(load, store, meta, micro, vec, bi, outs, refs):
    h_s, wq_s, wk_s, wv_s, wm_s, wi_s, wo_s, low_s, total_s, wide_s, m_s, f0_s, e0_s, e1_s, bias_s, valid_s = refs
    y_o, low_o, total_o, wide_o = outs
    rows, width = h_s.shape
    hidden = wi_s.shape[1]
    q_s, k_s, v_s, c_s, ml_s, y_s = (low_s.at[index] for index in (QUERY, KEYS, VALUE, CONTEXT, MIDDLE, RESULT))
    a1_s, a2_s = (total_s.at[0], total_s.at[1])
    u_s, gp_s = (wide_s.at[0], wide_s.at[1])
    load(0)
    by_span(meta, micro, lambda span: fill_masks(span, rows, meta, micro, bias_s, valid_s))
    load(1)
    q_s[...] = (rows_times(h_s[...], wq_s[...]) + vec(B_QUERY)).astype(BF16)
    load(2)
    k_s[...] = rows_times(h_s[...], wk_s[...]).astype(BF16)
    load(3)
    v_s[...] = (rows_times(h_s[...], wv_s[...]) + vec(B_VALUE)).astype(BF16)
    by_span(meta, micro, lambda span: attend_forward(span, rows, q_s, k_s, v_s, bias_s, c_s))
    store.start(low_s.at[0:4], low_o.at[0:4])
    load(4)
    f0_s[...] = rows_times(c_s[...], wm_s[...])
    offset_mixer, gain_one, shift_one = (vec(B_MIXER), vec(GAIN_ONE), vec(SHIFT_ONE))

    def first_norm(part):
        total = h_s[part, :].astype(F32) + (f0_s[part, :] + offset_mixer)
        a1_s[part, :] = total
        centred, scale = row_moments(total)
        middle = centred * scale * gain_one + shift_one
        m_s[part, :] = middle
        ml_s[part, :] = middle.astype(BF16)

    over_chunks(rows, first_norm)
    store.start(a1_s, total_o.at[0])
    store.start(ml_s, low_o.at[MIDDLE])
    load(5)
    tile = FFN_TILE
    tiles = hidden // tile

    def project(buffer, which):
        columns = pl.ds(pl.multiple_of(which * tile, tile), tile)
        buffer[...] = rows_times(ml_s[...], wi_s[:, columns])

    def activate(buffer, which):
        columns = pl.ds(pl.multiple_of(which * tile, tile), tile)
        offset = bi(columns)
        for start in range(0, rows, 32):
            part = slice(start, start + 32)
            value, slope = gelu_with_slope(buffer[part, :] + offset)
            u_s[part, columns] = value.astype(BF16)
            gp_s[part, columns] = slope.astype(BF16)

    project(e0_s, 0)

    def two_tiles(index, carry):
        project(e1_s, 2 * index + 1)
        activate(e0_s, 2 * index)
        project(e0_s, jnp.minimum(2 * index + 2, tiles - 1))
        activate(e1_s, 2 * index + 1)
        return carry

    lax.fori_loop(0, tiles // 2, two_tiles, 0)
    store.start(wide_s, wide_o)
    load(6)
    f0_s[...] = rows_times(u_s[...], wo_s[...])
    offset_outer, gain_two, shift_two = (vec(B_OUTER), vec(GAIN_TWO), vec(SHIFT_TWO))

    def second_norm(part):
        total = m_s[part, :] + (f0_s[part, :] + offset_outer)
        a2_s[part, :] = total
        centred, scale = row_moments(total)
        y_s[part, :] = ((centred * scale * gain_two + shift_two) * valid_s[part, :]).astype(BF16)

    over_chunks(rows, second_norm)
    store.start(y_s, y_o)
    store.start(a2_s, total_o.at[1])
    store.wait()


def forward_loads(loads, hidden_start, weights, others, take_other, targets):
    names = ("wq", "wk", "wv", "wm", "wi", "wo")

    def begin(index):
        other = None if others is None else others[index].at[0]
        loads.start(names[index], weights[index].at[0], targets[index], other, take_other)

    def load(step):
        if step == 0:
            hidden_start()
            for index in range(3):
                begin(index)
            return
        if step == 1:
            loads.wait("h")
        loads.wait(names[step - 1])
        if step <= 3:
            begin(step + 2)

    return load


def first_forward_kernel(
    index, bucket, count, lengths, tok, wq, wk, wv, wm, wi, wo, bq, bv, bm, g1, s1, bo, g2, s2, bi,
    y_o, low_o, total_o, wide_o, vec_o,
    h_s, wq_s, wk_s, wv_s, wm_s, wi_s, wo_s, low_s, total_s, wide_s, m_s, f0_s, e0_s, e1_s, bias_s, valid_s, in_sem, out_sem,
):
    vectors = (bq, bv, bm, g1, s1, bo, g2, s2)
    for place, vector in enumerate(vectors):
        vec_o[place : place + 1, :] = vector[...]

    @pl.when(lax.axis_index("section") == 0)
    def _():
        loads = Loads(in_sem)
        load = forward_loads(
            loads, lambda: loads.start("h", tok.at[index], h_s), (wq, wk, wv, wm, wi, wo), None, None,
            (wq_s, wk_s, wv_s, wm_s, wi_s, wo_s),
        )
        forward_body(
            load, Stores(out_sem), (bucket, count, lengths), index, lambda place: vectors[place][...], lambda columns: bi[:, columns],
            (y_o, low_o, total_o, wide_o),
            (h_s, wq_s, wk_s, wv_s, wm_s, wi_s, wo_s, low_s, total_s, wide_s, m_s, f0_s, e0_s, e1_s, bias_s, valid_s),
        )


def second_forward_kernel(
    bucket, count, lengths, y_own, y_other, wq, wk, wv, wm, wi, wo, xq, xk, xv, xm, xi, xo, vec_own, vec_other, bi_own, bi_other,
    y_o, low_o, total_o, wide_o,
    h_s, wq_s, wk_s, wv_s, wm_s, wi_s, wo_s, low_s, total_s, wide_s, m_s, f0_s, e0_s, e1_s, bias_s, valid_s, in_sem, out_sem,
):
    section = lax.axis_index("section")
    first = section == 0
    loads = Loads(in_sem)
    load = forward_loads(
        loads, lambda: loads.start("h", y_other, h_s, y_own, first), (wq, wk, wv, wm, wi, wo), (xq, xk, xv, xm, xi, xo), first,
        (wq_s, wk_s, wv_s, wm_s, wi_s, wo_s),
    )

    def vec(place):
        return jnp.where(first, vec_other[place : place + 1, :], vec_own[place : place + 1, :])

    forward_body(
        load, Stores(out_sem), (bucket, count, lengths), section, vec,
        lambda columns: jnp.where(first, bi_other[:, columns], bi_own[:, columns]),
        (y_o, low_o, total_o, wide_o),
        (h_s, wq_s, wk_s, wv_s, wm_s, wi_s, wo_s, low_s, total_s, wide_s, m_s, f0_s, e0_s, e1_s, bias_s, valid_s),
    )


def run_kernel(kernel, outs, out_specs, in_specs, scratch, loads, stores, flops, bytes_moved, name):
    return pl.pallas_call(
        kernel,
        out_shape=outs,
        in_specs=in_specs,
        out_specs=out_specs,
        scratch_shapes=list(scratch) + [pltpu.SemaphoreType.DMA((loads,)), pltpu.SemaphoreType.DMA((stores,))],
        compiler_params=pltpu.CompilerParams(vmem_limit_bytes=VMEM_LIMIT),
        cost_estimate=pl.CostEstimate(flops=flops, bytes_accessed=bytes_moved, transcendentals=0),
        name=name,
    )


def forward_shapes(rows, width, hidden):
    flat = (rows, width)
    square = (width, width)
    outs = (S(flat, BF16), S((5,) + flat, BF16), S((2,) + flat, F32), S((2, rows, hidden), BF16))
    scratch = [
        V(flat, BF16), V(square, BF16), V(square, BF16), V(square, BF16), V(square, BF16), V((width, hidden), BF16),
        V((hidden, width), BF16), V((6,) + flat, BF16), V((2,) + flat, F32), V((2, rows, hidden), BF16), V(flat, F32),
        V(flat, F32), V((rows, FFN_TILE), F32), V((rows, FFN_TILE), F32), V((rows, 3 * BUCKET), F32), V((rows, 1), F32),
    ]
    flops = 2 * rows * width * (4 * width + 2 * hidden)
    return outs, scratch, flops


def first_forward(meta, tokens, index, weights, vectors, bi):
    rows, width = tokens.shape[1:]
    outs, scratch, flops = forward_shapes(rows, width, bi.shape[1])
    return run_kernel(
        functools.partial(first_forward_kernel, index), outs + (S((8, width), F32),), [ANY] * 4 + [VM],
        [SM] * 3 + [ANY] * 7 + [VM] * 9, scratch, 7, 6, flops, 25_000_000, "first_forward",
    )(*meta, tokens, *weights, *vectors, bi)


def second_forward(meta, y_own, y_other, weights, others, vec_own, vec_other, bi_own, bi_other):
    rows, width = y_own.shape
    outs, scratch, flops = forward_shapes(rows, width, bi_own.shape[1])
    return run_kernel(
        second_forward_kernel, outs, [ANY] * 4, [SM] * 3 + [ANY] * 14 + [VM] * 4, scratch, 7, 6, flops, 25_000_000,
        "second_forward",
    )(*meta, y_own, y_other, *weights, *others, vec_own, vec_other, bi_own, bi_other)


def norm_backward(grad, total, gain):
    centred, scale = row_moments(total)
    unit = centred * scale
    spread = grad * gain
    first = jnp.mean(spread, axis=-1, keepdims=True)
    second = jnp.mean(spread * unit, axis=-1, keepdims=True)
    return (spread - first - unit * second) * scale, grad * unit


def fold_rows(values):
    return jnp.sum(values.reshape(values.shape[0] // 8, 8, values.shape[1]), axis=0)


def layer_of(layer):
    return lax.axis_index("section") != layer


def taken(layer, own, other, place):
    return jnp.where(layer_of(layer), other[place : place + 1, :], own[place : place + 1, :])


def send_units(store, w_s, away_o, home_o):
    section = lax.axis_index("section")
    store.start(w_s.at[pl.ds(2 * (1 - section), 2)], away_o)
    store.start(w_s.at[pl.ds(2 * section, 2)], home_o)


def outer_kernel(
    layer, orders, bucket, count, lengths, g, total, total_x, wide, wide_x, vec_own, vec_other,
    da2_o, dz_o, away_o, home_o, small_o,
    g_s, a2_s, u_s, da2_s, dz_s, w_s, valid_s, sums_s, in_sem, out_sem,
):
    section = lax.axis_index("section")
    rows, width = a2_s.shape
    hidden = u_s.shape[1]
    second = section == 1
    loads = Loads(in_sem)
    store = Stores(out_sem)
    other = (lambda ref: ref) if layer == 0 else (lambda ref: None)
    loads.start("g", g.at[section] if layer == 1 else g, g_s)
    loads.start("a2", total.at[1], a2_s, other(total_x.at[1]), second)
    loads.start("u", wide.at[0], u_s, other(wide_x.at[0]), second)
    meta = (bucket, count, lengths)
    by_span(meta, section, lambda span: fill_masks(span, rows, meta, section, None, valid_s))
    sums_s[...] = jnp.zeros_like(sums_s)
    gain = taken(layer, vec_own, vec_other, GAIN_TWO)
    loads.wait("g", "a2")

    def second_norm(part):
        grad = g_s[part, :].astype(F32) * valid_s[part, :]
        moved, gained = norm_backward(grad, a2_s[part, :], gain)
        da2_s[part, :] = moved
        low = moved.astype(BF16)
        dz_s[part, :] = low
        sums_s[0] += fold_rows(gained)
        sums_s[1] += fold_rows(grad)
        sums_s[2] += fold_rows(low.astype(F32))

    over_chunks(rows, second_norm)
    store.start(da2_s, da2_o)
    store.start(dz_s, dz_o)
    for index in range(3):
        small_o[index : index + 1, :] = jnp.sum(sums_s[index], axis=0, keepdims=True)
    loads.wait("u")
    me = lax.axis_index("dp")
    for tile in range(hidden // width):
        columns = slice(tile * width, (tile + 1) * width)
        put_blocks(w_s, transposed_times(u_s[:, columns], dz_s[...]), 0, tile, orders, me, True)
    send_units(store, w_s, away_o, home_o)
    store.wait()


def inner_kernel(
    layer, orders, dz, wide, wide_x, low, low_x, wo, wo_x,
    df_o, away_o, home_o, small_o,
    dz_s, gp_s, ml_s, wo_s, df_s, w_s, e0_s, e1_s, sums_s, in_sem, out_sem,
):
    section = lax.axis_index("section")
    rows, width = dz_s.shape
    hidden = df_s.shape[1]
    second = section == 1
    loads = Loads(in_sem)
    store = Stores(out_sem)
    other = (lambda ref: ref) if layer == 0 else (lambda ref: None)
    loads.start("dz", dz, dz_s)
    loads.start("wo", wo.at[0], wo_s, wo_x.at[0], layer_of(layer))
    loads.start("gp", wide.at[1], gp_s, other(wide_x.at[1]), second)
    loads.start("ml", low.at[MIDDLE], ml_s, other(low_x.at[MIDDLE]), second)
    tile = FFN_TILE
    tiles = hidden // tile
    sums_s[...] = jnp.zeros_like(sums_s)

    def project(buffer, which):
        columns = pl.ds(pl.multiple_of(which * tile, tile), tile)
        buffer[...] = rows_times_transposed(dz_s[...], wo_s[columns, :])

    def slope(buffer, which):
        columns = pl.ds(pl.multiple_of(which * tile, tile), tile)
        total = None
        for start in range(0, rows, 32):
            part = slice(start, start + 32)
            low_part = (buffer[part, :] * gp_s[part, columns].astype(F32)).astype(BF16)
            df_s[part, columns] = low_part
            term = fold_rows(low_part.astype(F32))
            total = term if total is None else total + term
        sums_s[:, columns] = total

    loads.wait("dz", "wo")
    project(e0_s, 0)
    loads.wait("gp")

    def two_tiles(index, carry):
        project(e1_s, 2 * index + 1)
        slope(e0_s, 2 * index)
        project(e0_s, jnp.minimum(2 * index + 2, tiles - 1))
        slope(e1_s, 2 * index + 1)
        return carry

    lax.fori_loop(0, tiles // 2, two_tiles, 0)
    store.start(df_s, df_o)
    small_o[...] = jnp.sum(sums_s[...], axis=0, keepdims=True)
    loads.wait("ml")
    me = lax.axis_index("dp")
    for which in range(hidden // width):
        columns = slice(which * width, (which + 1) * width)
        put_blocks(w_s, transposed_times(ml_s[...], df_s[:, columns]), 0, which, orders, me, False)
    send_units(store, w_s, away_o, home_o)
    store.wait()


def mixer_kernel(
    layer, orders, df, wi, wi_x, da2, total, total_x, low, low_x, wm, wm_x, vec_own, vec_other,
    da1_o, dc_o, mix_o, small_o,
    df_s, wi_s, da2_s, a1_s, c_s, wm_s, dm_s, da1_s, da_s, dc_s, w_s, sums_s, in_sem, out_sem,
):
    section = lax.axis_index("section")
    rows, width = dm_s.shape
    second = section == 1
    loads = Loads(in_sem)
    store = Stores(out_sem)
    other = (lambda ref: ref) if layer == 0 else (lambda ref: None)
    loads.start("df", df, df_s)
    loads.start("wi", wi.at[0], wi_s, wi_x.at[0], layer_of(layer))
    loads.start("da2", da2, da2_s)
    loads.start("a1", total.at[0], a1_s, other(total_x.at[0]), second)
    loads.start("c", low.at[CONTEXT], c_s, other(low_x.at[CONTEXT]), second)
    loads.start("wm", wm.at[0], wm_s, wm_x.at[0], layer_of(layer))
    sums_s[...] = jnp.zeros_like(sums_s)
    gain = taken(layer, vec_own, vec_other, GAIN_ONE)
    loads.wait("df", "wi")
    dm_s[...] = rows_times_transposed(df_s[...], wi_s[...])
    loads.wait("da2", "a1")

    def first_norm(part):
        grad = dm_s[part, :] + da2_s[part, :]
        moved, gained = norm_backward(grad, a1_s[part, :], gain)
        da1_s[part, :] = moved
        low_part = moved.astype(BF16)
        da_s[part, :] = low_part
        sums_s[0] += fold_rows(gained)
        sums_s[1] += fold_rows(grad)
        sums_s[2] += fold_rows(low_part.astype(F32))

    over_chunks(rows, first_norm)
    store.start(da1_s, da1_o)
    for index in range(3):
        small_o[index : index + 1, :] = jnp.sum(sums_s[index], axis=0, keepdims=True)
    loads.wait("c", "wm")
    dc_s[...] = rows_times_transposed(da_s[...], wm_s[...]).astype(BF16)
    store.start(dc_s, dc_o)
    put_blocks(w_s, transposed_times(c_s[...], da_s[...]), 0, 0, orders[1:], lax.axis_index("dp"), False)
    store.start(w_s.at[0], mix_o)
    store.wait()


def attend_backward(span_rows, row_count, q_ref, k_ref, v_ref, dc_ref, bias_ref, dq_ref, dk_ref, dv_ref):
    blocks = row_count // span_rows
    scale = HEAD_DIM ** (-0.5)

    def one_pair(pair, carry):
        columns = pl.ds(pl.multiple_of(pair * PAIR, PAIR), PAIR)
        lane = lax.broadcasted_iota(jnp.int32, (span_rows, PAIR), 1)
        halves = (lane < HEAD_DIM, lane >= HEAD_DIM)
        for block in range(blocks):
            rows = slice(block * span_rows, (block + 1) * span_rows)
            query = q_ref[rows, columns] * jnp.asarray(scale, BF16)
            keys = k_ref[rows, columns]
            value = v_ref[rows, columns]
            grad = dc_ref[rows, columns]
            zero = jnp.zeros_like(keys)
            bias = bias_ref[rows, 0:span_rows]
            dq = dk = dv = None
            for mine in halves:
                keys_own = jnp.where(mine, keys, zero)
                scores = rows_times_transposed(query, keys_own) + bias
                grad_part = rows_times_transposed(grad, jnp.where(mine, value, zero))
                top = jnp.max(scores, axis=-1, keepdims=True)
                weight = jnp.exp(scores - top)
                part = weight * (1.0 / jnp.sum(weight, axis=-1, keepdims=True))
                mean = jnp.sum(grad_part * part, axis=-1, keepdims=True)
                grad_scores = (part * (grad_part - mean)).astype(BF16)
                terms = (
                    rows_times(grad_scores, keys_own),
                    transposed_times(grad_scores, jnp.where(mine, query, zero)),
                    transposed_times(part.astype(BF16), jnp.where(mine, grad, zero)),
                )
                if dq is None:
                    dq, dk, dv = terms
                else:
                    dq, dk, dv = (dq + terms[0], dk + terms[1], dv + terms[2])
            dq_ref[rows, columns] = (dq * scale).astype(BF16)
            dk_ref[rows, columns] = dk.astype(BF16)
            dv_ref[rows, columns] = dv.astype(BF16)
        return carry

    lax.fori_loop(0, HEADS // 2, one_pair, 0)


def attend_kernel(
    layer, orders, bucket, count, lengths, low, low_x, dc, h_one, h_two, da1, wq, wk, wv, xq, xk, xv, mix,
    dh_o, dlow_o, away_o, home_o, small_o,
    q_s, k_s, v_s, dc_s, h_s, dh_s, dlow_s, wq_s, wk_s, wv_s, dq_s, dk_s, dv_s, w_s, bias_s, sums_s, in_sem, out_sem,
):
    section = lax.axis_index("section")
    rows, width = q_s.shape
    second = section == 1
    loads = Loads(in_sem)
    store = Stores(out_sem)
    other = (lambda ref: ref) if layer == 0 else (lambda ref: None)
    for name, index, target in (("q", QUERY, q_s), ("k", KEYS, k_s), ("v", VALUE, v_s)):
        loads.start(name, low.at[index], target, other(low_x.at[index]), second)
    loads.start("dc", dc, dc_s)
    meta = (bucket, count, lengths)
    by_span(meta, section, lambda span: fill_masks(span, rows, meta, section, bias_s, None))
    loads.wait("q", "k", "v", "dc")
    if layer == 0:
        loads.start("h", h_one.at[section], h_s)
    else:
        loads.start("h", h_one, h_s, h_two, second)
    loads.start("mix", mix, w_s.at[3])
    loads.start("da1", da1, dh_s)
    for name, own, received, target in (("wq", wq, xq, wq_s), ("wk", wk, xk, wk_s), ("wv", wv, xv, wv_s)):
        loads.start(name, own.at[0], target, received.at[0], layer_of(layer))
    by_span(meta, section, lambda span: attend_backward(span, rows, q_s, k_s, v_s, dc_s, bias_s, dq_s, dk_s, dv_s))
    loads.wait("h", "mix")
    me = lax.axis_index("dp")
    for unit, grad in enumerate((dq_s, dk_s, dv_s)):
        put_blocks(w_s, transposed_times(h_s[...], grad[...]), 0, unit, orders, me, False)
    send_units(store, w_s, away_o, home_o)
    loads.wait("da1", "wq", "wk", "wv")
    dh_s[...] += rows_times_transposed(dq_s[...], wq_s[...])
    dh_s[...] += rows_times_transposed(dk_s[...], wk_s[...])
    dh_s[...] += rows_times_transposed(dv_s[...], wv_s[...])
    store.start(dh_s, dh_o)
    sums_s[...] = jnp.zeros_like(sums_s)

    def finish(part):
        dlow_s[part, :] = dh_s[part, :].astype(BF16)
        sums_s[0] += fold_rows(dq_s[part, :].astype(F32))
        sums_s[1] += fold_rows(dv_s[part, :].astype(F32))

    over_chunks(rows, finish)
    store.start(dlow_s, dlow_o)
    for index in range(2):
        small_o[index : index + 1, :] = jnp.sum(sums_s[index], axis=0, keepdims=True)
    store.wait()


def unit_shapes(count, width):
    block = (count, width // count, width)
    return block, S((2,) + block, BF16)


def outer_gradient(layer, orders, count, meta, g, total, total_x, wide, wide_x, vec_own, vec_other):
    rows, width = total.shape[1:]
    hidden = wide.shape[2]
    flat = (rows, width)
    block, units = unit_shapes(count, width)
    return run_kernel(
        functools.partial(outer_kernel, layer, orders), (S(flat, F32), S(flat, BF16), units, units, S((3, width), F32)),
        [ANY] * 4 + [VM], [SM] * 3 + [ANY] * 5 + [VM] * 2,
        [V(flat, g.dtype), V(flat, F32), V((rows, hidden), BF16), V(flat, F32), V(flat, BF16), V((4,) + block, BF16), V((rows, 1), F32), V((3, 8, width), F32)],
        3, 4, 2 * rows * width * hidden, 12_000_000, "outer_gradient",
    )(*meta, g, total, total_x, wide, wide_x, vec_own, vec_other)


def inner_gradient(layer, orders, count, dz, wide, wide_x, low, low_x, wo, wo_x):
    rows, width = dz.shape
    hidden = wide.shape[2]
    flat = (rows, width)
    block, units = unit_shapes(count, width)
    return run_kernel(
        functools.partial(inner_kernel, layer, orders), (S((rows, hidden), BF16), units, units, S((1, hidden), F32)),
        [ANY] * 3 + [VM], [ANY] * 7,
        [V(flat, BF16), V((rows, hidden), BF16), V(flat, BF16), V((hidden, width), BF16), V((rows, hidden), BF16), V((4,) + block, BF16), V((rows, FFN_TILE), F32), V((rows, FFN_TILE), F32), V((8, hidden), F32)],
        4, 3, 4 * rows * width * hidden, 18_000_000, "inner_gradient",
    )(dz, wide, wide_x, low, low_x, wo, wo_x)


def mixer_gradient(layer, orders, count, df, wi, wi_x, da2, total, total_x, low, low_x, wm, wm_x, vec_own, vec_other):
    rows, width = da2.shape
    hidden = df.shape[1]
    flat = (rows, width)
    block, _ = unit_shapes(count, width)
    return run_kernel(
        functools.partial(mixer_kernel, layer, orders), (S(flat, F32), S(flat, BF16), S(block, BF16), S((3, width), F32)),
        [ANY] * 3 + [VM], [ANY] * 10 + [VM] * 2,
        [V((rows, hidden), BF16), V((width, hidden), BF16), V(flat, F32), V(flat, F32), V(flat, BF16), V((width, width), BF16), V(flat, F32), V(flat, F32), V(flat, BF16), V(flat, BF16), V((1,) + block, BF16), V((3, 8, width), F32)],
        6, 3, 2 * rows * width * (hidden + 2 * width), 15_000_000, "mixer_gradient",
    )(df, wi, wi_x, da2, total, total_x, low, low_x, wm, wm_x, vec_own, vec_other)


def attend_gradient(layer, orders, count, meta, low, low_x, dc, h_one, h_two, da1, weights, others, mix):
    rows, width = da1.shape
    flat = (rows, width)
    square = (width, width)
    block, units = unit_shapes(count, width)
    return run_kernel(
        functools.partial(attend_kernel, layer, orders), (S(flat, F32), S(flat, BF16), units, units, S((2, width), F32)),
        [ANY] * 4 + [VM], [SM] * 3 + [ANY] * 13,
        [V(flat, BF16)] * 5 + [V(flat, F32), V(flat, BF16)] + [V(square, BF16)] * 3 + [V(flat, BF16)] * 3 + [V((4,) + block, BF16), V((rows, 3 * BUCKET), F32), V((2, 8, width), F32)],
        10, 4, 12 * rows * width * width, 15_000_000, "attend_gradient",
    )(*meta, low, low_x, dc, h_one, h_two, da1, *weights, *others, mix)


def exchange(value, bit):
    count = lax.axis_size("dp")
    return lax.ppermute(value, "dp", [(index, index ^ bit) for index in range(count)])


def swap(value):
    return lax.ppermute(value, "section", [(0, 1), (1, 0)])


def hand_over(value, source):
    return lax.ppermute(value, "section", [(source, 1 - source)])


def widen(value):
    return value.astype(F32)


class UnitSum:
    def __init__(self, orders, away, home, extra=None):
        self.paths = [EXCHANGES[order] for order in orders]
        self.home = home
        self.extra = extra
        self.flying = swap(away)
        self.flying_extra = None if extra is None else swap(extra)
        self.step = -1
        self.result = None

    def arrive(self):
        if self.step == -1:
            totals = [widen(self.home[color]) + widen(self.flying[color]) for color in range(2)]
            if self.extra is not None:
                extra = widen(self.extra) + widen(self.flying_extra)
                totals[1] = jnp.concatenate([totals[1], extra], axis=1)
        else:
            totals = [widen(keep) + widen(part) for keep, part in zip(self.keeps, self.flying)]
        self.step += 1
        if self.step == 4:
            self.result = [total[0] for total in totals]
            return self.result
        half = totals[0].shape[0] // 2
        self.keeps = [total[:half].astype(BF16) for total in totals]
        self.sends = [total[half:].astype(BF16) for total in totals]
        return self.sends

    def depart(self):
        bits = [path[self.step] for path in self.paths]
        if bits[0] == bits[1]:
            height = self.sends[0].shape[1]
            both = exchange(jnp.concatenate(self.sends, axis=1), bits[0])
            self.flying = [both[:, :height], both[:, height:]]
        else:
            self.flying = [exchange(value, bit) for value, bit in zip(self.sends, bits)]


def per_device(
    tokens, cotangent, bucket, batch_size, lengths, query_weight, query_offset, keys_weight, value_weight, value_offset,
    mixer_weight, mixer_offset, first_gain, first_shift, inner_weight, inner_offset, outer_weight, outer_offset,
    second_gain, second_shift,
):
    section = lax.axis_index("section")
    groups = lax.axis_size("dp")
    width = tokens.shape[2]
    hidden = inner_offset.shape[1]
    height = width // groups
    hypercube = groups == 16 and width % (16 * groups) == 0
    count = groups if hypercube else 1
    meta = (bucket, batch_size, lengths)
    weights = (query_weight, keys_weight, value_weight, mixer_weight, inner_weight, outer_weight)
    vectors = (query_offset, value_offset, mixer_offset, first_gain, first_shift, outer_offset, second_gain, second_shift)
    others = tuple(swap(weight) for weight in weights)
    bi_other = swap(inner_offset)
    y_a, low_a, total_a, wide_a, vec_own = first_forward(meta, tokens, 0, weights, vectors, inner_offset)
    vec_other = swap(vec_own)
    y_b, low_b, total_b, wide_b, _ = first_forward(meta, tokens, 1, weights, vectors, inner_offset)
    y_x = hand_over(y_b, 0)
    y_c, low_c, total_c, wide_c = second_forward(
        meta, y_a, y_x, weights, others, vec_own, vec_other, inner_offset, bi_other
    )
    low_x, total_x, wide_x = (hand_over(value, 0) for value in (low_b, total_b, wide_b))
    y_cx = hand_over(y_c, 0)
    kept = {1: (low_c, low_c, total_c, total_c, wide_c, wide_c), 0: (low_a, low_x, total_a, total_x, wide_a, wide_x)}
    entries = {1: (y_a, y_x), 0: (tokens, tokens)}
    orders = ((0, 1), (2, 3), (0, 1))
    sums = {}
    pending = []

    def boundary(value, moves):
        ready = []
        for name in moves:
            ready.extend(sums[name].arrive())
        if not ready:
            return value
        held = lax.optimization_barrier((value, *ready))
        ready = list(held[1:])
        for name in moves:
            unit = sums[name]
            if unit.step == 4:
                unit.result = [ready.pop(0), ready.pop(0)]
            else:
                unit.sends = [ready.pop(0), ready.pop(0)]
                unit.depart()
        return held[0]

    grad = cotangent
    moves = SCHEDULE if hypercube else ((),) * 9
    raw = {}
    dh = {}
    for layer in (1, 0):
        low, lowx, total, totalx, wide, widex = kept[layer]
        turn = 4 * (1 - layer)
        grad = boundary(grad, moves[turn])
        da2, dz, outer_away, outer_home, small_two = outer_gradient(
            layer, orders[0], count, meta, grad, total, totalx, wide, widex, vec_own, vec_other
        )
        if hypercube:
            sums["o", layer] = UnitSum(orders[0], outer_away, outer_home)
        dz = boundary(dz, moves[turn + 1])
        df, inner_away, inner_home, small_inner = inner_gradient(
            layer, orders[1], count, dz, wide, widex, low, lowx, outer_weight, others[5]
        )
        if hypercube:
            sums["i", layer] = UnitSum(orders[1], inner_away, inner_home)
        df = boundary(df, moves[turn + 2])
        da1, dc, mix, small_one = mixer_gradient(
            layer, orders[2], count, df, inner_weight, others[4], da2, total, totalx, low, lowx, mixer_weight, others[3],
            vec_own, vec_other,
        )
        dc = boundary(dc, moves[turn + 3])
        dh[layer], grad, attend_away, attend_home, small_attend = attend_gradient(
            layer, orders[2], count, meta, low, lowx, dc, entries[layer][0], entries[layer][1], da1, weights[:3],
            others[:3], mix,
        )
        smalls = jnp.concatenate([small_attend, small_one, small_two], axis=0)
        if hypercube:
            flat = smalls.reshape(8, groups, height).transpose(1, 0, 2).reshape(groups, 8 * height)
            blocks = jnp.concatenate([flat, small_inner.reshape(groups, hidden // groups)], axis=1)
            blocks = jnp.pad(blocks, ((0, 0), (0, width - blocks.shape[1])))
            dest = jnp.arange(groups, dtype=jnp.int32)
            spot = spot_of(orders[2][1], dest, lax.axis_index("dp"))
            picked = (spot[None, :] == dest[:, None]).astype(F32)
            blocks = jnp.sum(picked[:, :, None] * blocks[None, :, :], axis=1)
            extra = jnp.pad(blocks[:, None, :], ((0, 0), (0, 7), (0, 0))).astype(BF16)
            sums["t", layer] = UnitSum(orders[2], attend_away, attend_home, extra)
        else:
            raw[layer] = [(outer_away, outer_home), (inner_away, inner_home), (attend_away, attend_home), smalls, small_inner]
    dh_x1 = hand_over(dh[1], 0)
    dh_x0 = hand_over(dh[0], 1)
    first = section == 0
    layer_out = jnp.stack([jnp.where(first, y_a, y_cx), jnp.where(first, y_b, y_c)])
    input_grad = jnp.stack([jnp.where(first, dh[0], dh_x1), jnp.where(first, dh_x0, dh[1])])
    if hypercube:
        dependent = jnp.zeros((), F32)
        for names in moves[8:]:
            dependent = boundary(dependent, names)
        found = {name: unit.result for name, unit in sums.items()}
    else:
        found = {}

        def scatter(value, dimension=0):
            return lax.psum_scatter(value, "dp", scatter_dimension=dimension, tiled=True)

        for layer in (1, 0):
            for name, (away, home) in zip("oit", raw[layer][:3]):
                total = (widen(home) + widen(swap(away))).astype(BF16)[:, 0]
                found[name, layer] = [widen(scatter(total[color])) for color in range(2)]
    finals = []
    for name in "oit":
        early, late = (found[name, 1], found[name, 0])
        send = jnp.stack([jnp.where(first, a[:height], b[:height]) for a, b in zip(early, late)])
        back = swap(send)
        mine = [jnp.where(first, b, a) for a, b in zip(early, late)]
        low_units = [jnp.where(first, mine[color][:height], back[color]) for color in range(2)]
        high_units = [jnp.where(first, back[color], mine[color][:height]) for color in range(2)]
        finals.append(low_units + high_units)
        if name == "t":
            mixed = mine[1]
    query_grad, keys_grad, value_grad, mixer_grad = finals[2]
    inner_grad = jnp.concatenate(finals[1], axis=1)
    if hypercube:
        outer_grad = jnp.concatenate(finals[0], axis=0)
        line = mixed[height]
        small = [line[index * height : (index + 1) * height] for index in range(8)]
        small_wide = line[8 * height : 8 * height + hidden // groups]
    else:
        parts = [[], []]
        for layer in (1, 0):
            smalls, small_inner = raw[layer][3:]
            smalls = smalls + swap(smalls)
            small_inner = small_inner + swap(small_inner)
            parts[layer] = [scatter(smalls[index]) for index in range(8)] + [scatter(small_inner[0])]
        chosen = [jnp.where(first, a, b) for a, b in zip(parts[0], parts[1])]
        small, small_wide = (chosen[:8], chosen[8])
        wholes = []
        for layer in (1, 0):
            away, home = raw[layer][0]
            whole = (widen(home) + widen(swap(away))).astype(BF16)[:, 0]
            pair = swap(whole)
            ordered = jnp.where(first, jnp.concatenate([whole, pair]), jnp.concatenate([pair, whole]))
            wholes.append(scatter(ordered.reshape(hidden, width)))
        outer_grad = widen(jnp.where(first, wholes[1], wholes[0]))
    grad_query_offset, grad_value_offset, grad_first_gain, grad_first_shift, grad_mixer_offset = small[:5]
    grad_second_gain, grad_second_shift, grad_outer_offset = small[5:8]
    outputs = (
        layer_out, input_grad, query_grad, grad_query_offset, keys_grad, value_grad, grad_value_offset, mixer_grad,
        grad_mixer_offset, grad_first_gain, grad_first_shift, inner_grad, small_wide, outer_grad, grad_outer_offset,
        grad_second_gain, grad_second_shift,
    )
    return tuple(piece[None] for piece in outputs)


O1, I1, T1, O0, I0, T0 = (("o", 1), ("i", 1), ("t", 1), ("o", 0), ("i", 0), ("t", 0))
SCHEDULE = (
    (),
    (),
    (O1,),
    (I1,),
    (O1,),
    (I1, T1),
    (O1, O0),
    (T1, I1, I0),
    (O1, O0, T1, T0),
    (I1, O1),
    (I0, O0, T0),
    (T1, I1),
    (O0, I0, T0),
    (T1, O0),
    (I0, T0),
    (I0, T0),
)


def solution(mesh):
    matrix = P("section", None, None)
    vector = P("section", None)
    in_specs = (
        P("dp", None, None), P("dp", None, None), P("dp"), P("dp"), P("dp", None), matrix, vector, matrix, matrix, vector,
        matrix, vector, vector, vector, matrix, vector, matrix, vector, vector, vector,
    )
    rows = P("section", "dp", None, None)
    grad = P("section", "dp", None)
    small = P("section", "dp")
    out_specs = (rows, rows, grad, small, grad, grad, small, grad, small, small, small, grad, small, grad, small, small, small)
    return jax.shard_map(per_device, mesh=mesh, in_specs=in_specs, out_specs=out_specs, check_vma=False)
```

```python
import functools
import jax
import jax.numpy as jnp
from jax import lax
from jax.experimental import pallas as pl
from jax.experimental.pallas import tpu as pltpu
from jax.sharding import PartitionSpec as P

HEADS = 12
HEAD_DIM = 64
BUCKET = 64
PAIR = 2 * HEAD_DIM
masked_score = -1000000000.0
norm_epsilon = 1e-06
F32 = jnp.float32
BF16 = jnp.bfloat16
CHUNK = 16
FFN_TILE = 512
ATT_UNROLL = 3


def rows_times(left, right):
    return lax.dot_general(left, right, (((1,), (0,)), ((), ())), preferred_element_type=F32)


def rows_times_transposed(left, right):
    return lax.dot_general(left, right, (((1,), (1,)), ((), ())), preferred_element_type=F32)


def transposed_times(left, right):
    return lax.dot_general(left, right, (((0,), (0,)), ((), ())), preferred_element_type=F32)


def slot_facts(block, span_rows, place, meta, micro):
    bucket_ref, count_ref, lengths_ref = meta
    bucket = bucket_ref[micro]
    count = count_ref[micro]

    def length_of(slot):
        return jnp.where(slot < count, lengths_ref[micro, slot], 0)

    if span_rows == 2 * BUCKET:
        return (jnp.full_like(place, block), place, jnp.full_like(place, length_of(block)))
    short = bucket == 0
    first = 3 * block
    slot_short = first + place // BUCKET
    length_short = jnp.where(
        place < BUCKET,
        length_of(first),
        jnp.where(place < 2 * BUCKET, length_of(first + 1), length_of(first + 2)),
    )
    slot = jnp.where(short, slot_short, block)
    inner = jnp.where(short, place % BUCKET, place)
    length = jnp.where(short, length_short, length_of(block))
    return (slot, inner, length)


def fill_masks(span_rows, row_count, meta, micro, bias_ref, valid_ref):
    for block in range(row_count // span_rows):
        row_place = lax.broadcasted_iota(jnp.int32, (span_rows, 1), 0)
        row_slot, row_inner, row_length = slot_facts(block, span_rows, row_place, meta, micro)
        rows = slice(block * span_rows, (block + 1) * span_rows)
        if bias_ref is not None:
            key_place = lax.broadcasted_iota(jnp.int32, (1, span_rows), 1)
            key_slot, key_inner, key_length = slot_facts(block, span_rows, key_place, meta, micro)
            key_tag = jnp.where(key_inner < key_length, key_slot, -1)
            allowed = (row_slot == key_tag) | (row_place == key_place)
            bias_ref[rows, 0:span_rows] = jnp.where(allowed, 0.0, masked_score)
        if valid_ref is not None:
            valid_ref[rows, :] = jnp.where(row_inner < row_length, 1.0, 0.0)


def by_span(meta, micro, body):
    even = meta[0][micro] == 1

    @pl.when(even)
    def _():
        body(2 * BUCKET)

    @pl.when(jnp.logical_not(even))
    def _():
        body(3 * BUCKET)


def attend_forward(span_rows, row_count, q_ref, k_ref, v_ref, bias_ref, c_ref):
    blocks = row_count // span_rows

    def one_pair(pair, carry):
        columns = pl.ds(pl.multiple_of(pair * PAIR, PAIR), PAIR)
        lane = lax.broadcasted_iota(jnp.int32, (span_rows, PAIR), 1)
        first_half = lane < HEAD_DIM
        weights = []
        for block in range(blocks):
            rows = slice(block * span_rows, (block + 1) * span_rows)
            query = q_ref[rows, columns] * jnp.asarray(HEAD_DIM ** (-0.5), BF16)
            keys = k_ref[rows, columns]
            zero = jnp.zeros_like(keys)
            bias = bias_ref[rows, 0:span_rows]
            for mine in (first_half, jnp.logical_not(first_half)):
                scores = rows_times_transposed(query, jnp.where(mine, keys, zero)) + bias
                top = jnp.max(scores, axis=-1, keepdims=True)
                weights.append(jnp.exp(scores - top).astype(BF16))
        for block in range(blocks):
            rows = slice(block * span_rows, (block + 1) * span_rows)
            value = v_ref[rows, columns]
            one = jnp.ones_like(value)
            left = rows_times(weights[2 * block], jnp.where(first_half, value, one))
            right = rows_times(weights[2 * block + 1], jnp.where(first_half, one, value))
            above = jnp.where(first_half, left, right)
            below = pltpu.roll(jnp.where(first_half, right, left), HEAD_DIM, 1)
            c_ref[rows, columns] = (above / below).astype(BF16)
        return carry

    lax.fori_loop(0, HEADS // 2, one_pair, 0, unroll=ATT_UNROLL)


def row_moments(values):
    center = jnp.mean(values, axis=-1, keepdims=True)
    centred = values - center
    spread = jnp.mean(centred * centred, axis=-1, keepdims=True)
    return centred, lax.rsqrt(spread + norm_epsilon)


def over_chunks(row_count, body, rows=CHUNK, group=6):
    def step(index, carry):
        for inner in range(group):
            start = pl.multiple_of(index * (rows * group) + inner * rows, rows)
            body(pl.ds(start, rows))
        return carry

    lax.fori_loop(0, row_count // (rows * group), step, 0)


def over_chunks_with_sums(row_count, body, sums_ref, rows=CHUNK, group=6):
    def step(index, carry):
        total = None
        for inner in range(group):
            start = pl.multiple_of(index * (rows * group) + inner * rows, rows)
            terms = [fold_rows(term) for term in body(pl.ds(start, rows))]
            total = terms if total is None else [a + b for a, b in zip(total, terms)]
        for place, term in enumerate(total):
            sums_ref[place] += term
        return carry

    lax.fori_loop(0, row_count // (rows * group), step, 0)


def fold_rows(values):
    return jnp.sum(values.reshape(values.shape[0] // 8, 8, values.shape[1]), axis=0)


def gelu_with_slope(values):
    cumulative = 0.5 + 0.5 * lax.erf(values * (0.5 ** 0.5))
    density = jnp.exp(values * values * -0.5) * 0.3989422804014327
    return values * cumulative, cumulative + values * density


ANY = pl.BlockSpec(memory_space=pl.ANY)
VM = pl.BlockSpec(memory_space=pltpu.VMEM)
SM = pl.BlockSpec(memory_space=pltpu.SMEM)
VMEM_LIMIT = 63_000 * 1024
S = jax.ShapeDtypeStruct
V = pltpu.VMEM
B_QUERY, B_VALUE, B_MIXER, GAIN_ONE, SHIFT_ONE, B_OUTER, GAIN_TWO, SHIFT_TWO = range(8)
X_BIT, Y_BIT, NEAR_BIT, FAR_BIT = (0, 1, 2, 3)
SMALL_ROWS = 16


class Loads:
    def __init__(self, semaphores):
        self.semaphores = semaphores
        self.copies = {}

    def start(self, name, source, target, other=None, take_other=None):
        semaphore = self.semaphores.at[len(self.copies)]
        copy = pltpu.make_async_copy(source, target, semaphore)
        self.copies[name] = copy
        if other is None:
            copy.start()
            return
        second = pltpu.make_async_copy(other, target, semaphore)

        @pl.when(take_other)
        def _():
            second.start()

        @pl.when(jnp.logical_not(take_other))
        def _():
            copy.start()

    def wait(self, *names):
        for name in names:
            self.copies[name].wait()


class Stores:
    def __init__(self, semaphores):
        self.semaphores = semaphores
        self.copies = []

    def start(self, source, target):
        copy = pltpu.make_async_copy(source, target, self.semaphores.at[len(self.copies)])
        copy.start()
        self.copies.append(copy)

    def wait(self):
        for copy in self.copies:
            copy.wait()


def run_kernel(kernel, outs, out_specs, in_specs, scratch, loads, stores, flops, bytes_moved, name):
    return pl.pallas_call(
        kernel,
        out_shape=outs,
        in_specs=in_specs,
        out_specs=out_specs,
        scratch_shapes=list(scratch) + [pltpu.SemaphoreType.DMA((loads,)), pltpu.SemaphoreType.DMA((stores,))],
        compiler_params=pltpu.CompilerParams(vmem_limit_bytes=VMEM_LIMIT),
        cost_estimate=pl.CostEstimate(flops=flops, bytes_accessed=bytes_moved, transcendentals=0),
        name=name,
    )


def spot_of(near_first, dest):
    relative = jnp.bitwise_xor(dest, lax.axis_index("dp"))

    def bit(index):
        return jnp.bitwise_and(lax.shift_right_logical(relative, index), 1)

    first = lax.axis_index("section") == 0
    lead = jnp.where(first, bit(X_BIT), bit(Y_BIT))
    follow = jnp.where(first, bit(Y_BIT), bit(X_BIT))
    if near_first:
        return bit(NEAR_BIT) * 8 + lead * 4 + follow * 2 + bit(FAR_BIT)
    return lead * 8 + follow * 4 + bit(NEAR_BIT) * 2 + bit(FAR_BIT)


def step_bits(near_first):
    cross = [(X_BIT, Y_BIT), (Y_BIT, X_BIT)]
    if near_first:
        return [(NEAR_BIT, NEAR_BIT)] + cross + [(FAR_BIT, FAR_BIT)]
    return cross + [(NEAR_BIT, NEAR_BIT), (FAR_BIT, FAR_BIT)]


def forward_matrix_loads(loads, hidden_start, weights, others, take_other, targets):
    names = ("wq", "wk", "wv", "wm", "wi", "wo")

    def begin(index):
        other = None if others is None else others[index].at[0]
        loads.start(names[index], weights[index].at[0], targets[index], other, take_other)

    def load(step):
        if step == 0:
            hidden_start()
            for index in range(3):
                begin(index)
            return
        if step == 1:
            loads.wait("h")
        loads.wait(names[step - 1])
        if step <= 3:
            begin(step + 2)

    return load


def forward_body(load, store, meta, micros, vec, bi, outs, refs):
    h_s, wq_s, wk_s, wv_s, wm_s, wi_s, wo_s, qkv_s, c_s, ml_s, a1_s, a2_s, u_s, gp_s, y_s, m_s, f0_s, e0_s, e1_s, bias_s, valid_s = refs
    y_o, qkv_o, c_o, ml_o, a1_o, a2_o, u_o, gp_o = outs
    rows, width = h_s.shape
    hidden = wi_s.shape[1]
    each = rows // len(micros)
    parts = [slice(place * each, (place + 1) * each) for place in range(len(micros))]

    def send(source, target):
        for place, part in enumerate(parts):
            store.start(source.at[part], target.at[place])

    load(0)
    for part, micro in zip(parts, micros):
        by_span(meta, micro, lambda span: fill_masks(span, each, meta, micro, bias_s.at[part], valid_s.at[part]))
    load(1)
    qkv_s[0] = (rows_times(h_s[...], wq_s[...]) + vec(B_QUERY)).astype(BF16)
    load(2)
    qkv_s[1] = rows_times(h_s[...], wk_s[...]).astype(BF16)
    load(3)
    qkv_s[2] = (rows_times(h_s[...], wv_s[...]) + vec(B_VALUE)).astype(BF16)
    for place, part in enumerate(parts):
        store.start(qkv_s.at[:, part], qkv_o.at[place])
    for part, micro in zip(parts, micros):
        by_span(
            meta, micro,
            lambda span: attend_forward(
                span, each, qkv_s.at[0, part], qkv_s.at[1, part], qkv_s.at[2, part], bias_s.at[part], c_s.at[part]
            ),
        )
    send(c_s, c_o)
    load(4)
    f0_s[...] = rows_times(c_s[...], wm_s[...])
    offset_mixer, gain_one, shift_one = (vec(B_MIXER), vec(GAIN_ONE), vec(SHIFT_ONE))

    def first_norm(part):
        total = h_s[part, :].astype(F32) + (f0_s[part, :] + offset_mixer)
        a1_s[part, :] = total
        centred, scale = row_moments(total)
        middle = centred * scale * gain_one + shift_one
        m_s[part, :] = middle
        ml_s[part, :] = middle.astype(BF16)

    over_chunks(rows, first_norm)
    send(a1_s, a1_o)
    send(ml_s, ml_o)
    load(5)
    tile = FFN_TILE
    tiles = hidden // tile

    def project(buffer, which):
        columns = pl.ds(pl.multiple_of(which * tile, tile), tile)
        buffer[...] = rows_times(ml_s[...], wi_s[:, columns])

    def activate(buffer, which):
        columns = pl.ds(pl.multiple_of(which * tile, tile), tile)
        offset = bi(columns)
        for start in range(0, rows, 32):
            part = slice(start, start + 32)
            value, slope = gelu_with_slope(buffer[part, :] + offset)
            u_s[part, columns] = value.astype(BF16)
            gp_s[part, columns] = slope.astype(BF16)

    project(e0_s, 0)

    def two_tiles(index, carry):
        project(e1_s, 2 * index + 1)
        activate(e0_s, 2 * index)
        project(e0_s, jnp.minimum(2 * index + 2, tiles - 1))
        activate(e1_s, 2 * index + 1)
        return carry

    lax.fori_loop(0, tiles // 2, two_tiles, 0)
    send(u_s, u_o)
    send(gp_s, gp_o)
    load(6)
    f0_s[...] = rows_times(u_s[...], wo_s[...])
    offset_outer, gain_two, shift_two = (vec(B_OUTER), vec(GAIN_TWO), vec(SHIFT_TWO))

    def second_norm(part):
        total = m_s[part, :] + (f0_s[part, :] + offset_outer)
        a2_s[part, :] = total
        centred, scale = row_moments(total)
        y_s[part, :] = ((centred * scale * gain_two + shift_two) * valid_s[part, :]).astype(BF16)

    over_chunks(rows, second_norm)
    send(y_s, y_o)
    send(a2_s, a2_o)
    store.wait()


def first_forward_kernel(
    micro_count, bucket, count, lengths, tok, wq, wk, wv, wm, wi, wo, bq, bv, bm, g1, s1, bo, g2, s2, bi,
    y_o, qkv_o, c_o, ml_o, a1_o, a2_o, u_o, gp_o, vec_o, *scratch
):
    *refs, in_sem, out_sem = scratch
    h_s, wq_s, wk_s, wv_s, wm_s, wi_s, wo_s = refs[:7]
    vectors = (bq, bv, bm, g1, s1, bo, g2, s2)
    for place, vector in enumerate(vectors):
        vec_o[place : place + 1, :] = vector[...]

    @pl.when(lax.axis_index("section") == 0)
    def _():
        loads = Loads(in_sem)
        each = h_s.shape[0] // micro_count

        def hidden_start():
            for micro in range(1, micro_count):
                loads.start(("h", micro), tok.at[micro], h_s.at[micro * each : (micro + 1) * each])
            loads.start("h", tok.at[0], h_s.at[0:each])

        inner_load = forward_matrix_loads(
            loads, hidden_start, (wq, wk, wv, wm, wi, wo), None, None, (wq_s, wk_s, wv_s, wm_s, wi_s, wo_s)
        )

        def load(step):
            if step == 1:
                for micro in range(1, micro_count):
                    loads.wait(("h", micro))
            inner_load(step)

        forward_body(
            load, Stores(out_sem), (bucket, count, lengths), tuple(range(micro_count)), lambda place: vectors[place][...],
            lambda columns: bi[:, columns], (y_o, qkv_o, c_o, ml_o, a1_o, a2_o, u_o, gp_o), refs,
        )


def second_forward_kernel(
    bucket, count, lengths, y_own, y_other, wq, wk, wv, wm, wi, wo, xq, xk, xv, xm, xi, xo, vec_own, vec_other, bi_own, bi_other,
    y_o, qkv_o, c_o, ml_o, a1_o, a2_o, u_o, gp_o, *scratch
):
    *refs, in_sem, out_sem = scratch
    h_s, wq_s, wk_s, wv_s, wm_s, wi_s, wo_s = refs[:7]
    section = lax.axis_index("section")
    first = section == 0
    loads = Loads(in_sem)
    load = forward_matrix_loads(
        loads, lambda: loads.start("h", y_other.at[section], h_s, y_own.at[section], first), (wq, wk, wv, wm, wi, wo),
        (xq, xk, xv, xm, xi, xo), first, (wq_s, wk_s, wv_s, wm_s, wi_s, wo_s),
    )

    def vec(place):
        return jnp.where(first, vec_other[place : place + 1, :], vec_own[place : place + 1, :])

    forward_body(
        load, Stores(out_sem), (bucket, count, lengths), (section,), vec,
        lambda columns: jnp.where(first, bi_other[:, columns], bi_own[:, columns]),
        (y_o, qkv_o, c_o, ml_o, a1_o, a2_o, u_o, gp_o), refs,
    )


def forward_shapes(micro_count, each, width, hidden):
    rows = micro_count * each
    flat = (rows, width)
    wide = (rows, hidden)
    square = (width, width)

    def out(*tail):
        return (micro_count,) + tail

    outs = (
        S(out(each, width), BF16), S(out(3, each, width), BF16), S(out(each, width), BF16), S(out(each, width), BF16),
        S(out(each, width), F32), S(out(each, width), F32), S(out(each, hidden), BF16), S(out(each, hidden), BF16),
    )
    scratch = [
        V(flat, BF16), V(square, BF16), V(square, BF16), V(square, BF16), V(square, BF16), V((width, hidden), BF16),
        V((hidden, width), BF16), V((3,) + flat, BF16), V(flat, BF16), V(flat, BF16), V(flat, F32), V(flat, F32),
        V(wide, BF16), V(wide, BF16), V(flat, BF16), V(flat, F32), V(flat, F32), V((rows, FFN_TILE), F32),
        V((rows, FFN_TILE), F32), V((rows, 3 * BUCKET), F32), V((rows, 1), F32),
    ]
    flops = 2 * rows * width * (4 * width + 2 * hidden)
    return outs, scratch, flops


def first_forward(meta, tokens, weights, vectors, bi):
    micro_count, each, width = tokens.shape
    outs, scratch, flops = forward_shapes(micro_count, each, width, bi.shape[1])
    return run_kernel(
        functools.partial(first_forward_kernel, micro_count), outs + (S((8, width), F32),), [ANY] * 8 + [VM],
        [SM] * 3 + [ANY] * 7 + [VM] * 9, scratch, 6 + micro_count, 8 * micro_count, flops, 40_000_000, "first_forward",
    )(*meta, tokens, *weights, *vectors, bi)


def second_forward(meta, y_own, y_other, weights, others, vec_own, vec_other, bi_own, bi_other):
    _, each, width = y_own.shape
    outs, scratch, flops = forward_shapes(1, each, width, bi_own.shape[1])
    return run_kernel(
        second_forward_kernel, outs, [ANY] * 8, [SM] * 3 + [ANY] * 14 + [VM] * 4, scratch, 7, 8, flops, 25_000_000,
        "second_forward",
    )(*meta, y_own, y_other, *weights, *others, vec_own, vec_other, bi_own, bi_other)


def norm_backward(grad, total, gain):
    centred, scale = row_moments(total)
    unit = centred * scale
    spread = grad * gain
    first = jnp.mean(spread, axis=-1, keepdims=True)
    second = jnp.mean(spread * unit, axis=-1, keepdims=True)
    return (spread - first - unit * second) * scale, grad * unit


def layer_of(layer):
    return lax.axis_index("section") != layer


def taken(layer, own, other, place):
    return jnp.where(layer_of(layer), other[place : place + 1, :], own[place : place + 1, :])


def kept_of(layer, own, other):
    if layer == 1:
        return own.at[0], None
    section = lax.axis_index("section")
    return own.at[section], other.at[section]


def feed_kernel(
    layer, bucket, count, lengths, g, a2, a2_x, gp, gp_x, a1, a1_x, wo, wo_x, wi, wi_x, wm, wm_x, vec_own, vec_other,
    dz_home_o, dz_away_o, df_home_o, df_away_o, da1_o, da_o, dc_o, small_o,
    g_s, a2_s, gp_s, a1_s, wo_s, wi_s, wm_s, da2_s, dz_s, df_s, dm_s, da1_s, da_s, dc_s, e0_s, e1_s, valid_s, sums_s, wide_s, in_sem, out_sem,
):
    section = lax.axis_index("section")
    rows, width = a2_s.shape
    hidden = df_s.shape[1]
    second = section == 1
    loads = Loads(in_sem)
    store = Stores(out_sem)
    loads.start("g", g.at[section] if layer == 1 else g, g_s)
    loads.start("a2", kept_of(layer, a2, a2_x)[0], a2_s, kept_of(layer, a2, a2_x)[1], second)
    loads.start("wo", wo.at[0], wo_s, wo_x.at[0], layer_of(layer))
    meta = (bucket, count, lengths)
    by_span(meta, section, lambda span: fill_masks(span, rows, meta, section, None, valid_s))
    sums_s[...] = jnp.zeros_like(sums_s)
    gain_two = taken(layer, vec_own, vec_other, GAIN_TWO)
    gain_one = taken(layer, vec_own, vec_other, GAIN_ONE)
    loads.wait("g", "a2")
    loads.start("gp", kept_of(layer, gp, gp_x)[0], gp_s, kept_of(layer, gp, gp_x)[1], second)
    loads.start("wi", wi.at[0], wi_s, wi_x.at[0], layer_of(layer))

    def second_norm(part):
        grad = g_s[part, :].astype(F32) * valid_s[part, :]
        moved, gained = norm_backward(grad, a2_s[part, :], gain_two)
        da2_s[part, :] = moved
        low = moved.astype(BF16)
        dz_s[part, :] = low
        return gained, grad, low.astype(F32)

    over_chunks_with_sums(rows, second_norm, sums_s.at[0:3])
    half = width // 2
    store.start(dz_s.at[:, pl.ds(pl.multiple_of(section * half, half), half)], dz_home_o)
    store.start(dz_s.at[:, pl.ds(pl.multiple_of((1 - section) * half, half), half)], dz_away_o)
    tile = FFN_TILE
    tiles = hidden // tile

    def project(buffer, which):
        columns = pl.ds(pl.multiple_of(which * tile, tile), tile)
        buffer[...] = rows_times_transposed(dz_s[...], wo_s[columns, :])

    def slope(buffer, which):
        columns = pl.ds(pl.multiple_of(which * tile, tile), tile)
        total = None
        for start in range(0, rows, 32):
            part = slice(start, start + 32)
            low_part = (buffer[part, :] * gp_s[part, columns].astype(F32)).astype(BF16)
            df_s[part, columns] = low_part
            term = fold_rows(low_part.astype(F32))
            total = term if total is None else total + term
        wide_s[:, columns] = total

    loads.wait("wo")
    loads.start("a1", kept_of(layer, a1, a1_x)[0], a1_s, kept_of(layer, a1, a1_x)[1], second)
    loads.start("wm", wm.at[0], wm_s, wm_x.at[0], layer_of(layer))
    project(e0_s, 0)
    loads.wait("gp")

    def two_tiles(index, carry):
        project(e1_s, 2 * index + 1)
        slope(e0_s, 2 * index)
        project(e0_s, jnp.minimum(2 * index + 2, tiles - 1))
        slope(e1_s, 2 * index + 1)
        return carry

    lax.fori_loop(0, tiles // 2, two_tiles, 0)
    half = hidden // 2
    store.start(df_s.at[:, pl.ds(pl.multiple_of(section * half, half), half)], df_home_o)
    store.start(df_s.at[:, pl.ds(pl.multiple_of((1 - section) * half, half), half)], df_away_o)
    loads.wait("wi")
    dm_s[...] = rows_times_transposed(df_s[...], wi_s[...])
    loads.wait("a1")

    def first_norm(part):
        grad = dm_s[part, :] + da2_s[part, :]
        moved, gained = norm_backward(grad, a1_s[part, :], gain_one)
        da1_s[part, :] = moved
        low_part = moved.astype(BF16)
        da_s[part, :] = low_part
        return gained, grad, low_part.astype(F32)

    over_chunks_with_sums(rows, first_norm, sums_s.at[3:6])
    store.start(da1_s, da1_o)
    store.start(da_s, da_o)
    for index in range(6):
        small_o[index : index + 1, :] = jnp.sum(sums_s[index], axis=0, keepdims=True)
    inner_sum = jnp.sum(wide_s[...], axis=0, keepdims=True)
    for index in range(hidden // width):
        small_o[8 + index : 9 + index, :] = inner_sum[:, index * width : (index + 1) * width]
    loads.wait("wm")
    dc_s[...] = rows_times_transposed(da_s[...], wm_s[...]).astype(BF16)
    store.start(dc_s, dc_o)
    store.wait()


def feed_gradient(layer, meta, g, kept, kept_x, weights, others, vec_own, vec_other):
    a1, a2, gp = (kept[name] for name in ("a1", "a2", "gp"))
    a1_x, a2_x, gp_x = (kept_x[name] for name in ("a1", "a2", "gp"))
    rows, width = a1.shape[1:]
    hidden = gp.shape[2]
    flat = (rows, width)
    half = S((rows, width // 2), BF16)
    half_wide = S((rows, hidden // 2), BF16)
    return run_kernel(
        functools.partial(feed_kernel, layer),
        (half, half, half_wide, half_wide, S(flat, F32), S(flat, BF16), S(flat, BF16), S((SMALL_ROWS, width), F32)),
        [ANY] * 7 + [VM], [SM] * 3 + [ANY] * 13 + [VM] * 2,
        [
            V(flat, g.dtype), V(flat, F32), V((rows, hidden), BF16), V(flat, F32), V((hidden, width), BF16), V((width, hidden), BF16),
            V((width, width), BF16), V(flat, F32), V(flat, BF16), V((rows, hidden), BF16), V(flat, F32), V(flat, F32), V(flat, BF16),
            V(flat, BF16), V((rows, FFN_TILE), F32), V((rows, FFN_TILE), F32), V((rows, 1), F32), V((6, 8, width), F32),
            V((8, hidden), F32),
        ],
        7, 7, 2 * rows * width * (2 * hidden + width), 25_000_000, "feed_gradient",
    )(*meta, g, a2, a2_x, gp, gp_x, a1, a1_x, weights[5], others[5], weights[4], others[4], weights[3], others[3], vec_own, vec_other)


def attend_backward(span_rows, row_count, q_ref, k_ref, v_ref, dc_ref, bias_ref, dq_ref, dk_ref, dv_ref):
    blocks = row_count // span_rows
    scale = HEAD_DIM ** (-0.5)

    def one_pair(pair, carry):
        columns = pl.ds(pl.multiple_of(pair * PAIR, PAIR), PAIR)
        lane = lax.broadcasted_iota(jnp.int32, (span_rows, PAIR), 1)
        halves = (lane < HEAD_DIM, lane >= HEAD_DIM)
        for block in range(blocks):
            rows = slice(block * span_rows, (block + 1) * span_rows)
            query = q_ref[rows, columns] * jnp.asarray(scale, BF16)
            keys = k_ref[rows, columns]
            value = v_ref[rows, columns]
            grad = dc_ref[rows, columns]
            zero = jnp.zeros_like(keys)
            bias = bias_ref[rows, 0:span_rows]
            dq = dk = dv = None
            for mine in halves:
                keys_own = jnp.where(mine, keys, zero)
                scores = rows_times_transposed(query, keys_own) + bias
                grad_part = rows_times_transposed(grad, jnp.where(mine, value, zero))
                top = jnp.max(scores, axis=-1, keepdims=True)
                weight = jnp.exp(scores - top)
                part = weight * (1.0 / jnp.sum(weight, axis=-1, keepdims=True))
                mean = jnp.sum(grad_part * part, axis=-1, keepdims=True)
                grad_scores = (part * (grad_part - mean)).astype(BF16)
                terms = (
                    rows_times(grad_scores, keys_own),
                    transposed_times(grad_scores, jnp.where(mine, query, zero)),
                    transposed_times(part.astype(BF16), jnp.where(mine, grad, zero)),
                )
                if dq is None:
                    dq, dk, dv = terms
                else:
                    dq, dk, dv = (dq + terms[0], dk + terms[1], dv + terms[2])
            dq_ref[rows, columns] = (dq * scale).astype(BF16)
            dk_ref[rows, columns] = dk.astype(BF16)
            dv_ref[rows, columns] = dv.astype(BF16)
        return carry

    lax.fori_loop(0, HEADS // 2, one_pair, 0)


def attend_kernel(
    layer, bucket, count, lengths, qkv, qkv_x, dc, da, da1, wq, wk, wv, xq, xk, xv,
    dh_o, dlow_o, home_o, away_o, small_o,
    qkv_s, dc_s, da_s, dh_s, dlow_s, wq_s, wk_s, wv_s, dq_s, dk_s, dv_s, bias_s, sums_s, in_sem, out_sem,
):
    section = lax.axis_index("section")
    rows, width = dc_s.shape
    second = section == 1
    loads = Loads(in_sem)
    store = Stores(out_sem)
    loads.start("qkv", kept_of(layer, qkv, qkv_x)[0], qkv_s, kept_of(layer, qkv, qkv_x)[1], second)
    loads.start("dc", dc, dc_s)
    meta = (bucket, count, lengths)
    by_span(meta, section, lambda span: fill_masks(span, rows, meta, section, bias_s, None))
    loads.wait("qkv", "dc")
    loads.start("da", da, da_s)
    loads.start("da1", da1, dh_s)
    for name, own, received, target in (("wq", wq, xq, wq_s), ("wk", wk, xk, wk_s), ("wv", wv, xv, wv_s)):
        loads.start(name, own.at[0], target, received.at[0], layer_of(layer))
    by_span(
        meta, section,
        lambda span: attend_backward(span, rows, qkv_s.at[0], qkv_s.at[1], qkv_s.at[2], dc_s, bias_s, dq_s, dk_s, dv_s),
    )
    loads.wait("da")
    pairs = ((dq_s, dk_s), (dv_s, da_s))
    for core in range(2):
        @pl.when(section == core)
        def _(core=core):
            for place in range(2):
                pltpu.make_async_copy(pairs[core][place], home_o.at[place], out_sem.at[place]).start()
                pltpu.make_async_copy(pairs[1 - core][place], away_o.at[place], out_sem.at[2 + place]).start()
    loads.wait("da1", "wq", "wk", "wv")
    dh_s[...] += rows_times_transposed(dq_s[...], wq_s[...])
    dh_s[...] += rows_times_transposed(dk_s[...], wk_s[...])
    dh_s[...] += rows_times_transposed(dv_s[...], wv_s[...])
    sums_s[...] = jnp.zeros_like(sums_s)

    def finish(part):
        dlow_s[part, :] = dh_s[part, :].astype(BF16)
        return dq_s[part, :].astype(F32), dv_s[part, :].astype(F32)

    over_chunks_with_sums(rows, finish, sums_s)
    last = [
        pltpu.make_async_copy(dh_s, dh_o, out_sem.at[4]),
        pltpu.make_async_copy(dlow_s, dlow_o, out_sem.at[5]),
    ]
    for copy in last:
        copy.start()
    for index in range(2):
        small_o[index : index + 1, :] = jnp.sum(sums_s[index], axis=0, keepdims=True)
    for place in range(2):
        pltpu.make_async_copy(pairs[0][place], home_o.at[place], out_sem.at[place]).wait()
        pltpu.make_async_copy(pairs[1][place], away_o.at[place], out_sem.at[2 + place]).wait()
    for copy in last:
        copy.wait()


def attend_gradient(layer, meta, kept, kept_x, dc, da, da1, weights, others):
    rows, width = da1.shape
    flat = (rows, width)
    square = (width, width)
    return run_kernel(
        functools.partial(attend_kernel, layer),
        (S(flat, F32), S(flat, BF16), S((2,) + flat, BF16), S((2,) + flat, BF16), S((8, width), F32)),
        [ANY] * 4 + [VM], [SM] * 3 + [ANY] * 11,
        [V((3,) + flat, BF16), V(flat, BF16), V(flat, BF16), V(flat, F32), V(flat, BF16)] + [V(square, BF16)] * 3 + [V(flat, BF16)] * 3
        + [V((rows, 3 * BUCKET), F32), V((2, 8, width), F32)],
        7, 6, 6 * rows * width * width, 15_000_000, "attend_gradient",
    )(*meta, kept["qkv"], kept_x["qkv"], dc, da, da1, *weights[:3], *others[:3])


def by_owner(loads, name, own, other, target):
    rows = target.shape[0] // 2
    section = lax.axis_index("section")
    loads.start((name, 0), own, target.at[pl.ds(pl.multiple_of(section * rows, rows), rows)])
    loads.start((name, 1), other, target.at[pl.ds(pl.multiple_of((1 - section) * rows, rows), rows)])


def both_micros(layer, loads, name, own, other, target):
    if layer == 1:
        by_owner(loads, name, own.at[0], other.at[0], target)
        return
    rows = target.shape[0] // 2
    for micro in range(2):
        part = target.at[micro * rows : (micro + 1) * rows]
        loads.start((name, micro), own.at[micro], part, other.at[micro], lax.axis_index("section") == 1)


def put_rows(target, near_first, value, at_row, at_lane, dest):
    spot = 0 if target.shape[0] == 1 else spot_of(near_first, dest)
    rows, lanes = value.shape
    target[spot, at_row : at_row + rows, at_lane : at_lane + lanes] = value.astype(BF16)


def feed_weights_kernel(
    layer, near_first, u, u_x, ml, ml_x, dz, dz_x, df, df_x,
    send_o, keep_o,
    u_s, ml_s, dz_s, df_s, w_s, in_sem, out_sem,
):
    hidden = u_s.shape[1]
    width = ml_s.shape[1]
    rows = dz.shape[0]
    spots = w_s.shape[0]
    loads = Loads(in_sem)
    store = Stores(out_sem)
    by_owner(loads, "dz", dz, dz_x, dz_s)
    both_micros(layer, loads, "u", u, u_x, u_s)
    loads.wait(("dz", 0), ("dz", 1), ("u", 0), ("u", 1))
    both_micros(layer, loads, "ml", ml, ml_x, ml_s)
    by_owner(loads, "df", df, df_x, df_s)
    half_rows = hidden // spots // 2
    tile = min(width, half_rows * 2) if spots == 1 else width
    for index in range(hidden // tile):
        product = transposed_times(u_s[:, index * tile : (index + 1) * tile], dz_s[...])
        block = min(half_rows, tile)
        for inner in range(tile // block):
            row = index * tile + inner * block
            dest, offset = divmod(row, 2 * half_rows)
            side, at_row = divmod(offset, half_rows)
            put_rows(w_s, near_first, product[inner * block : (inner + 1) * block, :], at_row, side * (width // 2), dest)
    loads.wait(("ml", 0), ("ml", 1), ("df", 0), ("df", 1))
    height = width // spots
    for side in range(2):
        product = transposed_times(ml_s[...], df_s[:, side * width : (side + 1) * width])
        for dest in range(spots):
            put_rows(w_s, near_first, product[dest * height : (dest + 1) * height, :], half_rows + side * height, 0, dest)
    split = spots // 2
    if spots > 1:
        store.start(w_s.at[split:spots], send_o)
        store.start(w_s.at[0:split], keep_o)
    else:
        store.start(w_s, send_o)
        store.start(w_s, keep_o)
    store.wait()


def unit_outs(spots, rows, width):
    half = S((max(spots // 2, 1), rows, width), BF16)
    return half, half


def feed_weights(layer, near_first, spots, kept, kept_x, dz, dz_x, df, df_x):
    u, u_x, ml, ml_x = (kept["u"], kept_x["u"], kept["ml"], kept_x["ml"])
    rows, width = ml.shape[1:]
    hidden = u.shape[2]
    total = hidden // spots // 2 + 2 * (width // spots)
    return run_kernel(
        functools.partial(feed_weights_kernel, layer, near_first), unit_outs(spots, total, width), [ANY] * 2, [ANY] * 8,
        [
            V((2 * rows, hidden), BF16), V((2 * rows, width), BF16), V((2 * rows, width // 2), BF16), V((2 * rows, hidden // 2), BF16),
            V((spots, total, width), BF16),
        ],
        8, 2, 4 * rows * width * hidden, 18_000_000, "feed_weights",
    )(u, u_x, ml, ml_x, dz, dz_x, df, df_x)


def attend_weights_kernel(
    layer, near_first, h, h_x, c, c_x, grads, grads_x, small_one, small_one_x, small_two, small_two_x,
    send_o, keep_o,
    left_s, right_s, w_s, in_sem, out_sem,
):
    section = lax.axis_index("section")
    second = section == 1
    rows, width = grads.shape[1:]
    spots = w_s.shape[0]
    loads = Loads(in_sem)
    store = Stores(out_sem)
    for micro in range(2):
        part = slice(micro * rows, (micro + 1) * rows)
        loads.start(("h", micro), h.at[micro], left_s.at[0, part], h_x.at[micro], second)
    by_owner(loads, "g", grads.at[0], grads_x.at[0], right_s.at[0])
    if layer == 0:
        for micro in range(2):
            part = slice(micro * rows, (micro + 1) * rows)
            loads.start(("c", micro), h.at[micro], left_s.at[1, part], c_x.at[micro], second)
    else:
        for place, (plain, context) in enumerate(((h, c), (h_x, c_x))):
            micro = section if place == 0 else 1 - section
            part = left_s.at[1, pl.ds(pl.multiple_of(micro * rows, rows), rows)]
            loads.start(("c", place), h.at[micro], part, context.at[0], second)
    by_owner(loads, "f", grads.at[1], grads_x.at[1], right_s.at[1])
    height = width // spots
    small = jnp.concatenate([small_one[0:6, :] + small_one_x[0:6, :], small_two[0:2, :] + small_two_x[0:2, :], small_one[8:16, :] + small_one_x[8:16, :]], axis=0)
    low = small.astype(BF16)
    for spot in range(spots):
        w_s[spot, 2 * height : 2 * height + SMALL_ROWS, :] = low
    for side, name in enumerate(("h", "c")):
        grad_name = ("g", "f")[side]
        loads.wait((name, 0), (name, 1), (grad_name, 0), (grad_name, 1))
        product = transposed_times(left_s[side], right_s[side])
        for dest in range(spots):
            put_rows(w_s, near_first, product[dest * height : (dest + 1) * height, :], side * height, 0, dest)
    split = spots // 2
    if spots > 1:
        store.start(w_s.at[split:spots], send_o)
        store.start(w_s.at[0:split], keep_o)
    else:
        store.start(w_s, send_o)
        store.start(w_s, keep_o)
    store.wait()


def attend_weights(layer, near_first, spots, h, h_x, c, c_x, grads, grads_x, smalls):
    rows, width = grads.shape[1:]
    total = 2 * (width // spots) + SMALL_ROWS
    return run_kernel(
        functools.partial(attend_weights_kernel, layer, near_first), unit_outs(spots, total, width), [ANY] * 2, [ANY] * 6 + [VM] * 4,
        [V((2, 2 * rows, width), BF16), V((2, 2 * rows, width), BF16), V((spots, total, width), BF16)],
        8, 2, 8 * rows * width * width, 10_000_000, "attend_weights",
    )(h, h_x, c, c_x, grads, grads_x, *smalls)


def add_kernel(count, *refs):
    keeps = refs[0:count]
    parts = refs[count : 2 * count]
    outs = list(refs[2 * count :])
    for keep, part in zip(keeps, parts):
        spots, rows, _ = keep.shape
        if spots == 1:
            target = outs.pop(0)
            target[...] = keep[0].astype(F32) + part[0].astype(F32)
            continue
        halves = (outs.pop(0), outs.pop(0))
        for half in range(2):
            base = (1 - half) * (spots // 2)

            def one(spot, carry):
                halves[half][spot] = (keep[base + spot].astype(F32) + part[base + spot].astype(F32)).astype(BF16)
                return carry

            lax.fori_loop(0, spots // 2, one, 0)


def add_arrived(pairs):
    outs = []
    for keep, _ in pairs:
        spots, rows, width = keep.shape
        if spots == 1:
            outs.append(S((rows, width), F32))
        else:
            outs.extend([S((spots // 2, rows, width), BF16)] * 2)
    moved = sum(3 * keep.size for keep, _ in pairs)
    results = list(
        pl.pallas_call(
            functools.partial(add_kernel, len(pairs)),
            out_shape=tuple(outs),
            in_specs=[VM] * (2 * len(pairs)),
            out_specs=(VM,) * len(outs),
            compiler_params=pltpu.CompilerParams(vmem_limit_bytes=ADD_LIMIT),
            cost_estimate=pl.CostEstimate(flops=moved, bytes_accessed=2 * moved, transcendentals=0),
            name="add_arrived",
        )(*[keep for keep, _ in pairs], *[part for _, part in pairs])
    )
    taken_back = []
    for keep, _ in pairs:
        if keep.shape[0] == 1:
            taken_back.append((results.pop(0),))
        else:
            taken_back.append((results.pop(0), results.pop(0)))
    return taken_back


ADD_LIMIT = 40_000 * 1024


def finish_kernel(
    feed_first, feed_second, attend_first, attend_second, feed_back_first, feed_back_second, attend_back_first, attend_back_second,
    q_o, k_o, v_o, m_o, i_o, o_o, small_o, wide_o,
):
    section = lax.axis_index("section")
    groups = lax.axis_size("dp")
    me = lax.axis_index("dp")
    height, width = q_o.shape
    half_rows = o_o.shape[0] // 2
    hidden = i_o.shape[1]
    for core in range(2):
        @pl.when(section == core)
        def _(core=core):
            mine = (feed_first, attend_first) if core == 0 else (feed_second, attend_second)
            back = (feed_back_first, attend_back_first) if core == 0 else (feed_back_second, attend_back_second)
            sides = (mine, back) if core == 0 else (back, mine)
            for side, (feed, attend) in enumerate(sides):
                for part in range(2):
                    o_o[part * half_rows : (part + 1) * half_rows, side * (width // 2) : (side + 1) * (width // 2)] = feed[
                        0:half_rows, part * (width // 2) : (part + 1) * (width // 2)
                    ]
                    i_o[:, (2 * side + part) * width : (2 * side + part + 1) * width] = feed[
                        half_rows + part * height : half_rows + (part + 1) * height, :
                    ]
            q_o[...] = sides[0][1][0:height, :]
            k_o[...] = sides[0][1][height : 2 * height, :]
            v_o[...] = sides[1][1][0:height, :]
            m_o[...] = sides[1][1][height : 2 * height, :]
            lines = mine[1][2 * height : 2 * height + SMALL_ROWS, :]
            small_o[...] = pltpu.roll(lines[0:8, :], jnp.bitwise_and(width - me * height, 1023) % width, 1)
            span = hidden // groups
            row = me // (width // span)
            pick = lax.broadcasted_iota(jnp.int32, (8, width), 0) == row
            chosen = jnp.sum(jnp.where(pick, lines[8:16, :], 0.0), axis=0, keepdims=True)
            offset = (me % (width // span)) * span
            wide_o[...] = pltpu.roll(jnp.broadcast_to(chosen, (8, width)), (width - offset) % width, 1)


def finish(groups, width, hidden, results):
    height = width // groups
    square = S((height, width), F32)
    return pl.pallas_call(
        finish_kernel,
        out_shape=(square, square, square, square, S((height, hidden), F32), S((hidden // groups, width), F32), S((8, width), F32), S((8, width), F32)),
        in_specs=[VM] * 8,
        out_specs=(VM,) * 8,
        compiler_params=pltpu.CompilerParams(vmem_limit_bytes=ADD_LIMIT),
        name="finish_gradients",
    )(*results)


def exchange(value, bits):
    groups = lax.axis_size("dp")
    pairs = [(2 * group + core, 2 * (group ^ (1 << bits[core])) + core) for group in range(groups) for core in range(2)]
    return lax.ppermute(value, ("dp", "section"), pairs)


def swap(value):
    return lax.ppermute(value, "section", [(0, 1), (1, 0)])


def hand_over(value, source):
    return lax.ppermute(value, "section", [(source, 1 - source)])


NAMES = ("qkv", "c", "ml", "a1", "a2", "u", "gp")
F1, T1, F0, T0 = (("f", 1), ("t", 1), ("f", 0), ("t", 0))
NEAR_FIRST = {F1: False, T1: True, F0: False, T0: True}
SCHEDULE = (
    (),
    (),
    (),
    (),
    (),
    (F1, T1),
    (),
    (F1, T1),
    (F1, T1),
    (F0,),
    (F1, T1, T0),
    (F0, T0),
    (F0, T0),
    (F0, T0),
)


def per_device(
    tokens, cotangent, bucket, batch_size, lengths, query_weight, query_offset, keys_weight, value_weight, value_offset,
    mixer_weight, mixer_offset, first_gain, first_shift, inner_weight, inner_offset, outer_weight, outer_offset,
    second_gain, second_shift,
):
    section = lax.axis_index("section")
    groups = lax.axis_size("dp")
    width = tokens.shape[2]
    hidden = inner_offset.shape[1]
    hypercube = groups == 16
    spots = groups if hypercube else 1
    first = section == 0
    meta = (bucket, batch_size, lengths)
    weights = (query_weight, keys_weight, value_weight, mixer_weight, inner_weight, outer_weight)
    vectors = (query_offset, value_offset, mixer_offset, first_gain, first_shift, outer_offset, second_gain, second_shift)
    others = tuple(swap(weight) for weight in weights)
    bi_other = swap(inner_offset)
    y_first, *kept_first, vec_own = first_forward(meta, tokens, weights, vectors, inner_offset)
    vec_other = swap(vec_own)
    y_x = hand_over(y_first, 0)
    y_second, *kept_second = second_forward(meta, y_first, y_x, weights, others, vec_own, vec_other, inner_offset, bi_other)
    kept = {0: dict(zip(NAMES, kept_first)), 1: dict(zip(NAMES, kept_second))}
    kept_x = {0: {name: hand_over(value, 0) for name, value in kept[0].items()}, 1: dict(kept[1])}
    for name in ("u", "ml", "c"):
        kept_x[1][name] = swap(kept[1][name])
    entries = {1: (y_first, y_x), 0: (tokens, tokens)}
    y_last_x = hand_over(y_second, 0)
    moving = {}
    results = {}

    def boundary(value, names):
        if not names or not hypercube:
            return value
        added = add_arrived([(moving[name][0], moving[name][1]) for name in names])
        held = lax.optimization_barrier((value, added))
        for name, parts in zip(names, held[1]):
            if len(parts) == 1:
                results[name] = parts[0]
            else:
                step = moving[name][2] + 1
                moving[name] = (parts[1], exchange(parts[0], step_bits(NEAR_FIRST[name])[step]), step)
        return held[0]

    def begin(name, send, keep):
        if hypercube:
            moving[name] = (keep, exchange(send, step_bits(NEAR_FIRST[name])[0]), 0)
        else:
            moving[name] = send

    grad = cotangent
    dh = {}
    for layer in (1, 0):
        turn = 4 * (1 - layer)
        grad = boundary(grad, SCHEDULE[turn])
        dz, dz_away, df, df_away, da1, da, dc, small_one = feed_gradient(
            layer, meta, grad, kept[layer], kept_x[layer], weights, others, vec_own, vec_other
        )
        dz_x, df_x, small_one_x = (swap(dz_away), swap(df_away), swap(small_one))
        dz = boundary(dz, SCHEDULE[turn + 1])
        begin(("f", layer), *feed_weights(layer, NEAR_FIRST["f", layer], spots, kept[layer], kept_x[layer], dz, dz_x, df, df_x))
        dc = boundary(lax.optimization_barrier((dc, moving["f", layer][0]))[0], SCHEDULE[turn + 2])
        dh[layer], grad, grads, grads_away, small_two = attend_gradient(
            layer, meta, kept[layer], kept_x[layer], dc, da, da1, weights, others
        )
        grads_x, small_two_x = (swap(grads_away), swap(small_two))
        grads = boundary(grads, SCHEDULE[turn + 3])
        begin(
            ("t", layer),
            *attend_weights(
                layer, NEAR_FIRST["t", layer], spots, *entries[layer], kept[layer]["c"], kept_x[layer]["c"], grads, grads_x,
                (small_one, small_one_x, small_two, small_two_x),
            ),
        )
        grad = lax.optimization_barrier((grad, moving["t", layer][0]))[0]
    dh_x1 = hand_over(dh[1], 0)
    dh_x0 = hand_over(dh[0], 1)
    layer_out = jnp.stack([jnp.where(first, y_first[0], y_last_x[0]), jnp.where(first, y_first[1], y_second[0])])
    input_grad = jnp.stack([jnp.where(first, dh[0], dh_x1), jnp.where(first, dh_x0, dh[1])])
    if hypercube:
        anchor = jnp.zeros((), F32)
        for names in SCHEDULE[8:]:
            anchor = boundary(anchor, names)
        back = {name: hand_over(results[name], 1 - name[1]) for name in (F1, T1, F0, T0)}
        done = finish(
            groups, width, hidden,
            (results[F0], results[F1], results[T0], results[T1], back[F0], back[F1], back[T0], back[T1]),
        )
        query_grad, keys_grad, value_grad, mixer_grad, inner_grad, outer_grad, lines, wide_line = done
        height = width // groups
        small = [lines[index, :height] for index in range(8)]
        small_wide = wide_line[0, : hidden // groups]
    else:
        def scatter(value):
            return lax.psum_scatter(value, "dp", scatter_dimension=0, tiled=True).astype(F32)

        found = []
        for layer in (1, 0):
            feed = moving["f", layer][0]
            attend = moving["t", layer][0]
            half_rows = hidden // 2
            outer_half = jnp.concatenate([feed[:half_rows, : width // 2], feed[:half_rows, width // 2 :]], axis=0)
            parts = [scatter(outer_half), scatter(feed[half_rows : half_rows + width]), scatter(feed[half_rows + width :])]
            parts += [scatter(attend[:width]), scatter(attend[width : 2 * width])]
            lines = attend[2 * width :].astype(F32)
            parts += [scatter(lines[index]) for index in range(8)] + [scatter(lines[8:12].reshape(-1))]
            found.append(parts)
        mine = [jnp.where(first, b, a) for a, b in zip(*found)]
        back = [swap(jnp.where(first, a, b)) for a, b in zip(found[0][:5], found[1][:5])]
        low = [jnp.where(first, a, b) for a, b in zip(mine, back)]
        high = [jnp.where(first, b, a) for a, b in zip(mine, back)]
        outer_grad = jnp.concatenate([low[0], high[0]], axis=1)
        inner_grad = jnp.concatenate([low[1], low[2], high[1], high[2]], axis=1)
        query_grad, keys_grad, value_grad, mixer_grad = (low[3], low[4], high[3], high[4])
        small, small_wide = (mine[5:13], mine[13])
    second_gain_grad, second_shift_grad, outer_offset_grad, first_gain_grad, first_shift_grad, mixer_offset_grad = small[:6]
    outputs = (
        layer_out, input_grad, query_grad, small[6], keys_grad, value_grad, small[7], mixer_grad, mixer_offset_grad,
        first_gain_grad, first_shift_grad, inner_grad, small_wide, outer_grad, outer_offset_grad, second_gain_grad,
        second_shift_grad,
    )
    return tuple(piece[None] for piece in outputs)


def solution(mesh):
    matrix = P("section", None, None)
    vector = P("section", None)
    in_specs = (
        P("dp", None, None), P("dp", None, None), P("dp"), P("dp"), P("dp", None), matrix, vector, matrix, matrix, vector,
        matrix, vector, vector, vector, matrix, vector, matrix, vector, vector, vector,
    )
    rows = P("section", "dp", None, None)
    grad = P("section", "dp", None)
    small = P("section", "dp")
    out_specs = (rows, rows, grad, small, grad, grad, small, grad, small, small, small, grad, small, grad, small, small, small)
    return jax.shard_map(per_device, mesh=mesh, in_specs=in_specs, out_specs=out_specs, check_vma=False)
```

```python
import functools
import jax
import jax.numpy as jnp
from jax import lax
from jax.experimental import pallas as pl
from jax.experimental.pallas import tpu as pltpu
from jax.sharding import PartitionSpec as P

HEADS = 12
HEAD_DIM = 64
BUCKET = 64
PAIR = 2 * HEAD_DIM
masked_score = -1000000000.0
norm_epsilon = 1e-06
F32 = jnp.float32
BF16 = jnp.bfloat16
CHUNK = 16
FFN_TILE = 512
ATT_UNROLL = 3


def rows_times(left, right):
    return lax.dot_general(left, right, (((1,), (0,)), ((), ())), preferred_element_type=F32)


def rows_times_transposed(left, right):
    return lax.dot_general(left, right, (((1,), (1,)), ((), ())), preferred_element_type=F32)


def transposed_times(left, right):
    return lax.dot_general(left, right, (((0,), (0,)), ((), ())), preferred_element_type=F32)


def slot_facts(block, span_rows, place, meta, micro):
    bucket_ref, count_ref, lengths_ref = meta
    bucket = bucket_ref[micro]
    count = count_ref[micro]

    def length_of(slot):
        return jnp.where(slot < count, lengths_ref[micro, slot], 0)

    if span_rows == 2 * BUCKET:
        return (jnp.full_like(place, block), place, jnp.full_like(place, length_of(block)))
    short = bucket == 0
    first = 3 * block
    slot_short = first + place // BUCKET
    length_short = jnp.where(
        place < BUCKET,
        length_of(first),
        jnp.where(place < 2 * BUCKET, length_of(first + 1), length_of(first + 2)),
    )
    slot = jnp.where(short, slot_short, block)
    inner = jnp.where(short, place % BUCKET, place)
    length = jnp.where(short, length_short, length_of(block))
    return (slot, inner, length)


def fill_masks(span_rows, row_count, meta, micro, bias_ref, valid_ref):
    for block in range(row_count // span_rows):
        row_place = lax.broadcasted_iota(jnp.int32, (span_rows, 1), 0)
        row_slot, row_inner, row_length = slot_facts(block, span_rows, row_place, meta, micro)
        rows = slice(block * span_rows, (block + 1) * span_rows)
        if bias_ref is not None:
            key_place = lax.broadcasted_iota(jnp.int32, (1, span_rows), 1)
            key_slot, key_inner, key_length = slot_facts(block, span_rows, key_place, meta, micro)
            key_tag = jnp.where(key_inner < key_length, key_slot, -1)
            allowed = (row_slot == key_tag) | (row_place == key_place)
            bias_ref[rows, 0:span_rows] = jnp.where(allowed, 0.0, masked_score)
        if valid_ref is not None:
            valid_ref[rows, :] = jnp.where(row_inner < row_length, 1.0, 0.0)


def by_span(meta, micro, body):
    even = meta[0][micro] == 1

    @pl.when(even)
    def _():
        body(2 * BUCKET)

    @pl.when(jnp.logical_not(even))
    def _():
        body(3 * BUCKET)


def attend_forward(span_rows, row_count, q_ref, k_ref, v_ref, bias_ref, c_ref):
    blocks = row_count // span_rows

    def one_pair(pair, carry):
        columns = pl.ds(pl.multiple_of(pair * PAIR, PAIR), PAIR)
        lane = lax.broadcasted_iota(jnp.int32, (span_rows, PAIR), 1)
        first_half = lane < HEAD_DIM
        weights = []
        for block in range(blocks):
            rows = slice(block * span_rows, (block + 1) * span_rows)
            query = q_ref[rows, columns] * jnp.asarray(HEAD_DIM ** (-0.5), BF16)
            keys = k_ref[rows, columns]
            zero = jnp.zeros_like(keys)
            bias = bias_ref[rows, 0:span_rows]
            for mine in (first_half, jnp.logical_not(first_half)):
                scores = rows_times_transposed(query, jnp.where(mine, keys, zero)) + bias
                top = jnp.max(scores, axis=-1, keepdims=True)
                weights.append(jnp.exp(scores - top).astype(BF16))
        for block in range(blocks):
            rows = slice(block * span_rows, (block + 1) * span_rows)
            value = v_ref[rows, columns]
            one = jnp.ones_like(value)
            left = rows_times(weights[2 * block], jnp.where(first_half, value, one))
            right = rows_times(weights[2 * block + 1], jnp.where(first_half, one, value))
            above = jnp.where(first_half, left, right)
            below = pltpu.roll(jnp.where(first_half, right, left), HEAD_DIM, 1)
            c_ref[rows, columns] = (above / below).astype(BF16)
        return carry

    lax.fori_loop(0, HEADS // 2, one_pair, 0, unroll=ATT_UNROLL)


def row_moments(values):
    center = jnp.mean(values, axis=-1, keepdims=True)
    centred = values - center
    spread = jnp.mean(centred * centred, axis=-1, keepdims=True)
    return centred, lax.rsqrt(spread + norm_epsilon)


def over_chunks(row_count, body, rows=CHUNK, group=6):
    def step(index, carry):
        for inner in range(group):
            start = pl.multiple_of(index * (rows * group) + inner * rows, rows)
            body(pl.ds(start, rows))
        return carry

    lax.fori_loop(0, row_count // (rows * group), step, 0)


def over_chunks_with_sums(row_count, body, sums_ref, rows=CHUNK, group=6):
    def step(index, carry):
        total = None
        for inner in range(group):
            start = pl.multiple_of(index * (rows * group) + inner * rows, rows)
            terms = [fold_rows(term) for term in body(pl.ds(start, rows))]
            total = terms if total is None else [a + b for a, b in zip(total, terms)]
        for place, term in enumerate(total):
            sums_ref[place] += term
        return carry

    lax.fori_loop(0, row_count // (rows * group), step, 0)


def fold_rows(values):
    return jnp.sum(values.reshape(values.shape[0] // 8, 8, values.shape[1]), axis=0)


def gelu_with_slope(values):
    cumulative = 0.5 + 0.5 * lax.erf(values * (0.5 ** 0.5))
    density = jnp.exp(values * values * -0.5) * 0.3989422804014327
    return values * cumulative, cumulative + values * density


ANY = pl.BlockSpec(memory_space=pl.ANY)
VM = pl.BlockSpec(memory_space=pltpu.VMEM)
SM = pl.BlockSpec(memory_space=pltpu.SMEM)
VMEM_LIMIT = 63_000 * 1024
S = jax.ShapeDtypeStruct
V = pltpu.VMEM
B_QUERY, B_VALUE, B_MIXER, GAIN_ONE, SHIFT_ONE, B_OUTER, GAIN_TWO, SHIFT_TWO = range(8)
QUERY, FIRST_SUM, SECOND_SUM, SLOPE = (0, 3, 4, 5)
ACTIVE, MIDDLE, CONTEXT = (0, 4, 5)
X_BIT, Y_BIT, NEAR_BIT, FAR_BIT = (0, 1, 2, 3)
SMALL_ROWS = 16


class Loads:
    def __init__(self, semaphores):
        self.semaphores = semaphores
        self.copies = {}

    def start(self, name, source, target, other=None, take_other=None):
        semaphore = self.semaphores.at[len(self.copies)]
        copy = pltpu.make_async_copy(source, target, semaphore)
        self.copies[name] = copy
        if other is None:
            copy.start()
            return
        second = pltpu.make_async_copy(other, target, semaphore)

        @pl.when(take_other)
        def _():
            second.start()

        @pl.when(jnp.logical_not(take_other))
        def _():
            copy.start()

    def wait(self, *names):
        for name in names:
            self.copies[name].wait()


class Stores:
    def __init__(self, semaphores):
        self.semaphores = semaphores
        self.copies = []

    def start(self, source, target):
        copy = pltpu.make_async_copy(source, target, self.semaphores.at[len(self.copies)])
        copy.start()
        self.copies.append(copy)

    def wait(self):
        for copy in self.copies:
            copy.wait()


def run_kernel(kernel, outs, out_specs, in_specs, scratch, loads, stores, flops, bytes_moved, name):
    return pl.pallas_call(
        kernel,
        out_shape=outs,
        in_specs=in_specs,
        out_specs=out_specs,
        scratch_shapes=list(scratch) + [pltpu.SemaphoreType.DMA((loads,)), pltpu.SemaphoreType.DMA((stores,))],
        compiler_params=pltpu.CompilerParams(vmem_limit_bytes=VMEM_LIMIT),
        cost_estimate=pl.CostEstimate(flops=1000, bytes_accessed=1000, transcendentals=0),
        name=name,
    )


def spot_of(near_first, dest):
    relative = jnp.bitwise_xor(dest, lax.axis_index("dp"))

    def bit(index):
        return jnp.bitwise_and(lax.shift_right_logical(relative, index), 1)

    first = lax.axis_index("section") == 0
    lead = jnp.where(first, bit(X_BIT), bit(Y_BIT))
    follow = jnp.where(first, bit(Y_BIT), bit(X_BIT))
    if near_first:
        return bit(NEAR_BIT) * 8 + lead * 4 + follow * 2 + bit(FAR_BIT)
    return lead * 8 + follow * 4 + bit(NEAR_BIT) * 2 + bit(FAR_BIT)


def step_bits(near_first):
    cross = [(X_BIT, Y_BIT), (Y_BIT, X_BIT)]
    if near_first:
        return [(NEAR_BIT, NEAR_BIT)] + cross + [(FAR_BIT, FAR_BIT)]
    return cross + [(NEAR_BIT, NEAR_BIT), (FAR_BIT, FAR_BIT)]


def forward_matrix_loads(loads, hidden_start, weights, others, take_other, targets):
    names = ("wq", "wk", "wv", "wm", "wi", "wo")

    def begin(index):
        other = None if others is None else others[index]
        loads.start(names[index], weights[index].at[0], targets[index], other, take_other)

    def load(step):
        if step == 0:
            hidden_start()
            for index in range(3):
                begin(index)
            return
        if step == 1:
            loads.wait("h")
        loads.wait(names[step - 1])
        if step <= 3:
            begin(step + 2)

    return load


def forward_body(load, store, meta, micros, vec, outs, refs):
    h_s, wq_s, wk_s, wv_s, wm_s, wi_s, wo_s, qkv_s, c_s, ml_s, a1_s, a2_s, u_s, gp_s, y_s, m_s, f0_s, e0_s, e1_s, bias_s, valid_s, bi_s = refs
    y_o, own_o, shared_o = outs
    rows, width = h_s.shape
    hidden = wi_s.shape[1]
    each = rows // len(micros)
    parts = [slice(place * each, (place + 1) * each) for place in range(len(micros))]

    def send(source, plane, shared=False):
        for place, part in enumerate(parts):
            target = shared_o.at[place] if shared else own_o[place]
            for index in range(source.shape[1] // width):
                store.start(source.at[part, index * width : (index + 1) * width], target.at[plane + index])

    load(0)
    for part, micro in zip(parts, micros):
        by_span(meta, micro, lambda span: fill_masks(span, each, meta, micro, bias_s.at[part], valid_s.at[part]))
    load(1)
    qkv_s[0] = (rows_times(h_s[...], wq_s[...]) + vec(B_QUERY)).astype(BF16)
    load(2)
    qkv_s[1] = rows_times(h_s[...], wk_s[...]).astype(BF16)
    load(3)
    qkv_s[2] = (rows_times(h_s[...], wv_s[...]) + vec(B_VALUE)).astype(BF16)
    for place, part in enumerate(parts):
        store.start(qkv_s.at[:, part], own_o[place].at[QUERY : QUERY + 3])
    for part, micro in zip(parts, micros):
        by_span(
            meta, micro,
            lambda span: attend_forward(
                span, each, qkv_s.at[0, part], qkv_s.at[1, part], qkv_s.at[2, part], bias_s.at[part], c_s.at[part]
            ),
        )
    send(c_s, CONTEXT, True)
    load(4)
    f0_s[...] = rows_times(c_s[...], wm_s[...])
    offset_mixer, gain_one, shift_one = (vec(B_MIXER), vec(GAIN_ONE), vec(SHIFT_ONE))

    def first_norm(part):
        total = h_s[part, :].astype(F32) + (f0_s[part, :] + offset_mixer)
        a1_s[part, :] = total.astype(BF16)
        centred, scale = row_moments(total)
        middle = centred * scale * gain_one + shift_one
        m_s[part, :] = middle
        ml_s[part, :] = middle.astype(BF16)

    over_chunks(rows, first_norm)
    send(a1_s, FIRST_SUM)
    send(ml_s, MIDDLE, True)
    load(5)
    tile = FFN_TILE
    tiles = hidden // tile

    def project(buffer, which):
        columns = pl.ds(pl.multiple_of(which * tile, tile), tile)
        buffer[...] = rows_times(ml_s[...], wi_s[:, columns])

    def activate(buffer, which):
        columns = pl.ds(pl.multiple_of(which * tile, tile), tile)
        offset = bi_s[0:1, columns]
        for start in range(0, rows, 32):
            part = slice(start, start + 32)
            value, slope = gelu_with_slope(buffer[part, :] + offset)
            u_s[part, columns] = value.astype(BF16)
            gp_s[part, columns] = slope.astype(BF16)

    for index in range(hidden // width):
        bi_s[0:1, index * width : (index + 1) * width] = vec(8 + index)
    project(e0_s, 0)

    def two_tiles(index, carry):
        project(e1_s, 2 * index + 1)
        activate(e0_s, 2 * index)
        project(e0_s, jnp.minimum(2 * index + 2, tiles - 1))
        activate(e1_s, 2 * index + 1)
        return carry

    lax.fori_loop(0, tiles // 2, two_tiles, 0)
    send(u_s, ACTIVE, True)
    send(gp_s, SLOPE)
    load(6)
    f0_s[...] = rows_times(u_s[...], wo_s[...])
    offset_outer, gain_two, shift_two = (vec(B_OUTER), vec(GAIN_TWO), vec(SHIFT_TWO))

    def second_norm(part):
        total = m_s[part, :] + (f0_s[part, :] + offset_outer)
        a2_s[part, :] = total.astype(BF16)
        centred, scale = row_moments(total)
        y_s[part, :] = ((centred * scale * gain_two + shift_two) * valid_s[part, :]).astype(BF16)

    over_chunks(rows, second_norm)
    for place, part in enumerate(parts):
        store.start(y_s.at[part], y_o.at[place])
    send(a2_s, SECOND_SUM)
    store.wait()


def first_forward_kernel(
    micro_count, bucket, count, lengths, tok, wq, wk, wv, wm, wi, wo, vec, *rest
):
    y_o, shared_o = rest[:2]
    own_o = rest[2 : 2 + micro_count]
    *refs, in_sem, out_sem = rest[2 + micro_count :]
    h_s, wq_s, wk_s, wv_s, wm_s, wi_s, wo_s = refs[:7]

    @pl.when(lax.axis_index("section") == 0)
    def _():
        loads = Loads(in_sem)
        each = h_s.shape[0] // micro_count

        def hidden_start():
            for micro in range(1, micro_count):
                loads.start(("h", micro), tok.at[micro], h_s.at[micro * each : (micro + 1) * each])
            loads.start("h", tok.at[0], h_s.at[0:each])

        inner_load = forward_matrix_loads(
            loads, hidden_start, (wq, wk, wv, wm, wi, wo), None, None, (wq_s, wk_s, wv_s, wm_s, wi_s, wo_s)
        )

        def load(step):
            if step == 1:
                for micro in range(1, micro_count):
                    loads.wait(("h", micro))
            inner_load(step)

        forward_body(
            load, Stores(out_sem), (bucket, count, lengths), tuple(range(micro_count)),
            lambda place: vec[place : place + 1, :], (y_o, own_o, shared_o), refs,
        )


def second_forward_kernel(
    bucket, count, lengths, y_own, y_other, wq, wk, wv, wm, wi, wo, packed, xi, xo, vec_own,
    y_o, shared_o, own_o, *scratch
):
    *refs, other_s, vec_s, in_sem, out_sem = scratch
    h_s, wq_s, wk_s, wv_s, wm_s, wi_s, wo_s = refs[:7]
    section = lax.axis_index("section")
    first = section == 0
    loads = Loads(in_sem)
    load = forward_matrix_loads(
        loads, lambda: loads.start("h", y_other.at[section], h_s, y_own.at[section], first), (wq, wk, wv, wm, wi, wo),
        tuple(square_of(packed, index) for index in range(4)) + (xi.at[0], xo.at[0]), first, (wq_s, wk_s, wv_s, wm_s, wi_s, wo_s),
    )
    vectors = Vectors(loads, packed, vec_own, other_s, first)

    def ready(step):
        load(step)
        if step == 0:
            loads.wait("vectors")
            for place in range(12):
                vec_s[place : place + 1, :] = vectors(place)

    forward_body(
        ready, Stores(out_sem), (bucket, count, lengths), (section,), lambda place: vec_s[place : place + 1, :],
        (y_o, (own_o,), shared_o), refs,
    )


def forward_shapes(micro_count, each, width, hidden):
    rows = micro_count * each
    flat = (rows, width)
    wide = (rows, hidden)
    square = (width, width)

    def out(*tail):
        return (micro_count,) + tail

    wides = hidden // width
    outs = (S(out(each, width), BF16), S(out(wides + 2, each, width), BF16)) + (S((wides + 5, each, width), BF16),) * micro_count
    scratch = [
        V(flat, BF16), V(square, BF16), V(square, BF16), V(square, BF16), V(square, BF16), V((width, hidden), BF16),
        V((hidden, width), BF16), V((3,) + flat, BF16), V(flat, BF16), V(flat, BF16), V(flat, BF16), V(flat, BF16),
        V(wide, BF16), V(wide, BF16), V(flat, BF16), V(flat, F32), V(flat, F32), V((rows, FFN_TILE), F32),
        V((rows, FFN_TILE), F32), V((rows, 3 * BUCKET), F32), V((rows, 1), F32),
        V((8, hidden), F32),
    ]
    flops = 2 * rows * width * (4 * width + 2 * hidden)
    return outs, scratch, flops


def first_forward(meta, tokens, weights, vec):
    micro_count, each, width = tokens.shape
    outs, scratch, flops = forward_shapes(micro_count, each, width, weights[4].shape[2])
    return run_kernel(
        functools.partial(first_forward_kernel, micro_count), outs, [ANY] * (2 + micro_count), [SM] * 3 + [ANY] * 7 + [VM],
        scratch, 6 + micro_count, 14 * micro_count, flops, 40_000_000, "first_forward",
    )(*meta, tokens, *weights, vec)


def second_forward(meta, y_own, y_other, weights, others, vec_own):
    _, each, width = y_own.shape
    outs, scratch, flops = forward_shapes(1, each, width, weights[4].shape[2])
    scratch = scratch + [V((VECTOR_ROWS, width), BF16), V((16, width), F32)]
    return run_kernel(
        second_forward_kernel, outs, [ANY] * 3, [SM] * 3 + [ANY] * 11 + [VM], scratch, 8, 14, flops, 25_000_000,
        "second_forward",
    )(*meta, y_own, y_other, *weights, *others, vec_own)


VECTOR_ROWS = 32


def pack_kernel(wq, wk, wv, wm, bq, bv, bm, g1, s1, bo, g2, s2, bi, packed_o, vec_o, hold_s, low_s, in_sem, out_sem):
    loads = Loads(in_sem)
    store = Stores(out_sem)
    width = wq.shape[1]
    for index, weight in enumerate((wq, wk, wv, wm)):
        loads.start(index, weight.at[0], hold_s.at[index * width : (index + 1) * width])
    vec_o[...] = jnp.zeros_like(vec_o)
    for place, vector in enumerate((bq, bv, bm, g1, s1, bo, g2, s2)):
        vec_o[place : place + 1, :] = vector[...]
    for index in range(bi.shape[1] // width):
        vec_o[8 + index : 9 + index, :] = bi[:, index * width : (index + 1) * width]
    high = vec_o[...].astype(BF16)
    low_s[0:16, :] = high
    low_s[16:32, :] = (vec_o[...] - high.astype(F32)).astype(BF16)
    store.start(low_s, packed_o.at[4 * width : 4 * width + VECTOR_ROWS])
    for index in range(4):
        loads.wait(index)
        rows = slice(index * width, (index + 1) * width)
        store.start(hold_s.at[rows], packed_o.at[rows])
    store.wait()


def pack(weights, vectors, bi):
    _, width, _ = weights[0].shape
    rows = 4 * width + VECTOR_ROWS
    return run_kernel(
        pack_kernel, (S((rows, width), BF16), S((16, width), F32)), [ANY, VM], [ANY] * 4 + [VM] * 9,
        [V((4 * width, width), BF16), V((VECTOR_ROWS, width), BF16)], 4, 5, 0, 10_000_000, "pack_weights",
    )(*weights[:4], *vectors, bi)


def square_of(packed, index):
    width = packed.shape[1]
    return packed.at[index * width : (index + 1) * width]


class Vectors:
    def __init__(self, loads, packed, own, other_s, take_other):
        width = packed.shape[1]
        self.own = own
        self.other_s = other_s
        self.take_other = take_other
        loads.start("vectors", packed.at[4 * width : 4 * width + VECTOR_ROWS], other_s)

    def __call__(self, place):
        other = self.other_s[place : place + 1, :].astype(F32) + self.other_s[16 + place : 17 + place, :].astype(F32)
        return jnp.where(self.take_other, other, self.own[place : place + 1, :])


def norm_backward(grad, total, gain):
    centred, scale = row_moments(total)
    unit = centred * scale
    spread = grad * gain
    first = jnp.mean(spread, axis=-1, keepdims=True)
    second = jnp.mean(spread * unit, axis=-1, keepdims=True)
    return (spread - first - unit * second) * scale, grad * unit


def layer_of(layer):
    return lax.axis_index("section") != layer


def load_planes(layer, loads, name, own, other, plane, target):
    width = own.shape[2]
    take_other = lax.axis_index("section") == 1
    for index in range(target.shape[1] // width):
        part = target if target.shape[1] == width else target.at[:, index * width : (index + 1) * width]
        received = None if layer == 1 else other.at[plane + index]
        loads.start((name, index), own.at[plane + index], part, received, take_other)


def feed_kernel(
    layer, bucket, count, lengths, g, own, own_x, wo, wo_x, wi, wi_x, wm, packed, vec_own,
    dz_o, df_o, away_o, da1_o, da_o, dc_o, small_o,
    g_s, a2_s, gp_s, a1_s, wo_s, wi_s, wm_s, da2_s, dz_s, df_s, dm_s, da1_s, da_s, dc_s, e0_s, e1_s, valid_s, sums_s, wide_s, other_s, in_sem, out_sem,
):
    section = lax.axis_index("section")
    rows, width = a2_s.shape
    hidden = df_s.shape[1]
    loads = Loads(in_sem)
    store = Stores(out_sem)
    wides = range(hidden // width)
    loads.start("g", g.at[section] if layer == 1 else g, g_s)
    load_planes(layer, loads, "a2", own, own_x, SECOND_SUM, a2_s)
    loads.start("wo", wo.at[0], wo_s, wo_x.at[0], layer_of(layer))
    meta = (bucket, count, lengths)
    by_span(meta, section, lambda span: fill_masks(span, rows, meta, section, None, valid_s))
    sums_s[...] = jnp.zeros_like(sums_s)
    vectors = Vectors(loads, packed, vec_own, other_s, layer_of(layer))
    loads.wait("g", ("a2", 0), "vectors")
    gain_two, gain_one = (vectors(GAIN_TWO), vectors(GAIN_ONE))
    load_planes(layer, loads, "gp", own, own_x, SLOPE, gp_s)
    loads.start("wi", wi.at[0], wi_s, wi_x.at[0], layer_of(layer))

    def second_norm(part):
        grad = g_s[part, :].astype(F32) * valid_s[part, :]
        moved, gained = norm_backward(grad, a2_s[part, :].astype(F32), gain_two)
        da2_s[part, :] = moved
        low = moved.astype(BF16)
        dz_s[part, :] = low
        return gained, grad, low.astype(F32)

    over_chunks_with_sums(rows, second_norm, sums_s.at[0:3])
    half = width // 2
    store.start(dz_s.at[:, pl.ds(pl.multiple_of(section * half, half), half)], dz_o)
    store.start(dz_s.at[:, pl.ds(pl.multiple_of((1 - section) * half, half), half)], away_o.at[2, :, 0:half])
    tile = FFN_TILE
    tiles = hidden // tile

    def project(buffer, which):
        columns = pl.ds(pl.multiple_of(which * tile, tile), tile)
        buffer[...] = rows_times_transposed(dz_s[...], wo_s[columns, :])

    def slope(buffer, which):
        columns = pl.ds(pl.multiple_of(which * tile, tile), tile)
        total = None
        for start in range(0, rows, 32):
            part = slice(start, start + 32)
            low_part = (buffer[part, :] * gp_s[part, columns].astype(F32)).astype(BF16)
            df_s[part, columns] = low_part
            term = fold_rows(low_part.astype(F32))
            total = term if total is None else total + term
        wide_s[:, columns] = total

    loads.wait("wo")
    load_planes(layer, loads, "a1", own, own_x, FIRST_SUM, a1_s)
    loads.start("wm", wm.at[0], wm_s, square_of(packed, 3), layer_of(layer))
    project(e0_s, 0)
    for index in wides:
        loads.wait(("gp", index))

    def two_tiles(index, carry):
        project(e1_s, 2 * index + 1)
        slope(e0_s, 2 * index)
        project(e0_s, jnp.minimum(2 * index + 2, tiles - 1))
        slope(e1_s, 2 * index + 1)
        return carry

    lax.fori_loop(0, tiles // 2, two_tiles, 0)
    half = hidden // 2
    store.start(df_s.at[:, pl.ds(pl.multiple_of(section * half, half), half)], df_o)
    for index in range(2):
        start = pl.multiple_of((1 - section) * half + index * width, width)
        store.start(df_s.at[:, pl.ds(start, width)], away_o.at[index])
    loads.wait("wi")
    dm_s[...] = rows_times_transposed(df_s[...], wi_s[...])
    loads.wait(("a1", 0))

    def first_norm(part):
        grad = dm_s[part, :] + da2_s[part, :]
        moved, gained = norm_backward(grad, a1_s[part, :].astype(F32), gain_one)
        da1_s[part, :] = moved
        low_part = moved.astype(BF16)
        da_s[part, :] = low_part
        return gained, grad, low_part.astype(F32)

    over_chunks_with_sums(rows, first_norm, sums_s.at[3:6])
    store.start(da1_s, da1_o)
    store.start(da_s, da_o)
    for index in range(6):
        small_o[index : index + 1, :] = jnp.sum(sums_s[index], axis=0, keepdims=True)
    inner_sum = jnp.sum(wide_s[...], axis=0, keepdims=True)
    for index in range(hidden // width):
        small_o[8 + index : 9 + index, :] = inner_sum[:, index * width : (index + 1) * width]
    loads.wait("wm")
    dc_s[...] = rows_times_transposed(da_s[...], wm_s[...]).astype(BF16)
    store.start(dc_s, dc_o)
    store.wait()


def feed_gradient(layer, meta, g, own, own_x, weights, others, vec_own):
    _, rows, width = own.shape
    hidden = weights[4].shape[2]
    flat = (rows, width)
    packed, xi, xo = others
    return run_kernel(
        functools.partial(feed_kernel, layer),
        (S((rows, width // 2), BF16), S((rows, hidden // 2), BF16), S((3,) + flat, BF16), S(flat, F32), S(flat, BF16), S(flat, BF16), S((SMALL_ROWS, width), F32)),
        [ANY] * 6 + [VM], [SM] * 3 + [ANY] * 9 + [VM],
        [
            V(flat, g.dtype), V(flat, BF16), V((rows, hidden), BF16), V(flat, BF16), V((hidden, width), BF16), V((width, hidden), BF16),
            V((width, width), BF16), V(flat, F32), V(flat, BF16), V((rows, hidden), BF16), V(flat, F32), V(flat, F32), V(flat, BF16),
            V(flat, BF16), V((rows, FFN_TILE), F32), V((rows, FFN_TILE), F32), V((rows, 1), F32), V((6, 8, width), F32),
            V((8, hidden), F32), V((VECTOR_ROWS, width), BF16),
        ],
        7 + hidden // width, 8, 2 * rows * width * (2 * hidden + width), 25_000_000, "feed_gradient",
    )(*meta, g, own, own_x, weights[5], xo, weights[4], xi, weights[3], packed, vec_own)


def attend_backward(span_rows, row_count, q_ref, k_ref, v_ref, dc_ref, bias_ref, dq_ref, dk_ref, dv_ref):
    blocks = row_count // span_rows
    scale = HEAD_DIM ** (-0.5)

    def one_pair(pair, carry):
        columns = pl.ds(pl.multiple_of(pair * PAIR, PAIR), PAIR)
        lane = lax.broadcasted_iota(jnp.int32, (span_rows, PAIR), 1)
        halves = (lane < HEAD_DIM, lane >= HEAD_DIM)
        for block in range(blocks):
            rows = slice(block * span_rows, (block + 1) * span_rows)
            query = q_ref[rows, columns] * jnp.asarray(scale, BF16)
            keys = k_ref[rows, columns]
            value = v_ref[rows, columns]
            grad = dc_ref[rows, columns]
            zero = jnp.zeros_like(keys)
            bias = bias_ref[rows, 0:span_rows]
            dq = dk = dv = None
            for mine in halves:
                keys_own = jnp.where(mine, keys, zero)
                scores = rows_times_transposed(query, keys_own) + bias
                grad_part = rows_times_transposed(grad, jnp.where(mine, value, zero))
                top = jnp.max(scores, axis=-1, keepdims=True)
                weight = jnp.exp(scores - top)
                part = weight * (1.0 / jnp.sum(weight, axis=-1, keepdims=True))
                mean = jnp.sum(grad_part * part, axis=-1, keepdims=True)
                grad_scores = (part * (grad_part - mean)).astype(BF16)
                terms = (
                    rows_times(grad_scores, keys_own),
                    transposed_times(grad_scores, jnp.where(mine, query, zero)),
                    transposed_times(part.astype(BF16), jnp.where(mine, grad, zero)),
                )
                if dq is None:
                    dq, dk, dv = terms
                else:
                    dq, dk, dv = (dq + terms[0], dk + terms[1], dv + terms[2])
            dq_ref[rows, columns] = (dq * scale).astype(BF16)
            dk_ref[rows, columns] = dk.astype(BF16)
            dv_ref[rows, columns] = dv.astype(BF16)
        return carry

    lax.fori_loop(0, HEADS // 2, one_pair, 0)


def attend_kernel(
    layer, bucket, count, lengths, own, own_x, dc, da, da1, wq, wk, wv, packed, small_one,
    dh_o, dlow_o, home_o, away_o, small_o,
    qkv_s, dc_s, da_s, dh_s, dlow_s, wq_s, wk_s, wv_s, dq_s, dk_s, dv_s, bias_s, sums_s, low_s, in_sem, out_sem,
):
    section = lax.axis_index("section")
    rows, width = dc_s.shape
    second = section == 1
    loads = Loads(in_sem)
    received = None if layer == 1 else own_x.at[QUERY : QUERY + 3]
    loads.start("qkv", own.at[QUERY : QUERY + 3], qkv_s, received, second)
    loads.start("dc", dc, dc_s)
    meta = (bucket, count, lengths)
    by_span(meta, section, lambda span: fill_masks(span, rows, meta, section, bias_s, None))
    loads.wait("qkv", "dc")
    loads.start("da", da, da_s)
    loads.start("da1", da1, dh_s)
    for index, (name, weight, target) in enumerate((("wq", wq, wq_s), ("wk", wk, wk_s), ("wv", wv, wv_s))):
        loads.start(name, weight.at[0], target, square_of(packed, index), layer_of(layer))
    by_span(
        meta, section,
        lambda span: attend_backward(span, rows, qkv_s.at[0], qkv_s.at[1], qkv_s.at[2], dc_s, bias_s, dq_s, dk_s, dv_s),
    )
    loads.wait("da")
    pairs = ((dq_s, dk_s), (dv_s, da_s))
    for core in range(2):
        @pl.when(section == core)
        def _(core=core):
            for place in range(2):
                pltpu.make_async_copy(pairs[core][place], home_o.at[place], out_sem.at[place]).start()
                pltpu.make_async_copy(
                    pairs[1 - core][place], away_o.at[place * rows : (place + 1) * rows], out_sem.at[2 + place]
                ).start()
    loads.wait("da1", "wq", "wk", "wv")
    dh_s[...] += rows_times_transposed(dq_s[...], wq_s[...])
    dh_s[...] += rows_times_transposed(dk_s[...], wk_s[...])
    dh_s[...] += rows_times_transposed(dv_s[...], wv_s[...])
    sums_s[...] = jnp.zeros_like(sums_s)

    def finish(part):
        dlow_s[part, :] = dh_s[part, :].astype(BF16)
        return dq_s[part, :].astype(F32), dv_s[part, :].astype(F32)

    over_chunks_with_sums(rows, finish, sums_s)
    last = [
        pltpu.make_async_copy(dh_s, dh_o, out_sem.at[4]),
        pltpu.make_async_copy(dlow_s, dlow_o, out_sem.at[5]),
    ]
    for copy in last:
        copy.start()
    small_o[0:6, :] = small_one[0:6, :]
    for index in range(2):
        small_o[6 + index : 7 + index, :] = jnp.sum(sums_s[index], axis=0, keepdims=True)
    small_o[8:16, :] = small_one[8:16, :]
    low_s[...] = small_o[...].astype(BF16)
    smalls = pltpu.make_async_copy(low_s, away_o.at[2 * rows : 2 * rows + SMALL_ROWS], out_sem.at[6])
    smalls.start()
    for place in range(2):
        pltpu.make_async_copy(pairs[0][place], home_o.at[place], out_sem.at[place]).wait()
        pltpu.make_async_copy(
            pairs[1][place], away_o.at[place * rows : (place + 1) * rows], out_sem.at[2 + place]
        ).wait()
    for copy in last:
        copy.wait()
    smalls.wait()


def attend_gradient(layer, meta, own, own_x, dc, da, da1, weights, squares, small_one):
    rows, width = da1.shape
    flat = (rows, width)
    square = (width, width)
    return run_kernel(
        functools.partial(attend_kernel, layer),
        (S(flat, F32), S(flat, BF16), S((2,) + flat, BF16), S((2 * rows + SMALL_ROWS, width), BF16), S((SMALL_ROWS, width), F32)),
        [ANY] * 4 + [VM], [SM] * 3 + [ANY] * 9 + [VM],
        [V((3,) + flat, BF16), V(flat, BF16), V(flat, BF16), V(flat, F32), V(flat, BF16)] + [V(square, BF16)] * 3 + [V(flat, BF16)] * 3
        + [V((rows, 3 * BUCKET), F32), V((2, 8, width), F32), V((SMALL_ROWS, width), BF16)],
        7, 7, 6 * rows * width * width, 15_000_000, "attend_gradient",
    )(*meta, own, own_x, dc, da, da1, *weights[:3], squares, small_one)


def by_owner(loads, name, own, other, target):
    rows = target.shape[0] // 2
    section = lax.axis_index("section")
    loads.start((name, 0), own, target.at[pl.ds(pl.multiple_of(section * rows, rows), rows)])
    loads.start((name, 1), other, target.at[pl.ds(pl.multiple_of((1 - section) * rows, rows), rows)])


def both_micros(layer, loads, name, own, other, plane, target):
    width = own.shape[3]
    rows = target.shape[0] // 2
    second = lax.axis_index("section") == 1
    for index in range(target.shape[1] // width):
        columns = target if target.shape[1] == width else target.at[:, index * width : (index + 1) * width]
        if layer == 1:
            by_owner(loads, (name, index), own.at[0, plane + index], other.at[0, plane + index], columns)
            continue
        for micro in range(2):
            part = columns.at[micro * rows : (micro + 1) * rows]
            loads.start(((name, index), micro), own.at[micro, plane + index], part, other.at[micro, plane + index], second)


def wait_both(loads, name, count):
    for index in range(count):
        loads.wait(((name, index), 0), ((name, index), 1))


def put_rows(target, near_first, value, at_row, at_lane, dest):
    spot = 0 if target.shape[0] == 1 else spot_of(near_first, dest)
    rows, lanes = value.shape
    target[spot, at_row : at_row + rows, at_lane : at_lane + lanes] = value.astype(BF16)


def feed_weights_kernel(
    layer, near_first, shared, shared_x, dz, df, away_x,
    outer_o, inner_o, keep_o,
    u_s, ml_s, dz_s, df_s, w_s, in_sem, out_sem,
):
    hidden = u_s.shape[1]
    width = ml_s.shape[1]
    rows = dz.shape[0]
    spots = w_s.shape[0]
    loads = Loads(in_sem)
    store = Stores(out_sem)
    by_owner(loads, "dz", dz, away_x.at[2, :, 0 : width // 2], dz_s)
    both_micros(layer, loads, "u", shared, shared_x, ACTIVE, u_s)
    loads.wait(("dz", 0), ("dz", 1))
    wait_both(loads, "u", hidden // width)
    both_micros(layer, loads, "ml", shared, shared_x, MIDDLE, ml_s)
    for index in range(2):
        columns = slice(index * width, (index + 1) * width)
        by_owner(loads, ("df", index), df.at[:, columns], away_x.at[index], df_s.at[:, columns])
    half_rows = hidden // spots // 2
    tile = min(width, half_rows * 2) if spots == 1 else width
    for index in range(hidden // tile):
        product = transposed_times(u_s[:, index * tile : (index + 1) * tile], dz_s[...])
        block = min(half_rows, tile)
        for inner in range(tile // block):
            row = index * tile + inner * block
            dest, offset = divmod(row, 2 * half_rows)
            side, at_row = divmod(offset, half_rows)
            put_rows(w_s, near_first, product[inner * block : (inner + 1) * block, :], at_row, side * (width // 2), dest)
    wait_both(loads, "ml", 1)
    wait_both(loads, "df", 2)
    height = width // spots
    for side in range(2):
        product = transposed_times(ml_s[...], df_s[:, side * width : (side + 1) * width])
        for dest in range(spots):
            put_rows(w_s, near_first, product[dest * height : (dest + 1) * height, :], half_rows + side * height, 0, dest)
    split = spots // 2
    store.start(w_s.at[split:spots, 0:half_rows], outer_o)
    store.start(w_s.at[split:spots, half_rows : half_rows + 2 * height], inner_o)
    store.start(w_s.at[0 : spots - split], keep_o)
    store.wait()


def unit_outs(spots, rows, width):
    half = S((max(spots // 2, 1), rows, width), BF16)
    return half, half


def feed_weights(layer, near_first, spots, shared, shared_x, dz, df, away_x):
    rows, width = shared.shape[2:]
    hidden = 2 * df.shape[1]
    total = hidden // spots // 2 + 2 * (width // spots)
    split = spots - spots // 2
    outs = (
        S((split, hidden // spots // 2, width), BF16), S((split, 2 * (width // spots), width), BF16), S((split, total, width), BF16),
    )
    return run_kernel(
        functools.partial(feed_weights_kernel, layer, near_first), outs, [ANY] * 3, [ANY] * 5,
        [
            V((2 * rows, hidden), BF16), V((2 * rows, width), BF16), V((2 * rows, width // 2), BF16), V((2 * rows, hidden // 2), BF16),
            V((spots, total, width), BF16),
        ],
        8 + 2 * (hidden // width), 3, 4 * rows * width * hidden, 18_000_000, "feed_weights",
    )(shared, shared_x, dz, df, away_x)


def attend_weights_kernel(
    layer, near_first, h, h_x, shared, shared_x, grads, away_x, small,
    send_o, keep_o,
    left_s, right_s, w_s, small_s, in_sem, out_sem,
):
    section = lax.axis_index("section")
    second = section == 1
    rows, width = grads.shape[1:]
    spots = w_s.shape[0]
    loads = Loads(in_sem)
    store = Stores(out_sem)
    for micro in range(2):
        part = slice(micro * rows, (micro + 1) * rows)
        loads.start(("h", micro), h.at[micro], left_s.at[0, part], h_x.at[micro], second)
    by_owner(loads, "g", grads.at[0], away_x.at[0:rows], right_s.at[0])
    if layer == 0:
        for micro in range(2):
            part = slice(micro * rows, (micro + 1) * rows)
            loads.start(("c", micro), h.at[micro], left_s.at[1, part], shared_x.at[micro, CONTEXT], second)
    else:
        for place, (plain, context) in enumerate(((h, shared), (h, shared_x))):
            micro = section if place == 0 else 1 - section
            part = left_s.at[1, pl.ds(pl.multiple_of(micro * rows, rows), rows)]
            loads.start(("c", place), plain.at[micro], part, context.at[0, CONTEXT], second)
    by_owner(loads, "f", grads.at[1], away_x.at[rows : 2 * rows], right_s.at[1])
    height = width // spots
    loads.start("small", away_x.at[2 * rows : 2 * rows + SMALL_ROWS], small_s)
    loads.wait("small")
    low = (small[...] + small_s[...].astype(F32)).astype(BF16)
    for spot in range(spots):
        w_s[spot, 2 * height : 2 * height + SMALL_ROWS, :] = low
    for side, name in enumerate(("h", "c")):
        grad_name = ("g", "f")[side]
        loads.wait((name, 0), (name, 1), (grad_name, 0), (grad_name, 1))
        product = transposed_times(left_s[side], right_s[side])
        for dest in range(spots):
            put_rows(w_s, near_first, product[dest * height : (dest + 1) * height, :], side * height, 0, dest)
    split = spots // 2
    if spots > 1:
        store.start(w_s.at[split:spots], send_o)
        store.start(w_s.at[0:split], keep_o)
    else:
        store.start(w_s, send_o)
        store.start(w_s, keep_o)
    store.wait()


def attend_weights(layer, near_first, spots, h, h_x, shared, shared_x, grads, away_x, small):
    rows, width = grads.shape[1:]
    total = 2 * (width // spots) + SMALL_ROWS
    return run_kernel(
        functools.partial(attend_weights_kernel, layer, near_first), unit_outs(spots, total, width), [ANY] * 2, [ANY] * 6 + [VM],
        [V((2, 2 * rows, width), BF16), V((2, 2 * rows, width), BF16), V((spots, total, width), BF16), V((SMALL_ROWS, width), BF16)],
        9, 2, 8 * rows * width * width, 10_000_000, "attend_weights",
    )(h, h_x, shared, shared_x, grads, away_x, small)


def add_kernel(shapes, pieces, *refs):
    count = len(shapes)
    keeps, refs = (refs[0:count], refs[count:])
    parts, refs = (refs[0 : sum(pieces)], refs[sum(pieces) :])
    *rest, in_sem, out_sem = refs
    out_count = sum(1 if spots == 1 else 2 for spots, _, _ in shapes)
    outs, holds = (list(rest[:out_count]), list(rest[out_count:]))
    keep_s, part_s, total_s = (holds[0:count], holds[count : 2 * count], holds[2 * count :])
    loads = Loads(in_sem)
    store = Stores(out_sem)
    at = 0
    waits = []
    for index in range(count):
        loads.start(("keep", index), keeps[index], keep_s[index])
        names = [("keep", index)]
        row = 0
        for piece in range(pieces[index]):
            height = parts[at].shape[1]
            loads.start(("part", index, piece), parts[at], part_s[index].at[:, row : row + height])
            names.append(("part", index, piece))
            row += height
            at += 1
        waits.append(names)
    place = 0
    for index, (spots, rows, _) in enumerate(shapes):
        loads.wait(*waits[index])
        if spots == 1:
            total_s[index][...] = keep_s[index][0].astype(F32) + part_s[index][0].astype(F32)
            store.start(total_s[index], outs[place])
            place += 1
            continue

        def one(spot, carry, index=index):
            total_s[index][spot] = (keep_s[index][spot].astype(F32) + part_s[index][spot].astype(F32)).astype(BF16)
            return carry

        lax.fori_loop(0, spots, one, 0)
        store.start(total_s[index].at[spots // 2 : spots], outs[place])
        store.start(total_s[index].at[0 : spots // 2], outs[place + 1])
        place += 2
    store.wait()


def add_arrived(pairs):
    shapes = [keep.shape for keep, _ in pairs]
    pieces = [len(arrived) for _, arrived in pairs]
    outs = []
    totals = []
    for spots, rows, width in shapes:
        if spots > 1:
            outs.extend([S((spots // 2, rows, width), BF16)] * 2)
            totals.append(V((spots, rows, width), BF16))
        else:
            outs.append(S((rows, width), F32))
            totals.append(V((rows, width), F32))
    count = len(pairs) + sum(pieces)
    results = list(
        pl.pallas_call(
            functools.partial(add_kernel, shapes, pieces),
            out_shape=tuple(outs),
            in_specs=[ANY] * count,
            out_specs=(ANY,) * len(outs),
            scratch_shapes=[V(shape, BF16) for shape in shapes] * 2 + totals
            + [pltpu.SemaphoreType.DMA((count,)), pltpu.SemaphoreType.DMA((len(outs),))],
            compiler_params=pltpu.CompilerParams(vmem_limit_bytes=ADD_LIMIT),
            cost_estimate=pl.CostEstimate(flops=1000, bytes_accessed=1000, transcendentals=0),
            name="add_arrived",
        )(*[keep for keep, _ in pairs], *[part for _, arrived in pairs for part in arrived])
    )
    return [(results.pop(0),) if spots == 1 else (results.pop(0), results.pop(0)) for spots, _, _ in shapes]


ADD_LIMIT = 24_000 * 1024


def finish_kernel(feed_one, feed_two, tail_one, tail_two, feed_one_x, feed_two_x, tail_one_x, tail_two_x, q_o, k_o, v_o, m_o, i_o, o_o, small_o, wide_o):
    section = lax.axis_index("section")
    groups = lax.axis_size("dp")
    me = lax.axis_index("dp")
    height, width = q_o.shape
    half_rows = o_o.shape[0] // 2
    hidden = i_o.shape[1]
    for core in range(2):
        @pl.when(section == core)
        def _(core=core):
            mine, back = ((feed_one, tail_one), (feed_one_x, tail_one_x)) if core == 0 else ((feed_two, tail_two), (feed_two_x, tail_two_x))
            sides = (mine, back) if core == 0 else (back, mine)
            half = width // 2
            for side, (feed, _) in enumerate(sides):
                for part in range(2):
                    o_o[part * half_rows : (part + 1) * half_rows, side * half : (side + 1) * half] = feed[
                        0:half_rows, part * half : (part + 1) * half
                    ]
                    i_o[:, (2 * side + part) * width : (2 * side + part + 1) * width] = feed[
                        half_rows + part * height : half_rows + (part + 1) * height, :
                    ]
            q_o[...] = sides[0][1][0:height, :]
            k_o[...] = sides[0][1][height : 2 * height, :]
            v_o[...] = sides[1][1][0:height, :]
            m_o[...] = sides[1][1][height : 2 * height, :]
            lines = mine[1][2 * height : 2 * height + SMALL_ROWS, :]
            small_o[...] = pltpu.roll(lines[0:8, :], lax.rem(width - me * height, width), 1)
            span = hidden // groups
            each = width // span
            pick = lax.broadcasted_iota(jnp.int32, (8, width), 0) == lax.div(me, each)
            chosen = jnp.sum(jnp.where(pick, lines[8:16, :], 0.0), axis=0, keepdims=True)
            wide_o[...] = pltpu.roll(jnp.broadcast_to(chosen, (8, width)), lax.rem(width - lax.rem(me, each) * span, width), 1)


def finish(groups, width, hidden, results):
    height = width // groups
    square = S((height, width), F32)
    return pl.pallas_call(
        finish_kernel,
        out_shape=(square, square, square, square, S((height, hidden), F32), S((hidden // groups, width), F32), S((8, width), F32), S((8, width), F32)),
        in_specs=[VM] * 8,
        out_specs=(VM,) * 8,
        compiler_params=pltpu.CompilerParams(vmem_limit_bytes=ADD_LIMIT),
        name="finish_gradients",
    )(*results)


def exchange(value, bits):
    groups = lax.axis_size("dp")
    pairs = [(2 * group + core, 2 * (group ^ (1 << bits[core])) + core) for group in range(groups) for core in range(2)]
    return lax.ppermute(value, ("dp", "section"), pairs)


def swap(value):
    return lax.ppermute(value, "section", [(0, 1), (1, 0)])


F1, T1, F0, T0 = (("f", 1), ("t", 1), ("f", 0), ("t", 0))
NEAR_FIRST = {F1: False, T1: False, F0: False, T0: False}
SCHEDULE = (
    (),
    (),
    (),
    (F1,),
    (F1,),
    (),
    (F1, T1),
    (F1, T1, F0),
    (F0, F1, T1),
    (F0, T1, T0),
    (F0, T0),
    (F0, T0),
    (T0,),
)


def per_device(
    tokens, cotangent, bucket, batch_size, lengths, query_weight, query_offset, keys_weight, value_weight, value_offset,
    mixer_weight, mixer_offset, first_gain, first_shift, inner_weight, inner_offset, outer_weight, outer_offset,
    second_gain, second_shift,
):
    section = lax.axis_index("section")
    groups = lax.axis_size("dp")
    width = tokens.shape[2]
    hidden = inner_offset.shape[1]
    hypercube = groups == 16
    spots = groups if hypercube else 1
    first = section == 0
    meta = (bucket, batch_size, lengths)
    weights = (query_weight, keys_weight, value_weight, mixer_weight, inner_weight, outer_weight)
    vectors = (query_offset, value_offset, mixer_offset, first_gain, first_shift, outer_offset, second_gain, second_shift)
    packed, vec_own = pack(weights, vectors, inner_offset)
    others = (swap(packed), swap(inner_weight), swap(outer_weight))
    y_first, shared_first, own_first, own_handed = first_forward(meta, tokens, weights, vec_own)
    handed, others = lax.optimization_barrier((y_first, others))
    y_x = swap(handed)
    y_second, shared_second, own_second = second_forward(meta, y_first, y_x, weights, others, vec_own)
    shared_x = swap(lax.optimization_barrier((shared_first, y_x))[0])
    own_second, shared_x = lax.optimization_barrier((own_second, shared_x))
    own = {1: (own_second, own_second)}
    shared = {0: (shared_first, shared_x), 1: (shared_second, swap(shared_second))}
    entries = {1: (y_first, y_x), 0: (tokens, tokens)}
    y_last_x = swap(y_second)
    moving = {}
    results = {}

    def boundary(turn, value, other):
        names = SCHEDULE[turn] if hypercube else ()
        if not names:
            return value, other
        landed = {name: moving[name][1] for name in names}
        other, landed = lax.optimization_barrier((other, landed))
        ready = []
        for name in names:
            keep, _, waiting, arrived, step = moving[name]
            arrived = arrived + [landed[name]]
            if waiting:
                moving[name] = (keep, None, waiting[1:], arrived, step)
                ready.append(name)
            else:
                moving[name] = (keep, None, [], arrived, step + 1)
        done = [name for name in names if name not in ready]
        if done:
            added = add_arrived([(moving[name][0], moving[name][3]) for name in done])
            value, added = lax.optimization_barrier((value, added))
            for name, parts in zip(done, added):
                step = moving[name][4]
                if len(parts) == 1:
                    results[name] = parts[0]
                else:
                    moving[name] = (parts[1], exchange(parts[0], step_bits(NEAR_FIRST[name])[step]), [], [], step)
        else:
            value = lax.optimization_barrier((value, landed))[0]
        for name in ready:
            keep, _, waiting, arrived, step = moving[name]
            piece = pieces[name].pop(0)
            piece = lax.optimization_barrier((piece, landed, value))[0]
            moving[name] = (keep, exchange(piece, step_bits(NEAR_FIRST[name])[0]), waiting, arrived, step)
        return value, other

    pieces = {}

    def begin(name, sends, keep):
        if hypercube:
            pieces[name] = list(sends[1:])
            moving[name] = (keep, exchange(sends[0], step_bits(NEAR_FIRST[name])[0]), list(sends[1:]), [], 0)
        else:
            moving[name] = sends

    def feed(layer, grad):
        return feed_gradient(layer, meta, grad, *own[layer], weights, others, vec_own)

    def feed_sum(layer, dz, df, away_x):
        *sends, keep = feed_weights(layer, False, spots, *shared[layer], dz, df, away_x)
        begin(F1 if layer else F0, sends, keep)
        return keep

    def attend(layer, dc, da, da1, small):
        return attend_gradient(layer, meta, *own[layer], dc, da, da1, weights, others[0], small)

    def attend_sum(layer, grads, away_x, small):
        send, keep = attend_weights(layer, False, spots, *entries[layer], *shared[layer], grads, away_x, small)
        begin(T1 if layer else T0, [send], keep)
        return keep

    def tie(value, other):
        return lax.optimization_barrier((value, other))[0]

    dh = {}
    low_gradient = {}
    dz, df, away, da1, da, dc, small_feed = feed(1, cotangent)
    held = feed_sum(1, dz, df, swap(away))
    own[0] = (own_first, swap(tie(own_handed, held)))
    dh[1], low_gradient[1], grads, away, small = attend(1, tie(dc, held), da, da1, small_feed)
    attend_away_x = swap(away)
    grad, _ = boundary(3, low_gradient[1], held)
    dz, df, away, da1, da, dc, small_feed = feed(0, grad)
    grads, away = boundary(4, tie(grads, dz), away)
    feed_away_x = swap(away)
    held = attend_sum(1, grads, attend_away_x, small)
    dz, _ = boundary(5, tie(dz, held), held)
    held = feed_sum(0, dz, df, feed_away_x)
    dc, _ = boundary(6, tie(dc, held), held)
    dh[0], low_gradient[0], grads, away, small = attend(0, dc, da, da1, small_feed)
    grads, away = boundary(7, grads, away)
    held = attend_sum(0, grads, swap(away), small)
    dh_x = swap(jnp.where(first, low_gradient[1], low_gradient[0])).astype(F32)
    layer_out = jnp.stack([jnp.where(first, y_first[0], y_last_x[0]), jnp.where(first, y_first[1], y_second[0])])
    input_grad = jnp.stack([jnp.where(first, dh[0], dh_x), jnp.where(first, dh_x, dh[1])])
    if hypercube:
        for turn in range(8, len(SCHEDULE)):
            (layer_out, input_grad), held = boundary(turn, (layer_out, input_grad), held)
        order = (F0, F1, T0, T1)
        done = finish(groups, width, hidden, [results[name] for name in order] + [swap(results[name]) for name in order])
        query_grad, keys_grad, value_grad, mixer_grad, inner_grad, outer_grad, lines, wide_line = done
        height = width // groups
        small = [lines[index, :height] for index in range(8)]
        small_wide = wide_line[0, : hidden // groups]
    else:
        def scatter(value):
            return lax.psum_scatter(value, "dp", scatter_dimension=0, tiled=True).astype(F32)

        found = []
        for layer in (1, 0):
            outer_part, inner_part = (value[0] for value in moving["f", layer])
            attend = moving["t", layer][0][0]
            half = width // 2
            outer_half = jnp.concatenate([outer_part[:, :half], outer_part[:, half:]], axis=0)
            parts = [scatter(outer_half), scatter(inner_part[:width]), scatter(inner_part[width:])]
            parts += [scatter(attend[:width]), scatter(attend[width : 2 * width])]
            lines = attend[2 * width :].astype(F32)
            parts += [scatter(lines[index]) for index in range(8)] + [scatter(lines[8:12].reshape(-1))]
            found.append(parts)
        mine = [jnp.where(first, b, a) for a, b in zip(*found)]
        back = [swap(jnp.where(first, a, b)) for a, b in zip(found[0][:5], found[1][:5])]
        low = [jnp.where(first, a, b) for a, b in zip(mine, back)]
        high = [jnp.where(first, b, a) for a, b in zip(mine, back)]
        outer_grad = jnp.concatenate([low[0], high[0]], axis=1)
        inner_grad = jnp.concatenate([low[1], low[2], high[1], high[2]], axis=1)
        query_grad, keys_grad, value_grad, mixer_grad = (low[3], low[4], high[3], high[4])
        small, small_wide = (mine[5:13], mine[13])
    second_gain_grad, second_shift_grad, outer_offset_grad, first_gain_grad, first_shift_grad, mixer_offset_grad = small[:6]
    outputs = (
        layer_out, input_grad, query_grad, small[6], keys_grad, value_grad, small[7], mixer_grad, mixer_offset_grad,
        first_gain_grad, first_shift_grad, inner_grad, small_wide, outer_grad, outer_offset_grad, second_gain_grad,
        second_shift_grad,
    )
    return tuple(piece[None] for piece in outputs)


def solution(mesh):
    matrix = P("section", None, None)
    vector = P("section", None)
    in_specs = (
        P("dp", None, None), P("dp", None, None), P("dp"), P("dp"), P("dp", None), matrix, vector, matrix, matrix, vector,
        matrix, vector, vector, vector, matrix, vector, matrix, vector, vector, vector,
    )
    rows = P("section", "dp", None, None)
    grad = P("section", "dp", None)
    small = P("section", "dp")
    out_specs = (rows, rows, grad, small, grad, grad, small, grad, small, small, small, grad, small, grad, small, small, small)
    return jax.shard_map(per_device, mesh=mesh, in_specs=in_specs, out_specs=out_specs, check_vma=False)
```

```python
import functools
import jax
import jax.numpy as jnp
from jax import lax
from jax.experimental import pallas as pl
from jax.experimental.pallas import tpu as pltpu
from jax.sharding import PartitionSpec as P

HEADS = 12
HEAD_DIM = 64
BUCKET = 64
PAIR = 2 * HEAD_DIM
masked_score = -1000000000.0
norm_epsilon = 1e-06
F32 = jnp.float32
BF16 = jnp.bfloat16
CHUNK = 16
FFN_TILE = 512
ATT_UNROLL = 3


def rows_times(left, right):
    return lax.dot_general(left, right, (((1,), (0,)), ((), ())), preferred_element_type=F32)


def rows_times_transposed(left, right):
    return lax.dot_general(left, right, (((1,), (1,)), ((), ())), preferred_element_type=F32)


def transposed_times(left, right):
    return lax.dot_general(left, right, (((0,), (0,)), ((), ())), preferred_element_type=F32)


def slot_facts(block, span_rows, place, meta, micro):
    bucket_ref, count_ref, lengths_ref = meta
    bucket = bucket_ref[micro]
    count = count_ref[micro]

    def length_of(slot):
        return jnp.where(slot < count, lengths_ref[micro, slot], 0)

    if span_rows == 2 * BUCKET:
        return (jnp.full_like(place, block), place, jnp.full_like(place, length_of(block)))
    short = bucket == 0
    first = 3 * block
    slot_short = first + place // BUCKET
    length_short = jnp.where(
        place < BUCKET,
        length_of(first),
        jnp.where(place < 2 * BUCKET, length_of(first + 1), length_of(first + 2)),
    )
    slot = jnp.where(short, slot_short, block)
    inner = jnp.where(short, place % BUCKET, place)
    length = jnp.where(short, length_short, length_of(block))
    return (slot, inner, length)


def fill_masks(span_rows, row_count, meta, micro, bias_ref, valid_ref, keys_down=False):
    for block in range(row_count // span_rows):
        row_place = lax.broadcasted_iota(jnp.int32, (span_rows, 1), 0)
        row_slot, row_inner, row_length = slot_facts(block, span_rows, row_place, meta, micro)
        rows = slice(block * span_rows, (block + 1) * span_rows)
        if bias_ref is not None:
            other_place = lax.broadcasted_iota(jnp.int32, (1, span_rows), 1)
            other_slot, other_inner, other_length = slot_facts(block, span_rows, other_place, meta, micro)
            if keys_down:
                allowed = other_slot == jnp.where(row_inner < row_length, row_slot, -1)
            else:
                allowed = row_slot == jnp.where(other_inner < other_length, other_slot, -1)
            allowed = allowed | (row_place == other_place)
            bias_ref[rows, 0:span_rows] = jnp.where(allowed, 0.0, masked_score)
        if valid_ref is not None:
            valid_ref[rows, :] = jnp.where(row_inner < row_length, 1.0, 0.0)


def by_span(meta, micro, body):
    even = meta[0][micro] == 1

    @pl.when(even)
    def _():
        body(2 * BUCKET)

    @pl.when(jnp.logical_not(even))
    def _():
        body(3 * BUCKET)


def attend_forward(span_rows, row_count, q_ref, k_ref, v_ref, bias_ref, c_ref):
    blocks = row_count // span_rows

    def one_pair(pair, carry):
        columns = pl.ds(pl.multiple_of(pair * PAIR, PAIR), PAIR)
        lane = lax.broadcasted_iota(jnp.int32, (span_rows, PAIR), 1)
        first_half = lane < HEAD_DIM
        weights = []
        for block in range(blocks):
            rows = slice(block * span_rows, (block + 1) * span_rows)
            query = q_ref[rows, columns] * jnp.asarray(HEAD_DIM ** (-0.5), BF16)
            keys = k_ref[rows, columns]
            zero = jnp.zeros_like(keys)
            bias = bias_ref[rows, 0:span_rows]
            for mine in (first_half, jnp.logical_not(first_half)):
                scores = rows_times_transposed(query, jnp.where(mine, keys, zero)) + bias
                top = jnp.max(scores, axis=-1, keepdims=True)
                weights.append(jnp.exp(scores - top).astype(BF16))
        for block in range(blocks):
            rows = slice(block * span_rows, (block + 1) * span_rows)
            value = v_ref[rows, columns]
            one = jnp.ones_like(value)
            left = rows_times(weights[2 * block], jnp.where(first_half, value, one))
            right = rows_times(weights[2 * block + 1], jnp.where(first_half, one, value))
            above = jnp.where(first_half, left, right)
            below = pltpu.roll(jnp.where(first_half, right, left), HEAD_DIM, 1)
            c_ref[rows, columns] = (above / below).astype(BF16)
        return carry

    lax.fori_loop(0, HEADS // 2, one_pair, 0, unroll=ATT_UNROLL)


def row_moments(values):
    center = jnp.mean(values, axis=-1, keepdims=True)
    centred = values - center
    spread = jnp.mean(centred * centred, axis=-1, keepdims=True)
    return centred, lax.rsqrt(spread + norm_epsilon)


def over_chunks(row_count, body, rows=CHUNK, group=6):
    def step(index, carry):
        for inner in range(group):
            start = pl.multiple_of(index * (rows * group) + inner * rows, rows)
            body(pl.ds(start, rows))
        return carry

    lax.fori_loop(0, row_count // (rows * group), step, 0)


def over_chunks_with_sums(row_count, body, sums_ref, rows=CHUNK, group=6):
    def step(index, carry):
        total = None
        for inner in range(group):
            start = pl.multiple_of(index * (rows * group) + inner * rows, rows)
            terms = [fold_rows(term) for term in body(pl.ds(start, rows))]
            total = terms if total is None else [a + b for a, b in zip(total, terms)]
        for place, term in enumerate(total):
            sums_ref[place] += term
        return carry

    lax.fori_loop(0, row_count // (rows * group), step, 0)


def fold_rows(values):
    return jnp.sum(values.reshape(values.shape[0] // 8, 8, values.shape[1]), axis=0)


def gelu_with_slope(values):
    cumulative = 0.5 + 0.5 * lax.erf(values * (0.5 ** 0.5))
    density = jnp.exp(values * values * -0.5) * 0.3989422804014327
    return values * cumulative, cumulative + values * density


ANY = pl.BlockSpec(memory_space=pl.ANY)
VM = pl.BlockSpec(memory_space=pltpu.VMEM)
SM = pl.BlockSpec(memory_space=pltpu.SMEM)
VMEM_LIMIT = 63_000 * 1024
S = jax.ShapeDtypeStruct
V = pltpu.VMEM
B_QUERY, B_VALUE, B_MIXER, GAIN_ONE, SHIFT_ONE, B_OUTER, GAIN_TWO, SHIFT_TWO = range(8)
QUERY, FIRST_SUM, SECOND_SUM, SLOPE = (0, 3, 4, 5)
ACTIVE, MIDDLE, CONTEXT = (0, 4, 5)
X_BIT, Y_BIT, NEAR_BIT, FAR_BIT = (0, 1, 2, 3)
SMALL_ROWS = 16


class Loads:
    def __init__(self, semaphores):
        self.semaphores = semaphores
        self.copies = {}

    def start(self, name, source, target, other=None, take_other=None):
        semaphore = self.semaphores.at[len(self.copies)]
        copy = pltpu.make_async_copy(source, target, semaphore)
        self.copies[name] = copy
        if other is None:
            copy.start()
            return
        second = pltpu.make_async_copy(other, target, semaphore)

        @pl.when(take_other)
        def _():
            second.start()

        @pl.when(jnp.logical_not(take_other))
        def _():
            copy.start()

    def wait(self, *names):
        for name in names:
            self.copies[name].wait()


class Stores:
    def __init__(self, semaphores):
        self.semaphores = semaphores
        self.copies = []

    def start(self, source, target):
        copy = pltpu.make_async_copy(source, target, self.semaphores.at[len(self.copies)])
        copy.start()
        self.copies.append(copy)

    def wait(self):
        for copy in self.copies:
            copy.wait()


def run_kernel(kernel, outs, out_specs, in_specs, scratch, loads, stores, flops, bytes_moved, name):
    return pl.pallas_call(
        kernel,
        out_shape=outs,
        in_specs=in_specs,
        out_specs=out_specs,
        scratch_shapes=list(scratch) + [pltpu.SemaphoreType.DMA((loads,)), pltpu.SemaphoreType.DMA((stores,))],
        compiler_params=pltpu.CompilerParams(vmem_limit_bytes=VMEM_LIMIT),
        cost_estimate=pl.CostEstimate(flops=1000, bytes_accessed=1000, transcendentals=0),
        name=name,
    )


def spot_of(near_first, dest):
    relative = jnp.bitwise_xor(dest, lax.axis_index("dp"))

    def bit(index):
        return jnp.bitwise_and(lax.shift_right_logical(relative, index), 1)

    first = lax.axis_index("section") == 0
    lead = jnp.where(first, bit(X_BIT), bit(Y_BIT))
    follow = jnp.where(first, bit(Y_BIT), bit(X_BIT))
    if near_first:
        return bit(NEAR_BIT) * 8 + lead * 4 + follow * 2 + bit(FAR_BIT)
    return lead * 8 + follow * 4 + bit(NEAR_BIT) * 2 + bit(FAR_BIT)


def step_bits(near_first):
    cross = [(X_BIT, Y_BIT), (Y_BIT, X_BIT)]
    if near_first:
        return [(NEAR_BIT, NEAR_BIT)] + cross + [(FAR_BIT, FAR_BIT)]
    return cross + [(NEAR_BIT, NEAR_BIT), (FAR_BIT, FAR_BIT)]


def forward_matrix_loads(loads, hidden_start, weights, others, take_other, targets):
    names = ("wq", "wk", "wv", "wm", "wi", "wo")

    def begin(index):
        other = None if others is None else others[index]
        loads.start(names[index], weights[index].at[0], targets[index], other, take_other)

    def load(step):
        if step == 0:
            hidden_start()
            for index in range(3):
                begin(index)
            return
        if step == 1:
            loads.wait("h")
        loads.wait(names[step - 1])
        if step <= 3:
            begin(step + 2)

    return load


def forward_body(load, store, meta, micros, vec, outs, refs):
    h_s, wq_s, wk_s, wv_s, wm_s, wi_s, wo_s, qkv_s, c_s, ml_s, a1_s, a2_s, u_s, gp_s, y_s, m_s, f0_s, e0_s, e1_s, bias_s, valid_s, bi_s = refs
    y_o, own_o, shared_o = outs
    rows, width = h_s.shape
    hidden = wi_s.shape[1]
    each = rows // len(micros)
    parts = [slice(place * each, (place + 1) * each) for place in range(len(micros))]

    def send(source, plane, shared=False):
        for place, part in enumerate(parts):
            target = shared_o.at[place] if shared else own_o[place]
            for index in range(source.shape[1] // width):
                store.start(source.at[part, index * width : (index + 1) * width], target.at[plane + index])

    load(0)
    for part, micro in zip(parts, micros):
        by_span(meta, micro, lambda span: fill_masks(span, each, meta, micro, bias_s.at[part], valid_s.at[part]))
    load(1)
    qkv_s[0] = (rows_times(h_s[...], wq_s[...]) + vec(B_QUERY)).astype(BF16)
    load(2)
    qkv_s[1] = rows_times(h_s[...], wk_s[...]).astype(BF16)
    load(3)
    qkv_s[2] = (rows_times(h_s[...], wv_s[...]) + vec(B_VALUE)).astype(BF16)
    for place, part in enumerate(parts):
        store.start(qkv_s.at[:, part], own_o[place].at[QUERY : QUERY + 3])
    for part, micro in zip(parts, micros):
        by_span(
            meta, micro,
            lambda span: attend_forward(
                span, each, qkv_s.at[0, part], qkv_s.at[1, part], qkv_s.at[2, part], bias_s.at[part], c_s.at[part]
            ),
        )
    send(c_s, CONTEXT, True)
    load(4)
    f0_s[...] = rows_times(c_s[...], wm_s[...])
    offset_mixer, gain_one, shift_one = (vec(B_MIXER), vec(GAIN_ONE), vec(SHIFT_ONE))

    def first_norm(part):
        total = h_s[part, :].astype(F32) + (f0_s[part, :] + offset_mixer)
        a1_s[part, :] = total.astype(BF16)
        centred, scale = row_moments(total)
        middle = centred * scale * gain_one + shift_one
        m_s[part, :] = middle
        ml_s[part, :] = middle.astype(BF16)

    over_chunks(rows, first_norm)
    send(a1_s, FIRST_SUM)
    send(ml_s, MIDDLE, True)
    load(5)
    tile = FFN_TILE
    tiles = hidden // tile

    def project(buffer, which):
        columns = pl.ds(pl.multiple_of(which * tile, tile), tile)
        buffer[...] = rows_times(ml_s[...], wi_s[:, columns])

    def activate(buffer, which):
        columns = pl.ds(pl.multiple_of(which * tile, tile), tile)
        offset = bi_s[0:1, columns]
        for start in range(0, rows, 32):
            part = slice(start, start + 32)
            value, slope = gelu_with_slope(buffer[part, :] + offset)
            u_s[part, columns] = value.astype(BF16)
            gp_s[part, columns] = slope.astype(BF16)

    for index in range(hidden // width):
        bi_s[0:1, index * width : (index + 1) * width] = vec(8 + index)
    project(e0_s, 0)

    def two_tiles(index, carry):
        project(e1_s, 2 * index + 1)
        activate(e0_s, 2 * index)
        project(e0_s, jnp.minimum(2 * index + 2, tiles - 1))
        activate(e1_s, 2 * index + 1)
        return carry

    lax.fori_loop(0, tiles // 2, two_tiles, 0)
    send(u_s, ACTIVE, True)
    send(gp_s, SLOPE)
    load(6)
    f0_s[...] = rows_times(u_s[...], wo_s[...])
    offset_outer, gain_two, shift_two = (vec(B_OUTER), vec(GAIN_TWO), vec(SHIFT_TWO))

    def second_norm(part):
        total = m_s[part, :] + (f0_s[part, :] + offset_outer)
        a2_s[part, :] = total.astype(BF16)
        centred, scale = row_moments(total)
        y_s[part, :] = ((centred * scale * gain_two + shift_two) * valid_s[part, :]).astype(BF16)

    over_chunks(rows, second_norm)
    for place, part in enumerate(parts):
        store.start(y_s.at[part], y_o.at[place])
    send(a2_s, SECOND_SUM)
    store.wait()


def first_forward_kernel(
    micro_count, bucket, count, lengths, tok, wq, wk, wv, wm, wi, wo, bq, bv, bm, g1, s1, bo, g2, s2, bi, *rest
):
    y_o, shared_o = rest[:2]
    own_o = rest[2 : 2 + micro_count]
    packed_o, vec_o = rest[2 + micro_count : 4 + micro_count]
    *refs, hold_s, low_s, pack_sem, in_sem, out_sem = rest[4 + micro_count :]
    h_s, wq_s, wk_s, wv_s, wm_s, wi_s, wo_s = refs[:7]
    width = h_s.shape[1]
    gather = pltpu.make_async_copy(wm.at[0], hold_s, pack_sem.at[0])
    hand = pltpu.make_async_copy(hold_s, packed_o.at[0:width], pack_sem.at[1])
    hand_low = pltpu.make_async_copy(low_s, packed_o.at[width : width + VECTOR_ROWS], pack_sem.at[2])
    vec_o[...] = jnp.zeros_like(vec_o)
    for place, vector in enumerate((bq, bv, bm, g1, s1, bo, g2, s2)):
        vec_o[place : place + 1, :] = vector[...]
    for index in range(bi.shape[1] // width):
        vec_o[8 + index : 9 + index, :] = bi[:, index * width : (index + 1) * width]
    high = vec_o[...].astype(BF16)
    low_s[0:16, :] = high
    low_s[16:32, :] = (vec_o[...] - high.astype(F32)).astype(BF16)
    hand_low.start()

    @pl.when(lax.axis_index("section") != 0)
    def _():
        gather.start()
        gather.wait()
        hand.start()

    @pl.when(lax.axis_index("section") == 0)
    def _():
        loads = Loads(in_sem)
        each = h_s.shape[0] // micro_count

        def hidden_start():
            for micro in range(1, micro_count):
                loads.start(("h", micro), tok.at[micro], h_s.at[micro * each : (micro + 1) * each])
            loads.start("h", tok.at[0], h_s.at[0:each])

        inner_load = forward_matrix_loads(
            loads, hidden_start, (wq, wk, wv, wm, wi, wo), None, None, (wq_s, wk_s, wv_s, wm_s, wi_s, wo_s)
        )

        def load(step):
            if step == 1:
                for micro in range(1, micro_count):
                    loads.wait(("h", micro))
            if step == 4:
                gather.start()
            if step == 6:
                gather.wait()
                hand.start()
            inner_load(step)

        forward_body(
            load, Stores(out_sem), (bucket, count, lengths), tuple(range(micro_count)),
            lambda place: vec_o[place : place + 1, :], (y_o, own_o, shared_o), refs,
        )

    hand.wait()
    hand_low.wait()


def second_forward_kernel(
    bucket, count, lengths, y_own, y_other, wq, wk, wv, wm, wi, wo, xq, xk, xv, xi, xo, packed, vec_own,
    y_o, shared_o, own_o, *scratch
):
    *refs, other_s, vec_s, in_sem, out_sem = scratch
    h_s, wq_s, wk_s, wv_s, wm_s, wi_s, wo_s = refs[:7]
    section = lax.axis_index("section")
    first = section == 0
    width = h_s.shape[1]
    loads = Loads(in_sem)
    load = forward_matrix_loads(
        loads, lambda: loads.start("h", y_other.at[section], h_s, y_own.at[section], first), (wq, wk, wv, wm, wi, wo),
        (xq.at[0], xk.at[0], xv.at[0], packed.at[0:width], xi.at[0], xo.at[0]), first, (wq_s, wk_s, wv_s, wm_s, wi_s, wo_s),
    )
    vectors = Vectors(loads, packed, vec_own, other_s, first)

    def ready(step):
        load(step)
        if step == 0:
            loads.wait("vectors")
            for place in range(12):
                vec_s[place : place + 1, :] = vectors(place)

    forward_body(
        ready, Stores(out_sem), (bucket, count, lengths), (section,), lambda place: vec_s[place : place + 1, :],
        (y_o, (own_o,), shared_o), refs,
    )


def forward_shapes(micro_count, each, width, hidden):
    rows = micro_count * each
    flat = (rows, width)
    wide = (rows, hidden)
    square = (width, width)

    def out(*tail):
        return (micro_count,) + tail

    wides = hidden // width
    outs = (S(out(each, width), BF16), S(out(wides + 2, each, width), BF16)) + (S((wides + 5, each, width), BF16),) * micro_count
    scratch = [
        V(flat, BF16), V(square, BF16), V(square, BF16), V(square, BF16), V(square, BF16), V((width, hidden), BF16),
        V((hidden, width), BF16), V((3,) + flat, BF16), V(flat, BF16), V(flat, BF16), V(flat, BF16), V(flat, BF16),
        V(wide, BF16), V(wide, BF16), V(flat, BF16), V(flat, F32), V(flat, F32), V((rows, FFN_TILE), F32),
        V((rows, FFN_TILE), F32), V((rows, 3 * BUCKET), F32), V((rows, 1), F32),
        V((8, hidden), F32),
    ]
    flops = 2 * rows * width * (4 * width + 2 * hidden)
    return outs, scratch, flops


def first_forward(meta, tokens, weights, vectors, bi):
    micro_count, each, width = tokens.shape
    outs, scratch, flops = forward_shapes(micro_count, each, width, bi.shape[1])
    outs = outs + (S((width + VECTOR_ROWS, width), BF16), S((16, width), F32))
    scratch = scratch + [V((width, width), BF16), V((VECTOR_ROWS, width), BF16), pltpu.SemaphoreType.DMA((3,))]
    return run_kernel(
        functools.partial(first_forward_kernel, micro_count), outs, [ANY] * (3 + micro_count) + [VM], [SM] * 3 + [ANY] * 7 + [VM] * 9,
        scratch, 6 + micro_count, 14 * micro_count, flops, 40_000_000, "first_forward",
    )(*meta, tokens, *weights, *vectors, bi)


def second_forward(meta, y_own, y_other, weights, others, vec_own):
    _, each, width = y_own.shape
    outs, scratch, flops = forward_shapes(1, each, width, weights[4].shape[2])
    scratch = scratch + [V((VECTOR_ROWS, width), BF16), V((16, width), F32)]
    return run_kernel(
        second_forward_kernel, outs, [ANY] * 3, [SM] * 3 + [ANY] * 14 + [VM], scratch, 8, 14, flops, 25_000_000,
        "second_forward",
    )(*meta, y_own, y_other, *weights, *others, vec_own)


VECTOR_ROWS = 32


class Vectors:
    def __init__(self, loads, packed, own, other_s, take_other):
        width = packed.shape[1]
        self.own = own
        self.other_s = other_s
        self.take_other = take_other
        loads.start("vectors", packed.at[width : width + VECTOR_ROWS], other_s)

    def __call__(self, place):
        other = self.other_s[place : place + 1, :].astype(F32) + self.other_s[16 + place : 17 + place, :].astype(F32)
        return jnp.where(self.take_other, other, self.own[place : place + 1, :])


def norm_backward(grad, total, gain):
    centred, scale = row_moments(total)
    unit = centred * scale
    spread = grad * gain
    first = jnp.mean(spread, axis=-1, keepdims=True)
    second = jnp.mean(spread * unit, axis=-1, keepdims=True)
    return (spread - first - unit * second) * scale, grad * unit


def layer_of(layer):
    return lax.axis_index("section") != layer


def load_planes(layer, loads, name, own, other, plane, target):
    width = own.shape[2]
    take_other = lax.axis_index("section") == 1
    for index in range(target.shape[1] // width):
        part = target if target.shape[1] == width else target.at[:, index * width : (index + 1) * width]
        received = None if layer == 1 else other.at[plane + index]
        loads.start((name, index), own.at[plane + index], part, received, take_other)


def feed_kernel(
    layer, bucket, count, lengths, g, own, own_x, wo, wo_x, wi, wi_x, wm, packed, vec_own,
    dz_o, df_o, away_o, da1_o, da_o, dc_o, small_o,
    g_s, a2_s, gp_s, a1_s, wo_s, wi_s, wm_s, da2_s, dz_s, df_s, dm_s, da1_s, da_s, dc_s, e0_s, e1_s, valid_s, sums_s, wide_s, other_s, in_sem, out_sem,
):
    section = lax.axis_index("section")
    rows, width = a2_s.shape
    hidden = df_s.shape[1]
    loads = Loads(in_sem)
    store = Stores(out_sem)
    wides = range(hidden // width)
    loads.start("g", g.at[section] if layer == 1 else g, g_s)
    load_planes(layer, loads, "a2", own, own_x, SECOND_SUM, a2_s)
    loads.start("wo", wo.at[0], wo_s, wo_x.at[0], layer_of(layer))
    meta = (bucket, count, lengths)
    by_span(meta, section, lambda span: fill_masks(span, rows, meta, section, None, valid_s))
    sums_s[...] = jnp.zeros_like(sums_s)
    vectors = Vectors(loads, packed, vec_own, other_s, layer_of(layer))
    loads.wait("g", ("a2", 0), "vectors")
    gain_two, gain_one = (vectors(GAIN_TWO), vectors(GAIN_ONE))
    load_planes(layer, loads, "gp", own, own_x, SLOPE, gp_s)
    loads.start("wi", wi.at[0], wi_s, wi_x.at[0], layer_of(layer))

    def second_norm(part):
        grad = g_s[part, :].astype(F32) * valid_s[part, :]
        moved, gained = norm_backward(grad, a2_s[part, :].astype(F32), gain_two)
        da2_s[part, :] = moved
        low = moved.astype(BF16)
        dz_s[part, :] = low
        return gained, grad, low.astype(F32)

    over_chunks_with_sums(rows, second_norm, sums_s.at[0:3])
    half = width // 2
    store.start(dz_s.at[:, pl.ds(pl.multiple_of(section * half, half), half)], dz_o)
    store.start(dz_s.at[:, pl.ds(pl.multiple_of((1 - section) * half, half), half)], away_o.at[2, :, 0:half])
    tile = FFN_TILE
    tiles = hidden // tile

    def project(buffer, which):
        columns = pl.ds(pl.multiple_of(which * tile, tile), tile)
        buffer[...] = rows_times_transposed(dz_s[...], wo_s[columns, :])

    def slope(buffer, which):
        columns = pl.ds(pl.multiple_of(which * tile, tile), tile)
        total = None
        for start in range(0, rows, 32):
            part = slice(start, start + 32)
            low_part = (buffer[part, :] * gp_s[part, columns].astype(F32)).astype(BF16)
            df_s[part, columns] = low_part
            term = fold_rows(low_part.astype(F32))
            total = term if total is None else total + term
        wide_s[:, columns] = total

    loads.wait("wo")
    load_planes(layer, loads, "a1", own, own_x, FIRST_SUM, a1_s)
    loads.start("wm", wm.at[0], wm_s, packed.at[0:width], layer_of(layer))
    project(e0_s, 0)
    for index in wides:
        loads.wait(("gp", index))

    def two_tiles(index, carry):
        project(e1_s, 2 * index + 1)
        slope(e0_s, 2 * index)
        project(e0_s, jnp.minimum(2 * index + 2, tiles - 1))
        slope(e1_s, 2 * index + 1)
        return carry

    lax.fori_loop(0, tiles // 2, two_tiles, 0)
    half = hidden // 2
    store.start(df_s.at[:, pl.ds(pl.multiple_of(section * half, half), half)], df_o)
    for index in range(2):
        start = pl.multiple_of((1 - section) * half + index * width, width)
        store.start(df_s.at[:, pl.ds(start, width)], away_o.at[index])
    loads.wait("wi")
    dm_s[...] = rows_times_transposed(df_s[...], wi_s[...])
    loads.wait(("a1", 0))

    def first_norm(part):
        grad = dm_s[part, :] + da2_s[part, :]
        moved, gained = norm_backward(grad, a1_s[part, :].astype(F32), gain_one)
        da1_s[part, :] = moved
        low_part = moved.astype(BF16)
        da_s[part, :] = low_part
        return gained, grad, low_part.astype(F32)

    over_chunks_with_sums(rows, first_norm, sums_s.at[3:6])
    store.start(da1_s, da1_o)
    store.start(da_s, da_o)
    for index in range(6):
        small_o[index : index + 1, :] = jnp.sum(sums_s[index], axis=0, keepdims=True)
    inner_sum = jnp.sum(wide_s[...], axis=0, keepdims=True)
    for index in range(hidden // width):
        small_o[8 + index : 9 + index, :] = inner_sum[:, index * width : (index + 1) * width]
    loads.wait("wm")
    dc_s[...] = rows_times_transposed(da_s[...], wm_s[...]).astype(BF16)
    store.start(dc_s, dc_o)
    store.wait()


def feed_gradient(layer, meta, g, own, own_x, weights, others, vec_own):
    _, rows, width = own.shape
    hidden = weights[4].shape[2]
    flat = (rows, width)
    _, _, _, xi, xo, packed = others
    return run_kernel(
        functools.partial(feed_kernel, layer),
        (S((rows, width // 2), BF16), S((rows, hidden // 2), BF16), S((3,) + flat, BF16), S(flat, F32), S(flat, BF16), S(flat, BF16), S((SMALL_ROWS, width), F32)),
        [ANY] * 6 + [VM], [SM] * 3 + [ANY] * 9 + [VM],
        [
            V(flat, g.dtype), V(flat, BF16), V((rows, hidden), BF16), V(flat, BF16), V((hidden, width), BF16), V((width, hidden), BF16),
            V((width, width), BF16), V(flat, F32), V(flat, BF16), V((rows, hidden), BF16), V(flat, F32), V(flat, F32), V(flat, BF16),
            V(flat, BF16), V((rows, FFN_TILE), F32), V((rows, FFN_TILE), F32), V((rows, 1), F32), V((6, 8, width), F32),
            V((8, hidden), F32), V((VECTOR_ROWS, width), BF16),
        ],
        7 + hidden // width, 8, 2 * rows * width * (2 * hidden + width), 25_000_000, "feed_gradient",
    )(*meta, g, own, own_x, weights[5], xo, weights[4], xi, weights[3], packed, vec_own)


def attend_backward(span_rows, row_count, q_ref, k_ref, v_ref, dc_ref, bias_ref, dq_ref, dk_ref, dv_ref):
    blocks = row_count // span_rows
    scale = HEAD_DIM ** (-0.5)

    def one_pair(pair, carry):
        columns = pl.ds(pl.multiple_of(pair * PAIR, PAIR), PAIR)
        lane = lax.broadcasted_iota(jnp.int32, (span_rows, PAIR), 1)
        halves = (lane < HEAD_DIM, lane >= HEAD_DIM)
        for block in range(blocks):
            rows = slice(block * span_rows, (block + 1) * span_rows)
            query = q_ref[rows, columns] * jnp.asarray(scale, BF16)
            keys = k_ref[rows, columns]
            value = v_ref[rows, columns]
            grad = dc_ref[rows, columns]
            zero = jnp.zeros_like(keys)
            bias = bias_ref[rows, 0:span_rows]
            dq = dk = dv = None
            for mine in halves:
                keys_own = jnp.where(mine, keys, zero)
                scores = rows_times_transposed(keys_own, query) + bias
                grad_part = rows_times_transposed(jnp.where(mine, value, zero), grad)
                weight = jnp.exp(scores - jnp.max(scores, axis=0, keepdims=True))
                part = weight * (1.0 / jnp.sum(weight, axis=0, keepdims=True))
                mean = jnp.sum(grad_part * part, axis=0, keepdims=True)
                grad_scores = (part * (grad_part - mean)).astype(BF16)
                terms = (
                    transposed_times(grad_scores, keys_own),
                    rows_times(grad_scores, jnp.where(mine, query, zero)),
                    rows_times(part.astype(BF16), jnp.where(mine, grad, zero)),
                )
                if dq is None:
                    dq, dk, dv = terms
                else:
                    dq, dk, dv = (dq + terms[0], dk + terms[1], dv + terms[2])
            dq_ref[rows, columns] = (dq * scale).astype(BF16)
            dk_ref[rows, columns] = dk.astype(BF16)
            dv_ref[rows, columns] = dv.astype(BF16)
        return carry

    lax.fori_loop(0, HEADS // 2, one_pair, 0)


def attend_kernel(
    layer, bucket, count, lengths, own, own_x, dc, da, da1, wq, wk, wv, xq, xk, xv, small_one,
    dh_o, dlow_o, home_o, away_o, small_o,
    qkv_s, dc_s, da_s, dh_s, dlow_s, wq_s, wk_s, wv_s, dq_s, dk_s, dv_s, bias_s, sums_s, low_s, in_sem, out_sem,
):
    section = lax.axis_index("section")
    rows, width = dc_s.shape
    second = section == 1
    loads = Loads(in_sem)
    received = None if layer == 1 else own_x.at[QUERY : QUERY + 3]
    loads.start("qkv", own.at[QUERY : QUERY + 3], qkv_s, received, second)
    loads.start("dc", dc, dc_s)
    meta = (bucket, count, lengths)
    by_span(meta, section, lambda span: fill_masks(span, rows, meta, section, bias_s, None, True))
    loads.wait("qkv", "dc")
    loads.start("da", da, da_s)
    loads.start("da1", da1, dh_s)
    for name, weight, other, target in (("wq", wq, xq, wq_s), ("wk", wk, xk, wk_s), ("wv", wv, xv, wv_s)):
        loads.start(name, weight.at[0], target, other.at[0], layer_of(layer))
    by_span(
        meta, section,
        lambda span: attend_backward(span, rows, qkv_s.at[0], qkv_s.at[1], qkv_s.at[2], dc_s, bias_s, dq_s, dk_s, dv_s),
    )
    loads.wait("da")
    pairs = ((dq_s, dk_s), (dv_s, da_s))
    for core in range(2):
        @pl.when(section == core)
        def _(core=core):
            for place in range(2):
                pltpu.make_async_copy(pairs[core][place], home_o.at[place], out_sem.at[place]).start()
                pltpu.make_async_copy(
                    pairs[1 - core][place], away_o.at[place * rows : (place + 1) * rows], out_sem.at[2 + place]
                ).start()
    loads.wait("da1", "wq", "wk", "wv")
    dh_s[...] += rows_times_transposed(dq_s[...], wq_s[...])
    dh_s[...] += rows_times_transposed(dk_s[...], wk_s[...])
    dh_s[...] += rows_times_transposed(dv_s[...], wv_s[...])
    sums_s[...] = jnp.zeros_like(sums_s)

    def finish(part):
        dlow_s[part, :] = dh_s[part, :].astype(BF16)
        return dq_s[part, :].astype(F32), dv_s[part, :].astype(F32)

    over_chunks_with_sums(rows, finish, sums_s)
    last = [
        pltpu.make_async_copy(dh_s, dh_o, out_sem.at[4]),
        pltpu.make_async_copy(dlow_s, dlow_o, out_sem.at[5]),
    ]
    for copy in last:
        copy.start()
    small_o[0:6, :] = small_one[0:6, :]
    for index in range(2):
        small_o[6 + index : 7 + index, :] = jnp.sum(sums_s[index], axis=0, keepdims=True)
    small_o[8:16, :] = small_one[8:16, :]
    low_s[...] = small_o[...].astype(BF16)
    smalls = pltpu.make_async_copy(low_s, away_o.at[2 * rows : 2 * rows + SMALL_ROWS], out_sem.at[6])
    smalls.start()
    for place in range(2):
        pltpu.make_async_copy(pairs[0][place], home_o.at[place], out_sem.at[place]).wait()
        pltpu.make_async_copy(
            pairs[1][place], away_o.at[place * rows : (place + 1) * rows], out_sem.at[2 + place]
        ).wait()
    for copy in last:
        copy.wait()
    smalls.wait()


def attend_gradient(layer, meta, own, own_x, dc, da, da1, weights, others, small_one):
    rows, width = da1.shape
    flat = (rows, width)
    square = (width, width)
    return run_kernel(
        functools.partial(attend_kernel, layer),
        (S(flat, F32), S(flat, BF16), S((2,) + flat, BF16), S((2 * rows + SMALL_ROWS, width), BF16), S((SMALL_ROWS, width), F32)),
        [ANY] * 4 + [VM], [SM] * 3 + [ANY] * 11 + [VM],
        [V((3,) + flat, BF16), V(flat, BF16), V(flat, BF16), V(flat, F32), V(flat, BF16)] + [V(square, BF16)] * 3 + [V(flat, BF16)] * 3
        + [V((rows, 3 * BUCKET), F32), V((2, 8, width), F32), V((SMALL_ROWS, width), BF16)],
        7, 7, 6 * rows * width * width, 15_000_000, "attend_gradient",
    )(*meta, own, own_x, dc, da, da1, *weights[:3], *others[:3], small_one)


def by_owner(loads, name, own, other, target):
    rows = target.shape[0] // 2
    section = lax.axis_index("section")
    loads.start((name, 0), own, target.at[pl.ds(pl.multiple_of(section * rows, rows), rows)])
    loads.start((name, 1), other, target.at[pl.ds(pl.multiple_of((1 - section) * rows, rows), rows)])


def both_micros(layer, loads, name, own, other, plane, target, index):
    width = own.shape[3]
    rows = target.shape[0] // 2
    columns = target if target.shape[1] == width else target.at[:, index * width : (index + 1) * width]
    if layer == 1:
        by_owner(loads, (name, index), own.at[0, plane + index], other.at[0, plane + index], columns)
        return
    for micro in range(2):
        part = columns.at[micro * rows : (micro + 1) * rows]
        take_other = lax.axis_index("section") == 1
        loads.start(((name, index), micro), own.at[micro, plane + index], part, other.at[micro, plane + index], take_other)


def wait_both(loads, name, index):
    loads.wait(((name, index), 0), ((name, index), 1))


def put_rows(target, near_first, value, at_row, at_lane, dest):
    spot = 0 if target.shape[0] == 1 else spot_of(near_first, dest)
    rows, lanes = value.shape
    target[spot, at_row : at_row + rows, at_lane : at_lane + lanes] = value.astype(BF16)


def feed_weights_kernel(
    layer, near_first, shared, shared_x, dz, df, away_x,
    outer_o, inner_o, keep_o,
    u_s, ml_s, dz_s, df_s, w_s, in_sem, out_sem,
):
    hidden = u_s.shape[1]
    width = ml_s.shape[1]
    rows = dz.shape[0]
    spots = w_s.shape[0]
    loads = Loads(in_sem)
    store = Stores(out_sem)
    by_owner(loads, "dz", dz, away_x.at[2, :, 0 : width // 2], dz_s)

    def begin_u(index):
        both_micros(layer, loads, "u", shared, shared_x, ACTIVE, u_s, index)

    def begin_inner():
        both_micros(layer, loads, "ml", shared, shared_x, MIDDLE, ml_s, 0)
        for index in range(2):
            columns = slice(index * width, (index + 1) * width)
            by_owner(loads, ("df", index), df.at[:, columns], away_x.at[index], df_s.at[:, columns])

    planes = hidden // width
    begin_u(0)
    begin_u(1)
    loads.wait(("dz", 0), ("dz", 1))
    half_rows = hidden // spots // 2
    split = spots // 2
    for index in range(planes):
        wait_both(loads, "u", index)
        if index + 2 < planes:
            begin_u(index + 2)
        elif index + 2 == planes:
            begin_inner()
        product = transposed_times(u_s[:, index * width : (index + 1) * width], dz_s[...])
        block = min(half_rows, width)
        for inner in range(width // block):
            row = index * width + inner * block
            dest, offset = divmod(row, 2 * half_rows)
            side, at_row = divmod(offset, half_rows)
            put_rows(w_s, near_first, product[inner * block : (inner + 1) * block, :], at_row, side * (width // 2), dest)
    store.start(w_s.at[split:spots, 0:half_rows], outer_o)
    store.start(w_s.at[0 : spots - split, 0:half_rows], keep_o.at[:, 0:half_rows])
    wait_both(loads, "ml", 0)
    height = width // spots
    for side in range(2):
        wait_both(loads, "df", side)
        product = transposed_times(ml_s[...], df_s[:, side * width : (side + 1) * width])
        for dest in range(spots):
            put_rows(w_s, near_first, product[dest * height : (dest + 1) * height, :], half_rows + side * height, 0, dest)
    rest = slice(half_rows, half_rows + 2 * height)
    store.start(w_s.at[split:spots, rest], inner_o)
    store.start(w_s.at[0 : spots - split, rest], keep_o.at[:, rest])
    store.wait()


def unit_outs(spots, rows, width):
    half = S((max(spots // 2, 1), rows, width), BF16)
    return half, half


def feed_weights(layer, near_first, spots, shared, shared_x, dz, df, away_x):
    rows, width = shared.shape[2:]
    hidden = 2 * df.shape[1]
    total = hidden // spots // 2 + 2 * (width // spots)
    split = spots - spots // 2
    outs = (
        S((split, hidden // spots // 2, width), BF16), S((split, 2 * (width // spots), width), BF16), S((split, total, width), BF16),
    )
    return run_kernel(
        functools.partial(feed_weights_kernel, layer, near_first), outs, [ANY] * 3, [ANY] * 5,
        [
            V((2 * rows, hidden), BF16), V((2 * rows, width), BF16), V((2 * rows, width // 2), BF16), V((2 * rows, hidden // 2), BF16),
            V((spots, total, width), BF16),
        ],
        8 + 2 * (hidden // width), 4, 4 * rows * width * hidden, 18_000_000, "feed_weights",
    )(shared, shared_x, dz, df, away_x)


def attend_weights_kernel(
    layer, near_first, h, h_x, shared, shared_x, grads, away_x, small,
    send_o, keep_o,
    left_s, right_s, w_s, small_s, in_sem, out_sem,
):
    section = lax.axis_index("section")
    second = section == 1
    rows, width = grads.shape[1:]
    spots = w_s.shape[0]
    loads = Loads(in_sem)
    store = Stores(out_sem)
    for micro in range(2):
        part = slice(micro * rows, (micro + 1) * rows)
        loads.start(("h", micro), h.at[micro], left_s.at[0, part], h_x.at[micro], second)
    by_owner(loads, "g", grads.at[0], away_x.at[0:rows], right_s.at[0])
    if layer == 0:
        for micro in range(2):
            part = slice(micro * rows, (micro + 1) * rows)
            loads.start(("c", micro), h.at[micro], left_s.at[1, part], shared_x.at[micro, CONTEXT], second)
    else:
        for place, (plain, context) in enumerate(((h, shared), (h, shared_x))):
            micro = section if place == 0 else 1 - section
            part = left_s.at[1, pl.ds(pl.multiple_of(micro * rows, rows), rows)]
            loads.start(("c", place), plain.at[micro], part, context.at[0, CONTEXT], second)
    by_owner(loads, "f", grads.at[1], away_x.at[rows : 2 * rows], right_s.at[1])
    height = width // spots
    loads.start("small", away_x.at[2 * rows : 2 * rows + SMALL_ROWS], small_s)
    loads.wait("small")
    low = (small[...] + small_s[...].astype(F32)).astype(BF16)
    for spot in range(spots):
        w_s[spot, 2 * height : 2 * height + SMALL_ROWS, :] = low
    for side, name in enumerate(("h", "c")):
        grad_name = ("g", "f")[side]
        loads.wait((name, 0), (name, 1), (grad_name, 0), (grad_name, 1))
        product = transposed_times(left_s[side], right_s[side])
        for dest in range(spots):
            put_rows(w_s, near_first, product[dest * height : (dest + 1) * height, :], side * height, 0, dest)
    split = spots // 2
    if spots > 1:
        store.start(w_s.at[split:spots], send_o)
        store.start(w_s.at[0:split], keep_o)
    else:
        store.start(w_s, send_o)
        store.start(w_s, keep_o)
    store.wait()


def attend_weights(layer, near_first, spots, h, h_x, shared, shared_x, grads, away_x, small):
    rows, width = grads.shape[1:]
    total = 2 * (width // spots) + SMALL_ROWS
    return run_kernel(
        functools.partial(attend_weights_kernel, layer, near_first), unit_outs(spots, total, width), [ANY] * 2, [ANY] * 6 + [VM],
        [V((2, 2 * rows, width), BF16), V((2, 2 * rows, width), BF16), V((spots, total, width), BF16), V((SMALL_ROWS, width), BF16)],
        9, 2, 8 * rows * width * width, 10_000_000, "attend_weights",
    )(h, h_x, shared, shared_x, grads, away_x, small)


def add_kernel(shapes, pieces, *refs):
    count = len(shapes)
    keeps, refs = (refs[0:count], refs[count:])
    parts, refs = (refs[0 : sum(pieces)], refs[sum(pieces) :])
    *rest, in_sem, out_sem = refs
    out_count = sum(1 if spots == 1 else 2 for spots, _, _ in shapes)
    outs, holds = (list(rest[:out_count]), list(rest[out_count:]))
    keep_s, part_s, total_s = (holds[0:count], holds[count : 2 * count], holds[2 * count :])
    loads = Loads(in_sem)
    store = Stores(out_sem)
    at = 0
    waits = []
    for index in range(count):
        loads.start(("keep", index), keeps[index], keep_s[index])
        names = [("keep", index)]
        row = 0
        for piece in range(pieces[index]):
            height = parts[at].shape[1]
            loads.start(("part", index, piece), parts[at], part_s[index].at[:, row : row + height])
            names.append(("part", index, piece))
            row += height
            at += 1
        waits.append(names)
    place = 0
    for index, (spots, rows, _) in enumerate(shapes):
        loads.wait(*waits[index])
        if spots == 1:
            total_s[index][...] = keep_s[index][0].astype(F32) + part_s[index][0].astype(F32)
            store.start(total_s[index], outs[place])
            place += 1
            continue

        def one(spot, carry, index=index):
            total_s[index][spot] = (keep_s[index][spot].astype(F32) + part_s[index][spot].astype(F32)).astype(BF16)
            return carry

        lax.fori_loop(0, spots, one, 0)
        store.start(total_s[index].at[spots // 2 : spots], outs[place])
        store.start(total_s[index].at[0 : spots // 2], outs[place + 1])
        place += 2
    store.wait()


def add_arrived(pairs):
    shapes = [keep.shape for keep, _ in pairs]
    pieces = [len(arrived) for _, arrived in pairs]
    outs = []
    totals = []
    for spots, rows, width in shapes:
        if spots > 1:
            outs.extend([S((spots // 2, rows, width), BF16)] * 2)
            totals.append(V((spots, rows, width), BF16))
        else:
            outs.append(S((rows, width), F32))
            totals.append(V((rows, width), F32))
    count = len(pairs) + sum(pieces)
    results = list(
        pl.pallas_call(
            functools.partial(add_kernel, shapes, pieces),
            out_shape=tuple(outs),
            in_specs=[ANY] * count,
            out_specs=(ANY,) * len(outs),
            scratch_shapes=[V(shape, BF16) for shape in shapes] * 2 + totals
            + [pltpu.SemaphoreType.DMA((count,)), pltpu.SemaphoreType.DMA((len(outs),))],
            compiler_params=pltpu.CompilerParams(vmem_limit_bytes=ADD_LIMIT),
            cost_estimate=pl.CostEstimate(flops=1000, bytes_accessed=1000, transcendentals=0),
            name="add_arrived",
        )(*[keep for keep, _ in pairs], *[part for _, arrived in pairs for part in arrived])
    )
    return [(results.pop(0),) if spots == 1 else (results.pop(0), results.pop(0)) for spots, _, _ in shapes]


ADD_LIMIT = 24_000 * 1024


def finish_kernel(feed_one, feed_two, tail_one, tail_two, feed_one_x, feed_two_x, tail_one_x, tail_two_x, q_o, k_o, v_o, m_o, i_o, o_o, small_o, wide_o):
    section = lax.axis_index("section")
    groups = lax.axis_size("dp")
    me = lax.axis_index("dp")
    height, width = q_o.shape
    half_rows = o_o.shape[0] // 2
    hidden = i_o.shape[1]
    for core in range(2):
        @pl.when(section == core)
        def _(core=core):
            mine, back = ((feed_one, tail_one), (feed_one_x, tail_one_x)) if core == 0 else ((feed_two, tail_two), (feed_two_x, tail_two_x))
            sides = (mine, back) if core == 0 else (back, mine)
            half = width // 2
            for side, (feed, _) in enumerate(sides):
                for part in range(2):
                    o_o[part * half_rows : (part + 1) * half_rows, side * half : (side + 1) * half] = feed[
                        0:half_rows, part * half : (part + 1) * half
                    ]
                    i_o[:, (2 * side + part) * width : (2 * side + part + 1) * width] = feed[
                        half_rows + part * height : half_rows + (part + 1) * height, :
                    ]
            q_o[...] = sides[0][1][0:height, :]
            k_o[...] = sides[0][1][height : 2 * height, :]
            v_o[...] = sides[1][1][0:height, :]
            m_o[...] = sides[1][1][height : 2 * height, :]
            lines = mine[1][2 * height : 2 * height + SMALL_ROWS, :]
            small_o[...] = pltpu.roll(lines[0:8, :], lax.rem(width - me * height, width), 1)
            span = hidden // groups
            each = width // span
            pick = lax.broadcasted_iota(jnp.int32, (8, width), 0) == lax.div(me, each)
            chosen = jnp.sum(jnp.where(pick, lines[8:16, :], 0.0), axis=0, keepdims=True)
            wide_o[...] = pltpu.roll(jnp.broadcast_to(chosen, (8, width)), lax.rem(width - lax.rem(me, each) * span, width), 1)


def finish(groups, width, hidden, results):
    height = width // groups
    square = S((height, width), F32)
    return pl.pallas_call(
        finish_kernel,
        out_shape=(square, square, square, square, S((height, hidden), F32), S((hidden // groups, width), F32), S((8, width), F32), S((8, width), F32)),
        in_specs=[VM] * 8,
        out_specs=(VM,) * 8,
        compiler_params=pltpu.CompilerParams(vmem_limit_bytes=ADD_LIMIT),
        name="finish_gradients",
    )(*results)


def exchange(value, bits):
    groups = lax.axis_size("dp")
    pairs = [(2 * group + core, 2 * (group ^ (1 << bits[core])) + core) for group in range(groups) for core in range(2)]
    return lax.ppermute(value, ("dp", "section"), pairs)


def swap(value):
    return lax.ppermute(value, "section", [(0, 1), (1, 0)])


F1, T1, F0, T0 = (("f", 1), ("t", 1), ("f", 0), ("t", 0))
NEAR_FIRST = {F1: False, T1: False, F0: False, T0: False}
SCHEDULE = (
    (),
    (),
    (),
    (F1,),
    (F1,),
    (F1,),
    (F1, T1),
    (F1, T1, F0),
    (F0, T1),
    (F0, T1, T0),
    (F0, T0),
    (F0, T0),
    (T0,),
)


def per_device(
    tokens, cotangent, bucket, batch_size, lengths, query_weight, query_offset, keys_weight, value_weight, value_offset,
    mixer_weight, mixer_offset, first_gain, first_shift, inner_weight, inner_offset, outer_weight, outer_offset,
    second_gain, second_shift,
):
    section = lax.axis_index("section")
    groups = lax.axis_size("dp")
    width = tokens.shape[2]
    hidden = inner_offset.shape[1]
    hypercube = groups == 16
    spots = groups if hypercube else 1
    first = section == 0
    meta = (bucket, batch_size, lengths)
    weights = (query_weight, keys_weight, value_weight, mixer_weight, inner_weight, outer_weight)
    vectors = (query_offset, value_offset, mixer_offset, first_gain, first_shift, outer_offset, second_gain, second_shift)
    others = tuple(swap(weight) for index, weight in enumerate(weights) if index != 3)
    y_first, shared_first, own_first, own_handed, packed, vec_own = first_forward(meta, tokens, weights, vectors, inner_offset)
    handed, packed, others = lax.optimization_barrier((y_first, packed, others))
    y_x = swap(handed)
    others = others + (swap(packed),)
    y_second, shared_second, own_second = second_forward(meta, y_first, y_x, weights, others, vec_own)
    shared_x = swap(lax.optimization_barrier((shared_first, y_x, others[-1]))[0])
    own_second, shared_x = lax.optimization_barrier((own_second, shared_x))
    own = {1: (own_second, own_second)}
    shared = {0: (shared_first, shared_x), 1: (shared_second, swap(shared_second))}
    entries = {1: (y_first, y_x), 0: (tokens, tokens)}
    y_last_x = swap(y_second)
    moving = {}
    results = {}

    def boundary(turn, value, other):
        names = SCHEDULE[turn] if hypercube else ()
        if not names:
            return value, other
        landed = {name: moving[name][1] for name in names}
        other, landed = lax.optimization_barrier((other, landed))
        ready = []
        for name in names:
            keep, _, waiting, arrived, step = moving[name]
            arrived = arrived + [landed[name]]
            if waiting:
                moving[name] = (keep, None, waiting[1:], arrived, step)
                ready.append(name)
            else:
                moving[name] = (keep, None, [], arrived, step + 1)
        done = [name for name in names if name not in ready]
        if done:
            added = add_arrived([(moving[name][0], moving[name][3]) for name in done])
            value, added = lax.optimization_barrier((value, added))
            for name, parts in zip(done, added):
                step = moving[name][4]
                if len(parts) == 1:
                    results[name] = parts[0]
                else:
                    moving[name] = (parts[1], exchange(parts[0], step_bits(NEAR_FIRST[name])[step]), [], [], step)
        else:
            value = lax.optimization_barrier((value, landed))[0]
        for name in ready:
            keep, _, waiting, arrived, step = moving[name]
            piece = pieces[name].pop(0)
            piece = lax.optimization_barrier((piece, landed, value))[0]
            moving[name] = (keep, exchange(piece, step_bits(NEAR_FIRST[name])[0]), waiting, arrived, step)
        return value, other

    pieces = {}

    def begin(name, sends, keep):
        if hypercube:
            pieces[name] = list(sends[1:])
            moving[name] = (keep, exchange(sends[0], step_bits(NEAR_FIRST[name])[0]), list(sends[1:]), [], 0)
        else:
            moving[name] = sends

    def feed(layer, grad):
        return feed_gradient(layer, meta, grad, *own[layer], weights, others, vec_own)

    def feed_sum(layer, dz, df, away_x):
        *sends, keep = feed_weights(layer, False, spots, *shared[layer], dz, df, away_x)
        begin(F1 if layer else F0, sends, keep)
        return keep

    def attend(layer, dc, da, da1, small):
        return attend_gradient(layer, meta, *own[layer], dc, da, da1, weights, others, small)

    def attend_sum(layer, grads, away_x, small):
        send, keep = attend_weights(layer, False, spots, *entries[layer], *shared[layer], grads, away_x, small)
        begin(T1 if layer else T0, [send], keep)
        return keep

    def tie(value, other):
        return lax.optimization_barrier((value, other))[0]

    dh = {}
    low_gradient = {}
    dz, df, away, da1, da, dc, small_feed = feed(1, cotangent)
    held = feed_sum(1, dz, df, swap(away))
    own[0] = (own_first, swap(tie(own_handed, held)))
    dh[1], low_gradient[1], grads, away, small = attend(1, tie(dc, held), da, da1, small_feed)
    attend_away_x = swap(away)
    grad, _ = boundary(3, low_gradient[1], held)
    dz, df, away, da1, da, dc, small_feed = feed(0, grad)
    grads, away = boundary(4, tie(grads, dz), away)
    feed_away_x = swap(away)
    held = attend_sum(1, grads, attend_away_x, small)
    dz, _ = boundary(5, tie(dz, held), held)
    held = feed_sum(0, dz, df, feed_away_x)
    dc, _ = boundary(6, tie(dc, held), held)
    dh[0], low_gradient[0], grads, away, small = attend(0, dc, da, da1, small_feed)
    grads, away = boundary(7, grads, away)
    held = attend_sum(0, grads, swap(away), small)
    dh_x = swap(jnp.where(first, low_gradient[1], low_gradient[0])).astype(F32)
    layer_out = jnp.stack([jnp.where(first, y_first[0], y_last_x[0]), jnp.where(first, y_first[1], y_second[0])])
    input_grad = jnp.stack([jnp.where(first, dh[0], dh_x), jnp.where(first, dh_x, dh[1])])
    if hypercube:
        for turn in range(8, len(SCHEDULE)):
            (layer_out, input_grad), held = boundary(turn, (layer_out, input_grad), held)
        order = (F0, F1, T0, T1)
        done = finish(groups, width, hidden, [results[name] for name in order] + [swap(results[name]) for name in order])
        query_grad, keys_grad, value_grad, mixer_grad, inner_grad, outer_grad, lines, wide_line = done
        height = width // groups
        small = [lines[index, :height] for index in range(8)]
        small_wide = wide_line[0, : hidden // groups]
    else:
        def scatter(value):
            return lax.psum_scatter(value, "dp", scatter_dimension=0, tiled=True).astype(F32)

        found = []
        for layer in (1, 0):
            outer_part, inner_part = (value[0] for value in moving["f", layer])
            attend = moving["t", layer][0][0]
            half = width // 2
            outer_half = jnp.concatenate([outer_part[:, :half], outer_part[:, half:]], axis=0)
            parts = [scatter(outer_half), scatter(inner_part[:width]), scatter(inner_part[width:])]
            parts += [scatter(attend[:width]), scatter(attend[width : 2 * width])]
            lines = attend[2 * width :].astype(F32)
            parts += [scatter(lines[index]) for index in range(8)] + [scatter(lines[8:12].reshape(-1))]
            found.append(parts)
        mine = [jnp.where(first, b, a) for a, b in zip(*found)]
        back = [swap(jnp.where(first, a, b)) for a, b in zip(found[0][:5], found[1][:5])]
        low = [jnp.where(first, a, b) for a, b in zip(mine, back)]
        high = [jnp.where(first, b, a) for a, b in zip(mine, back)]
        outer_grad = jnp.concatenate([low[0], high[0]], axis=1)
        inner_grad = jnp.concatenate([low[1], low[2], high[1], high[2]], axis=1)
        query_grad, keys_grad, value_grad, mixer_grad = (low[3], low[4], high[3], high[4])
        small, small_wide = (mine[5:13], mine[13])
    second_gain_grad, second_shift_grad, outer_offset_grad, first_gain_grad, first_shift_grad, mixer_offset_grad = small[:6]
    outputs = (
        layer_out, input_grad, query_grad, small[6], keys_grad, value_grad, small[7], mixer_grad, mixer_offset_grad,
        first_gain_grad, first_shift_grad, inner_grad, small_wide, outer_grad, outer_offset_grad, second_gain_grad,
        second_shift_grad,
    )
    return tuple(piece[None] for piece in outputs)


def solution(mesh):
    matrix = P("section", None, None)
    vector = P("section", None)
    in_specs = (
        P("dp", None, None), P("dp", None, None), P("dp"), P("dp"), P("dp", None), matrix, vector, matrix, matrix, vector,
        matrix, vector, vector, vector, matrix, vector, matrix, vector, vector, vector,
    )
    rows = P("section", "dp", None, None)
    grad = P("section", "dp", None)
    small = P("section", "dp")
    out_specs = (rows, rows, grad, small, grad, grad, small, grad, small, small, small, grad, small, grad, small, small, small)
    return jax.shard_map(per_device, mesh=mesh, in_specs=in_specs, out_specs=out_specs, check_vma=False)
```

```python
import functools
import jax
import jax.numpy as jnp
from jax import lax
from jax.experimental import pallas as pl
from jax.experimental.pallas import tpu as pltpu
from jax.sharding import PartitionSpec as P

HEADS = 12
HEAD_DIM = 64
BUCKET = 64
PAIR = 2 * HEAD_DIM
masked_score = -1000000000.0
norm_epsilon = 1e-06
F32 = jnp.float32
BF16 = jnp.bfloat16
CHUNK = 16
FFN_TILE = 512
ATT_UNROLL = 3


def rows_times(left, right):
    return lax.dot_general(left, right, (((1,), (0,)), ((), ())), preferred_element_type=F32)


def rows_times_transposed(left, right):
    return lax.dot_general(left, right, (((1,), (1,)), ((), ())), preferred_element_type=F32)


def transposed_times(left, right):
    return lax.dot_general(left, right, (((0,), (0,)), ((), ())), preferred_element_type=F32)


def slot_facts(block, span_rows, place, meta, micro):
    bucket_ref, count_ref, lengths_ref = meta
    bucket = bucket_ref[micro]
    count = count_ref[micro]

    def length_of(slot):
        return jnp.where(slot < count, lengths_ref[micro, slot], 0)

    if span_rows == 2 * BUCKET:
        return (jnp.full_like(place, block), place, jnp.full_like(place, length_of(block)))
    short = bucket == 0
    first = 3 * block
    slot_short = first + place // BUCKET
    length_short = jnp.where(
        place < BUCKET,
        length_of(first),
        jnp.where(place < 2 * BUCKET, length_of(first + 1), length_of(first + 2)),
    )
    slot = jnp.where(short, slot_short, block)
    inner = jnp.where(short, place % BUCKET, place)
    length = jnp.where(short, length_short, length_of(block))
    return (slot, inner, length)


def fill_masks(span_rows, row_count, meta, micro, bias_ref, valid_ref, keys_down=False):
    for block in range(row_count // span_rows):
        row_place = lax.broadcasted_iota(jnp.int32, (span_rows, 1), 0)
        row_slot, row_inner, row_length = slot_facts(block, span_rows, row_place, meta, micro)
        rows = slice(block * span_rows, (block + 1) * span_rows)
        if bias_ref is not None:
            other_place = lax.broadcasted_iota(jnp.int32, (1, span_rows), 1)
            other_slot, other_inner, other_length = slot_facts(block, span_rows, other_place, meta, micro)
            if keys_down:
                allowed = other_slot == jnp.where(row_inner < row_length, row_slot, -1)
            else:
                allowed = row_slot == jnp.where(other_inner < other_length, other_slot, -1)
            allowed = allowed | (row_place == other_place)
            bias_ref[rows, 0:span_rows] = jnp.where(allowed, 0.0, masked_score)
        if valid_ref is not None:
            valid_ref[rows, :] = jnp.where(row_inner < row_length, 1.0, 0.0)


def by_span(meta, micro, body):
    even = meta[0][micro] == 1

    @pl.when(even)
    def _():
        body(2 * BUCKET)

    @pl.when(jnp.logical_not(even))
    def _():
        body(3 * BUCKET)


def attend_forward(span_rows, row_count, q_ref, k_ref, v_ref, bias_ref, c_ref):
    blocks = row_count // span_rows

    def one_pair(pair, carry):
        columns = pl.ds(pl.multiple_of(pair * PAIR, PAIR), PAIR)
        lane = lax.broadcasted_iota(jnp.int32, (span_rows, PAIR), 1)
        first_half = lane < HEAD_DIM
        weights = []
        for block in range(blocks):
            rows = slice(block * span_rows, (block + 1) * span_rows)
            query = q_ref[rows, columns] * jnp.asarray(HEAD_DIM ** (-0.5), BF16)
            keys = k_ref[rows, columns]
            zero = jnp.zeros_like(keys)
            bias = bias_ref[rows, 0:span_rows]
            for mine in (first_half, jnp.logical_not(first_half)):
                scores = rows_times_transposed(query, jnp.where(mine, keys, zero)) + bias
                top = jnp.max(scores, axis=-1, keepdims=True)
                weights.append(jnp.exp(scores - top).astype(BF16))
        for block in range(blocks):
            rows = slice(block * span_rows, (block + 1) * span_rows)
            value = v_ref[rows, columns]
            one = jnp.ones_like(value)
            left = rows_times(weights[2 * block], jnp.where(first_half, value, one))
            right = rows_times(weights[2 * block + 1], jnp.where(first_half, one, value))
            above = jnp.where(first_half, left, right)
            below = pltpu.roll(jnp.where(first_half, right, left), HEAD_DIM, 1)
            c_ref[rows, columns] = (above / below).astype(BF16)
        return carry

    lax.fori_loop(0, HEADS // 2, one_pair, 0, unroll=ATT_UNROLL)


def row_moments(values):
    center = jnp.mean(values, axis=-1, keepdims=True)
    centred = values - center
    spread = jnp.mean(centred * centred, axis=-1, keepdims=True)
    return centred, lax.rsqrt(spread + norm_epsilon)


def over_chunks(row_count, body, rows=CHUNK, group=6):
    def step(index, carry):
        for inner in range(group):
            start = pl.multiple_of(index * (rows * group) + inner * rows, rows)
            body(pl.ds(start, rows))
        return carry

    lax.fori_loop(0, row_count // (rows * group), step, 0)


def over_chunks_with_sums(row_count, body, sums_ref, rows=CHUNK, group=6):
    def step(index, carry):
        total = None
        for inner in range(group):
            start = pl.multiple_of(index * (rows * group) + inner * rows, rows)
            terms = [fold_rows(term) for term in body(pl.ds(start, rows))]
            total = terms if total is None else [a + b for a, b in zip(total, terms)]
        for place, term in enumerate(total):
            sums_ref[place] += term
        return carry

    lax.fori_loop(0, row_count // (rows * group), step, 0)


def fold_rows(values):
    return jnp.sum(values.reshape(values.shape[0] // 8, 8, values.shape[1]), axis=0)


def gelu_with_slope(values):
    cumulative = 0.5 + 0.5 * lax.erf(values * (0.5 ** 0.5))
    density = jnp.exp(values * values * -0.5) * 0.3989422804014327
    return values * cumulative, cumulative + values * density


ANY = pl.BlockSpec(memory_space=pl.ANY)
VM = pl.BlockSpec(memory_space=pltpu.VMEM)
SM = pl.BlockSpec(memory_space=pltpu.SMEM)
VMEM_LIMIT = 63_000 * 1024
S = jax.ShapeDtypeStruct
V = pltpu.VMEM
B_QUERY, B_VALUE, B_MIXER, GAIN_ONE, SHIFT_ONE, B_OUTER, GAIN_TWO, SHIFT_TWO = range(8)
QUERY, FIRST_SUM, SECOND_SUM, SLOPE = (0, 3, 4, 5)
ACTIVE, MIDDLE, CONTEXT = (0, 4, 5)
X_BIT, Y_BIT, NEAR_BIT, FAR_BIT = (0, 1, 2, 3)
SMALL_ROWS = 16


class Loads:
    def __init__(self, semaphores):
        self.semaphores = semaphores
        self.copies = {}

    def start(self, name, source, target, other=None, take_other=None):
        semaphore = self.semaphores.at[len(self.copies)]
        copy = pltpu.make_async_copy(source, target, semaphore)
        self.copies[name] = copy
        if other is None:
            copy.start()
            return
        second = pltpu.make_async_copy(other, target, semaphore)

        @pl.when(take_other)
        def _():
            second.start()

        @pl.when(jnp.logical_not(take_other))
        def _():
            copy.start()

    def wait(self, *names):
        for name in names:
            self.copies[name].wait()


class Stores:
    def __init__(self, semaphores):
        self.semaphores = semaphores
        self.copies = []

    def start(self, source, target):
        copy = pltpu.make_async_copy(source, target, self.semaphores.at[len(self.copies)])
        copy.start()
        self.copies.append(copy)

    def wait(self):
        for copy in self.copies:
            copy.wait()


def run_kernel(kernel, outs, out_specs, in_specs, scratch, loads, stores, flops, bytes_moved, name):
    return pl.pallas_call(
        kernel,
        out_shape=outs,
        in_specs=in_specs,
        out_specs=out_specs,
        scratch_shapes=list(scratch) + [pltpu.SemaphoreType.DMA((loads,)), pltpu.SemaphoreType.DMA((stores,))],
        compiler_params=pltpu.CompilerParams(vmem_limit_bytes=VMEM_LIMIT),
        cost_estimate=pl.CostEstimate(flops=1000, bytes_accessed=1000, transcendentals=0),
        name=name,
    )


def spot_of(near_first, dest):
    relative = jnp.bitwise_xor(dest, lax.axis_index("dp"))

    def bit(index):
        return jnp.bitwise_and(lax.shift_right_logical(relative, index), 1)

    first = lax.axis_index("section") == 0
    lead = jnp.where(first, bit(X_BIT), bit(Y_BIT))
    follow = jnp.where(first, bit(Y_BIT), bit(X_BIT))
    if near_first:
        return bit(NEAR_BIT) * 8 + lead * 4 + follow * 2 + bit(FAR_BIT)
    return lead * 8 + follow * 4 + bit(NEAR_BIT) * 2 + bit(FAR_BIT)


def step_bits(near_first):
    cross = [(X_BIT, Y_BIT), (Y_BIT, X_BIT)]
    if near_first:
        return [(NEAR_BIT, NEAR_BIT)] + cross + [(FAR_BIT, FAR_BIT)]
    return cross + [(NEAR_BIT, NEAR_BIT), (FAR_BIT, FAR_BIT)]


def forward_matrix_loads(loads, hidden_start, weights, others, take_other, targets):
    names = ("wq", "wk", "wv", "wm", "wi", "wo")

    def begin(index):
        other = None if others is None else others[index]
        loads.start(names[index], weights[index].at[0], targets[index], other, take_other)

    def load(step):
        if step == 0:
            hidden_start()
            for index in range(3):
                begin(index)
            return
        if step == 1:
            loads.wait("h")
        loads.wait(names[step - 1])
        if step <= 3:
            begin(step + 2)

    return load


def forward_body(load, store, meta, micros, vec, outs, refs):
    h_s, wq_s, wk_s, wv_s, wm_s, wi_s, wo_s, qkv_s, c_s, ml_s, a1_s, a2_s, u_s, gp_s, y_s, m_s, f0_s, e0_s, e1_s, bias_s, valid_s, bi_s = refs
    y_o, own_o, shared_o = outs
    rows, width = h_s.shape
    hidden = wi_s.shape[1]
    each = rows // len(micros)
    parts = [slice(place * each, (place + 1) * each) for place in range(len(micros))]

    def send(source, plane, shared=False):
        for place, part in enumerate(parts):
            target = shared_o.at[place] if shared else own_o[place]
            for index in range(source.shape[1] // width):
                store.start(source.at[part, index * width : (index + 1) * width], target.at[plane + index])

    load(0)
    for part, micro in zip(parts, micros):
        by_span(meta, micro, lambda span: fill_masks(span, each, meta, micro, bias_s.at[part], valid_s.at[part]))
    load(1)
    qkv_s[0] = (rows_times(h_s[...], wq_s[...]) + vec(B_QUERY)).astype(BF16)
    load(2)
    qkv_s[1] = rows_times(h_s[...], wk_s[...]).astype(BF16)
    load(3)
    qkv_s[2] = (rows_times(h_s[...], wv_s[...]) + vec(B_VALUE)).astype(BF16)
    for place, part in enumerate(parts):
        store.start(qkv_s.at[:, part], own_o[place].at[QUERY : QUERY + 3])
    for part, micro in zip(parts, micros):
        by_span(
            meta, micro,
            lambda span: attend_forward(
                span, each, qkv_s.at[0, part], qkv_s.at[1, part], qkv_s.at[2, part], bias_s.at[part], c_s.at[part]
            ),
        )
    send(c_s, CONTEXT, True)
    load(4)
    f0_s[...] = rows_times(c_s[...], wm_s[...])
    offset_mixer, gain_one, shift_one = (vec(B_MIXER), vec(GAIN_ONE), vec(SHIFT_ONE))

    def first_norm(part):
        total = h_s[part, :].astype(F32) + (f0_s[part, :] + offset_mixer)
        a1_s[part, :] = total.astype(BF16)
        centred, scale = row_moments(total)
        middle = centred * scale * gain_one + shift_one
        m_s[part, :] = middle
        ml_s[part, :] = middle.astype(BF16)

    over_chunks(rows, first_norm)
    send(a1_s, FIRST_SUM)
    send(ml_s, MIDDLE, True)
    load(5)
    tile = FFN_TILE
    tiles = hidden // tile

    def project(buffer, which):
        columns = pl.ds(pl.multiple_of(which * tile, tile), tile)
        buffer[...] = rows_times(ml_s[...], wi_s[:, columns])

    def activate(buffer, which):
        columns = pl.ds(pl.multiple_of(which * tile, tile), tile)
        offset = bi_s[0:1, columns]
        for start in range(0, rows, 32):
            part = slice(start, start + 32)
            value, slope = gelu_with_slope(buffer[part, :] + offset)
            u_s[part, columns] = value.astype(BF16)
            gp_s[part, columns] = slope.astype(BF16)

    for index in range(hidden // width):
        bi_s[0:1, index * width : (index + 1) * width] = vec(8 + index)
    project(e0_s, 0)

    def two_tiles(index, carry):
        project(e1_s, 2 * index + 1)
        activate(e0_s, 2 * index)
        project(e0_s, jnp.minimum(2 * index + 2, tiles - 1))
        activate(e1_s, 2 * index + 1)
        return carry

    lax.fori_loop(0, tiles // 2, two_tiles, 0)
    send(u_s, ACTIVE, True)
    send(gp_s, SLOPE)
    load(6)
    f0_s[...] = rows_times(u_s[...], wo_s[...])
    offset_outer, gain_two, shift_two = (vec(B_OUTER), vec(GAIN_TWO), vec(SHIFT_TWO))

    def second_norm(part):
        total = m_s[part, :] + (f0_s[part, :] + offset_outer)
        a2_s[part, :] = total.astype(BF16)
        centred, scale = row_moments(total)
        y_s[part, :] = ((centred * scale * gain_two + shift_two) * valid_s[part, :]).astype(BF16)

    over_chunks(rows, second_norm)
    for place, part in enumerate(parts):
        store.start(y_s.at[part], y_o.at[place])
    send(a2_s, SECOND_SUM)
    store.wait()


def first_forward_kernel(
    micro_count, bucket, count, lengths, tok, wq, wk, wv, wm, wi, wo, bq, bv, bm, g1, s1, bo, g2, s2, bi, *rest
):
    y_o, shared_o = rest[:2]
    own_o = rest[2 : 2 + micro_count]
    packed_o, vec_o = rest[2 + micro_count : 4 + micro_count]
    *refs, hold_s, low_s, pack_sem, in_sem, out_sem = rest[4 + micro_count :]
    h_s, wq_s, wk_s, wv_s, wm_s, wi_s, wo_s = refs[:7]
    width = h_s.shape[1]
    gather = pltpu.make_async_copy(wm.at[0], hold_s, pack_sem.at[0])
    hand = pltpu.make_async_copy(hold_s, packed_o.at[0:width], pack_sem.at[1])
    hand_low = pltpu.make_async_copy(low_s, packed_o.at[width : width + VECTOR_ROWS], pack_sem.at[2])
    vec_o[...] = jnp.zeros_like(vec_o)
    for place, vector in enumerate((bq, bv, bm, g1, s1, bo, g2, s2)):
        vec_o[place : place + 1, :] = vector[...]
    for index in range(bi.shape[1] // width):
        vec_o[8 + index : 9 + index, :] = bi[:, index * width : (index + 1) * width]
    high = vec_o[...].astype(BF16)
    low_s[0:16, :] = high
    low_s[16:32, :] = (vec_o[...] - high.astype(F32)).astype(BF16)
    hand_low.start()

    @pl.when(lax.axis_index("section") != 0)
    def _():
        gather.start()
        gather.wait()
        hand.start()

    @pl.when(lax.axis_index("section") == 0)
    def _():
        loads = Loads(in_sem)
        each = h_s.shape[0] // micro_count

        def hidden_start():
            for micro in range(1, micro_count):
                loads.start(("h", micro), tok.at[micro], h_s.at[micro * each : (micro + 1) * each])
            loads.start("h", tok.at[0], h_s.at[0:each])

        inner_load = forward_matrix_loads(
            loads, hidden_start, (wq, wk, wv, wm, wi, wo), None, None, (wq_s, wk_s, wv_s, wm_s, wi_s, wo_s)
        )

        def load(step):
            if step == 1:
                for micro in range(1, micro_count):
                    loads.wait(("h", micro))
            if step == 4:
                gather.start()
            if step == 6:
                gather.wait()
                hand.start()
            inner_load(step)

        forward_body(
            load, Stores(out_sem), (bucket, count, lengths), tuple(range(micro_count)),
            lambda place: vec_o[place : place + 1, :], (y_o, own_o, shared_o), refs,
        )

    hand.wait()
    hand_low.wait()


def second_forward_kernel(
    bucket, count, lengths, y_own, y_other, wq, wk, wv, wm, wi, wo, xq, xk, xv, xi, xo, packed, vec_own,
    y_o, shared_o, own_o, *scratch
):
    *refs, other_s, vec_s, in_sem, out_sem = scratch
    h_s, wq_s, wk_s, wv_s, wm_s, wi_s, wo_s = refs[:7]
    section = lax.axis_index("section")
    first = section == 0
    width = h_s.shape[1]
    loads = Loads(in_sem)
    load = forward_matrix_loads(
        loads, lambda: loads.start("h", y_other.at[section], h_s, y_own.at[section], first), (wq, wk, wv, wm, wi, wo),
        (xq.at[0], xk.at[0], xv.at[0], packed.at[0:width], xi.at[0], xo.at[0]), first, (wq_s, wk_s, wv_s, wm_s, wi_s, wo_s),
    )
    vectors = Vectors(loads, packed, vec_own, other_s, first)

    def ready(step):
        load(step)
        if step == 0:
            loads.wait("vectors")
            for place in range(12):
                vec_s[place : place + 1, :] = vectors(place)

    forward_body(
        ready, Stores(out_sem), (bucket, count, lengths), (section,), lambda place: vec_s[place : place + 1, :],
        (y_o, (own_o,), shared_o), refs,
    )


def forward_shapes(micro_count, each, width, hidden):
    rows = micro_count * each
    flat = (rows, width)
    wide = (rows, hidden)
    square = (width, width)

    def out(*tail):
        return (micro_count,) + tail

    wides = hidden // width
    outs = (S(out(each, width), BF16), S(out(wides + 2, each, width), BF16)) + (S((wides + 5, each, width), BF16),) * micro_count
    scratch = [
        V(flat, BF16), V(square, BF16), V(square, BF16), V(square, BF16), V(square, BF16), V((width, hidden), BF16),
        V((hidden, width), BF16), V((3,) + flat, BF16), V(flat, BF16), V(flat, BF16), V(flat, BF16), V(flat, BF16),
        V(wide, BF16), V(wide, BF16), V(flat, BF16), V(flat, F32), V(flat, F32), V((rows, FFN_TILE), F32),
        V((rows, FFN_TILE), F32), V((rows, 3 * BUCKET), F32), V((rows, 1), F32),
        V((8, hidden), F32),
    ]
    flops = 2 * rows * width * (4 * width + 2 * hidden)
    return outs, scratch, flops


def first_forward(meta, tokens, weights, vectors, bi):
    micro_count, each, width = tokens.shape
    outs, scratch, flops = forward_shapes(micro_count, each, width, bi.shape[1])
    outs = outs + (S((width + VECTOR_ROWS, width), BF16), S((16, width), F32))
    scratch = scratch + [V((width, width), BF16), V((VECTOR_ROWS, width), BF16), pltpu.SemaphoreType.DMA((3,))]
    return run_kernel(
        functools.partial(first_forward_kernel, micro_count), outs, [ANY] * (3 + micro_count) + [VM], [SM] * 3 + [ANY] * 7 + [VM] * 9,
        scratch, 6 + micro_count, 14 * micro_count, flops, 40_000_000, "first_forward",
    )(*meta, tokens, *weights, *vectors, bi)


def second_forward(meta, y_own, y_other, weights, others, vec_own):
    _, each, width = y_own.shape
    outs, scratch, flops = forward_shapes(1, each, width, weights[4].shape[2])
    scratch = scratch + [V((VECTOR_ROWS, width), BF16), V((16, width), F32)]
    return run_kernel(
        second_forward_kernel, outs, [ANY] * 3, [SM] * 3 + [ANY] * 14 + [VM], scratch, 8, 14, flops, 25_000_000,
        "second_forward",
    )(*meta, y_own, y_other, *weights, *others, vec_own)


VECTOR_ROWS = 32


class Vectors:
    def __init__(self, loads, packed, own, other_s, take_other):
        width = packed.shape[1]
        self.own = own
        self.other_s = other_s
        self.take_other = take_other
        loads.start("vectors", packed.at[width : width + VECTOR_ROWS], other_s)

    def __call__(self, place):
        other = self.other_s[place : place + 1, :].astype(F32) + self.other_s[16 + place : 17 + place, :].astype(F32)
        return jnp.where(self.take_other, other, self.own[place : place + 1, :])


def norm_backward(grad, total, gain):
    centred, scale = row_moments(total)
    unit = centred * scale
    spread = grad * gain
    first = jnp.mean(spread, axis=-1, keepdims=True)
    second = jnp.mean(spread * unit, axis=-1, keepdims=True)
    return (spread - first - unit * second) * scale, grad * unit


def layer_of(layer):
    return lax.axis_index("section") != layer


def load_planes(layer, loads, name, own, other, plane, target):
    width = own.shape[2]
    take_other = lax.axis_index("section") == 1
    for index in range(target.shape[1] // width):
        part = target if target.shape[1] == width else target.at[:, index * width : (index + 1) * width]
        received = None if layer == 1 else other.at[plane + index]
        loads.start((name, index), own.at[plane + index], part, received, take_other)


def feed_kernel(
    layer, bucket, count, lengths, g, own, own_x, wo, wo_x, wi, wi_x, wm, packed, vec_own,
    dz_o, df_o, away_o, da1_o, da_o, dc_o, small_o,
    g_s, a2_s, gp_s, a1_s, wo_s, wi_s, wm_s, da2_s, dz_s, df_s, dm_s, da1_s, da_s, dc_s, e0_s, e1_s, valid_s, sums_s, wide_s, other_s, in_sem, out_sem,
):
    section = lax.axis_index("section")
    rows, width = a2_s.shape
    hidden = df_s.shape[1]
    loads = Loads(in_sem)
    store = Stores(out_sem)
    wides = range(hidden // width)
    loads.start("g", g.at[section] if layer == 1 else g, g_s)
    load_planes(layer, loads, "a2", own, own_x, SECOND_SUM, a2_s)
    loads.start("wo", wo.at[0], wo_s, wo_x.at[0], layer_of(layer))
    meta = (bucket, count, lengths)
    by_span(meta, section, lambda span: fill_masks(span, rows, meta, section, None, valid_s))
    sums_s[...] = jnp.zeros_like(sums_s)
    vectors = Vectors(loads, packed, vec_own, other_s, layer_of(layer))
    loads.wait("g", ("a2", 0), "vectors")
    gain_two, gain_one = (vectors(GAIN_TWO), vectors(GAIN_ONE))
    load_planes(layer, loads, "gp", own, own_x, SLOPE, gp_s)
    loads.start("wi", wi.at[0], wi_s, wi_x.at[0], layer_of(layer))

    def second_norm(part):
        grad = g_s[part, :].astype(F32) * valid_s[part, :]
        moved, gained = norm_backward(grad, a2_s[part, :].astype(F32), gain_two)
        da2_s[part, :] = moved
        low = moved.astype(BF16)
        dz_s[part, :] = low
        return gained, grad, low.astype(F32)

    over_chunks_with_sums(rows, second_norm, sums_s.at[0:3])
    half = width // 2
    store.start(dz_s.at[:, pl.ds(pl.multiple_of(section * half, half), half)], dz_o)
    store.start(dz_s.at[:, pl.ds(pl.multiple_of((1 - section) * half, half), half)], away_o.at[2, :, 0:half])
    tile = FFN_TILE
    tiles = hidden // tile

    def project(buffer, which):
        columns = pl.ds(pl.multiple_of(which * tile, tile), tile)
        buffer[...] = rows_times_transposed(dz_s[...], wo_s[columns, :])

    def slope(buffer, which):
        columns = pl.ds(pl.multiple_of(which * tile, tile), tile)
        total = None
        for start in range(0, rows, 32):
            part = slice(start, start + 32)
            low_part = (buffer[part, :] * gp_s[part, columns].astype(F32)).astype(BF16)
            df_s[part, columns] = low_part
            term = fold_rows(low_part.astype(F32))
            total = term if total is None else total + term
        wide_s[:, columns] = total

    loads.wait("wo")
    load_planes(layer, loads, "a1", own, own_x, FIRST_SUM, a1_s)
    loads.start("wm", wm.at[0], wm_s, packed.at[0:width], layer_of(layer))
    project(e0_s, 0)
    for index in wides:
        loads.wait(("gp", index))

    def two_tiles(index, carry):
        project(e1_s, 2 * index + 1)
        slope(e0_s, 2 * index)
        project(e0_s, jnp.minimum(2 * index + 2, tiles - 1))
        slope(e1_s, 2 * index + 1)
        return carry

    lax.fori_loop(0, tiles // 2, two_tiles, 0)
    half = hidden // 2
    store.start(df_s.at[:, pl.ds(pl.multiple_of(section * half, half), half)], df_o)
    for index in range(2):
        start = pl.multiple_of((1 - section) * half + index * width, width)
        store.start(df_s.at[:, pl.ds(start, width)], away_o.at[index])
    loads.wait("wi")
    dm_s[...] = rows_times_transposed(df_s[...], wi_s[...])
    loads.wait(("a1", 0))

    def first_norm(part):
        grad = dm_s[part, :] + da2_s[part, :]
        moved, gained = norm_backward(grad, a1_s[part, :].astype(F32), gain_one)
        da1_s[part, :] = moved
        low_part = moved.astype(BF16)
        da_s[part, :] = low_part
        return gained, grad, low_part.astype(F32)

    over_chunks_with_sums(rows, first_norm, sums_s.at[3:6])
    store.start(da1_s, da1_o)
    store.start(da_s, da_o)
    for index in range(6):
        small_o[index : index + 1, :] = jnp.sum(sums_s[index], axis=0, keepdims=True)
    inner_sum = jnp.sum(wide_s[...], axis=0, keepdims=True)
    for index in range(hidden // width):
        small_o[8 + index : 9 + index, :] = inner_sum[:, index * width : (index + 1) * width]
    loads.wait("wm")
    dc_s[...] = rows_times_transposed(da_s[...], wm_s[...]).astype(BF16)
    store.start(dc_s, dc_o)
    store.wait()


def feed_gradient(layer, meta, g, own, own_x, weights, others, vec_own):
    _, rows, width = own.shape
    hidden = weights[4].shape[2]
    flat = (rows, width)
    _, _, _, xi, xo, packed = others
    return run_kernel(
        functools.partial(feed_kernel, layer),
        (S((rows, width // 2), BF16), S((rows, hidden // 2), BF16), S((3,) + flat, BF16), S(flat, F32), S(flat, BF16), S(flat, BF16), S((SMALL_ROWS, width), F32)),
        [ANY] * 6 + [VM], [SM] * 3 + [ANY] * 9 + [VM],
        [
            V(flat, g.dtype), V(flat, BF16), V((rows, hidden), BF16), V(flat, BF16), V((hidden, width), BF16), V((width, hidden), BF16),
            V((width, width), BF16), V(flat, F32), V(flat, BF16), V((rows, hidden), BF16), V(flat, F32), V(flat, F32), V(flat, BF16),
            V(flat, BF16), V((rows, FFN_TILE), F32), V((rows, FFN_TILE), F32), V((rows, 1), F32), V((6, 8, width), F32),
            V((8, hidden), F32), V((VECTOR_ROWS, width), BF16),
        ],
        7 + hidden // width, 8, 2 * rows * width * (2 * hidden + width), 25_000_000, "feed_gradient",
    )(*meta, g, own, own_x, weights[5], xo, weights[4], xi, weights[3], packed, vec_own)


def attend_backward(span_rows, row_count, q_ref, k_ref, v_ref, dc_ref, bias_ref, dq_ref, dk_ref, dv_ref):
    blocks = row_count // span_rows
    scale = HEAD_DIM ** (-0.5)

    def one_pair(pair, carry):
        columns = pl.ds(pl.multiple_of(pair * PAIR, PAIR), PAIR)
        lane = lax.broadcasted_iota(jnp.int32, (span_rows, PAIR), 1)
        halves = (lane < HEAD_DIM, lane >= HEAD_DIM)
        for block in range(blocks):
            rows = slice(block * span_rows, (block + 1) * span_rows)
            query = q_ref[rows, columns] * jnp.asarray(scale, BF16)
            keys = k_ref[rows, columns]
            value = v_ref[rows, columns]
            grad = dc_ref[rows, columns]
            zero = jnp.zeros_like(keys)
            bias = bias_ref[rows, 0:span_rows]
            dq = dk = dv = None
            for mine in halves:
                keys_own = jnp.where(mine, keys, zero)
                scores = rows_times_transposed(keys_own, query) + bias
                grad_part = rows_times_transposed(jnp.where(mine, value, zero), grad)
                weight = jnp.exp(scores - jnp.max(scores, axis=0, keepdims=True))
                part = weight * (1.0 / jnp.sum(weight, axis=0, keepdims=True))
                mean = jnp.sum(grad_part * part, axis=0, keepdims=True)
                grad_scores = (part * (grad_part - mean)).astype(BF16)
                terms = (
                    transposed_times(grad_scores, keys_own),
                    rows_times(grad_scores, jnp.where(mine, query, zero)),
                    rows_times(part.astype(BF16), jnp.where(mine, grad, zero)),
                )
                if dq is None:
                    dq, dk, dv = terms
                else:
                    dq, dk, dv = (dq + terms[0], dk + terms[1], dv + terms[2])
            dq_ref[rows, columns] = (dq * scale).astype(BF16)
            dk_ref[rows, columns] = dk.astype(BF16)
            dv_ref[rows, columns] = dv.astype(BF16)
        return carry

    lax.fori_loop(0, HEADS // 2, one_pair, 0)


def attend_kernel(
    layer, bucket, count, lengths, own, own_x, dc, da, da1, wq, wk, wv, xq, xk, xv, small_one,
    dh_o, dlow_o, home_o, away_o, small_o,
    qkv_s, dc_s, da_s, dh_s, dlow_s, wq_s, wk_s, wv_s, dq_s, dk_s, dv_s, bias_s, sums_s, low_s, in_sem, out_sem,
):
    section = lax.axis_index("section")
    rows, width = dc_s.shape
    second = section == 1
    loads = Loads(in_sem)
    received = None if layer == 1 else own_x.at[QUERY : QUERY + 3]
    loads.start("qkv", own.at[QUERY : QUERY + 3], qkv_s, received, second)
    loads.start("dc", dc, dc_s)
    meta = (bucket, count, lengths)
    by_span(meta, section, lambda span: fill_masks(span, rows, meta, section, bias_s, None, True))
    loads.wait("qkv", "dc")
    loads.start("da", da, da_s)
    loads.start("da1", da1, dh_s)
    for name, weight, other, target in (("wq", wq, xq, wq_s), ("wk", wk, xk, wk_s), ("wv", wv, xv, wv_s)):
        loads.start(name, weight.at[0], target, other.at[0], layer_of(layer))
    by_span(
        meta, section,
        lambda span: attend_backward(span, rows, qkv_s.at[0], qkv_s.at[1], qkv_s.at[2], dc_s, bias_s, dq_s, dk_s, dv_s),
    )
    loads.wait("da")
    pairs = ((dq_s, dk_s), (dv_s, da_s))
    for core in range(2):
        @pl.when(section == core)
        def _(core=core):
            for place in range(2):
                pltpu.make_async_copy(pairs[core][place], home_o.at[place], out_sem.at[place]).start()
                pltpu.make_async_copy(
                    pairs[1 - core][place], away_o.at[place * rows : (place + 1) * rows], out_sem.at[2 + place]
                ).start()
    loads.wait("da1", "wq", "wk", "wv")
    dh_s[...] += rows_times_transposed(dq_s[...], wq_s[...])
    dh_s[...] += rows_times_transposed(dk_s[...], wk_s[...])
    dh_s[...] += rows_times_transposed(dv_s[...], wv_s[...])
    sums_s[...] = jnp.zeros_like(sums_s)

    def finish(part):
        dlow_s[part, :] = dh_s[part, :].astype(BF16)
        return dq_s[part, :].astype(F32), dv_s[part, :].astype(F32)

    over_chunks_with_sums(rows, finish, sums_s)
    last = [
        pltpu.make_async_copy(dh_s, dh_o, out_sem.at[4]),
        pltpu.make_async_copy(dlow_s, dlow_o, out_sem.at[5]),
    ]
    for copy in last:
        copy.start()
    small_o[0:6, :] = small_one[0:6, :]
    for index in range(2):
        small_o[6 + index : 7 + index, :] = jnp.sum(sums_s[index], axis=0, keepdims=True)
    small_o[8:16, :] = small_one[8:16, :]
    low_s[...] = small_o[...].astype(BF16)
    smalls = pltpu.make_async_copy(low_s, away_o.at[2 * rows : 2 * rows + SMALL_ROWS], out_sem.at[6])
    smalls.start()
    for place in range(2):
        pltpu.make_async_copy(pairs[0][place], home_o.at[place], out_sem.at[place]).wait()
        pltpu.make_async_copy(
            pairs[1][place], away_o.at[place * rows : (place + 1) * rows], out_sem.at[2 + place]
        ).wait()
    for copy in last:
        copy.wait()
    smalls.wait()


def attend_gradient(layer, meta, own, own_x, dc, da, da1, weights, others, small_one):
    rows, width = da1.shape
    flat = (rows, width)
    square = (width, width)
    return run_kernel(
        functools.partial(attend_kernel, layer),
        (S(flat, F32), S(flat, BF16), S((2,) + flat, BF16), S((2 * rows + SMALL_ROWS, width), BF16), S((SMALL_ROWS, width), F32)),
        [ANY] * 4 + [VM], [SM] * 3 + [ANY] * 11 + [VM],
        [V((3,) + flat, BF16), V(flat, BF16), V(flat, BF16), V(flat, F32), V(flat, BF16)] + [V(square, BF16)] * 3 + [V(flat, BF16)] * 3
        + [V((rows, 3 * BUCKET), F32), V((2, 8, width), F32), V((SMALL_ROWS, width), BF16)],
        7, 7, 6 * rows * width * width, 15_000_000, "attend_gradient",
    )(*meta, own, own_x, dc, da, da1, *weights[:3], *others[:3], small_one)


def by_owner(loads, name, own, other, target):
    rows = target.shape[0] // 2
    section = lax.axis_index("section")
    loads.start((name, 0), own, target.at[pl.ds(pl.multiple_of(section * rows, rows), rows)])
    loads.start((name, 1), other, target.at[pl.ds(pl.multiple_of((1 - section) * rows, rows), rows)])


def both_micros(layer, loads, name, own, other, plane, target, index):
    width = own.shape[3]
    rows = target.shape[0] // 2
    columns = target if target.shape[1] == width else target.at[:, index * width : (index + 1) * width]
    if layer == 1:
        by_owner(loads, (name, index), own.at[0, plane + index], other.at[0, plane + index], columns)
        return
    for micro in range(2):
        part = columns.at[micro * rows : (micro + 1) * rows]
        take_other = lax.axis_index("section") == 1
        loads.start(((name, index), micro), own.at[micro, plane + index], part, other.at[micro, plane + index], take_other)


def wait_both(loads, name, index):
    loads.wait(((name, index), 0), ((name, index), 1))


def put_rows(target, near_first, value, at_row, at_lane, dest):
    spot = 0 if target.shape[0] == 1 else spot_of(near_first, dest)
    rows, lanes = value.shape
    target[spot, at_row : at_row + rows, at_lane : at_lane + lanes] = value.astype(BF16)


def feed_weights_kernel(
    layer, near_first, shared, shared_x, dz, df, away_x,
    outer_o, inner_o, keep_o,
    u_s, ml_s, dz_s, df_s, w_s, in_sem, out_sem,
):
    hidden = u_s.shape[1]
    width = ml_s.shape[1]
    rows = dz.shape[0]
    spots = w_s.shape[0]
    loads = Loads(in_sem)
    store = Stores(out_sem)
    by_owner(loads, "dz", dz, away_x.at[2, :, 0 : width // 2], dz_s)

    def begin_u(index):
        both_micros(layer, loads, "u", shared, shared_x, ACTIVE, u_s, index)

    def begin_inner():
        both_micros(layer, loads, "ml", shared, shared_x, MIDDLE, ml_s, 0)
        for index in range(2):
            columns = slice(index * width, (index + 1) * width)
            by_owner(loads, ("df", index), df.at[:, columns], away_x.at[index], df_s.at[:, columns])

    planes = hidden // width
    begin_u(0)
    begin_u(1)
    loads.wait(("dz", 0), ("dz", 1))
    half_rows = hidden // spots // 2
    split = spots // 2
    for index in range(planes):
        wait_both(loads, "u", index)
        if index + 2 < planes:
            begin_u(index + 2)
        elif index + 2 == planes:
            begin_inner()
        product = transposed_times(u_s[:, index * width : (index + 1) * width], dz_s[...])
        block = min(half_rows, width)
        for inner in range(width // block):
            row = index * width + inner * block
            dest, offset = divmod(row, 2 * half_rows)
            side, at_row = divmod(offset, half_rows)
            put_rows(w_s, near_first, product[inner * block : (inner + 1) * block, :], at_row, side * (width // 2), dest)
    store.start(w_s.at[split:spots, 0:half_rows], outer_o)
    store.start(w_s.at[0 : spots - split, 0:half_rows], keep_o.at[:, 0:half_rows])
    wait_both(loads, "ml", 0)
    height = width // spots
    for side in range(2):
        wait_both(loads, "df", side)
        product = transposed_times(ml_s[...], df_s[:, side * width : (side + 1) * width])
        for dest in range(spots):
            put_rows(w_s, near_first, product[dest * height : (dest + 1) * height, :], half_rows + side * height, 0, dest)
    rest = slice(half_rows, half_rows + 2 * height)
    store.start(w_s.at[split:spots, rest], inner_o)
    store.start(w_s.at[0 : spots - split, rest], keep_o.at[:, rest])
    store.wait()


def feed_weights(layer, near_first, spots, shared, shared_x, dz, df, away_x):
    rows, width = shared.shape[2:]
    hidden = 2 * df.shape[1]
    total = hidden // spots // 2 + 2 * (width // spots)
    split = spots - spots // 2
    outs = (
        S((split, hidden // spots // 2, width), BF16), S((split, 2 * (width // spots), width), BF16), S((split, total, width), BF16),
    )
    return run_kernel(
        functools.partial(feed_weights_kernel, layer, near_first), outs, [ANY] * 3, [ANY] * 5,
        [
            V((2 * rows, hidden), BF16), V((2 * rows, width), BF16), V((2 * rows, width // 2), BF16), V((2 * rows, hidden // 2), BF16),
            V((spots, total, width), BF16),
        ],
        8 + 2 * (hidden // width), 4, 4 * rows * width * hidden, 18_000_000, "feed_weights",
    )(shared, shared_x, dz, df, away_x)


def attend_weights_kernel(
    layer, near_first, h, h_x, shared, shared_x, grads, away_x, small,
    *rest
):
    *sends_o, keep_o, left_s, right_s, w_s, small_s, in_sem, out_sem = rest
    section = lax.axis_index("section")
    second = section == 1
    rows, width = grads.shape[1:]
    spots = w_s.shape[0]
    loads = Loads(in_sem)
    store = Stores(out_sem)
    for micro in range(2):
        part = slice(micro * rows, (micro + 1) * rows)
        loads.start(("h", micro), h.at[micro], left_s.at[0, part], h_x.at[micro], second)
    by_owner(loads, "g", grads.at[0], away_x.at[0:rows], right_s.at[0])
    if layer == 0:
        for micro in range(2):
            part = slice(micro * rows, (micro + 1) * rows)
            loads.start(("c", micro), h.at[micro], left_s.at[1, part], shared_x.at[micro, CONTEXT], second)
    else:
        for place, (plain, context) in enumerate(((h, shared), (h, shared_x))):
            micro = section if place == 0 else 1 - section
            part = left_s.at[1, pl.ds(pl.multiple_of(micro * rows, rows), rows)]
            loads.start(("c", place), plain.at[micro], part, context.at[0, CONTEXT], second)
    by_owner(loads, "f", grads.at[1], away_x.at[rows : 2 * rows], right_s.at[1])
    height = width // spots
    loads.start("small", away_x.at[2 * rows : 2 * rows + SMALL_ROWS], small_s)
    loads.wait("small")
    low = (small[...] + small_s[...].astype(F32)).astype(BF16)
    for spot in range(spots):
        w_s[spot, 2 * height : 2 * height + SMALL_ROWS, :] = low
    for side, name in enumerate(("h", "c")):
        grad_name = ("g", "f")[side]
        loads.wait((name, 0), (name, 1), (grad_name, 0), (grad_name, 1))
        product = transposed_times(left_s[side], right_s[side])
        for dest in range(spots):
            put_rows(w_s, near_first, product[dest * height : (dest + 1) * height, :], side * height, 0, dest)
    split = spots // 2
    store.start(w_s.at[0 : spots - split], keep_o)
    cuts = (0, 2 * height + SMALL_ROWS) if len(sends_o) == 1 else (0, height, 2 * height + SMALL_ROWS)
    for place, send_o in enumerate(sends_o):
        store.start(w_s.at[split:spots, cuts[place] : cuts[place + 1]], send_o)
    store.wait()


def attend_weights(layer, near_first, spots, in_pieces, h, h_x, shared, shared_x, grads, away_x, small):
    rows, width = grads.shape[1:]
    height = width // spots
    total = 2 * height + SMALL_ROWS
    split = spots - spots // 2
    heights = (height, height + SMALL_ROWS) if in_pieces else (total,)
    outs = tuple(S((split, part, width), BF16) for part in heights + (total,))
    return run_kernel(
        functools.partial(attend_weights_kernel, layer, near_first), outs, [ANY] * len(outs), [ANY] * 6 + [VM],
        [V((2, 2 * rows, width), BF16), V((2, 2 * rows, width), BF16), V((spots, total, width), BF16), V((SMALL_ROWS, width), BF16)],
        9, 3, 8 * rows * width * width, 10_000_000, "attend_weights",
    )(h, h_x, shared, shared_x, grads, away_x, small)


def add_kernel(shapes, pieces, *refs):
    count = len(shapes)
    keeps, refs = (refs[0:count], refs[count:])
    parts, refs = (refs[0 : sum(pieces)], refs[sum(pieces) :])
    *rest, in_sem, out_sem = refs
    out_count = sum(1 if spots == 1 else 2 for spots, _, _ in shapes)
    outs, holds = (list(rest[:out_count]), list(rest[out_count:]))
    keep_s, part_s, total_s = (holds[0:count], holds[count : 2 * count], holds[2 * count :])
    loads = Loads(in_sem)
    store = Stores(out_sem)
    at = 0
    waits = []
    for index in range(count):
        loads.start(("keep", index), keeps[index], keep_s[index])
        names = [("keep", index)]
        row = 0
        for piece in range(pieces[index]):
            height = parts[at].shape[1]
            loads.start(("part", index, piece), parts[at], part_s[index].at[:, row : row + height])
            names.append(("part", index, piece))
            row += height
            at += 1
        waits.append(names)
    place = 0
    for index, (spots, rows, _) in enumerate(shapes):
        loads.wait(*waits[index])
        if spots == 1:
            total_s[index][...] = keep_s[index][0].astype(F32) + part_s[index][0].astype(F32)
            store.start(total_s[index], outs[place])
            place += 1
            continue

        def one(spot, carry, index=index):
            total_s[index][spot] = (keep_s[index][spot].astype(F32) + part_s[index][spot].astype(F32)).astype(BF16)
            return carry

        lax.fori_loop(0, spots, one, 0)
        store.start(total_s[index].at[spots // 2 : spots], outs[place])
        store.start(total_s[index].at[0 : spots // 2], outs[place + 1])
        place += 2
    store.wait()


def add_arrived(pairs, flops, limit):
    shapes = [keep.shape for keep, _ in pairs]
    pieces = [len(arrived) for _, arrived in pairs]
    outs = []
    totals = []
    for spots, rows, width in shapes:
        if spots > 1:
            outs.extend([S((spots // 2, rows, width), BF16)] * 2)
            totals.append(V((spots, rows, width), BF16))
        else:
            outs.append(S((rows, width), F32))
            totals.append(V((rows, width), F32))
    count = len(pairs) + sum(pieces)
    results = list(
        pl.pallas_call(
            functools.partial(add_kernel, shapes, pieces),
            out_shape=tuple(outs),
            in_specs=[ANY] * count,
            out_specs=(ANY,) * len(outs),
            scratch_shapes=[V(shape, BF16) for shape in shapes] * 2 + totals
            + [pltpu.SemaphoreType.DMA((count,)), pltpu.SemaphoreType.DMA((len(outs),))],
            compiler_params=pltpu.CompilerParams(vmem_limit_bytes=limit),
            cost_estimate=pl.CostEstimate(flops=flops, bytes_accessed=1000, transcendentals=0),
            name="add_arrived",
        )(*[keep for keep, _ in pairs], *[part for _, arrived in pairs for part in arrived])
    )
    return [(results.pop(0),) if spots == 1 else (results.pop(0), results.pop(0)) for spots, _, _ in shapes]


TAIL_LIMIT = 24_000 * 1024


def finish_kernel(feed_one, feed_two, tail_one, tail_two, feed_one_x, feed_two_x, tail_one_x, tail_two_x, q_o, k_o, v_o, m_o, i_o, o_o, small_o, wide_o):
    section = lax.axis_index("section")
    groups = lax.axis_size("dp")
    me = lax.axis_index("dp")
    height, width = q_o.shape
    half_rows = o_o.shape[0] // 2
    hidden = i_o.shape[1]
    for core in range(2):
        @pl.when(section == core)
        def _(core=core):
            mine, back = ((feed_one, tail_one), (feed_one_x, tail_one_x)) if core == 0 else ((feed_two, tail_two), (feed_two_x, tail_two_x))
            sides = (mine, back) if core == 0 else (back, mine)
            half = width // 2
            for side, (feed, _) in enumerate(sides):
                for part in range(2):
                    o_o[part * half_rows : (part + 1) * half_rows, side * half : (side + 1) * half] = feed[
                        0:half_rows, part * half : (part + 1) * half
                    ]
                    i_o[:, (2 * side + part) * width : (2 * side + part + 1) * width] = feed[
                        half_rows + part * height : half_rows + (part + 1) * height, :
                    ]
            q_o[...] = sides[0][1][0:height, :]
            k_o[...] = sides[0][1][height : 2 * height, :]
            v_o[...] = sides[1][1][0:height, :]
            m_o[...] = sides[1][1][height : 2 * height, :]
            lines = mine[1][2 * height : 2 * height + SMALL_ROWS, :]
            small_o[...] = pltpu.roll(lines[0:8, :], lax.rem(width - me * height, width), 1)
            span = hidden // groups
            each = width // span
            pick = lax.broadcasted_iota(jnp.int32, (8, width), 0) == lax.div(me, each)
            chosen = jnp.sum(jnp.where(pick, lines[8:16, :], 0.0), axis=0, keepdims=True)
            wide_o[...] = pltpu.roll(jnp.broadcast_to(chosen, (8, width)), lax.rem(width - lax.rem(me, each) * span, width), 1)


def finish(groups, width, hidden, results):
    height = width // groups
    square = S((height, width), F32)
    return pl.pallas_call(
        finish_kernel,
        out_shape=(square, square, square, square, S((height, hidden), F32), S((hidden // groups, width), F32), S((8, width), F32), S((8, width), F32)),
        in_specs=[VM] * 8,
        out_specs=(VM,) * 8,
        compiler_params=pltpu.CompilerParams(vmem_limit_bytes=TAIL_LIMIT),
        name="finish_gradients",
    )(*results)


def exchange(value, bits):
    groups = lax.axis_size("dp")
    pairs = [(2 * group + core, 2 * (group ^ (1 << bits[core])) + core) for group in range(groups) for core in range(2)]
    return lax.ppermute(value, ("dp", "section"), pairs)


def swap(value):
    return lax.ppermute(value, "section", [(0, 1), (1, 0)])


F1, T1, F0, T0 = (("f", 1), ("t", 1), ("f", 0), ("t", 0))
NEAR_FIRST = {F1: False, T1: True, F0: False, T0: False}
TOGETHER = (F0,)
WEIGHED = (50_000_000_000,) * 8 + (6_000_000_000,) + (1000,) * 4
SCHEDULE = (
    (),
    (),
    (),
    (F1,),
    (F1,),
    (),
    (F1,),
    (F1, F0, T1),
    (F1, T1, F0),
    (F0, T1, T0),
    (F0, T1, T0),
    (T1, T0),
    (T0,),
)


def widen(value):
    return value.astype(F32)


def per_device(
    tokens, cotangent, bucket, batch_size, lengths, query_weight, query_offset, keys_weight, value_weight, value_offset,
    mixer_weight, mixer_offset, first_gain, first_shift, inner_weight, inner_offset, outer_weight, outer_offset,
    second_gain, second_shift,
):
    section = lax.axis_index("section")
    groups = lax.axis_size("dp")
    width = tokens.shape[2]
    hidden = inner_offset.shape[1]
    hypercube = groups == 16
    spots = groups if hypercube else 1
    first = section == 0
    meta = (bucket, batch_size, lengths)
    weights = (query_weight, keys_weight, value_weight, mixer_weight, inner_weight, outer_weight)
    vectors = (query_offset, value_offset, mixer_offset, first_gain, first_shift, outer_offset, second_gain, second_shift)
    others = tuple(swap(weight) for index, weight in enumerate(weights) if index != 3)
    y_first, shared_first, own_first, own_handed, packed, vec_own = first_forward(meta, tokens, weights, vectors, inner_offset)
    handed, packed, others = lax.optimization_barrier((y_first, packed, others))
    y_x = swap(handed)
    others = others + (swap(packed),)
    y_second, shared_second, own_second = second_forward(meta, y_first, y_x, weights, others, vec_own)
    shared_x = swap(lax.optimization_barrier((shared_first, y_x, others[-1]))[0])
    own_second, shared_x = lax.optimization_barrier((own_second, shared_x))
    own = {1: (own_second, own_second)}
    shared = {0: (shared_first, shared_x), 1: (shared_second, swap(shared_second))}
    entries = {1: (y_first, y_x), 0: (tokens, tokens)}
    y_last_x = swap(y_second)
    moving = {}
    results = {}

    def boundary(turn, value, other):
        names = SCHEDULE[turn] if hypercube else ()
        if not names:
            return value, other
        landed = {name: moving[name][1] for name in names}
        other, landed = lax.optimization_barrier((other, landed))
        ready = []
        for name in names:
            keep, _, waiting, arrived, step = moving[name]
            arrived = arrived + landed[name]
            if waiting:
                moving[name] = (keep, None, waiting[1:], arrived, step)
                ready.append(name)
            else:
                moving[name] = (keep, None, [], arrived, step + 1)
        done = [name for name in names if name not in ready]
        if done:
            added = add_arrived([(moving[name][0], moving[name][3]) for name in done], WEIGHED[turn], VMEM_LIMIT if turn < 9 else TAIL_LIMIT)
            value, added = lax.optimization_barrier((value, added))
            for name, parts in zip(done, added):
                step = moving[name][4]
                if len(parts) == 1:
                    results[name] = parts[0]
                else:
                    moving[name] = (parts[1], [exchange(parts[0], step_bits(NEAR_FIRST[name])[step])], [], [], step)
        else:
            value = lax.optimization_barrier((value, landed))[0]
        for name in ready:
            keep, _, waiting, arrived, step = moving[name]
            piece = pieces[name].pop(0)
            piece = lax.optimization_barrier((piece, landed, value))[0]
            moving[name] = (keep, [exchange(piece, step_bits(NEAR_FIRST[name])[0])], waiting, arrived, step)
        return value, other

    pieces = {}

    def begin(name, sends, keep):
        if hypercube:
            pieces[name] = [] if name in TOGETHER else list(sends[1:])
            flying = [exchange(send, step_bits(NEAR_FIRST[name])[0]) for send in sends[: len(sends) - len(pieces[name])]]
            moving[name] = (keep, flying, list(pieces[name]), [], 0)
        else:
            moving[name] = sends

    def feed(layer, grad):
        return feed_gradient(layer, meta, grad, *own[layer], weights, others, vec_own)

    def feed_sum(layer, dz, df, away_x):
        *sends, keep = feed_weights(layer, False, spots, *shared[layer], dz, df, away_x)
        begin(F1 if layer else F0, sends, keep)
        return keep

    def attend(layer, dc, da, da1, small):
        return attend_gradient(layer, meta, *own[layer], dc, da, da1, weights, others, small)

    def attend_sum(layer, grads, away_x, small):
        name = T1 if layer else T0
        *sends, keep = attend_weights(layer, NEAR_FIRST[name], spots, layer == 1 and hypercube, *entries[layer], *shared[layer], grads, away_x, small)
        begin(name, sends, keep)
        return keep

    def tie(value, other):
        return lax.optimization_barrier((value, other))[0]

    dh = {}
    low_gradient = {}
    dz, df, away, da1, da, dc, small_feed = feed(1, cotangent)
    held = feed_sum(1, dz, df, swap(away))
    own[0] = (own_first, swap(tie(own_handed, held)))
    dh[1], low_gradient[1], grads, away, small = attend(1, tie(dc, held), da, da1, small_feed)
    dh_one_x = swap(low_gradient[1])
    attend_away_x = swap(away)
    grad, _ = boundary(3, low_gradient[1], held)
    dz, df, away, da1, da, dc, small_feed = feed(0, grad)
    dz, dh_one_x, y_last_x = lax.optimization_barrier((dz, dh_one_x, y_last_x))
    grads, away = boundary(4, tie(grads, dz), away)
    feed_away_x = swap(away)
    held = attend_sum(1, grads, attend_away_x, small)
    dz, _ = boundary(5, tie(dz, held), held)
    held = feed_sum(0, dz, df, feed_away_x)
    dc, _ = boundary(6, tie(dc, held), held)
    dh[0], low_gradient[0], grads, away, small = attend(0, dc, da, da1, small_feed)
    grads, away = boundary(7, grads, away)
    held = attend_sum(0, grads, swap(away), small)
    def outputs_of_rows(y_first, y_last_x, y_second, dh, dh_one_x, low):
        layer_out = jnp.stack([jnp.where(first, y_first[0], y_last_x[0]), jnp.where(first, y_first[1], y_second[0])])
        dh_zero_x = swap(low)
        input_grad = jnp.stack([jnp.where(first, dh[0], widen(dh_one_x)), jnp.where(first, widen(dh_zero_x), dh[1])])
        return layer_out, input_grad

    pieces_of_rows = (y_first, y_last_x, y_second, dh, dh_one_x, low_gradient[0])
    if hypercube:
        for turn in range(8, len(SCHEDULE)):
            if turn == 10:
                layer_out, input_grad = outputs_of_rows(*pieces_of_rows)
                pieces_of_rows = (layer_out, input_grad)
            pieces_of_rows, held = boundary(turn, pieces_of_rows, held)
        layer_out, input_grad = pieces_of_rows
        order = (F0, F1, T0, T1)
        done = finish(groups, width, hidden, [results[name] for name in order] + [swap(results[name]) for name in order])
        query_grad, keys_grad, value_grad, mixer_grad, inner_grad, outer_grad, lines, wide_line = done
        height = width // groups
        small = [lines[index, :height] for index in range(8)]
        small_wide = wide_line[0, : hidden // groups]
    else:
        layer_out, input_grad = outputs_of_rows(*pieces_of_rows)

        def scatter(value):
            return lax.psum_scatter(value, "dp", scatter_dimension=0, tiled=True).astype(F32)

        found = []
        for layer in (1, 0):
            outer_part, inner_part = (value[0] for value in moving["f", layer])
            attend = moving["t", layer][0][0]
            half = width // 2
            outer_half = jnp.concatenate([outer_part[:, :half], outer_part[:, half:]], axis=0)
            parts = [scatter(outer_half), scatter(inner_part[:width]), scatter(inner_part[width:])]
            parts += [scatter(attend[:width]), scatter(attend[width : 2 * width])]
            lines = attend[2 * width :].astype(F32)
            parts += [scatter(lines[index]) for index in range(8)] + [scatter(lines[8:12].reshape(-1))]
            found.append(parts)
        mine = [jnp.where(first, b, a) for a, b in zip(*found)]
        back = [swap(jnp.where(first, a, b)) for a, b in zip(found[0][:5], found[1][:5])]
        low = [jnp.where(first, a, b) for a, b in zip(mine, back)]
        high = [jnp.where(first, b, a) for a, b in zip(mine, back)]
        outer_grad = jnp.concatenate([low[0], high[0]], axis=1)
        inner_grad = jnp.concatenate([low[1], low[2], high[1], high[2]], axis=1)
        query_grad, keys_grad, value_grad, mixer_grad = (low[3], low[4], high[3], high[4])
        small, small_wide = (mine[5:13], mine[13])
    second_gain_grad, second_shift_grad, outer_offset_grad, first_gain_grad, first_shift_grad, mixer_offset_grad = small[:6]
    outputs = (
        layer_out, input_grad, query_grad, small[6], keys_grad, value_grad, small[7], mixer_grad, mixer_offset_grad,
        first_gain_grad, first_shift_grad, inner_grad, small_wide, outer_grad, outer_offset_grad, second_gain_grad,
        second_shift_grad,
    )
    return tuple(piece[None] for piece in outputs)


def solution(mesh):
    matrix = P("section", None, None)
    vector = P("section", None)
    in_specs = (
        P("dp", None, None), P("dp", None, None), P("dp"), P("dp"), P("dp", None), matrix, vector, matrix, matrix, vector,
        matrix, vector, vector, vector, matrix, vector, matrix, vector, vector, vector,
    )
    rows = P("section", "dp", None, None)
    grad = P("section", "dp", None)
    small = P("section", "dp")
    out_specs = (rows, rows, grad, small, grad, grad, small, grad, small, small, small, grad, small, grad, small, small, small)
    return jax.shard_map(per_device, mesh=mesh, in_specs=in_specs, out_specs=out_specs, check_vma=False)
```

```python
import functools
import jax
import jax.numpy as jnp
from jax import lax
from jax.experimental import pallas as pl
from jax.experimental.pallas import tpu as pltpu
from jax.sharding import PartitionSpec as P

HEADS = 12
HEAD_DIM = 64
BUCKET = 64
PAIR = 2 * HEAD_DIM
masked_score = -1000000000.0
norm_epsilon = 1e-06
F32 = jnp.float32
BF16 = jnp.bfloat16
CHUNK = 16
FFN_TILE = 512
ATT_UNROLL = 3


def rows_times(left, right):
    return lax.dot_general(left, right, (((1,), (0,)), ((), ())), preferred_element_type=F32)


def rows_times_transposed(left, right):
    return lax.dot_general(left, right, (((1,), (1,)), ((), ())), preferred_element_type=F32)


def transposed_times(left, right):
    return lax.dot_general(left, right, (((0,), (0,)), ((), ())), preferred_element_type=F32)


def slot_facts(block, span_rows, place, meta, micro):
    bucket_ref, count_ref, lengths_ref = meta
    bucket = bucket_ref[micro]
    count = count_ref[micro]

    def length_of(slot):
        return jnp.where(slot < count, lengths_ref[micro, slot], 0)

    if span_rows == 2 * BUCKET:
        return (jnp.full_like(place, block), place, jnp.full_like(place, length_of(block)))
    short = bucket == 0
    first = 3 * block
    slot_short = first + place // BUCKET
    length_short = jnp.where(
        place < BUCKET,
        length_of(first),
        jnp.where(place < 2 * BUCKET, length_of(first + 1), length_of(first + 2)),
    )
    slot = jnp.where(short, slot_short, block)
    inner = jnp.where(short, place % BUCKET, place)
    length = jnp.where(short, length_short, length_of(block))
    return (slot, inner, length)


def fill_masks(span_rows, row_count, meta, micro, bias_ref, valid_ref, keys_down=False):
    for block in range(row_count // span_rows):
        row_place = lax.broadcasted_iota(jnp.int32, (span_rows, 1), 0)
        row_slot, row_inner, row_length = slot_facts(block, span_rows, row_place, meta, micro)
        rows = slice(block * span_rows, (block + 1) * span_rows)
        if bias_ref is not None:
            other_place = lax.broadcasted_iota(jnp.int32, (1, span_rows), 1)
            other_slot, other_inner, other_length = slot_facts(block, span_rows, other_place, meta, micro)
            if keys_down:
                allowed = other_slot == jnp.where(row_inner < row_length, row_slot, -1)
            else:
                allowed = row_slot == jnp.where(other_inner < other_length, other_slot, -1)
            allowed = allowed | (row_place == other_place)
            bias_ref[rows, 0:span_rows] = jnp.where(allowed, 0.0, masked_score)
        if valid_ref is not None:
            valid_ref[rows, :] = jnp.where(row_inner < row_length, 1.0, 0.0)


def by_span(meta, micro, body):
    even = meta[0][micro] == 1

    @pl.when(even)
    def _():
        body(2 * BUCKET)

    @pl.when(jnp.logical_not(even))
    def _():
        body(3 * BUCKET)


def attend_forward(span_rows, row_count, q_ref, k_ref, v_ref, bias_ref, c_ref):
    blocks = row_count // span_rows

    def one_pair(pair, carry):
        columns = pl.ds(pl.multiple_of(pair * PAIR, PAIR), PAIR)
        lane = lax.broadcasted_iota(jnp.int32, (span_rows, PAIR), 1)
        first_half = lane < HEAD_DIM
        weights = []
        for block in range(blocks):
            rows = slice(block * span_rows, (block + 1) * span_rows)
            query = q_ref[rows, columns] * jnp.asarray(HEAD_DIM ** (-0.5), BF16)
            keys = k_ref[rows, columns]
            zero = jnp.zeros_like(keys)
            bias = bias_ref[rows, 0:span_rows]
            for mine in (first_half, jnp.logical_not(first_half)):
                scores = rows_times_transposed(query, jnp.where(mine, keys, zero)) + bias
                top = jnp.max(scores, axis=-1, keepdims=True)
                weights.append(jnp.exp(scores - top).astype(BF16))
        for block in range(blocks):
            rows = slice(block * span_rows, (block + 1) * span_rows)
            value = v_ref[rows, columns]
            one = jnp.ones_like(value)
            left = rows_times(weights[2 * block], jnp.where(first_half, value, one))
            right = rows_times(weights[2 * block + 1], jnp.where(first_half, one, value))
            above = jnp.where(first_half, left, right)
            below = pltpu.roll(jnp.where(first_half, right, left), HEAD_DIM, 1)
            c_ref[rows, columns] = (above / below).astype(BF16)
        return carry

    lax.fori_loop(0, HEADS // 2, one_pair, 0, unroll=ATT_UNROLL)


def row_moments(values):
    center = jnp.mean(values, axis=-1, keepdims=True)
    centred = values - center
    spread = jnp.mean(centred * centred, axis=-1, keepdims=True)
    return centred, lax.rsqrt(spread + norm_epsilon)


def over_chunks(row_count, body, rows=CHUNK, group=6):
    def step(index, carry):
        for inner in range(group):
            start = pl.multiple_of(index * (rows * group) + inner * rows, rows)
            body(pl.ds(start, rows))
        return carry

    lax.fori_loop(0, row_count // (rows * group), step, 0)


def over_chunks_with_sums(row_count, body, sums_ref, rows=CHUNK, group=6):
    def step(index, carry):
        total = None
        for inner in range(group):
            start = pl.multiple_of(index * (rows * group) + inner * rows, rows)
            terms = [fold_rows(term) for term in body(pl.ds(start, rows))]
            total = terms if total is None else [a + b for a, b in zip(total, terms)]
        for place, term in enumerate(total):
            sums_ref[place] += term
        return carry

    lax.fori_loop(0, row_count // (rows * group), step, 0)


def fold_rows(values):
    return jnp.sum(values.reshape(values.shape[0] // 8, 8, values.shape[1]), axis=0)


def gelu_with_slope(values):
    cumulative = 0.5 + 0.5 * lax.erf(values * (0.5 ** 0.5))
    density = jnp.exp(values * values * -0.5) * 0.3989422804014327
    return values * cumulative, cumulative + values * density


ANY = pl.BlockSpec(memory_space=pl.ANY)
VM = pl.BlockSpec(memory_space=pltpu.VMEM)
SM = pl.BlockSpec(memory_space=pltpu.SMEM)
VMEM_LIMIT = 64_500 * 1024
S = jax.ShapeDtypeStruct
V = pltpu.VMEM
B_QUERY, B_VALUE, B_MIXER, GAIN_ONE, SHIFT_ONE, B_OUTER, GAIN_TWO, SHIFT_TWO = range(8)
QUERY, FIRST_SUM, SECOND_SUM, SLOPE = (0, 3, 4, 5)
ACTIVE, MIDDLE, CONTEXT = (0, 4, 5)
X_BIT, Y_BIT, NEAR_BIT, FAR_BIT = (0, 1, 2, 3)
SMALL_ROWS = 16


class Loads:
    def __init__(self, semaphores):
        self.semaphores = semaphores
        self.copies = {}

    def start(self, name, source, target, other=None, take_other=None):
        semaphore = self.semaphores.at[len(self.copies)]
        copy = pltpu.make_async_copy(source, target, semaphore)
        self.copies[name] = copy
        if other is None:
            copy.start()
            return
        second = pltpu.make_async_copy(other, target, semaphore)

        @pl.when(take_other)
        def _():
            second.start()

        @pl.when(jnp.logical_not(take_other))
        def _():
            copy.start()

    def wait(self, *names):
        for name in names:
            self.copies[name].wait()


class Stores:
    def __init__(self, semaphores):
        self.semaphores = semaphores
        self.copies = []

    def start(self, source, target):
        copy = pltpu.make_async_copy(source, target, self.semaphores.at[len(self.copies)])
        copy.start()
        self.copies.append(copy)

    def wait(self):
        for copy in self.copies:
            copy.wait()


def run_kernel(kernel, outs, out_specs, in_specs, scratch, loads, stores, flops, bytes_moved, name):
    return pl.pallas_call(
        kernel,
        out_shape=outs,
        in_specs=in_specs,
        out_specs=out_specs,
        scratch_shapes=list(scratch) + [pltpu.SemaphoreType.DMA((loads,)), pltpu.SemaphoreType.DMA((stores,))],
        compiler_params=pltpu.CompilerParams(vmem_limit_bytes=VMEM_LIMIT),
        cost_estimate=pl.CostEstimate(flops=1000, bytes_accessed=1000, transcendentals=0),
        name=name,
    )


def spot_of(near_first, dest):
    relative = jnp.bitwise_xor(dest, lax.axis_index("dp"))

    def bit(index):
        return jnp.bitwise_and(lax.shift_right_logical(relative, index), 1)

    first = lax.axis_index("section") == 0
    lead = jnp.where(first, bit(X_BIT), bit(Y_BIT))
    follow = jnp.where(first, bit(Y_BIT), bit(X_BIT))
    if near_first:
        return bit(NEAR_BIT) * 8 + lead * 4 + follow * 2 + bit(FAR_BIT)
    return lead * 8 + follow * 4 + bit(NEAR_BIT) * 2 + bit(FAR_BIT)


def step_bits(near_first):
    cross = [(X_BIT, Y_BIT), (Y_BIT, X_BIT)]
    if near_first:
        return [(NEAR_BIT, NEAR_BIT)] + cross + [(FAR_BIT, FAR_BIT)]
    return cross + [(NEAR_BIT, NEAR_BIT), (FAR_BIT, FAR_BIT)]


def forward_matrix_loads(loads, hidden_start, weights, others, take_other, targets):
    names = ("wq", "wk", "wv", "wm", "wi", "wo")

    def begin(index):
        other = None if others is None else others[index]
        loads.start(names[index], weights[index].at[0], targets[index], other, take_other)

    def load(step):
        if step == 0:
            hidden_start()
            for index in range(3):
                begin(index)
            return
        if step == 1:
            loads.wait("h")
        loads.wait(names[step - 1])
        if step <= 3:
            begin(step + 2)

    return load


def forward_body(load, store, meta, micros, vec, outs, refs):
    h_s, wq_s, wk_s, wv_s, wm_s, wi_s, wo_s, qkv_s, c_s, ml_s, a1_s, a2_s, u_s, gp_s, y_s, m_s, f0_s, e0_s, e1_s, bias_s, valid_s, bi_s = refs
    y_o, own_o, shared_o = outs
    rows, width = h_s.shape
    hidden = wi_s.shape[1]
    each = rows // len(micros)
    parts = [slice(place * each, (place + 1) * each) for place in range(len(micros))]

    def send(source, plane, shared=False):
        for place, part in enumerate(parts):
            target = shared_o.at[place] if shared else own_o[place]
            for index in range(source.shape[1] // width):
                store.start(source.at[part, index * width : (index + 1) * width], target.at[plane + index])

    load(0)
    for part, micro in zip(parts, micros):
        by_span(meta, micro, lambda span: fill_masks(span, each, meta, micro, bias_s.at[part], valid_s.at[part]))
    load(1)
    qkv_s[0] = (rows_times(h_s[...], wq_s[...]) + vec(B_QUERY)).astype(BF16)
    load(2)
    qkv_s[1] = rows_times(h_s[...], wk_s[...]).astype(BF16)
    load(3)
    qkv_s[2] = (rows_times(h_s[...], wv_s[...]) + vec(B_VALUE)).astype(BF16)
    for place, part in enumerate(parts):
        store.start(qkv_s.at[:, part], own_o[place].at[QUERY : QUERY + 3])
    for part, micro in zip(parts, micros):
        by_span(
            meta, micro,
            lambda span: attend_forward(
                span, each, qkv_s.at[0, part], qkv_s.at[1, part], qkv_s.at[2, part], bias_s.at[part], c_s.at[part]
            ),
        )
    send(c_s, CONTEXT, True)
    load(4)
    f0_s[...] = rows_times(c_s[...], wm_s[...])
    offset_mixer, gain_one, shift_one = (vec(B_MIXER), vec(GAIN_ONE), vec(SHIFT_ONE))

    def first_norm(part):
        total = h_s[part, :].astype(F32) + (f0_s[part, :] + offset_mixer)
        a1_s[part, :] = total.astype(BF16)
        centred, scale = row_moments(total)
        middle = centred * scale * gain_one + shift_one
        m_s[part, :] = middle
        ml_s[part, :] = middle.astype(BF16)

    over_chunks(rows, first_norm)
    send(a1_s, FIRST_SUM)
    send(ml_s, MIDDLE, True)
    load(5)
    tile = FFN_TILE
    tiles = hidden // tile

    def project(buffer, which):
        columns = pl.ds(pl.multiple_of(which * tile, tile), tile)
        buffer[...] = rows_times(ml_s[...], wi_s[:, columns])

    def activate(buffer, which):
        columns = pl.ds(pl.multiple_of(which * tile, tile), tile)
        offset = bi_s[0:1, columns]
        for start in range(0, rows, 32):
            part = slice(start, start + 32)
            value, slope = gelu_with_slope(buffer[part, :] + offset)
            u_s[part, columns] = value.astype(BF16)
            gp_s[part, columns] = slope.astype(BF16)

    for index in range(hidden // width):
        bi_s[0:1, index * width : (index + 1) * width] = vec(8 + index)
    project(e0_s, 0)

    def two_tiles(index, carry):
        project(e1_s, 2 * index + 1)
        activate(e0_s, 2 * index)
        project(e0_s, jnp.minimum(2 * index + 2, tiles - 1))
        activate(e1_s, 2 * index + 1)
        return carry

    lax.fori_loop(0, tiles // 2, two_tiles, 0)
    send(u_s, ACTIVE, True)
    send(gp_s, SLOPE)
    load(6)
    f0_s[...] = rows_times(u_s[...], wo_s[...])
    offset_outer, gain_two, shift_two = (vec(B_OUTER), vec(GAIN_TWO), vec(SHIFT_TWO))

    def second_norm(part):
        total = m_s[part, :] + (f0_s[part, :] + offset_outer)
        a2_s[part, :] = total.astype(BF16)
        centred, scale = row_moments(total)
        y_s[part, :] = ((centred * scale * gain_two + shift_two) * valid_s[part, :]).astype(BF16)

    over_chunks(rows, second_norm)
    for place, part in enumerate(parts):
        store.start(y_s.at[part], y_o.at[place])
    send(a2_s, SECOND_SUM)
    store.wait()


def first_forward_kernel(
    micro_count, bucket, count, lengths, tok, wq, wk, wv, wm, wi, wo, bq, bv, bm, g1, s1, bo, g2, s2, bi, *rest
):
    y_o, shared_o = rest[:2]
    own_o = rest[2 : 2 + micro_count]
    packed_o, vec_o = rest[2 + micro_count : 4 + micro_count]
    *refs, hold_s, low_s, pack_sem, in_sem, out_sem = rest[4 + micro_count :]
    h_s, wq_s, wk_s, wv_s, wm_s, wi_s, wo_s = refs[:7]
    width = h_s.shape[1]
    gather = pltpu.make_async_copy(wm.at[0], hold_s, pack_sem.at[0])
    hand = pltpu.make_async_copy(hold_s, packed_o.at[0:width], pack_sem.at[1])
    hand_low = pltpu.make_async_copy(low_s, packed_o.at[width : width + VECTOR_ROWS], pack_sem.at[2])
    vec_o[...] = jnp.zeros_like(vec_o)
    for place, vector in enumerate((bq, bv, bm, g1, s1, bo, g2, s2)):
        vec_o[place : place + 1, :] = vector[...]
    for index in range(bi.shape[1] // width):
        vec_o[8 + index : 9 + index, :] = bi[:, index * width : (index + 1) * width]
    high = vec_o[...].astype(BF16)
    low_s[0:16, :] = high
    low_s[16:32, :] = (vec_o[...] - high.astype(F32)).astype(BF16)
    hand_low.start()

    @pl.when(lax.axis_index("section") != 0)
    def _():
        gather.start()
        gather.wait()
        hand.start()

    @pl.when(lax.axis_index("section") == 0)
    def _():
        loads = Loads(in_sem)
        each = h_s.shape[0] // micro_count

        def hidden_start():
            for micro in range(1, micro_count):
                loads.start(("h", micro), tok.at[micro], h_s.at[micro * each : (micro + 1) * each])
            loads.start("h", tok.at[0], h_s.at[0:each])

        inner_load = forward_matrix_loads(
            loads, hidden_start, (wq, wk, wv, wm, wi, wo), None, None, (wq_s, wk_s, wv_s, wm_s, wi_s, wo_s)
        )

        def load(step):
            if step == 1:
                for micro in range(1, micro_count):
                    loads.wait(("h", micro))
            if step == 4:
                gather.start()
            if step == 6:
                gather.wait()
                hand.start()
            inner_load(step)

        forward_body(
            load, Stores(out_sem), (bucket, count, lengths), tuple(range(micro_count)),
            lambda place: vec_o[place : place + 1, :], (y_o, own_o, shared_o), refs,
        )

    hand.wait()
    hand_low.wait()


def second_forward_kernel(
    bucket, count, lengths, y_own, y_other, wq, wk, wv, wm, wi, wo, xq, xk, xv, xi, xo, packed, vec_own,
    y_o, shared_o, own_o, *scratch
):
    *refs, other_s, vec_s, in_sem, out_sem = scratch
    h_s, wq_s, wk_s, wv_s, wm_s, wi_s, wo_s = refs[:7]
    section = lax.axis_index("section")
    first = section == 0
    width = h_s.shape[1]
    loads = Loads(in_sem)
    load = forward_matrix_loads(
        loads, lambda: loads.start("h", y_other.at[section], h_s, y_own.at[section], first), (wq, wk, wv, wm, wi, wo),
        (xq.at[0], xk.at[0], xv.at[0], packed.at[0:width], xi.at[0], xo.at[0]), first, (wq_s, wk_s, wv_s, wm_s, wi_s, wo_s),
    )
    vectors = Vectors(loads, packed, vec_own, other_s, first)

    def ready(step):
        load(step)
        if step == 0:
            loads.wait("vectors")
            for place in range(12):
                vec_s[place : place + 1, :] = vectors(place)

    forward_body(
        ready, Stores(out_sem), (bucket, count, lengths), (section,), lambda place: vec_s[place : place + 1, :],
        (y_o, (own_o,), shared_o), refs,
    )


def forward_shapes(micro_count, each, width, hidden):
    rows = micro_count * each
    flat = (rows, width)
    wide = (rows, hidden)
    square = (width, width)

    def out(*tail):
        return (micro_count,) + tail

    wides = hidden // width
    outs = (S(out(each, width), BF16), S(out(wides + 2, each, width), BF16)) + (S((wides + 5, each, width), BF16),) * micro_count
    scratch = [
        V(flat, BF16), V(square, BF16), V(square, BF16), V(square, BF16), V(square, BF16), V((width, hidden), BF16),
        V((hidden, width), BF16), V((3,) + flat, BF16), V(flat, BF16), V(flat, BF16), V(flat, BF16), V(flat, BF16),
        V(wide, BF16), V(wide, BF16), V(flat, BF16), V(flat, F32), V(flat, F32), V((rows, FFN_TILE), F32),
        V((rows, FFN_TILE), F32), V((rows, 3 * BUCKET), F32), V((rows, 1), F32),
        V((8, hidden), F32),
    ]
    flops = 2 * rows * width * (4 * width + 2 * hidden)
    return outs, scratch, flops


def first_forward(meta, tokens, weights, vectors, bi):
    micro_count, each, width = tokens.shape
    outs, scratch, flops = forward_shapes(micro_count, each, width, bi.shape[1])
    outs = outs + (S((width + VECTOR_ROWS, width), BF16), S((16, width), F32))
    scratch = scratch + [V((width, width), BF16), V((VECTOR_ROWS, width), BF16), pltpu.SemaphoreType.DMA((3,))]
    return run_kernel(
        functools.partial(first_forward_kernel, micro_count), outs, [ANY] * (3 + micro_count) + [VM], [SM] * 3 + [ANY] * 7 + [VM] * 9,
        scratch, 6 + micro_count, 14 * micro_count, flops, 40_000_000, "first_forward",
    )(*meta, tokens, *weights, *vectors, bi)


def second_forward(meta, y_own, y_other, weights, others, vec_own):
    _, each, width = y_own.shape
    outs, scratch, flops = forward_shapes(1, each, width, weights[4].shape[2])
    scratch = scratch + [V((VECTOR_ROWS, width), BF16), V((16, width), F32)]
    return run_kernel(
        second_forward_kernel, outs, [ANY] * 3, [SM] * 3 + [ANY] * 14 + [VM], scratch, 8, 14, flops, 25_000_000,
        "second_forward",
    )(*meta, y_own, y_other, *weights, *others, vec_own)


VECTOR_ROWS = 32


class Vectors:
    def __init__(self, loads, packed, own, other_s, take_other):
        width = packed.shape[1]
        self.own = own
        self.other_s = other_s
        self.take_other = take_other
        loads.start("vectors", packed.at[width : width + VECTOR_ROWS], other_s)

    def __call__(self, place):
        other = self.other_s[place : place + 1, :].astype(F32) + self.other_s[16 + place : 17 + place, :].astype(F32)
        return jnp.where(self.take_other, other, self.own[place : place + 1, :])


def norm_backward(grad, total, gain):
    centred, scale = row_moments(total)
    unit = centred * scale
    spread = grad * gain
    first = jnp.mean(spread, axis=-1, keepdims=True)
    second = jnp.mean(spread * unit, axis=-1, keepdims=True)
    return (spread - first - unit * second) * scale, grad * unit


def layer_of(layer):
    return lax.axis_index("section") != layer


def load_planes(layer, loads, name, own, other, plane, target):
    width = own.shape[2]
    take_other = lax.axis_index("section") == 1
    for index in range(target.shape[1] // width):
        part = target if target.shape[1] == width else target.at[:, index * width : (index + 1) * width]
        received = None if layer == 1 else other.at[plane + index]
        loads.start((name, index), own.at[plane + index], part, received, take_other)


def feed_kernel(
    layer, bucket, count, lengths, g, own, own_x, wo, wo_x, wi, wi_x, wm, packed, vec_own,
    dz_o, df_o, away_o, da1_o, da_o, dc_o, small_o,
    g_s, a2_s, gp_s, a1_s, wo_s, wi_s, wm_s, da2_s, dz_s, df_s, dm_s, da1_s, da_s, dc_s, e0_s, e1_s, valid_s, sums_s, wide_s, other_s, in_sem, out_sem,
):
    section = lax.axis_index("section")
    rows, width = a2_s.shape
    hidden = df_s.shape[1]
    loads = Loads(in_sem)
    store = Stores(out_sem)
    wides = range(hidden // width)
    loads.start("g", g.at[section] if layer == 1 else g, g_s)
    load_planes(layer, loads, "a2", own, own_x, SECOND_SUM, a2_s)
    loads.start("wo", wo.at[0], wo_s, wo_x.at[0], layer_of(layer))
    meta = (bucket, count, lengths)
    by_span(meta, section, lambda span: fill_masks(span, rows, meta, section, None, valid_s))
    sums_s[...] = jnp.zeros_like(sums_s)
    vectors = Vectors(loads, packed, vec_own, other_s, layer_of(layer))
    loads.wait("g", ("a2", 0), "vectors")
    gain_two, gain_one = (vectors(GAIN_TWO), vectors(GAIN_ONE))
    load_planes(layer, loads, "gp", own, own_x, SLOPE, gp_s)
    loads.start("wi", wi.at[0], wi_s, wi_x.at[0], layer_of(layer))

    def second_norm(part):
        grad = g_s[part, :].astype(F32) * valid_s[part, :]
        moved, gained = norm_backward(grad, a2_s[part, :].astype(F32), gain_two)
        da2_s[part, :] = moved
        low = moved.astype(BF16)
        dz_s[part, :] = low
        return gained, grad, low.astype(F32)

    over_chunks_with_sums(rows, second_norm, sums_s.at[0:3])
    half = width // 2
    store.start(dz_s.at[:, pl.ds(pl.multiple_of(section * half, half), half)], dz_o)
    store.start(dz_s.at[:, pl.ds(pl.multiple_of((1 - section) * half, half), half)], away_o.at[2, :, 0:half])
    tile = FFN_TILE
    tiles = hidden // tile

    def project(buffer, which):
        columns = pl.ds(pl.multiple_of(which * tile, tile), tile)
        buffer[...] = rows_times_transposed(dz_s[...], wo_s[columns, :])

    def slope(buffer, which):
        columns = pl.ds(pl.multiple_of(which * tile, tile), tile)
        total = None
        for start in range(0, rows, 32):
            part = slice(start, start + 32)
            low_part = (buffer[part, :] * gp_s[part, columns].astype(F32)).astype(BF16)
            df_s[part, columns] = low_part
            term = fold_rows(low_part.astype(F32))
            total = term if total is None else total + term
        wide_s[:, columns] = total

    loads.wait("wo")
    load_planes(layer, loads, "a1", own, own_x, FIRST_SUM, a1_s)
    loads.start("wm", wm.at[0], wm_s, packed.at[0:width], layer_of(layer))
    project(e0_s, 0)
    for index in wides:
        loads.wait(("gp", index))

    def two_tiles(index, carry):
        project(e1_s, 2 * index + 1)
        slope(e0_s, 2 * index)
        project(e0_s, jnp.minimum(2 * index + 2, tiles - 1))
        slope(e1_s, 2 * index + 1)
        return carry

    lax.fori_loop(0, tiles // 2, two_tiles, 0)
    half = hidden // 2
    store.start(df_s.at[:, pl.ds(pl.multiple_of(section * half, half), half)], df_o)
    for index in range(2):
        start = pl.multiple_of((1 - section) * half + index * width, width)
        store.start(df_s.at[:, pl.ds(start, width)], away_o.at[index])
    loads.wait("wi")
    dm_s[...] = rows_times_transposed(df_s[...], wi_s[...])
    loads.wait(("a1", 0))

    def first_norm(part):
        grad = dm_s[part, :] + da2_s[part, :]
        moved, gained = norm_backward(grad, a1_s[part, :].astype(F32), gain_one)
        da1_s[part, :] = moved
        low_part = moved.astype(BF16)
        da_s[part, :] = low_part
        return gained, grad, low_part.astype(F32)

    over_chunks_with_sums(rows, first_norm, sums_s.at[3:6])
    store.start(da1_s, da1_o)
    store.start(da_s, da_o)
    for index in range(6):
        small_o[index : index + 1, :] = jnp.sum(sums_s[index], axis=0, keepdims=True)
    inner_sum = jnp.sum(wide_s[...], axis=0, keepdims=True)
    for index in range(hidden // width):
        small_o[8 + index : 9 + index, :] = inner_sum[:, index * width : (index + 1) * width]
    loads.wait("wm")
    dc_s[...] = rows_times_transposed(da_s[...], wm_s[...]).astype(BF16)
    store.start(dc_s, dc_o)
    store.wait()


def feed_gradient(layer, meta, g, own, own_x, weights, others, vec_own):
    _, rows, width = own.shape
    hidden = weights[4].shape[2]
    flat = (rows, width)
    _, _, _, xi, xo, packed = others
    return run_kernel(
        functools.partial(feed_kernel, layer),
        (S((rows, width // 2), BF16), S((rows, hidden // 2), BF16), S((3,) + flat, BF16), S(flat, F32), S(flat, BF16), S(flat, BF16), S((SMALL_ROWS, width), F32)),
        [ANY] * 6 + [VM], [SM] * 3 + [ANY] * 9 + [VM],
        [
            V(flat, g.dtype), V(flat, BF16), V((rows, hidden), BF16), V(flat, BF16), V((hidden, width), BF16), V((width, hidden), BF16),
            V((width, width), BF16), V(flat, F32), V(flat, BF16), V((rows, hidden), BF16), V(flat, F32), V(flat, F32), V(flat, BF16),
            V(flat, BF16), V((rows, FFN_TILE), F32), V((rows, FFN_TILE), F32), V((rows, 1), F32), V((6, 8, width), F32),
            V((8, hidden), F32), V((VECTOR_ROWS, width), BF16),
        ],
        7 + hidden // width, 8, 2 * rows * width * (2 * hidden + width), 25_000_000, "feed_gradient",
    )(*meta, g, own, own_x, weights[5], xo, weights[4], xi, weights[3], packed, vec_own)


def attend_backward(span_rows, row_count, q_ref, k_ref, v_ref, dc_ref, bias_ref, dq_ref, dk_ref, dv_ref):
    blocks = row_count // span_rows
    scale = HEAD_DIM ** (-0.5)

    def one_pair(pair, carry):
        columns = pl.ds(pl.multiple_of(pair * PAIR, PAIR), PAIR)
        lane = lax.broadcasted_iota(jnp.int32, (span_rows, PAIR), 1)
        halves = (lane < HEAD_DIM, lane >= HEAD_DIM)
        for block in range(blocks):
            rows = slice(block * span_rows, (block + 1) * span_rows)
            query = q_ref[rows, columns] * jnp.asarray(scale, BF16)
            keys = k_ref[rows, columns]
            value = v_ref[rows, columns]
            grad = dc_ref[rows, columns]
            zero = jnp.zeros_like(keys)
            bias = bias_ref[rows, 0:span_rows]
            dq = dk = dv = None
            for mine in halves:
                keys_own = jnp.where(mine, keys, zero)
                scores = rows_times_transposed(keys_own, query) + bias
                grad_part = rows_times_transposed(jnp.where(mine, value, zero), grad)
                weight = jnp.exp(scores - jnp.max(scores, axis=0, keepdims=True))
                part = weight * (1.0 / jnp.sum(weight, axis=0, keepdims=True))
                mean = jnp.sum(grad_part * part, axis=0, keepdims=True)
                grad_scores = (part * (grad_part - mean)).astype(BF16)
                terms = (
                    transposed_times(grad_scores, keys_own),
                    rows_times(grad_scores, jnp.where(mine, query, zero)),
                    rows_times(part.astype(BF16), jnp.where(mine, grad, zero)),
                )
                if dq is None:
                    dq, dk, dv = terms
                else:
                    dq, dk, dv = (dq + terms[0], dk + terms[1], dv + terms[2])
            dq_ref[rows, columns] = (dq * scale).astype(BF16)
            dk_ref[rows, columns] = dk.astype(BF16)
            dv_ref[rows, columns] = dv.astype(BF16)
        return carry

    lax.fori_loop(0, HEADS // 2, one_pair, 0)


def attend_kernel(
    layer, bucket, count, lengths, own, own_x, dc, da, da1, wq, wk, wv, xq, xk, xv, small_one,
    dh_o, dlow_o, home_o, away_o, small_o,
    qkv_s, dc_s, da_s, dh_s, dlow_s, wq_s, wk_s, wv_s, dq_s, dk_s, dv_s, bias_s, sums_s, low_s, in_sem, out_sem,
):
    section = lax.axis_index("section")
    rows, width = dc_s.shape
    second = section == 1
    loads = Loads(in_sem)
    received = None if layer == 1 else own_x.at[QUERY : QUERY + 3]
    loads.start("qkv", own.at[QUERY : QUERY + 3], qkv_s, received, second)
    loads.start("dc", dc, dc_s)
    meta = (bucket, count, lengths)
    by_span(meta, section, lambda span: fill_masks(span, rows, meta, section, bias_s, None, True))
    loads.wait("qkv", "dc")
    loads.start("da", da, da_s)
    loads.start("da1", da1, dh_s)
    for name, weight, other, target in (("wq", wq, xq, wq_s), ("wk", wk, xk, wk_s), ("wv", wv, xv, wv_s)):
        loads.start(name, weight.at[0], target, other.at[0], layer_of(layer))
    by_span(
        meta, section,
        lambda span: attend_backward(span, rows, qkv_s.at[0], qkv_s.at[1], qkv_s.at[2], dc_s, bias_s, dq_s, dk_s, dv_s),
    )
    loads.wait("da")
    pairs = ((dq_s, dk_s), (dv_s, da_s))
    for core in range(2):
        @pl.when(section == core)
        def _(core=core):
            for place in range(2):
                pltpu.make_async_copy(pairs[core][place], home_o.at[place], out_sem.at[place]).start()
                pltpu.make_async_copy(
                    pairs[1 - core][place], away_o.at[place * rows : (place + 1) * rows], out_sem.at[2 + place]
                ).start()
    loads.wait("da1", "wq", "wk", "wv")
    dh_s[...] += rows_times_transposed(dq_s[...], wq_s[...])
    dh_s[...] += rows_times_transposed(dk_s[...], wk_s[...])
    dh_s[...] += rows_times_transposed(dv_s[...], wv_s[...])
    sums_s[...] = jnp.zeros_like(sums_s)

    def finish(part):
        dlow_s[part, :] = dh_s[part, :].astype(BF16)
        return dq_s[part, :].astype(F32), dv_s[part, :].astype(F32)

    over_chunks_with_sums(rows, finish, sums_s)
    last = [
        pltpu.make_async_copy(dh_s, dh_o, out_sem.at[4]),
        pltpu.make_async_copy(dlow_s, dlow_o, out_sem.at[5]),
    ]
    for copy in last:
        copy.start()
    small_o[0:6, :] = small_one[0:6, :]
    for index in range(2):
        small_o[6 + index : 7 + index, :] = jnp.sum(sums_s[index], axis=0, keepdims=True)
    small_o[8:16, :] = small_one[8:16, :]
    low_s[...] = small_o[...].astype(BF16)
    smalls = pltpu.make_async_copy(low_s, away_o.at[2 * rows : 2 * rows + SMALL_ROWS], out_sem.at[6])
    smalls.start()
    for place in range(2):
        pltpu.make_async_copy(pairs[0][place], home_o.at[place], out_sem.at[place]).wait()
        pltpu.make_async_copy(
            pairs[1][place], away_o.at[place * rows : (place + 1) * rows], out_sem.at[2 + place]
        ).wait()
    for copy in last:
        copy.wait()
    smalls.wait()


def attend_gradient(layer, meta, own, own_x, dc, da, da1, weights, others, small_one):
    rows, width = da1.shape
    flat = (rows, width)
    square = (width, width)
    return run_kernel(
        functools.partial(attend_kernel, layer),
        (S(flat, F32), S(flat, BF16), S((2,) + flat, BF16), S((2 * rows + SMALL_ROWS, width), BF16), S((SMALL_ROWS, width), F32)),
        [ANY] * 4 + [VM], [SM] * 3 + [ANY] * 11 + [VM],
        [V((3,) + flat, BF16), V(flat, BF16), V(flat, BF16), V(flat, F32), V(flat, BF16)] + [V(square, BF16)] * 3 + [V(flat, BF16)] * 3
        + [V((rows, 3 * BUCKET), F32), V((2, 8, width), F32), V((SMALL_ROWS, width), BF16)],
        7, 7, 6 * rows * width * width, 15_000_000, "attend_gradient",
    )(*meta, own, own_x, dc, da, da1, *weights[:3], *others[:3], small_one)


def by_owner(loads, name, own, other, target):
    rows = target.shape[0] // 2
    section = lax.axis_index("section")
    loads.start((name, 0), own, target.at[pl.ds(pl.multiple_of(section * rows, rows), rows)])
    loads.start((name, 1), other, target.at[pl.ds(pl.multiple_of((1 - section) * rows, rows), rows)])


def both_micros(layer, loads, name, own, other, plane, target, index):
    width = own.shape[3]
    rows = target.shape[0] // 2
    columns = target if target.shape[1] == width else target.at[:, index * width : (index + 1) * width]
    if layer == 1:
        by_owner(loads, (name, index), own.at[0, plane + index], other.at[0, plane + index], columns)
        return
    for micro in range(2):
        part = columns.at[micro * rows : (micro + 1) * rows]
        take_other = lax.axis_index("section") == 1
        loads.start(((name, index), micro), own.at[micro, plane + index], part, other.at[micro, plane + index], take_other)


def wait_both(loads, name, index):
    loads.wait(((name, index), 0), ((name, index), 1))


def put_rows(target, near_first, value, at_row, at_lane, dest):
    spot = 0 if target.shape[0] == 1 else spot_of(near_first, dest)
    rows, lanes = value.shape
    target[spot, at_row : at_row + rows, at_lane : at_lane + lanes] = value.astype(BF16)


def feed_weights_kernel(
    layer, near_first, shared, shared_x, dz, df, away_x,
    outer_o, inner_o, keep_o,
    u_s, ml_s, dz_s, df_s, w_s, in_sem, out_sem,
):
    hidden = u_s.shape[1]
    width = ml_s.shape[1]
    rows = dz.shape[0]
    spots = w_s.shape[0]
    loads = Loads(in_sem)
    store = Stores(out_sem)
    by_owner(loads, "dz", dz, away_x.at[2, :, 0 : width // 2], dz_s)

    def begin_u(index):
        both_micros(layer, loads, "u", shared, shared_x, ACTIVE, u_s, index)

    def begin_inner():
        both_micros(layer, loads, "ml", shared, shared_x, MIDDLE, ml_s, 0)
        for index in range(2):
            columns = slice(index * width, (index + 1) * width)
            by_owner(loads, ("df", index), df.at[:, columns], away_x.at[index], df_s.at[:, columns])

    planes = hidden // width
    begin_u(0)
    begin_u(1)
    loads.wait(("dz", 0), ("dz", 1))
    half_rows = hidden // spots // 2
    split = spots // 2
    for index in range(planes):
        wait_both(loads, "u", index)
        if index + 2 < planes:
            begin_u(index + 2)
        elif index + 2 == planes:
            begin_inner()
        product = transposed_times(u_s[:, index * width : (index + 1) * width], dz_s[...])
        block = min(half_rows, width)
        for inner in range(width // block):
            row = index * width + inner * block
            dest, offset = divmod(row, 2 * half_rows)
            side, at_row = divmod(offset, half_rows)
            put_rows(w_s, near_first, product[inner * block : (inner + 1) * block, :], at_row, side * (width // 2), dest)
    store.start(w_s.at[split:spots, 0:half_rows], outer_o)
    store.start(w_s.at[0 : spots - split, 0:half_rows], keep_o.at[:, 0:half_rows])
    wait_both(loads, "ml", 0)
    height = width // spots
    for side in range(2):
        wait_both(loads, "df", side)
        product = transposed_times(ml_s[...], df_s[:, side * width : (side + 1) * width])
        for dest in range(spots):
            put_rows(w_s, near_first, product[dest * height : (dest + 1) * height, :], half_rows + side * height, 0, dest)
    rest = slice(half_rows, half_rows + 2 * height)
    store.start(w_s.at[split:spots, rest], inner_o)
    store.start(w_s.at[0 : spots - split, rest], keep_o.at[:, rest])
    store.wait()


def feed_weights(layer, near_first, spots, shared, shared_x, dz, df, away_x):
    rows, width = shared.shape[2:]
    hidden = 2 * df.shape[1]
    total = hidden // spots // 2 + 2 * (width // spots)
    split = spots - spots // 2
    outs = (
        S((split, hidden // spots // 2, width), BF16), S((split, 2 * (width // spots), width), BF16), S((split, total, width), BF16),
    )
    return run_kernel(
        functools.partial(feed_weights_kernel, layer, near_first), outs, [ANY] * 3, [ANY] * 5,
        [
            V((2 * rows, hidden), BF16), V((2 * rows, width), BF16), V((2 * rows, width // 2), BF16), V((2 * rows, hidden // 2), BF16),
            V((spots, total, width), BF16),
        ],
        8 + 2 * (hidden // width), 4, 4 * rows * width * hidden, 18_000_000, "feed_weights",
    )(shared, shared_x, dz, df, away_x)


def attend_weights_kernel(
    layer, near_first, h, h_x, shared, shared_x, grads, away_x, small,
    *rest
):
    *sends_o, keep_o, left_s, right_s, w_s, small_s, in_sem, out_sem = rest
    section = lax.axis_index("section")
    second = section == 1
    rows, width = grads.shape[1:]
    spots = w_s.shape[0]
    loads = Loads(in_sem)
    store = Stores(out_sem)
    for micro in range(2):
        part = slice(micro * rows, (micro + 1) * rows)
        loads.start(("h", micro), h.at[micro], left_s.at[0, part], h_x.at[micro], second)
    by_owner(loads, "g", grads.at[0], away_x.at[0:rows], right_s.at[0])
    if layer == 0:
        for micro in range(2):
            part = slice(micro * rows, (micro + 1) * rows)
            loads.start(("c", micro), h.at[micro], left_s.at[1, part], shared_x.at[micro, CONTEXT], second)
    else:
        for place, (plain, context) in enumerate(((h, shared), (h, shared_x))):
            micro = section if place == 0 else 1 - section
            part = left_s.at[1, pl.ds(pl.multiple_of(micro * rows, rows), rows)]
            loads.start(("c", place), plain.at[micro], part, context.at[0, CONTEXT], second)
    by_owner(loads, "f", grads.at[1], away_x.at[rows : 2 * rows], right_s.at[1])
    height = width // spots
    loads.start("small", away_x.at[2 * rows : 2 * rows + SMALL_ROWS], small_s)
    loads.wait("small")
    low = (small[...] + small_s[...].astype(F32)).astype(BF16)
    for spot in range(spots):
        w_s[spot, 2 * height : 2 * height + SMALL_ROWS, :] = low
    for side, name in enumerate(("h", "c")):
        grad_name = ("g", "f")[side]
        loads.wait((name, 0), (name, 1), (grad_name, 0), (grad_name, 1))
        product = transposed_times(left_s[side], right_s[side])
        for dest in range(spots):
            put_rows(w_s, near_first, product[dest * height : (dest + 1) * height, :], side * height, 0, dest)
    split = spots // 2
    store.start(w_s.at[0 : spots - split], keep_o)
    cuts = (0, 2 * height + SMALL_ROWS) if len(sends_o) == 1 else (0, height, 2 * height + SMALL_ROWS)
    for place, send_o in enumerate(sends_o):
        store.start(w_s.at[split:spots, cuts[place] : cuts[place + 1]], send_o)
    store.wait()


def attend_weights(layer, near_first, spots, in_pieces, h, h_x, shared, shared_x, grads, away_x, small):
    rows, width = grads.shape[1:]
    height = width // spots
    total = 2 * height + SMALL_ROWS
    split = spots - spots // 2
    heights = (height, height + SMALL_ROWS) if in_pieces else (total,)
    outs = tuple(S((split, part, width), BF16) for part in heights + (total,))
    return run_kernel(
        functools.partial(attend_weights_kernel, layer, near_first), outs, [ANY] * len(outs), [ANY] * 6 + [VM],
        [V((2, 2 * rows, width), BF16), V((2, 2 * rows, width), BF16), V((spots, total, width), BF16), V((SMALL_ROWS, width), BF16)],
        9, 3, 8 * rows * width * width, 10_000_000, "attend_weights",
    )(h, h_x, shared, shared_x, grads, away_x, small)


def add_kernel(shapes, pieces, *refs):
    count = len(shapes)
    keeps, refs = (refs[0:count], refs[count:])
    parts, refs = (refs[0 : sum(pieces)], refs[sum(pieces) :])
    *rest, in_sem, out_sem = refs
    out_count = sum(1 if spots == 1 else 2 for spots, _, _ in shapes)
    outs, holds = (list(rest[:out_count]), list(rest[out_count:]))
    keep_s, part_s, total_s = (holds[0:count], holds[count : 2 * count], holds[2 * count :])
    loads = Loads(in_sem)
    store = Stores(out_sem)
    at = 0
    waits = []
    for index in range(count):
        loads.start(("keep", index), keeps[index], keep_s[index])
        names = [("keep", index)]
        row = 0
        for piece in range(pieces[index]):
            height = parts[at].shape[1]
            loads.start(("part", index, piece), parts[at], part_s[index].at[:, row : row + height])
            names.append(("part", index, piece))
            row += height
            at += 1
        waits.append(names)
    place = 0
    for index, (spots, rows, _) in enumerate(shapes):
        loads.wait(*waits[index])
        if spots == 1:
            total_s[index][...] = keep_s[index][0].astype(F32) + part_s[index][0].astype(F32)
            store.start(total_s[index], outs[place])
            place += 1
            continue

        def one(spot, carry, index=index):
            total_s[index][spot] = (keep_s[index][spot].astype(F32) + part_s[index][spot].astype(F32)).astype(BF16)
            return carry

        lax.fori_loop(0, spots, one, 0)
        store.start(total_s[index].at[spots // 2 : spots], outs[place])
        store.start(total_s[index].at[0 : spots // 2], outs[place + 1])
        place += 2
    store.wait()


def add_arrived(pairs, flops, limit):
    shapes = [keep.shape for keep, _ in pairs]
    pieces = [len(arrived) for _, arrived in pairs]
    outs = []
    totals = []
    for spots, rows, width in shapes:
        if spots > 1:
            outs.extend([S((spots // 2, rows, width), BF16)] * 2)
            totals.append(V((spots, rows, width), BF16))
        else:
            outs.append(S((rows, width), F32))
            totals.append(V((rows, width), F32))
    count = len(pairs) + sum(pieces)
    results = list(
        pl.pallas_call(
            functools.partial(add_kernel, shapes, pieces),
            out_shape=tuple(outs),
            in_specs=[ANY] * count,
            out_specs=(ANY,) * len(outs),
            scratch_shapes=[V(shape, BF16) for shape in shapes] * 2 + totals
            + [pltpu.SemaphoreType.DMA((count,)), pltpu.SemaphoreType.DMA((len(outs),))],
            compiler_params=pltpu.CompilerParams(vmem_limit_bytes=limit),
            cost_estimate=pl.CostEstimate(flops=flops, bytes_accessed=1000, transcendentals=0),
            name="add_arrived",
        )(*[keep for keep, _ in pairs], *[part for _, arrived in pairs for part in arrived])
    )
    return [(results.pop(0),) if spots == 1 else (results.pop(0), results.pop(0)) for spots, _, _ in shapes]


TAIL_LIMIT = 24_000 * 1024


def finish_kernel(feed_one, feed_two, tail_one, tail_two, feed_one_x, feed_two_x, tail_one_x, tail_two_x, q_o, k_o, v_o, m_o, i_o, o_o, small_o, wide_o):
    section = lax.axis_index("section")
    groups = lax.axis_size("dp")
    me = lax.axis_index("dp")
    height, width = q_o.shape
    half_rows = o_o.shape[0] // 2
    hidden = i_o.shape[1]
    for core in range(2):
        @pl.when(section == core)
        def _(core=core):
            mine, back = ((feed_one, tail_one), (feed_one_x, tail_one_x)) if core == 0 else ((feed_two, tail_two), (feed_two_x, tail_two_x))
            sides = (mine, back) if core == 0 else (back, mine)
            half = width // 2
            for side, (feed, _) in enumerate(sides):
                for part in range(2):
                    o_o[part * half_rows : (part + 1) * half_rows, side * half : (side + 1) * half] = feed[
                        0:half_rows, part * half : (part + 1) * half
                    ]
                    i_o[:, (2 * side + part) * width : (2 * side + part + 1) * width] = feed[
                        half_rows + part * height : half_rows + (part + 1) * height, :
                    ]
            q_o[...] = sides[0][1][0:height, :]
            k_o[...] = sides[0][1][height : 2 * height, :]
            v_o[...] = sides[1][1][0:height, :]
            m_o[...] = sides[1][1][height : 2 * height, :]
            lines = mine[1][2 * height : 2 * height + SMALL_ROWS, :]
            small_o[...] = pltpu.roll(lines[0:8, :], lax.rem(width - me * height, width), 1)
            span = hidden // groups
            each = width // span
            pick = lax.broadcasted_iota(jnp.int32, (8, width), 0) == lax.div(me, each)
            chosen = jnp.sum(jnp.where(pick, lines[8:16, :], 0.0), axis=0, keepdims=True)
            wide_o[...] = pltpu.roll(jnp.broadcast_to(chosen, (8, width)), lax.rem(width - lax.rem(me, each) * span, width), 1)


def finish(groups, width, hidden, results):
    height = width // groups
    square = S((height, width), F32)
    return pl.pallas_call(
        finish_kernel,
        out_shape=(square, square, square, square, S((height, hidden), F32), S((hidden // groups, width), F32), S((8, width), F32), S((8, width), F32)),
        in_specs=[VM] * 8,
        out_specs=(VM,) * 8,
        compiler_params=pltpu.CompilerParams(vmem_limit_bytes=TAIL_LIMIT),
        name="finish_gradients",
    )(*results)


def exchange(value, bits):
    groups = lax.axis_size("dp")
    pairs = [(2 * group + core, 2 * (group ^ (1 << bits[core])) + core) for group in range(groups) for core in range(2)]
    return lax.ppermute(value, ("dp", "section"), pairs)


def swap(value):
    return lax.ppermute(value, "section", [(0, 1), (1, 0)])


F1, T1, F0, T0 = (("f", 1), ("t", 1), ("f", 0), ("t", 0))
NEAR_FIRST = {F1: False, T1: True, F0: False, T0: False}
TOGETHER = (F0,)
WEIGHED = (50_000_000_000,) * 8 + (6_000_000_000,) + (1000,) * 4
SCHEDULE = (
    (),
    (),
    (),
    (F1,),
    (F1,),
    (),
    (F1,),
    (F1, F0, T1),
    (F1, T1, F0),
    (F0, T1, T0),
    (F0, T1, T0),
    (T1, T0),
    (T0,),
)


def widen(value):
    return value.astype(F32)


def per_device(
    tokens, cotangent, bucket, batch_size, lengths, query_weight, query_offset, keys_weight, value_weight, value_offset,
    mixer_weight, mixer_offset, first_gain, first_shift, inner_weight, inner_offset, outer_weight, outer_offset,
    second_gain, second_shift,
):
    section = lax.axis_index("section")
    groups = lax.axis_size("dp")
    width = tokens.shape[2]
    hidden = inner_offset.shape[1]
    hypercube = groups == 16
    spots = groups if hypercube else 1
    first = section == 0
    meta = (bucket, batch_size, lengths)
    weights = (query_weight, keys_weight, value_weight, mixer_weight, inner_weight, outer_weight)
    vectors = (query_offset, value_offset, mixer_offset, first_gain, first_shift, outer_offset, second_gain, second_shift)
    others = tuple(swap(weight) for index, weight in enumerate(weights) if index != 3)
    y_first, shared_first, own_first, own_handed, packed, vec_own = first_forward(meta, tokens, weights, vectors, inner_offset)
    handed, packed, others = lax.optimization_barrier((y_first, packed, others))
    y_x = swap(handed)
    others = others + (swap(packed),)
    y_second, shared_second, own_second = second_forward(meta, y_first, y_x, weights, others, vec_own)
    shared_x = swap(lax.optimization_barrier((shared_first, y_x, others[-1]))[0])
    own_second, shared_x = lax.optimization_barrier((own_second, shared_x))
    own = {1: (own_second, own_second)}
    shared = {0: (shared_first, shared_x), 1: (shared_second, swap(shared_second))}
    entries = {1: (y_first, y_x), 0: (tokens, tokens)}
    y_last_x = swap(y_second)
    moving = {}
    results = {}

    def boundary(turn, value, other):
        names = SCHEDULE[turn] if hypercube else ()
        if not names:
            return value, other
        landed = {name: moving[name][1] for name in names}
        other, landed = lax.optimization_barrier((other, landed))
        ready = []
        for name in names:
            keep, _, waiting, arrived, step = moving[name]
            arrived = arrived + landed[name]
            if waiting:
                moving[name] = (keep, None, waiting[1:], arrived, step)
                ready.append(name)
            else:
                moving[name] = (keep, None, [], arrived, step + 1)
        done = [name for name in names if name not in ready]
        if done:
            added = add_arrived([(moving[name][0], moving[name][3]) for name in done], WEIGHED[turn], VMEM_LIMIT if turn < 10 else TAIL_LIMIT)
            value, added = lax.optimization_barrier((value, added))
            for name, parts in zip(done, added):
                step = moving[name][4]
                if len(parts) == 1:
                    results[name] = parts[0]
                else:
                    moving[name] = (parts[1], [exchange(parts[0], step_bits(NEAR_FIRST[name])[step])], [], [], step)
        else:
            value = lax.optimization_barrier((value, landed))[0]
        for name in ready:
            keep, _, waiting, arrived, step = moving[name]
            piece = pieces[name].pop(0)
            piece = lax.optimization_barrier((piece, landed, value))[0]
            moving[name] = (keep, [exchange(piece, step_bits(NEAR_FIRST[name])[0])], waiting, arrived, step)
        return value, other

    pieces = {}

    def begin(name, sends, keep):
        if hypercube:
            pieces[name] = [] if name in TOGETHER else list(sends[1:])
            flying = [exchange(send, step_bits(NEAR_FIRST[name])[0]) for send in sends[: len(sends) - len(pieces[name])]]
            moving[name] = (keep, flying, list(pieces[name]), [], 0)
        else:
            moving[name] = sends

    def feed(layer, grad):
        return feed_gradient(layer, meta, grad, *own[layer], weights, others, vec_own)

    def feed_sum(layer, dz, df, away_x):
        *sends, keep = feed_weights(layer, False, spots, *shared[layer], dz, df, away_x)
        begin(F1 if layer else F0, sends, keep)
        return keep

    def attend(layer, dc, da, da1, small):
        return attend_gradient(layer, meta, *own[layer], dc, da, da1, weights, others, small)

    def attend_sum(layer, grads, away_x, small):
        name = T1 if layer else T0
        *sends, keep = attend_weights(layer, NEAR_FIRST[name], spots, layer == 1 and hypercube, *entries[layer], *shared[layer], grads, away_x, small)
        begin(name, sends, keep)
        return keep

    def tie(value, other):
        return lax.optimization_barrier((value, other))[0]

    dh = {}
    low_gradient = {}
    dz, df, away, da1, da, dc, small_feed = feed(1, cotangent)
    held = feed_sum(1, dz, df, swap(away))
    own[0] = (own_first, swap(tie(own_handed, held)))
    dh[1], low_gradient[1], grads, away, small = attend(1, tie(dc, held), da, da1, small_feed)
    dh_one_x = swap(low_gradient[1])
    attend_away_x = swap(away)
    grad, _ = boundary(3, low_gradient[1], held)
    dz, df, away, da1, da, dc, small_feed = feed(0, grad)
    dz, dh_one_x, y_last_x = lax.optimization_barrier((dz, dh_one_x, y_last_x))
    grads, away = boundary(4, tie(grads, dz), away)
    feed_away_x = swap(away)
    held = attend_sum(1, grads, attend_away_x, small)
    dz, _ = boundary(5, tie(dz, held), held)
    held = feed_sum(0, dz, df, feed_away_x)
    dc, _ = boundary(6, tie(dc, held), held)
    dh[0], low_gradient[0], grads, away, small = attend(0, dc, da, da1, small_feed)
    grads, away = boundary(7, grads, away)
    held = attend_sum(0, grads, swap(away), small)
    def outputs_of_rows(y_first, y_last_x, y_second, dh, dh_one_x, low):
        layer_out = jnp.stack([jnp.where(first, y_first[0], y_last_x[0]), jnp.where(first, y_first[1], y_second[0])])
        dh_zero_x = swap(low)
        input_grad = jnp.stack([jnp.where(first, dh[0], widen(dh_one_x)), jnp.where(first, widen(dh_zero_x), dh[1])])
        return layer_out, input_grad

    pieces_of_rows = (y_first, y_last_x, y_second, dh, dh_one_x, low_gradient[0])
    if hypercube:
        for turn in range(8, len(SCHEDULE)):
            if turn == 10:
                layer_out, input_grad = outputs_of_rows(*pieces_of_rows)
                pieces_of_rows = (layer_out, input_grad)
            pieces_of_rows, held = boundary(turn, pieces_of_rows, held)
        layer_out, input_grad = pieces_of_rows
        order = (F0, F1, T0, T1)
        done = finish(groups, width, hidden, [results[name] for name in order] + [swap(results[name]) for name in order])
        query_grad, keys_grad, value_grad, mixer_grad, inner_grad, outer_grad, lines, wide_line = done
        height = width // groups
        small = [lines[index, :height] for index in range(8)]
        small_wide = wide_line[0, : hidden // groups]
    else:
        layer_out, input_grad = outputs_of_rows(*pieces_of_rows)

        def scatter(value):
            return lax.psum_scatter(value, "dp", scatter_dimension=0, tiled=True).astype(F32)

        found = []
        for layer in (1, 0):
            outer_part, inner_part = (value[0] for value in moving["f", layer])
            attend = moving["t", layer][0][0]
            half = width // 2
            outer_half = jnp.concatenate([outer_part[:, :half], outer_part[:, half:]], axis=0)
            parts = [scatter(outer_half), scatter(inner_part[:width]), scatter(inner_part[width:])]
            parts += [scatter(attend[:width]), scatter(attend[width : 2 * width])]
            lines = attend[2 * width :].astype(F32)
            parts += [scatter(lines[index]) for index in range(8)] + [scatter(lines[8:12].reshape(-1))]
            found.append(parts)
        mine = [jnp.where(first, b, a) for a, b in zip(*found)]
        back = [swap(jnp.where(first, a, b)) for a, b in zip(found[0][:5], found[1][:5])]
        low = [jnp.where(first, a, b) for a, b in zip(mine, back)]
        high = [jnp.where(first, b, a) for a, b in zip(mine, back)]
        outer_grad = jnp.concatenate([low[0], high[0]], axis=1)
        inner_grad = jnp.concatenate([low[1], low[2], high[1], high[2]], axis=1)
        query_grad, keys_grad, value_grad, mixer_grad = (low[3], low[4], high[3], high[4])
        small, small_wide = (mine[5:13], mine[13])
    second_gain_grad, second_shift_grad, outer_offset_grad, first_gain_grad, first_shift_grad, mixer_offset_grad = small[:6]
    outputs = (
        layer_out, input_grad, query_grad, small[6], keys_grad, value_grad, small[7], mixer_grad, mixer_offset_grad,
        first_gain_grad, first_shift_grad, inner_grad, small_wide, outer_grad, outer_offset_grad, second_gain_grad,
        second_shift_grad,
    )
    return tuple(piece[None] for piece in outputs)


def solution(mesh):
    matrix = P("section", None, None)
    vector = P("section", None)
    in_specs = (
        P("dp", None, None), P("dp", None, None), P("dp"), P("dp"), P("dp", None), matrix, vector, matrix, matrix, vector,
        matrix, vector, vector, vector, matrix, vector, matrix, vector, vector, vector,
    )
    rows = P("section", "dp", None, None)
    grad = P("section", "dp", None)
    small = P("section", "dp")
    out_specs = (rows, rows, grad, small, grad, grad, small, grad, small, small, small, grad, small, grad, small, small, small)
    return jax.shard_map(per_device, mesh=mesh, in_specs=in_specs, out_specs=out_specs, check_vma=False)
```

```python
import functools
import jax
import jax.numpy as jnp
from jax import lax
from jax.experimental import pallas as pl
from jax.experimental.pallas import tpu as pltpu
from jax.sharding import PartitionSpec as P

HEADS = 12
HEAD_DIM = 64
BUCKET = 64
PAIR = 2 * HEAD_DIM
masked_score = -1000000000.0
norm_epsilon = 1e-06
F32 = jnp.float32
BF16 = jnp.bfloat16
CHUNK = 16
FFN_TILE = 512
ATT_UNROLL = 3


def rows_times(left, right):
    return lax.dot_general(left, right, (((1,), (0,)), ((), ())), preferred_element_type=F32)


def rows_times_transposed(left, right):
    return lax.dot_general(left, right, (((1,), (1,)), ((), ())), preferred_element_type=F32)


def transposed_times(left, right):
    return lax.dot_general(left, right, (((0,), (0,)), ((), ())), preferred_element_type=F32)


def slot_facts(block, span_rows, place, meta, micro):
    bucket_ref, count_ref, lengths_ref = meta
    bucket = bucket_ref[micro]
    count = count_ref[micro]

    def length_of(slot):
        return jnp.where(slot < count, lengths_ref[micro, slot], 0)

    if span_rows == 2 * BUCKET:
        return (jnp.full_like(place, block), place, jnp.full_like(place, length_of(block)))
    short = bucket == 0
    first = 3 * block
    slot_short = first + place // BUCKET
    length_short = jnp.where(
        place < BUCKET,
        length_of(first),
        jnp.where(place < 2 * BUCKET, length_of(first + 1), length_of(first + 2)),
    )
    slot = jnp.where(short, slot_short, block)
    inner = jnp.where(short, place % BUCKET, place)
    length = jnp.where(short, length_short, length_of(block))
    return (slot, inner, length)


def fill_masks(span_rows, row_count, meta, micro, bias_ref, valid_ref, keys_down=False):
    for block in range(row_count // span_rows):
        row_place = lax.broadcasted_iota(jnp.int32, (span_rows, 1), 0)
        row_slot, row_inner, row_length = slot_facts(block, span_rows, row_place, meta, micro)
        rows = slice(block * span_rows, (block + 1) * span_rows)
        if bias_ref is not None:
            other_place = lax.broadcasted_iota(jnp.int32, (1, span_rows), 1)
            other_slot, other_inner, other_length = slot_facts(block, span_rows, other_place, meta, micro)
            if keys_down:
                allowed = other_slot == jnp.where(row_inner < row_length, row_slot, -1)
            else:
                allowed = row_slot == jnp.where(other_inner < other_length, other_slot, -1)
            allowed = allowed | (row_place == other_place)
            bias_ref[rows, 0:span_rows] = jnp.where(allowed, 0.0, masked_score)
        if valid_ref is not None:
            valid_ref[rows, :] = jnp.where(row_inner < row_length, 1.0, 0.0)


def by_span(meta, micro, body):
    even = meta[0][micro] == 1

    @pl.when(even)
    def _():
        body(2 * BUCKET)

    @pl.when(jnp.logical_not(even))
    def _():
        body(3 * BUCKET)


def attend_forward(span_rows, row_count, q_ref, k_ref, v_ref, bias_ref, c_ref):
    blocks = row_count // span_rows

    def one_pair(pair, carry):
        columns = pl.ds(pl.multiple_of(pair * PAIR, PAIR), PAIR)
        lane = lax.broadcasted_iota(jnp.int32, (span_rows, PAIR), 1)
        first_half = lane < HEAD_DIM
        weights = []
        for block in range(blocks):
            rows = slice(block * span_rows, (block + 1) * span_rows)
            query = q_ref[rows, columns] * jnp.asarray(HEAD_DIM ** (-0.5), BF16)
            keys = k_ref[rows, columns]
            zero = jnp.zeros_like(keys)
            bias = bias_ref[rows, 0:span_rows]
            for mine in (first_half, jnp.logical_not(first_half)):
                scores = rows_times_transposed(query, jnp.where(mine, keys, zero)) + bias
                top = jnp.max(scores, axis=-1, keepdims=True)
                weights.append(jnp.exp(scores - top).astype(BF16))
        for block in range(blocks):
            rows = slice(block * span_rows, (block + 1) * span_rows)
            value = v_ref[rows, columns]
            one = jnp.ones_like(value)
            left = rows_times(weights[2 * block], jnp.where(first_half, value, one))
            right = rows_times(weights[2 * block + 1], jnp.where(first_half, one, value))
            above = jnp.where(first_half, left, right)
            below = pltpu.roll(jnp.where(first_half, right, left), HEAD_DIM, 1)
            c_ref[rows, columns] = (above / below).astype(BF16)
        return carry

    lax.fori_loop(0, HEADS // 2, one_pair, 0, unroll=ATT_UNROLL)


def row_moments(values):
    center = jnp.mean(values, axis=-1, keepdims=True)
    centred = values - center
    spread = jnp.mean(centred * centred, axis=-1, keepdims=True)
    return centred, lax.rsqrt(spread + norm_epsilon)


def over_chunks(row_count, body, rows=CHUNK, group=6):
    def step(index, carry):
        for inner in range(group):
            start = pl.multiple_of(index * (rows * group) + inner * rows, rows)
            body(pl.ds(start, rows))
        return carry

    lax.fori_loop(0, row_count // (rows * group), step, 0)


def over_chunks_with_sums(row_count, body, sums_ref, rows=CHUNK, group=6):
    def step(index, carry):
        total = None
        for inner in range(group):
            start = pl.multiple_of(index * (rows * group) + inner * rows, rows)
            terms = [fold_rows(term) for term in body(pl.ds(start, rows))]
            total = terms if total is None else [a + b for a, b in zip(total, terms)]
        for place, term in enumerate(total):
            sums_ref[place] += term
        return carry

    lax.fori_loop(0, row_count // (rows * group), step, 0)


def fold_rows(values):
    return jnp.sum(values.reshape(values.shape[0] // 8, 8, values.shape[1]), axis=0)


def gelu_with_slope(values):
    cumulative = 0.5 + 0.5 * lax.erf(values * (0.5 ** 0.5))
    density = jnp.exp(values * values * -0.5) * 0.3989422804014327
    return values * cumulative, cumulative + values * density


ANY = pl.BlockSpec(memory_space=pl.ANY)
VM = pl.BlockSpec(memory_space=pltpu.VMEM)
SM = pl.BlockSpec(memory_space=pltpu.SMEM)
VMEM_LIMIT = 64_500 * 1024
S = jax.ShapeDtypeStruct
V = pltpu.VMEM
B_QUERY, B_VALUE, B_MIXER, GAIN_ONE, SHIFT_ONE, B_OUTER, GAIN_TWO, SHIFT_TWO = range(8)
QUERY, FIRST_SUM, SECOND_SUM, SLOPE = (0, 3, 4, 5)
ACTIVE, MIDDLE, CONTEXT = (0, 4, 5)
X_BIT, Y_BIT, NEAR_BIT, FAR_BIT = (0, 1, 2, 3)
SMALL_ROWS = 16


class Loads:
    def __init__(self, semaphores):
        self.semaphores = semaphores
        self.copies = {}

    def start(self, name, source, target, other=None, take_other=None):
        semaphore = self.semaphores.at[len(self.copies)]
        copy = pltpu.make_async_copy(source, target, semaphore)
        self.copies[name] = copy
        if other is None:
            copy.start()
            return
        second = pltpu.make_async_copy(other, target, semaphore)

        @pl.when(take_other)
        def _():
            second.start()

        @pl.when(jnp.logical_not(take_other))
        def _():
            copy.start()

    def wait(self, *names):
        for name in names:
            self.copies[name].wait()


class Stores:
    def __init__(self, semaphores):
        self.semaphores = semaphores
        self.copies = []

    def start(self, source, target):
        copy = pltpu.make_async_copy(source, target, self.semaphores.at[len(self.copies)])
        copy.start()
        self.copies.append(copy)

    def wait(self):
        for copy in self.copies:
            copy.wait()


def run_kernel(kernel, outs, out_specs, in_specs, scratch, loads, stores, flops, bytes_moved, name):
    return pl.pallas_call(
        kernel,
        out_shape=outs,
        in_specs=in_specs,
        out_specs=out_specs,
        scratch_shapes=list(scratch) + [pltpu.SemaphoreType.DMA((loads,)), pltpu.SemaphoreType.DMA((stores,))],
        compiler_params=pltpu.CompilerParams(vmem_limit_bytes=VMEM_LIMIT),
        cost_estimate=pl.CostEstimate(flops=1000, bytes_accessed=1000, transcendentals=0),
        name=name,
    )


def spot_of(near_first, dest):
    relative = jnp.bitwise_xor(dest, lax.axis_index("dp"))

    def bit(index):
        return jnp.bitwise_and(lax.shift_right_logical(relative, index), 1)

    first = lax.axis_index("section") == 0
    lead = jnp.where(first, bit(X_BIT), bit(Y_BIT))
    follow = jnp.where(first, bit(Y_BIT), bit(X_BIT))
    if near_first:
        return bit(NEAR_BIT) * 8 + lead * 4 + follow * 2 + bit(FAR_BIT)
    return lead * 8 + follow * 4 + bit(NEAR_BIT) * 2 + bit(FAR_BIT)


def step_bits(near_first):
    cross = [(X_BIT, Y_BIT), (Y_BIT, X_BIT)]
    if near_first:
        return [(NEAR_BIT, NEAR_BIT)] + cross + [(FAR_BIT, FAR_BIT)]
    return cross + [(NEAR_BIT, NEAR_BIT), (FAR_BIT, FAR_BIT)]


def forward_matrix_loads(loads, hidden_start, weights, others, take_other, targets):
    names = ("wq", "wk", "wv", "wm", "wi", "wo")

    def begin(index):
        other = None if others is None else others[index]
        loads.start(names[index], weights[index].at[0], targets[index], other, take_other)

    def load(step):
        if step == 0:
            hidden_start()
            for index in range(3):
                begin(index)
            return
        if step == 1:
            loads.wait("h")
        loads.wait(names[step - 1])
        if step <= 3:
            begin(step + 2)

    return load


def forward_body(load, store, meta, micros, vec, outs, refs):
    h_s, wq_s, wk_s, wv_s, wm_s, wi_s, wo_s, qkv_s, c_s, ml_s, a1_s, a2_s, u_s, gp_s, y_s, m_s, f0_s, e0_s, e1_s, bias_s, valid_s, bi_s = refs
    y_o, own_o, shared_o = outs
    rows, width = h_s.shape
    hidden = wi_s.shape[1]
    each = rows // len(micros)
    parts = [slice(place * each, (place + 1) * each) for place in range(len(micros))]

    def send(source, plane, shared=False):
        for place, part in enumerate(parts):
            target = shared_o.at[place] if shared else own_o[place]
            for index in range(source.shape[1] // width):
                store.start(source.at[part, index * width : (index + 1) * width], target.at[plane + index])

    load(0)
    for part, micro in zip(parts, micros):
        by_span(meta, micro, lambda span: fill_masks(span, each, meta, micro, bias_s.at[part], valid_s.at[part]))
    load(1)
    qkv_s[0] = (rows_times(h_s[...], wq_s[...]) + vec(B_QUERY)).astype(BF16)
    load(2)
    qkv_s[1] = rows_times(h_s[...], wk_s[...]).astype(BF16)
    load(3)
    qkv_s[2] = (rows_times(h_s[...], wv_s[...]) + vec(B_VALUE)).astype(BF16)
    for place, part in enumerate(parts):
        store.start(qkv_s.at[:, part], own_o[place].at[QUERY : QUERY + 3])
    for part, micro in zip(parts, micros):
        by_span(
            meta, micro,
            lambda span: attend_forward(
                span, each, qkv_s.at[0, part], qkv_s.at[1, part], qkv_s.at[2, part], bias_s.at[part], c_s.at[part]
            ),
        )
    send(c_s, CONTEXT, True)
    load(4)
    f0_s[...] = rows_times(c_s[...], wm_s[...])
    offset_mixer, gain_one, shift_one = (vec(B_MIXER), vec(GAIN_ONE), vec(SHIFT_ONE))

    def first_norm(part):
        total = h_s[part, :].astype(F32) + (f0_s[part, :] + offset_mixer)
        a1_s[part, :] = total.astype(BF16)
        centred, scale = row_moments(total)
        middle = centred * scale * gain_one + shift_one
        m_s[part, :] = middle
        ml_s[part, :] = middle.astype(BF16)

    over_chunks(rows, first_norm)
    send(a1_s, FIRST_SUM)
    send(ml_s, MIDDLE, True)
    load(5)
    tile = FFN_TILE
    tiles = hidden // tile

    def project(buffer, which):
        columns = pl.ds(pl.multiple_of(which * tile, tile), tile)
        buffer[...] = rows_times(ml_s[...], wi_s[:, columns])

    def activate(buffer, which):
        columns = pl.ds(pl.multiple_of(which * tile, tile), tile)
        offset = bi_s[0:1, columns]
        for start in range(0, rows, 32):
            part = slice(start, start + 32)
            value, slope = gelu_with_slope(buffer[part, :] + offset)
            u_s[part, columns] = value.astype(BF16)
            gp_s[part, columns] = slope.astype(BF16)

    for index in range(hidden // width):
        bi_s[0:1, index * width : (index + 1) * width] = vec(8 + index)
    project(e0_s, 0)

    def two_tiles(index, carry):
        project(e1_s, 2 * index + 1)
        activate(e0_s, 2 * index)
        project(e0_s, jnp.minimum(2 * index + 2, tiles - 1))
        activate(e1_s, 2 * index + 1)
        return carry

    lax.fori_loop(0, tiles // 2, two_tiles, 0)
    send(u_s, ACTIVE, True)
    send(gp_s, SLOPE)
    load(6)
    f0_s[...] = rows_times(u_s[...], wo_s[...])
    offset_outer, gain_two, shift_two = (vec(B_OUTER), vec(GAIN_TWO), vec(SHIFT_TWO))

    def second_norm(part):
        total = m_s[part, :] + (f0_s[part, :] + offset_outer)
        a2_s[part, :] = total.astype(BF16)
        centred, scale = row_moments(total)
        y_s[part, :] = ((centred * scale * gain_two + shift_two) * valid_s[part, :]).astype(BF16)

    over_chunks(rows, second_norm)
    for place, part in enumerate(parts):
        store.start(y_s.at[part], y_o.at[place])
    send(a2_s, SECOND_SUM)
    store.wait()


def first_forward_kernel(
    micro_count, bucket, count, lengths, tok, wq, wk, wv, wm, wi, wo, bq, bv, bm, g1, s1, bo, g2, s2, bi, *rest
):
    y_o, shared_o = rest[:2]
    own_o = rest[2 : 2 + micro_count]
    packed_o, vec_o = rest[2 + micro_count : 4 + micro_count]
    *refs, hold_s, low_s, pack_sem, in_sem, out_sem = rest[4 + micro_count :]
    h_s, wq_s, wk_s, wv_s, wm_s, wi_s, wo_s = refs[:7]
    width = h_s.shape[1]
    gather = pltpu.make_async_copy(wm.at[0], hold_s, pack_sem.at[0])
    hand = pltpu.make_async_copy(hold_s, packed_o.at[0:width], pack_sem.at[1])
    hand_low = pltpu.make_async_copy(low_s, packed_o.at[width : width + VECTOR_ROWS], pack_sem.at[2])
    vec_o[...] = jnp.zeros_like(vec_o)
    for place, vector in enumerate((bq, bv, bm, g1, s1, bo, g2, s2)):
        vec_o[place : place + 1, :] = vector[...]
    for index in range(bi.shape[1] // width):
        vec_o[8 + index : 9 + index, :] = bi[:, index * width : (index + 1) * width]
    high = vec_o[...].astype(BF16)
    low_s[0:16, :] = high
    low_s[16:32, :] = (vec_o[...] - high.astype(F32)).astype(BF16)
    hand_low.start()

    @pl.when(lax.axis_index("section") != 0)
    def _():
        gather.start()
        gather.wait()
        hand.start()

    @pl.when(lax.axis_index("section") == 0)
    def _():
        loads = Loads(in_sem)
        each = h_s.shape[0] // micro_count

        def hidden_start():
            for micro in range(1, micro_count):
                loads.start(("h", micro), tok.at[micro], h_s.at[micro * each : (micro + 1) * each])
            loads.start("h", tok.at[0], h_s.at[0:each])

        inner_load = forward_matrix_loads(
            loads, hidden_start, (wq, wk, wv, wm, wi, wo), None, None, (wq_s, wk_s, wv_s, wm_s, wi_s, wo_s)
        )

        def load(step):
            if step == 1:
                for micro in range(1, micro_count):
                    loads.wait(("h", micro))
            if step == 4:
                gather.start()
            if step == 6:
                gather.wait()
                hand.start()
            inner_load(step)

        forward_body(
            load, Stores(out_sem), (bucket, count, lengths), tuple(range(micro_count)),
            lambda place: vec_o[place : place + 1, :], (y_o, own_o, shared_o), refs,
        )

    hand.wait()
    hand_low.wait()


def second_forward_kernel(
    bucket, count, lengths, y_own, y_other, wq, wk, wv, wm, wi, wo, xq, xk, xv, xi, xo, packed, vec_own,
    y_o, shared_o, own_o, *scratch
):
    *refs, other_s, vec_s, in_sem, out_sem = scratch
    h_s, wq_s, wk_s, wv_s, wm_s, wi_s, wo_s = refs[:7]
    section = lax.axis_index("section")
    first = section == 0
    width = h_s.shape[1]
    loads = Loads(in_sem)
    load = forward_matrix_loads(
        loads, lambda: loads.start("h", y_other.at[section], h_s, y_own.at[section], first), (wq, wk, wv, wm, wi, wo),
        (xq.at[0], xk.at[0], xv.at[0], packed.at[0:width], xi.at[0], xo.at[0]), first, (wq_s, wk_s, wv_s, wm_s, wi_s, wo_s),
    )
    vectors = Vectors(loads, packed, vec_own, other_s, first)

    def ready(step):
        load(step)
        if step == 0:
            loads.wait("vectors")
            for place in range(12):
                vec_s[place : place + 1, :] = vectors(place)

    forward_body(
        ready, Stores(out_sem), (bucket, count, lengths), (section,), lambda place: vec_s[place : place + 1, :],
        (y_o, (own_o,), shared_o), refs,
    )


def forward_shapes(micro_count, each, width, hidden):
    rows = micro_count * each
    flat = (rows, width)
    wide = (rows, hidden)
    square = (width, width)

    def out(*tail):
        return (micro_count,) + tail

    wides = hidden // width
    outs = (S(out(each, width), BF16), S(out(wides + 2, each, width), BF16)) + (S((wides + 5, each, width), BF16),) * micro_count
    scratch = [
        V(flat, BF16), V(square, BF16), V(square, BF16), V(square, BF16), V(square, BF16), V((width, hidden), BF16),
        V((hidden, width), BF16), V((3,) + flat, BF16), V(flat, BF16), V(flat, BF16), V(flat, BF16), V(flat, BF16),
        V(wide, BF16), V(wide, BF16), V(flat, BF16), V(flat, F32), V(flat, F32), V((rows, FFN_TILE), F32),
        V((rows, FFN_TILE), F32), V((rows, 3 * BUCKET), F32), V((rows, 1), F32),
        V((8, hidden), F32),
    ]
    flops = 2 * rows * width * (4 * width + 2 * hidden)
    return outs, scratch, flops


def first_forward(meta, tokens, weights, vectors, bi):
    micro_count, each, width = tokens.shape
    outs, scratch, flops = forward_shapes(micro_count, each, width, bi.shape[1])
    outs = outs + (S((width + VECTOR_ROWS, width), BF16), S((16, width), F32))
    scratch = scratch + [V((width, width), BF16), V((VECTOR_ROWS, width), BF16), pltpu.SemaphoreType.DMA((3,))]
    return run_kernel(
        functools.partial(first_forward_kernel, micro_count), outs, [ANY] * (3 + micro_count) + [VM], [SM] * 3 + [ANY] * 7 + [VM] * 9,
        scratch, 6 + micro_count, 14 * micro_count, flops, 40_000_000, "first_forward",
    )(*meta, tokens, *weights, *vectors, bi)


def second_forward(meta, y_own, y_other, weights, others, vec_own):
    _, each, width = y_own.shape
    outs, scratch, flops = forward_shapes(1, each, width, weights[4].shape[2])
    scratch = scratch + [V((VECTOR_ROWS, width), BF16), V((16, width), F32)]
    return run_kernel(
        second_forward_kernel, outs, [ANY] * 3, [SM] * 3 + [ANY] * 14 + [VM], scratch, 8, 14, flops, 25_000_000,
        "second_forward",
    )(*meta, y_own, y_other, *weights, *others, vec_own)


VECTOR_ROWS = 32


class Vectors:
    def __init__(self, loads, packed, own, other_s, take_other):
        width = packed.shape[1]
        self.own = own
        self.other_s = other_s
        self.take_other = take_other
        loads.start("vectors", packed.at[width : width + VECTOR_ROWS], other_s)

    def __call__(self, place):
        other = self.other_s[place : place + 1, :].astype(F32) + self.other_s[16 + place : 17 + place, :].astype(F32)
        return jnp.where(self.take_other, other, self.own[place : place + 1, :])


def norm_backward(grad, total, gain):
    centred, scale = row_moments(total)
    unit = centred * scale
    spread = grad * gain
    first = jnp.mean(spread, axis=-1, keepdims=True)
    second = jnp.mean(spread * unit, axis=-1, keepdims=True)
    return (spread - first - unit * second) * scale, grad * unit


def layer_of(layer):
    return lax.axis_index("section") != layer


def load_planes(layer, loads, name, own, other, plane, target):
    width = own.shape[2]
    take_other = lax.axis_index("section") == 1
    for index in range(target.shape[1] // width):
        part = target if target.shape[1] == width else target.at[:, index * width : (index + 1) * width]
        received = None if layer == 1 else other.at[plane + index]
        loads.start((name, index), own.at[plane + index], part, received, take_other)


def feed_kernel(
    layer, bucket, count, lengths, g, own, own_x, wo, wo_x, wi, wi_x, wm, packed, vec_own,
    dz_o, df_o, away_o, da1_o, da_o, dc_o, small_o,
    g_s, a2_s, gp_s, a1_s, wo_s, wi_s, wm_s, da2_s, dz_s, df_s, dm_s, da1_s, da_s, dc_s, e0_s, e1_s, valid_s, sums_s, wide_s, other_s, in_sem, out_sem,
):
    section = lax.axis_index("section")
    rows, width = a2_s.shape
    hidden = df_s.shape[1]
    loads = Loads(in_sem)
    store = Stores(out_sem)
    wides = range(hidden // width)
    loads.start("g", g.at[section] if layer == 1 else g, g_s)
    load_planes(layer, loads, "a2", own, own_x, SECOND_SUM, a2_s)
    loads.start("wo", wo.at[0], wo_s, wo_x.at[0], layer_of(layer))
    meta = (bucket, count, lengths)
    by_span(meta, section, lambda span: fill_masks(span, rows, meta, section, None, valid_s))
    sums_s[...] = jnp.zeros_like(sums_s)
    vectors = Vectors(loads, packed, vec_own, other_s, layer_of(layer))
    loads.wait("g", ("a2", 0), "vectors")
    gain_two, gain_one = (vectors(GAIN_TWO), vectors(GAIN_ONE))
    load_planes(layer, loads, "gp", own, own_x, SLOPE, gp_s)
    loads.start("wi", wi.at[0], wi_s, wi_x.at[0], layer_of(layer))

    def second_norm(part):
        grad = g_s[part, :].astype(F32) * valid_s[part, :]
        moved, gained = norm_backward(grad, a2_s[part, :].astype(F32), gain_two)
        da2_s[part, :] = moved
        low = moved.astype(BF16)
        dz_s[part, :] = low
        return gained, grad, low.astype(F32)

    over_chunks_with_sums(rows, second_norm, sums_s.at[0:3])
    half = width // 2
    store.start(dz_s.at[:, pl.ds(pl.multiple_of(section * half, half), half)], dz_o)
    store.start(dz_s.at[:, pl.ds(pl.multiple_of((1 - section) * half, half), half)], away_o.at[2, :, 0:half])
    tile = FFN_TILE
    tiles = hidden // tile

    def project(buffer, which):
        columns = pl.ds(pl.multiple_of(which * tile, tile), tile)
        buffer[...] = rows_times_transposed(dz_s[...], wo_s[columns, :])

    def slope(buffer, which):
        columns = pl.ds(pl.multiple_of(which * tile, tile), tile)
        total = None
        for start in range(0, rows, 32):
            part = slice(start, start + 32)
            low_part = (buffer[part, :] * gp_s[part, columns].astype(F32)).astype(BF16)
            df_s[part, columns] = low_part
            term = fold_rows(low_part.astype(F32))
            total = term if total is None else total + term
        wide_s[:, columns] = total

    loads.wait("wo")
    load_planes(layer, loads, "a1", own, own_x, FIRST_SUM, a1_s)
    loads.start("wm", wm.at[0], wm_s, packed.at[0:width], layer_of(layer))
    project(e0_s, 0)
    for index in wides:
        loads.wait(("gp", index))

    def two_tiles(index, carry):
        project(e1_s, 2 * index + 1)
        slope(e0_s, 2 * index)
        project(e0_s, jnp.minimum(2 * index + 2, tiles - 1))
        slope(e1_s, 2 * index + 1)
        return carry

    lax.fori_loop(0, tiles // 2, two_tiles, 0)
    half = hidden // 2
    store.start(df_s.at[:, pl.ds(pl.multiple_of(section * half, half), half)], df_o)
    for index in range(2):
        start = pl.multiple_of((1 - section) * half + index * width, width)
        store.start(df_s.at[:, pl.ds(start, width)], away_o.at[index])
    loads.wait("wi")
    dm_s[...] = rows_times_transposed(df_s[...], wi_s[...])
    loads.wait(("a1", 0))

    def first_norm(part):
        grad = dm_s[part, :] + da2_s[part, :]
        moved, gained = norm_backward(grad, a1_s[part, :].astype(F32), gain_one)
        da1_s[part, :] = moved
        low_part = moved.astype(BF16)
        da_s[part, :] = low_part
        return gained, grad, low_part.astype(F32)

    over_chunks_with_sums(rows, first_norm, sums_s.at[3:6])
    store.start(da1_s, da1_o)
    store.start(da_s, da_o)
    for index in range(6):
        small_o[index : index + 1, :] = jnp.sum(sums_s[index], axis=0, keepdims=True)
    inner_sum = jnp.sum(wide_s[...], axis=0, keepdims=True)
    for index in range(hidden // width):
        small_o[8 + index : 9 + index, :] = inner_sum[:, index * width : (index + 1) * width]
    loads.wait("wm")
    dc_s[...] = rows_times_transposed(da_s[...], wm_s[...]).astype(BF16)
    store.start(dc_s, dc_o)
    store.wait()


def feed_gradient(layer, meta, g, own, own_x, weights, others, vec_own):
    _, rows, width = own.shape
    hidden = weights[4].shape[2]
    flat = (rows, width)
    _, _, _, xi, xo, packed = others
    return run_kernel(
        functools.partial(feed_kernel, layer),
        (S((rows, width // 2), BF16), S((rows, hidden // 2), BF16), S((3,) + flat, BF16), S(flat, F32), S(flat, BF16), S(flat, BF16), S((SMALL_ROWS, width), F32)),
        [ANY] * 6 + [VM], [SM] * 3 + [ANY] * 9 + [VM],
        [
            V(flat, g.dtype), V(flat, BF16), V((rows, hidden), BF16), V(flat, BF16), V((hidden, width), BF16), V((width, hidden), BF16),
            V((width, width), BF16), V(flat, F32), V(flat, BF16), V((rows, hidden), BF16), V(flat, F32), V(flat, F32), V(flat, BF16),
            V(flat, BF16), V((rows, FFN_TILE), F32), V((rows, FFN_TILE), F32), V((rows, 1), F32), V((6, 8, width), F32),
            V((8, hidden), F32), V((VECTOR_ROWS, width), BF16),
        ],
        7 + hidden // width, 8, 2 * rows * width * (2 * hidden + width), 25_000_000, "feed_gradient",
    )(*meta, g, own, own_x, weights[5], xo, weights[4], xi, weights[3], packed, vec_own)


def attend_backward(span_rows, row_count, q_ref, k_ref, v_ref, dc_ref, bias_ref, dq_ref, dk_ref, dv_ref):
    blocks = row_count // span_rows
    scale = HEAD_DIM ** (-0.5)

    def one_pair(pair, carry):
        columns = pl.ds(pl.multiple_of(pair * PAIR, PAIR), PAIR)
        lane = lax.broadcasted_iota(jnp.int32, (span_rows, PAIR), 1)
        halves = (lane < HEAD_DIM, lane >= HEAD_DIM)
        for block in range(blocks):
            rows = slice(block * span_rows, (block + 1) * span_rows)
            query = q_ref[rows, columns] * jnp.asarray(scale, BF16)
            keys = k_ref[rows, columns]
            value = v_ref[rows, columns]
            grad = dc_ref[rows, columns]
            zero = jnp.zeros_like(keys)
            bias = bias_ref[rows, 0:span_rows]
            dq = dk = dv = None
            for mine in halves:
                keys_own = jnp.where(mine, keys, zero)
                scores = rows_times_transposed(keys_own, query) + bias
                grad_part = rows_times_transposed(jnp.where(mine, value, zero), grad)
                weight = jnp.exp(scores - jnp.max(scores, axis=0, keepdims=True))
                part = weight * (1.0 / jnp.sum(weight, axis=0, keepdims=True))
                mean = jnp.sum(grad_part * part, axis=0, keepdims=True)
                grad_scores = (part * (grad_part - mean)).astype(BF16)
                terms = (
                    transposed_times(grad_scores, keys_own),
                    rows_times(grad_scores, jnp.where(mine, query, zero)),
                    rows_times(part.astype(BF16), jnp.where(mine, grad, zero)),
                )
                if dq is None:
                    dq, dk, dv = terms
                else:
                    dq, dk, dv = (dq + terms[0], dk + terms[1], dv + terms[2])
            dq_ref[rows, columns] = (dq * scale).astype(BF16)
            dk_ref[rows, columns] = dk.astype(BF16)
            dv_ref[rows, columns] = dv.astype(BF16)
        return carry

    lax.fori_loop(0, HEADS // 2, one_pair, 0)


def attend_kernel(
    layer, bucket, count, lengths, own, own_x, dc, da, da1, wq, wk, wv, xq, xk, xv, small_one,
    dh_o, dlow_o, home_o, away_o, small_o,
    qkv_s, dc_s, da_s, dh_s, dlow_s, wq_s, wk_s, wv_s, dq_s, dk_s, dv_s, bias_s, sums_s, low_s, in_sem, out_sem,
):
    section = lax.axis_index("section")
    rows, width = dc_s.shape
    second = section == 1
    loads = Loads(in_sem)
    received = None if layer == 1 else own_x.at[QUERY : QUERY + 3]
    loads.start("qkv", own.at[QUERY : QUERY + 3], qkv_s, received, second)
    loads.start("dc", dc, dc_s)
    meta = (bucket, count, lengths)
    by_span(meta, section, lambda span: fill_masks(span, rows, meta, section, bias_s, None, True))
    loads.wait("qkv", "dc")
    loads.start("da", da, da_s)
    loads.start("da1", da1, dh_s)
    for name, weight, other, target in (("wq", wq, xq, wq_s), ("wk", wk, xk, wk_s), ("wv", wv, xv, wv_s)):
        loads.start(name, weight.at[0], target, other.at[0], layer_of(layer))
    by_span(
        meta, section,
        lambda span: attend_backward(span, rows, qkv_s.at[0], qkv_s.at[1], qkv_s.at[2], dc_s, bias_s, dq_s, dk_s, dv_s),
    )
    loads.wait("da")
    pairs = ((dq_s, dk_s), (dv_s, da_s))
    for core in range(2):
        @pl.when(section == core)
        def _(core=core):
            for place in range(2):
                pltpu.make_async_copy(pairs[core][place], home_o.at[place], out_sem.at[place]).start()
                pltpu.make_async_copy(
                    pairs[1 - core][place], away_o.at[place * rows : (place + 1) * rows], out_sem.at[2 + place]
                ).start()
    loads.wait("da1", "wq", "wk", "wv")
    dh_s[...] += rows_times_transposed(dq_s[...], wq_s[...])
    dh_s[...] += rows_times_transposed(dk_s[...], wk_s[...])
    dh_s[...] += rows_times_transposed(dv_s[...], wv_s[...])
    sums_s[...] = jnp.zeros_like(sums_s)

    def finish(part):
        dlow_s[part, :] = dh_s[part, :].astype(BF16)
        return dq_s[part, :].astype(F32), dv_s[part, :].astype(F32)

    over_chunks_with_sums(rows, finish, sums_s)
    last = [
        pltpu.make_async_copy(dh_s, dh_o, out_sem.at[4]),
        pltpu.make_async_copy(dlow_s, dlow_o, out_sem.at[5]),
    ]
    for copy in last:
        copy.start()
    small_o[0:6, :] = small_one[0:6, :]
    for index in range(2):
        small_o[6 + index : 7 + index, :] = jnp.sum(sums_s[index], axis=0, keepdims=True)
    small_o[8:16, :] = small_one[8:16, :]
    low_s[...] = small_o[...].astype(BF16)
    smalls = pltpu.make_async_copy(low_s, away_o.at[2 * rows : 2 * rows + SMALL_ROWS], out_sem.at[6])
    smalls.start()
    for place in range(2):
        pltpu.make_async_copy(pairs[0][place], home_o.at[place], out_sem.at[place]).wait()
        pltpu.make_async_copy(
            pairs[1][place], away_o.at[place * rows : (place + 1) * rows], out_sem.at[2 + place]
        ).wait()
    for copy in last:
        copy.wait()
    smalls.wait()


def attend_gradient(layer, meta, own, own_x, dc, da, da1, weights, others, small_one):
    rows, width = da1.shape
    flat = (rows, width)
    square = (width, width)
    return run_kernel(
        functools.partial(attend_kernel, layer),
        (S(flat, F32), S(flat, BF16), S((2,) + flat, BF16), S((2 * rows + SMALL_ROWS, width), BF16), S((SMALL_ROWS, width), F32)),
        [ANY] * 4 + [VM], [SM] * 3 + [ANY] * 11 + [VM],
        [V((3,) + flat, BF16), V(flat, BF16), V(flat, BF16), V(flat, F32), V(flat, BF16)] + [V(square, BF16)] * 3 + [V(flat, BF16)] * 3
        + [V((rows, 3 * BUCKET), F32), V((2, 8, width), F32), V((SMALL_ROWS, width), BF16)],
        7, 7, 6 * rows * width * width, 15_000_000, "attend_gradient",
    )(*meta, own, own_x, dc, da, da1, *weights[:3], *others[:3], small_one)


def by_owner(loads, name, own, other, target):
    rows = target.shape[0] // 2
    section = lax.axis_index("section")
    loads.start((name, 0), own, target.at[pl.ds(pl.multiple_of(section * rows, rows), rows)])
    loads.start((name, 1), other, target.at[pl.ds(pl.multiple_of((1 - section) * rows, rows), rows)])


def both_micros(layer, loads, name, own, other, plane, target, index):
    width = own.shape[3]
    rows = target.shape[0] // 2
    columns = target if target.shape[1] == width else target.at[:, index * width : (index + 1) * width]
    if layer == 1:
        by_owner(loads, (name, index), own.at[0, plane + index], other.at[0, plane + index], columns)
        return
    for micro in range(2):
        part = columns.at[micro * rows : (micro + 1) * rows]
        take_other = lax.axis_index("section") == 1
        loads.start(((name, index), micro), own.at[micro, plane + index], part, other.at[micro, plane + index], take_other)


def wait_both(loads, name, index):
    loads.wait(((name, index), 0), ((name, index), 1))


def put_rows(target, near_first, value, at_row, at_lane, dest):
    spot = 0 if target.shape[0] == 1 else spot_of(near_first, dest)
    rows, lanes = value.shape
    target[spot, at_row : at_row + rows, at_lane : at_lane + lanes] = value.astype(BF16)


def feed_weights_kernel(
    layer, near_first, shared, shared_x, dz, df, away_x,
    outer_o, inner_o, keep_o,
    u_s, ml_s, dz_s, df_s, w_s, in_sem, out_sem,
):
    hidden = u_s.shape[1]
    width = ml_s.shape[1]
    rows = dz.shape[0]
    spots = w_s.shape[0]
    loads = Loads(in_sem)
    store = Stores(out_sem)
    by_owner(loads, "dz", dz, away_x.at[2, :, 0 : width // 2], dz_s)

    def begin_u(index):
        both_micros(layer, loads, "u", shared, shared_x, ACTIVE, u_s, index)

    def begin_inner():
        both_micros(layer, loads, "ml", shared, shared_x, MIDDLE, ml_s, 0)
        for index in range(2):
            columns = slice(index * width, (index + 1) * width)
            by_owner(loads, ("df", index), df.at[:, columns], away_x.at[index], df_s.at[:, columns])

    planes = hidden // width
    begin_u(0)
    begin_u(1)
    loads.wait(("dz", 0), ("dz", 1))
    half_rows = hidden // spots // 2
    split = spots // 2
    for index in range(planes):
        wait_both(loads, "u", index)
        if index + 2 < planes:
            begin_u(index + 2)
        elif index + 2 == planes:
            begin_inner()
        product = transposed_times(u_s[:, index * width : (index + 1) * width], dz_s[...])
        block = min(half_rows, width)
        for inner in range(width // block):
            row = index * width + inner * block
            dest, offset = divmod(row, 2 * half_rows)
            side, at_row = divmod(offset, half_rows)
            put_rows(w_s, near_first, product[inner * block : (inner + 1) * block, :], at_row, side * (width // 2), dest)
    store.start(w_s.at[split:spots, 0:half_rows], outer_o)
    store.start(w_s.at[0 : spots - split, 0:half_rows], keep_o.at[:, 0:half_rows])
    wait_both(loads, "ml", 0)
    height = width // spots
    for side in range(2):
        wait_both(loads, "df", side)
        product = transposed_times(ml_s[...], df_s[:, side * width : (side + 1) * width])
        for dest in range(spots):
            put_rows(w_s, near_first, product[dest * height : (dest + 1) * height, :], half_rows + side * height, 0, dest)
    rest = slice(half_rows, half_rows + 2 * height)
    store.start(w_s.at[split:spots, rest], inner_o)
    store.start(w_s.at[0 : spots - split, rest], keep_o.at[:, rest])
    store.wait()


def feed_weights(layer, near_first, spots, shared, shared_x, dz, df, away_x):
    rows, width = shared.shape[2:]
    hidden = 2 * df.shape[1]
    total = hidden // spots // 2 + 2 * (width // spots)
    split = spots - spots // 2
    outs = (
        S((split, hidden // spots // 2, width), BF16), S((split, 2 * (width // spots), width), BF16), S((split, total, width), BF16),
    )
    return run_kernel(
        functools.partial(feed_weights_kernel, layer, near_first), outs, [ANY] * 3, [ANY] * 5,
        [
            V((2 * rows, hidden), BF16), V((2 * rows, width), BF16), V((2 * rows, width // 2), BF16), V((2 * rows, hidden // 2), BF16),
            V((spots, total, width), BF16),
        ],
        8 + 2 * (hidden // width), 4, 4 * rows * width * hidden, 18_000_000, "feed_weights",
    )(shared, shared_x, dz, df, away_x)


def attend_weights_kernel(
    layer, near_first, h, h_x, shared, shared_x, grads, away_x, small,
    *rest
):
    *sends_o, keep_o, left_s, right_s, w_s, small_s, in_sem, out_sem = rest
    section = lax.axis_index("section")
    second = section == 1
    rows, width = grads.shape[1:]
    spots = w_s.shape[0]
    loads = Loads(in_sem)
    store = Stores(out_sem)
    for micro in range(2):
        part = slice(micro * rows, (micro + 1) * rows)
        loads.start(("h", micro), h.at[micro], left_s.at[0, part], h_x.at[micro], second)
    by_owner(loads, "g", grads.at[0], away_x.at[0:rows], right_s.at[0])
    if layer == 0:
        for micro in range(2):
            part = slice(micro * rows, (micro + 1) * rows)
            loads.start(("c", micro), h.at[micro], left_s.at[1, part], shared_x.at[micro, CONTEXT], second)
    else:
        for place, (plain, context) in enumerate(((h, shared), (h, shared_x))):
            micro = section if place == 0 else 1 - section
            part = left_s.at[1, pl.ds(pl.multiple_of(micro * rows, rows), rows)]
            loads.start(("c", place), plain.at[micro], part, context.at[0, CONTEXT], second)
    by_owner(loads, "f", grads.at[1], away_x.at[rows : 2 * rows], right_s.at[1])
    height = width // spots
    loads.start("small", away_x.at[2 * rows : 2 * rows + SMALL_ROWS], small_s)
    loads.wait("small")
    low = (small[...] + small_s[...].astype(F32)).astype(BF16)
    for spot in range(spots):
        w_s[spot, 2 * height : 2 * height + SMALL_ROWS, :] = low
    for side, name in enumerate(("h", "c")):
        grad_name = ("g", "f")[side]
        loads.wait((name, 0), (name, 1), (grad_name, 0), (grad_name, 1))
        product = transposed_times(left_s[side], right_s[side])
        for dest in range(spots):
            put_rows(w_s, near_first, product[dest * height : (dest + 1) * height, :], side * height, 0, dest)
    split = spots // 2
    store.start(w_s.at[0 : spots - split], keep_o)
    cuts = (0, 2 * height + SMALL_ROWS) if len(sends_o) == 1 else (0, height, 2 * height + SMALL_ROWS)
    for place, send_o in enumerate(sends_o):
        store.start(w_s.at[split:spots, cuts[place] : cuts[place + 1]], send_o)
    store.wait()


def attend_weights(layer, near_first, spots, in_pieces, h, h_x, shared, shared_x, grads, away_x, small):
    rows, width = grads.shape[1:]
    height = width // spots
    total = 2 * height + SMALL_ROWS
    split = spots - spots // 2
    heights = (height, height + SMALL_ROWS) if in_pieces else (total,)
    outs = tuple(S((split, part, width), BF16) for part in heights + (total,))
    return run_kernel(
        functools.partial(attend_weights_kernel, layer, near_first), outs, [ANY] * len(outs), [ANY] * 6 + [VM],
        [V((2, 2 * rows, width), BF16), V((2, 2 * rows, width), BF16), V((spots, total, width), BF16), V((SMALL_ROWS, width), BF16)],
        9, 3, 8 * rows * width * width, 10_000_000, "attend_weights",
    )(h, h_x, shared, shared_x, grads, away_x, small)


def add_kernel(shapes, pieces, *refs):
    count = len(shapes)
    keeps, refs = (refs[0:count], refs[count:])
    parts, refs = (refs[0 : sum(pieces)], refs[sum(pieces) :])
    *rest, in_sem, out_sem = refs
    out_count = sum(1 if spots == 1 else 2 for spots, _, _ in shapes)
    outs, holds = (list(rest[:out_count]), list(rest[out_count:]))
    keep_s, part_s, total_s = (holds[0:count], holds[count : 2 * count], holds[2 * count :])
    loads = Loads(in_sem)
    store = Stores(out_sem)
    at = 0
    waits = []
    for index in range(count):
        loads.start(("keep", index), keeps[index], keep_s[index])
        names = [("keep", index)]
        row = 0
        for piece in range(pieces[index]):
            height = parts[at].shape[1]
            loads.start(("part", index, piece), parts[at], part_s[index].at[:, row : row + height])
            names.append(("part", index, piece))
            row += height
            at += 1
        waits.append(names)
    place = 0
    for index, (spots, rows, _) in enumerate(shapes):
        loads.wait(*waits[index])
        if spots == 1:
            total_s[index][...] = keep_s[index][0].astype(F32) + part_s[index][0].astype(F32)
            store.start(total_s[index], outs[place])
            place += 1
            continue

        def one(spot, carry, index=index):
            total_s[index][spot] = (keep_s[index][spot].astype(F32) + part_s[index][spot].astype(F32)).astype(BF16)
            return carry

        lax.fori_loop(0, spots, one, 0)
        store.start(total_s[index].at[spots // 2 : spots], outs[place])
        store.start(total_s[index].at[0 : spots // 2], outs[place + 1])
        place += 2
    store.wait()


def add_arrived(pairs, flops, limit):
    shapes = [keep.shape for keep, _ in pairs]
    pieces = [len(arrived) for _, arrived in pairs]
    outs = []
    totals = []
    for spots, rows, width in shapes:
        if spots > 1:
            outs.extend([S((spots // 2, rows, width), BF16)] * 2)
            totals.append(V((spots, rows, width), BF16))
        else:
            outs.append(S((rows, width), F32))
            totals.append(V((rows, width), F32))
    count = len(pairs) + sum(pieces)
    results = list(
        pl.pallas_call(
            functools.partial(add_kernel, shapes, pieces),
            out_shape=tuple(outs),
            in_specs=[ANY] * count,
            out_specs=(ANY,) * len(outs),
            scratch_shapes=[V(shape, BF16) for shape in shapes] * 2 + totals
            + [pltpu.SemaphoreType.DMA((count,)), pltpu.SemaphoreType.DMA((len(outs),))],
            compiler_params=pltpu.CompilerParams(vmem_limit_bytes=limit),
            cost_estimate=pl.CostEstimate(flops=flops, bytes_accessed=1000, transcendentals=0),
            name="add_arrived",
        )(*[keep for keep, _ in pairs], *[part for _, arrived in pairs for part in arrived])
    )
    return [(results.pop(0),) if spots == 1 else (results.pop(0), results.pop(0)) for spots, _, _ in shapes]


TAIL_LIMIT = 24_000 * 1024


def finish_kernel(feed_one, feed_two, tail_one, tail_two, feed_one_x, feed_two_x, tail_one_x, tail_two_x, q_o, k_o, v_o, m_o, i_o, o_o, small_o, wide_o):
    section = lax.axis_index("section")
    groups = lax.axis_size("dp")
    me = lax.axis_index("dp")
    height, width = q_o.shape
    half_rows = o_o.shape[0] // 2
    hidden = i_o.shape[1]
    for core in range(2):
        @pl.when(section == core)
        def _(core=core):
            mine, back = ((feed_one, tail_one), (feed_one_x, tail_one_x)) if core == 0 else ((feed_two, tail_two), (feed_two_x, tail_two_x))
            sides = (mine, back) if core == 0 else (back, mine)
            half = width // 2
            for side, (feed, _) in enumerate(sides):
                for part in range(2):
                    o_o[part * half_rows : (part + 1) * half_rows, side * half : (side + 1) * half] = feed[
                        0:half_rows, part * half : (part + 1) * half
                    ]
                    i_o[:, (2 * side + part) * width : (2 * side + part + 1) * width] = feed[
                        half_rows + part * height : half_rows + (part + 1) * height, :
                    ]
            q_o[...] = sides[0][1][0:height, :]
            k_o[...] = sides[0][1][height : 2 * height, :]
            v_o[...] = sides[1][1][0:height, :]
            m_o[...] = sides[1][1][height : 2 * height, :]
            lines = mine[1][2 * height : 2 * height + SMALL_ROWS, :]
            small_o[...] = pltpu.roll(lines[0:8, :], lax.rem(width - me * height, width), 1)
            span = hidden // groups
            each = width // span
            pick = lax.broadcasted_iota(jnp.int32, (8, width), 0) == lax.div(me, each)
            chosen = jnp.sum(jnp.where(pick, lines[8:16, :], 0.0), axis=0, keepdims=True)
            wide_o[...] = pltpu.roll(jnp.broadcast_to(chosen, (8, width)), lax.rem(width - lax.rem(me, each) * span, width), 1)


def finish(groups, width, hidden, results):
    height = width // groups
    square = S((height, width), F32)
    return pl.pallas_call(
        finish_kernel,
        out_shape=(square, square, square, square, S((height, hidden), F32), S((hidden // groups, width), F32), S((8, width), F32), S((8, width), F32)),
        in_specs=[VM] * 8,
        out_specs=(VM,) * 8,
        compiler_params=pltpu.CompilerParams(vmem_limit_bytes=TAIL_LIMIT),
        name="finish_gradients",
    )(*results)


def exchange(value, bits):
    groups = lax.axis_size("dp")
    pairs = [(2 * group + core, 2 * (group ^ (1 << bits[core])) + core) for group in range(groups) for core in range(2)]
    return lax.ppermute(value, ("dp", "section"), pairs)


def swap(value):
    return lax.ppermute(value, "section", [(0, 1), (1, 0)])


F1, T1, F0, T0 = (("f", 1), ("t", 1), ("f", 0), ("t", 0))
NEAR_FIRST = {F1: False, T1: True, F0: False, T0: False}
TOGETHER = (F0,)
WEIGHED = (50_000_000_000,) * 8 + (6_000_000_000,) + (1000,) * 4
SCHEDULE = (
    (),
    (),
    (),
    (F1,),
    (F1,),
    (),
    (F1,),
    (F1, F0, T1),
    (F1, T1, F0),
    (F0, T1, T0),
    (F0, T1, T0),
    (T0,),
    (T1, T0),
)


def widen(value):
    return value.astype(F32)


def per_device(
    tokens, cotangent, bucket, batch_size, lengths, query_weight, query_offset, keys_weight, value_weight, value_offset,
    mixer_weight, mixer_offset, first_gain, first_shift, inner_weight, inner_offset, outer_weight, outer_offset,
    second_gain, second_shift,
):
    section = lax.axis_index("section")
    groups = lax.axis_size("dp")
    width = tokens.shape[2]
    hidden = inner_offset.shape[1]
    hypercube = groups == 16
    spots = groups if hypercube else 1
    first = section == 0
    meta = (bucket, batch_size, lengths)
    weights = (query_weight, keys_weight, value_weight, mixer_weight, inner_weight, outer_weight)
    vectors = (query_offset, value_offset, mixer_offset, first_gain, first_shift, outer_offset, second_gain, second_shift)
    others = tuple(swap(weight) for index, weight in enumerate(weights) if index != 3)
    y_first, shared_first, own_first, own_handed, packed, vec_own = first_forward(meta, tokens, weights, vectors, inner_offset)
    handed, packed, others = lax.optimization_barrier((y_first, packed, others))
    y_x = swap(handed)
    others = others + (swap(packed),)
    y_second, shared_second, own_second = second_forward(meta, y_first, y_x, weights, others, vec_own)
    shared_x = swap(lax.optimization_barrier((shared_first, y_x, others[-1]))[0])
    own_second, shared_x = lax.optimization_barrier((own_second, shared_x))
    own = {1: (own_second, own_second)}
    shared = {0: (shared_first, shared_x), 1: (shared_second, swap(shared_second))}
    entries = {1: (y_first, y_x), 0: (tokens, tokens)}
    y_last_x = swap(y_second)
    moving = {}
    results = {}

    def boundary(turn, value, other):
        names = SCHEDULE[turn] if hypercube else ()
        if not names:
            return value, other
        landed = {name: moving[name][1] for name in names}
        other, landed = lax.optimization_barrier((other, landed))
        ready = []
        for name in names:
            keep, _, waiting, arrived, step = moving[name]
            arrived = arrived + landed[name]
            if waiting:
                moving[name] = (keep, None, waiting[1:], arrived, step)
                ready.append(name)
            else:
                moving[name] = (keep, None, [], arrived, step + 1)
        done = [name for name in names if name not in ready]
        if done:
            added = add_arrived([(moving[name][0], moving[name][3]) for name in done], WEIGHED[turn], VMEM_LIMIT if turn < 10 else TAIL_LIMIT)
            value, added = lax.optimization_barrier((value, added))
            for name, parts in zip(done, added):
                step = moving[name][4]
                if len(parts) == 1:
                    results[name] = parts[0]
                else:
                    moving[name] = (parts[1], [exchange(parts[0], step_bits(NEAR_FIRST[name])[step])], [], [], step)
        else:
            value = lax.optimization_barrier((value, landed))[0]
        for name in ready:
            keep, _, waiting, arrived, step = moving[name]
            piece = pieces[name].pop(0)
            piece = lax.optimization_barrier((piece, landed, value))[0]
            moving[name] = (keep, [exchange(piece, step_bits(NEAR_FIRST[name])[0])], waiting, arrived, step)
        return value, other

    pieces = {}

    def begin(name, sends, keep):
        if hypercube:
            pieces[name] = [] if name in TOGETHER else list(sends[1:])
            flying = [exchange(send, step_bits(NEAR_FIRST[name])[0]) for send in sends[: len(sends) - len(pieces[name])]]
            moving[name] = (keep, flying, list(pieces[name]), [], 0)
        else:
            moving[name] = sends

    def feed(layer, grad):
        return feed_gradient(layer, meta, grad, *own[layer], weights, others, vec_own)

    def feed_sum(layer, dz, df, away_x):
        *sends, keep = feed_weights(layer, False, spots, *shared[layer], dz, df, away_x)
        begin(F1 if layer else F0, sends, keep)
        return keep

    def attend(layer, dc, da, da1, small):
        return attend_gradient(layer, meta, *own[layer], dc, da, da1, weights, others, small)

    def attend_sum(layer, grads, away_x, small):
        name = T1 if layer else T0
        *sends, keep = attend_weights(layer, NEAR_FIRST[name], spots, layer == 1 and hypercube, *entries[layer], *shared[layer], grads, away_x, small)
        begin(name, sends, keep)
        return keep

    def tie(value, other):
        return lax.optimization_barrier((value, other))[0]

    dh = {}
    low_gradient = {}
    dz, df, away, da1, da, dc, small_feed = feed(1, cotangent)
    held = feed_sum(1, dz, df, swap(away))
    own[0] = (own_first, swap(tie(own_handed, held)))
    dh[1], low_gradient[1], grads, away, small = attend(1, tie(dc, held), da, da1, small_feed)
    dh_one_x = swap(low_gradient[1])
    attend_away_x = swap(away)
    grad, _ = boundary(3, low_gradient[1], held)
    dz, df, away, da1, da, dc, small_feed = feed(0, grad)
    dz, dh_one_x, y_last_x = lax.optimization_barrier((dz, dh_one_x, y_last_x))
    grads, away = boundary(4, tie(grads, dz), away)
    feed_away_x = swap(away)
    held = attend_sum(1, grads, attend_away_x, small)
    dz, _ = boundary(5, tie(dz, held), held)
    held = feed_sum(0, dz, df, feed_away_x)
    dc, _ = boundary(6, tie(dc, held), held)
    dh[0], low_gradient[0], grads, away, small = attend(0, dc, da, da1, small_feed)
    grads, away = boundary(7, grads, away)
    held = attend_sum(0, grads, swap(away), small)
    def outputs_of_rows(y_first, y_last_x, y_second, dh, dh_one_x, low):
        layer_out = jnp.stack([jnp.where(first, y_first[0], y_last_x[0]), jnp.where(first, y_first[1], y_second[0])])
        dh_zero_x = swap(low)
        input_grad = jnp.stack([jnp.where(first, dh[0], widen(dh_one_x)), jnp.where(first, widen(dh_zero_x), dh[1])])
        return layer_out, input_grad

    pieces_of_rows = (y_first, y_last_x, y_second, dh, dh_one_x, low_gradient[0])
    if hypercube:
        for turn in range(8, len(SCHEDULE)):
            if turn == 10:
                layer_out, input_grad = outputs_of_rows(*pieces_of_rows)
                pieces_of_rows = (layer_out, input_grad)
            pieces_of_rows, held = boundary(turn, pieces_of_rows, held)
        layer_out, input_grad = pieces_of_rows
        order = (F0, F1, T0, T1)
        done = finish(groups, width, hidden, [results[name] for name in order] + [swap(results[name]) for name in order])
        query_grad, keys_grad, value_grad, mixer_grad, inner_grad, outer_grad, lines, wide_line = done
        height = width // groups
        small = [lines[index, :height] for index in range(8)]
        small_wide = wide_line[0, : hidden // groups]
    else:
        layer_out, input_grad = outputs_of_rows(*pieces_of_rows)

        def scatter(value):
            return lax.psum_scatter(value, "dp", scatter_dimension=0, tiled=True).astype(F32)

        found = []
        for layer in (1, 0):
            outer_part, inner_part = (value[0] for value in moving["f", layer])
            attend = moving["t", layer][0][0]
            half = width // 2
            outer_half = jnp.concatenate([outer_part[:, :half], outer_part[:, half:]], axis=0)
            parts = [scatter(outer_half), scatter(inner_part[:width]), scatter(inner_part[width:])]
            parts += [scatter(attend[:width]), scatter(attend[width : 2 * width])]
            lines = attend[2 * width :].astype(F32)
            parts += [scatter(lines[index]) for index in range(8)] + [scatter(lines[8:12].reshape(-1))]
            found.append(parts)
        mine = [jnp.where(first, b, a) for a, b in zip(*found)]
        back = [swap(jnp.where(first, a, b)) for a, b in zip(found[0][:5], found[1][:5])]
        low = [jnp.where(first, a, b) for a, b in zip(mine, back)]
        high = [jnp.where(first, b, a) for a, b in zip(mine, back)]
        outer_grad = jnp.concatenate([low[0], high[0]], axis=1)
        inner_grad = jnp.concatenate([low[1], low[2], high[1], high[2]], axis=1)
        query_grad, keys_grad, value_grad, mixer_grad = (low[3], low[4], high[3], high[4])
        small, small_wide = (mine[5:13], mine[13])
    second_gain_grad, second_shift_grad, outer_offset_grad, first_gain_grad, first_shift_grad, mixer_offset_grad = small[:6]
    outputs = (
        layer_out, input_grad, query_grad, small[6], keys_grad, value_grad, small[7], mixer_grad, mixer_offset_grad,
        first_gain_grad, first_shift_grad, inner_grad, small_wide, outer_grad, outer_offset_grad, second_gain_grad,
        second_shift_grad,
    )
    return tuple(piece[None] for piece in outputs)


def solution(mesh):
    matrix = P("section", None, None)
    vector = P("section", None)
    in_specs = (
        P("dp", None, None), P("dp", None, None), P("dp"), P("dp"), P("dp", None), matrix, vector, matrix, matrix, vector,
        matrix, vector, vector, vector, matrix, vector, matrix, vector, vector, vector,
    )
    rows = P("section", "dp", None, None)
    grad = P("section", "dp", None)
    small = P("section", "dp")
    out_specs = (rows, rows, grad, small, grad, grad, small, grad, small, small, small, grad, small, grad, small, small, small)
    return jax.shard_map(per_device, mesh=mesh, in_specs=in_specs, out_specs=out_specs, check_vma=False)
```
